32 devices in a mesh: shard: 2 (over x), context: 4 (over y, core), tensor: 4 (over z).
Axes of the slice: x: 2, y: 2, z: 4, core: 2. Of those that a mesh axis runs over, the one named last changes fastest.
Arguments:
- tokens: bfloat16 [2, 2048, 2048], P('shard', 'context'), may hold values from -6 to 6
- block_order: int32 [2, 8], P('shard'), may hold values from 0 to 7, each once within a row
- w_query: bfloat16 [2048, 2048], P(('shard', 'context'), 'tensor'), may hold values from -0.5 to 0.5
- w_key: bfloat16 [2048, 512], P(('shard', 'context'), 'tensor'), may hold values from -0.5 to 0.5
- w_value: bfloat16 [2048, 512], P(('shard', 'context'), 'tensor'), may hold values from -0.125 to 0.125
- w_output: bfloat16 [2048, 2048], P('tensor', ('shard', 'context')), may hold values from -1.5 to 1.5
- w_gate: bfloat16 [2048, 8192], P(('shard', 'context'), 'tensor'), may hold values from -0.125 to 0.125
- w_up: bfloat16 [2048, 8192], P(('shard', 'context'), 'tensor'), may hold values from -0.125 to 0.125
- w_down: bfloat16 [8192, 2048], P('tensor', ('shard', 'context')), may hold values from -0.5 to 0.5
- norm_attn: bfloat16 [2048], P(('shard', 'context')), may hold values from 0.5 to 1.5
- norm_ffn: bfloat16 [2048], P(('shard', 'context')), may hold values from 0.5 to 1.5
- grad_out: bfloat16 [2, 2048, 2048], P('shard', 'context'), may hold values from -6 to 6
Outputs:
- layer_out: bfloat16 [2, 2048, 2048], P('shard', 'context')
- grad_tokens: float32 [2, 2048, 2048], P('shard', 'context')
- grad_w_query: float32 [2048, 2048], P(('shard', 'context'), 'tensor')
- grad_w_key: float32 [2048, 512], P(('shard', 'context'), 'tensor')
- grad_w_value: float32 [2048, 512], P(('shard', 'context'), 'tensor')
- grad_w_output: float32 [2048, 2048], P('tensor', ('shard', 'context'))
- grad_w_gate: float32 [2048, 8192], P(('shard', 'context'), 'tensor')
- grad_w_up: float32 [2048, 8192], P(('shard', 'context'), 'tensor')
- grad_w_down: float32 [8192, 2048], P('tensor', ('shard', 'context'))
- grad_norm_attn: float32 [2048], P(('shard', 'context'))
- grad_norm_ffn: float32 [2048], P(('shard', 'context'))
The draws below stay inside these ranges and needn't reach their ends.
Inputs may be any that keep to these rules, and one draw needn't show every extreme that they name: Each row is a permutation of the 8 blocks of its sequence; stored block j of sequence s holds the tokens of block block_order[s, j].
All inputs are finite; a program needn't handle non-finite values.
Results may differ from the reference program's by a relative error of at most 0.015.
Values may be sent and summed in bfloat16 or wider, within the bound.
A program may use at most 192 MiB of HBM per device.

```python
import math
import jax
import jax.numpy as jnp
from jax import lax

D = 2048
HEADS = 32
KV = 8
HD = 64
FF = 8192
LEN = 2048
BLK = 256
NBLK = 8
SEQ_ALL = 2


def levels(rng, extent, pieces, smallest, high):
    level = 1.0
    for dim, parts in pieces:
        heights = jax.random.uniform(jax.random.fold_in(jax.random.fold_in(rng, 6), dim), (parts,), jnp.float32, smallest / len(pieces), high / len(pieces))
        level = level * jnp.repeat(jnp.exp(heights), extent[dim] // parts).reshape((-1,) + (1,) * (len(extent) - 1 - dim))
    return level


def gaussian(own_key, extent, scale, reach, cuts=(), kind=jnp.bfloat16):
    values = jax.random.normal(own_key, extent, jnp.float32) * scale
    if len(cuts) > 0:
        values = levels(own_key, extent, cuts, -0.22, 0.18) * values
    return jnp.clip(values, min=-reach, max=reach).astype(kind)


def setup_inputs(seed: int = 0) -> dict:
    key_of = jax.random.split(jax.random.key(seed), 13)
    return {
        "tokens": gaussian(key_of[0], (SEQ_ALL, LEN, D), 1.0, 6.0, ((0, 2), (1, 4))),
        "block_order": jax.vmap(lambda own: jax.random.permutation(own, NBLK))(jax.random.split(key_of[1], SEQ_ALL)).reshape((SEQ_ALL, NBLK)).astype(jnp.int32),
        "w_query": gaussian(key_of[2], (D, HEADS * HD), (D // 16) ** -0.5, 0.5, ((0, 8), (1, 4))),
        "w_key": gaussian(key_of[3], (D, KV * HD), (D // 16) ** -0.5, 0.5, ((0, 8), (1, 4))),
        "w_value": gaussian(key_of[4], (D, KV * HD), D ** -0.5, 0.125, ((0, 8), (1, 4))),
        "w_output": gaussian(key_of[5], (HEADS * HD, D), (max(D // 128, 1)) ** -0.5, 1.5, ((0, 4), (1, 8))),
        "w_gate": gaussian(key_of[6], (D, FF), D ** -0.5, 0.125, ((0, 8), (1, 4))),
        "w_up": gaussian(key_of[7], (D, FF), D ** -0.5, 0.125, ((0, 8), (1, 4))),
        "w_down": gaussian(key_of[8], (FF, D), (max(FF // 64, 1)) ** -0.5, 0.5, ((0, 4), (1, 8))),
        "norm_attn": jnp.clip(1.0 + 0.1 * jax.random.normal(key_of[9], (D,), jnp.float32), 0.5, 1.5).astype(jnp.bfloat16),
        "norm_ffn": jnp.clip(1.0 + 0.1 * jax.random.normal(key_of[10], (D,), jnp.float32), 0.5, 1.5).astype(jnp.bfloat16),
        "grad_out": gaussian(key_of[11], (SEQ_ALL, LEN, D), 1.0, 6.0, ((0, 2), (1, 4))),
    }


EPSILON = 1e-05
SCORE_SCALE = 0.015625
RESIDUAL_SCALE = 0.22
ROPE_BASE = 10000000.0
MASKED_SCORE = -1e+30

@jax.custom_vjp
def low(v):
    return lax.optimization_barrier(v.astype(jnp.bfloat16)).astype(jnp.float32)

@jax.custom_vjp
def low_back(v):
    return v

def low_keep(v):
    return (low(v), None)

def low_pass(kept, grad):
    return (grad,)

def back_keep(v):
    return (v, None)

def back_low(kept, grad):
    return (low(grad),)
low.defvjp(low_keep, low_pass)
low_back.defvjp(back_keep, back_low)

def positions(order_row):
    offsets = jnp.arange(BLK, dtype=jnp.int32)
    return (order_row[:, None] * BLK + offsets[None, :]).reshape(-1)

def rope_tables(placed):
    half_dim = HD // 2
    inverse = jnp.exp(jnp.arange(half_dim, dtype=jnp.float32) * (-2.0 * math.log(ROPE_BASE) / HD))
    angles = placed.astype(jnp.float32)[:, None] * inverse[None, :]
    angles = jnp.concatenate([angles, angles], axis=1)
    return (jnp.cos(angles), jnp.sin(angles))

def rotate(values, cosine, sine):
    half_dim = values.shape[-1] // 2
    turned = jnp.concatenate([-values[..., half_dim:], values[..., :half_dim]], axis=-1)
    return values * cosine[:, None, :] + turned * sine[:, None, :]

def rms_norm(values, gain):
    return values * lax.rsqrt(lax.optimization_barrier(jnp.mean(values * values, axis=-1, keepdims=True)) + EPSILON) * gain

def matmul_hi(left, right):
    return jnp.dot(left, right, precision=lax.Precision.HIGHEST)

def attend_group(queries, key_rows, values, allowed):
    products = jnp.einsum('gqd,kd->gqk', queries, key_rows, precision=lax.Precision.HIGHEST)
    scores = low_back(SCORE_SCALE * products)
    scores = jnp.where(allowed[None], scores, MASKED_SCORE)
    row_max = lax.optimization_barrier(jnp.max(scores, axis=-1, keepdims=True))
    exponent = jnp.exp(scores - row_max)
    soft_weights = exponent / lax.optimization_barrier(jnp.sum(exponent, axis=-1, keepdims=True))
    return jnp.einsum('gqk,kd->gqd', low(soft_weights), values, precision=lax.Precision.HIGHEST)

def sequence_layer(tokens, order_row, weight_set):
    w_query, w_key, w_value, w_output, w_gate, w_up, w_down, norm_attn, norm_ffn = weight_set
    placed = positions(order_row)
    cosine, sine = rope_tables(placed)
    blocks = placed // BLK
    allowed = blocks[None, :] <= blocks[:, None]
    head_count = w_query.shape[1] // HD
    kv_count = w_key.shape[1] // HD
    group_size = head_count // kv_count
    length = tokens.shape[0]
    normed = low(rms_norm(tokens, norm_attn))
    queries = low_back(matmul_hi(normed, w_query)).reshape(length, head_count, HD)
    key_rows = low_back(matmul_hi(normed, w_key)).reshape(length, kv_count, HD)
    values = low(low_back(matmul_hi(normed, w_value))).reshape(length, kv_count, HD)
    queries = low(rotate(queries, cosine, sine))
    key_rows = low(rotate(key_rows, cosine, sine))
    grouped = queries.reshape(length, kv_count, group_size, HD).transpose(1, 2, 0, 3)
    step_fn = jax.checkpoint(lambda packed: attend_group(packed[0], packed[1], packed[2], allowed))
    mixture = lax.map(step_fn, (grouped, key_rows.transpose(1, 0, 2), values.transpose(1, 0, 2)))
    mixture = mixture.transpose(2, 0, 1, 3).reshape(length, head_count * HD)
    mixture = low(low_back(mixture))
    branch = low_back(matmul_hi(mixture, w_output))
    hidden = tokens + RESIDUAL_SCALE * branch
    normed_ffn = low(rms_norm(hidden, norm_ffn))
    gate_in = low_back(matmul_hi(normed_ffn, w_gate))
    upward = low_back(matmul_hi(normed_ffn, w_up))
    active = low(jax.nn.silu(gate_in) * upward)
    ffn_out = low_back(matmul_hi(active, w_down))
    return hidden + RESIDUAL_SCALE * ffn_out

def whole_layer(tokens, order, weight_set):
    step_fn = jax.checkpoint(lambda packed: sequence_layer(packed[0], packed[1], weight_set))
    return lax.map(step_fn, (tokens, order))

def reference(tokens, block_order, w_query, w_key, w_value, w_output, w_gate, w_up, w_down, norm_attn, norm_ffn, grad_out):

    def forward(inputs, f_query, f_key, f_value, f_output, f_gate, f_up, f_down, f_norm_attn, f_norm_ffn):
        return whole_layer(inputs, block_order, (f_query, f_key, f_value, f_output, f_gate, f_up, f_down, f_norm_attn, f_norm_ffn))
    layer_out, pull_back = jax.vjp(forward, tokens.astype(jnp.float32), w_query.astype(jnp.float32), w_key.astype(jnp.float32), w_value.astype(jnp.float32), w_output.astype(jnp.float32), w_gate.astype(jnp.float32), w_up.astype(jnp.float32), w_down.astype(jnp.float32), norm_attn.astype(jnp.float32), norm_ffn.astype(jnp.float32))
    grads = pull_back(grad_out.astype(jnp.float32))
    return (layer_out.astype(jnp.bfloat16), grads[0], grads[1], grads[2], grads[3], grads[4], grads[5], grads[6], grads[7], grads[8], grads[9])
```

```python
import functools
import math

import jax
import jax.numpy as jnp
from jax import lax
from jax.experimental import pallas as pl
from jax.experimental.pallas import tpu as pltpu
from jax.sharding import PartitionSpec as P

HD = 64
BLK = 256
LANES = 128
EPSILON = 1e-05
SCORE_SCALE = 0.015625
RESIDUAL_SCALE = 0.22
ROPE_BASE = 10000000.0
MASKED_SCORE = -1e30
PLANE = ("shard", "context")
VMEM_BYTES = 64000 * 1024


F32 = jnp.float32
BF16 = jnp.bfloat16


def plane_size():
    return lax.axis_size("shard") * lax.axis_size("context")


def plane_index():
    return lax.axis_index("shard") * lax.axis_size("context") + lax.axis_index("context")


def swap(value, axes, size, bit):
    return lax.ppermute(value, axes, [(i, i ^ bit) for i in range(size)])


def gather_pair(first, second):
    size = plane_size()
    bits = [1 << b for b in range(1, size.bit_length() - 1)]
    sides = [{0: first}, {0: second}]
    if len(bits) == 2:
        near, far = bits
        for side in sides:
            side[near] = swap(side[0], PLANE, size, near)
            side[far] = swap(side[0], PLANE, size, far)
        sides[0][near | far] = swap(sides[0][far], PLANE, size, near)
        sides[1][near | far] = swap(sides[1][near], PLANE, size, far)
    else:
        for side in sides:
            for bit in bits:
                for r in list(side):
                    side[r | bit] = swap(side[r], PLANE, size, bit)
    for side in sides:
        for r in list(side):
            side[r | 1] = swap(side[r], PLANE, size, 1)
    return [[side[r] for r in range(size)] for side in sides]


def widened(pieces):
    level = 1
    while pieces[0].shape[1] < LANES:
        upper = (plane_index() // level) % 2 == 1
        pairs = zip(pieces[0::2], pieces[1::2])
        pieces = [jnp.where(upper, jnp.concatenate([b, a], 1), jnp.concatenate([a, b], 1)) for a, b in pairs]
        level *= 2
    return pieces


def reduce_pair(first, second):
    size = plane_size()
    bits = [1 << b for b in range(1, size.bit_length() - 1)]
    sides = [dict(enumerate(first)), dict(enumerate(second))]

    def take(side, bit, kept):
        return side[kept].astype(F32) + swap(side[kept | bit].astype(BF16), PLANE, size, bit).astype(F32)

    sides = [{r: take(side, 1, r) for r in range(0, size, 2)} for side in sides]
    if len(bits) == 2:
        near, far = bits
        sides[0][near] = take(sides[0], far, near)
        sides[1][far] = take(sides[1], near, far)
        done = []
        for side in sides:
            a = swap(side[near].astype(BF16), PLANE, size, near).astype(F32)
            b = swap(side[far].astype(BF16), PLANE, size, far).astype(F32)
            done.append(side[0] + a + b)
        return done
    done = []
    for side in sides:
        for bit in reversed(bits):
            side = {r: take(side, bit, r) for r in side if not r & bit}
        done.append(side[0])
    return done


def gather_small(values):
    size = plane_size()
    stacked = values[None]
    bit = 1
    while bit < size:
        stacked = jnp.concatenate([stacked, swap(stacked, PLANE, size, bit)], axis=0)
        bit *= 2
    picks = jnp.arange(size, dtype=jnp.int32)[:, None] ^ plane_index()
    chosen = (picks == jnp.arange(size, dtype=jnp.int32)[None, :]).astype(F32)
    return jnp.einsum("ij,jkw->kiw", chosen, stacked.astype(F32), precision=lax.Precision.HIGHEST)


def chunk_of(rows, index, count):
    return lax.dynamic_slice_in_dim(rows, index * count, count, 0)


def rows_sum(partial):
    size = lax.axis_size("tensor")
    me = lax.axis_index("tensor")
    count = partial.shape[0] // size
    total = chunk_of(partial, me, count).astype(F32)
    for shift in range(1, size):
        sent = chunk_of(partial, lax.rem(me + shift, size), count)
        pairs = [(i, (i + shift) % size) for i in range(size)]
        total = total + lax.ppermute(sent, "tensor", pairs).astype(F32)
    return total


def rows_gather(chunk):
    size = lax.axis_size("tensor")
    me = lax.axis_index("tensor")
    count = chunk.shape[0]
    parts = [chunk]
    for shift in range(1, size):
        pairs = [(i, (i + shift) % size) for i in range(size)]
        parts.append(lax.ppermute(chunk, "tensor", pairs))
    whole = jnp.zeros((size * count,) + chunk.shape[1:], chunk.dtype)
    for shift in range(size):
        place = lax.rem(me - shift + size, size) * count
        whole = lax.dynamic_update_slice_in_dim(whole, parts[shift], place, 0)
    return whole


def params(steps):
    return pltpu.CompilerParams(
        dimension_semantics=("arbitrary",) * steps, vmem_limit_bytes=VMEM_BYTES
    )


def place_pieces(pieces, whole, sem, axis):
    size = len(pieces)
    me = plane_index() // (plane_size() // size)
    extent = whole.shape[axis] // size
    for r, piece in enumerate(pieces):
        start = pl.multiple_of((me ^ r) * extent, extent)
        target = whole.at[pl.ds(start, extent)] if axis == 0 else whole.at[:, pl.ds(start, extent)]
        pltpu.make_async_copy(piece, target, sem).start()


def await_whole(whole, sem):
    pltpu.make_async_copy(whole, whole, sem).wait()


ANYWHERE = pl.BlockSpec(memory_space=pl.ANY)


def turned(values, lane, sign):
    half = HD // 2
    upper = pltpu.roll(values, LANES - half, 1)
    lower = pltpu.roll(values, half, 1)
    return jnp.where(lane % HD < half, -sign * upper, sign * lower)


def qkv_body(count, scale_lanes, tokens, gain, cosine, sine, *rest):
    pieces, (normed, queries, keys_values, weight, sem) = rest[:count], rest[count:]

    @pl.when(pl.program_id(0) == 0)
    def _():
        place_pieces(pieces, weight, sem, 0)

    values = tokens[...].astype(F32)
    inverse = lax.rsqrt(jnp.mean(values * values, axis=1, keepdims=True) + EPSILON)
    low = (values * inverse * gain[...]).astype(BF16)
    normed[...] = low

    @pl.when(pl.program_id(0) == 0)
    def _():
        await_whole(weight, sem)

    cos, sin = cosine[...], sine[...]
    lane = lax.broadcasted_iota(jnp.int32, cos.shape, 1)
    q_width = queries.shape[1]
    k_width = keys_values.shape[1] // 2
    for start in range(0, weight.shape[1], LANES):
        part = jnp.dot(low, weight[:, start : start + LANES * 1], preferred_element_type=F32)
        if start < q_width + k_width:
            part = part * cos + turned(part, lane, 1.0) * sin
        if start < q_width:
            queries[:, start : start + LANES] = (part.astype(BF16) * SCORE_SCALE).astype(BF16)
        else:
            keys_values[:, start - q_width : start - q_width + LANES] = part.astype(BF16)


def project_qkv(tokens, gain, cosine, sine, pieces, q_width):
    rows, width = tokens.shape
    total = pieces[0].shape[1]
    tile = min(rows, 256)
    row_spec = lambda w: pl.BlockSpec((tile, w), lambda i: (i, 0))
    return pl.pallas_call(
        functools.partial(qkv_body, len(pieces), q_width),
        grid=(rows // tile,),
        in_specs=[row_spec(width), pl.BlockSpec((1, width), lambda i: (0, 0)), row_spec(LANES), row_spec(LANES)]
        + [ANYWHERE] * len(pieces),
        out_specs=[row_spec(width), row_spec(q_width), row_spec(total - q_width)],
        out_shape=[
            jax.ShapeDtypeStruct((rows, width), BF16),
            jax.ShapeDtypeStruct((rows, q_width), BF16),
            jax.ShapeDtypeStruct((rows, total - q_width), BF16),
        ],
        scratch_shapes=[pltpu.VMEM((width, total), BF16), pltpu.SemaphoreType.DMA],
        compiler_params=params(1),
        cost_estimate=pl.CostEstimate(
            flops=2 * rows * width * total, bytes_accessed=2 * (2 * rows * width + width * total), transcendentals=0
        ),
        name="project_qkv",
    )(tokens, gain, cosine, sine, *pieces)


def qkv_back_body(count, d_queries, d_keys_values, cosine, sine, *rest):
    pieces, (d_all, d_normed, weight, sem) = rest[:count], rest[count:]

    @pl.when(pl.program_id(0) == 0)
    def _():
        place_pieces(pieces, weight, sem, 0)

    cos, sin = cosine[...], sine[...]
    lane = lax.broadcasted_iota(jnp.int32, cos.shape, 1)
    q_width = d_queries.shape[1]
    k_width = d_keys_values.shape[1] // 2
    for start in range(0, d_all.shape[1], LANES):
        if start < q_width:
            part = d_queries[:, start : start + LANES]
        else:
            part = d_keys_values[:, start - q_width : start - q_width + LANES]
        if start < q_width + k_width:
            part = part * cos + turned(part * sin, lane, -1.0)
        d_all[:, start : start + LANES] = part.astype(BF16)

    @pl.when(pl.program_id(0) == 0)
    def _():
        await_whole(weight, sem)

    step = 512
    for start in range(0, weight.shape[0], step):
        d_normed[:, start : start + step] = lax.dot_general(
            d_all[...], weight[start : start + step, :], (((1,), (1,)), ((), ())), preferred_element_type=F32
        ).astype(BF16)


def project_qkv_back(d_queries, d_keys_values, cosine, sine, pieces):
    rows, q_width = d_queries.shape
    total = pieces[0].shape[1]
    width = pieces[0].shape[0] * len(pieces)
    tile = min(rows, 256)
    row_spec = lambda w: pl.BlockSpec((tile, w), lambda i: (i, 0))
    return pl.pallas_call(
        functools.partial(qkv_back_body, len(pieces)),
        grid=(rows // tile,),
        in_specs=[row_spec(q_width), row_spec(total - q_width), row_spec(LANES), row_spec(LANES)]
        + [ANYWHERE] * len(pieces),
        out_specs=[row_spec(total), row_spec(width)],
        out_shape=[jax.ShapeDtypeStruct((rows, total), BF16), jax.ShapeDtypeStruct((rows, width), BF16)],
        scratch_shapes=[pltpu.VMEM((width, total), BF16), pltpu.SemaphoreType.DMA],
        compiler_params=params(1),
        cost_estimate=pl.CostEstimate(
            flops=2 * rows * width * total, bytes_accessed=2 * (2 * rows * width + width * total), transcendentals=0
        ),
        name="project_qkv_back",
    )(d_queries, d_keys_values, cosine, sine, *pieces)


def gathered_body(count, axis, transposed, left, *rest):
    pieces, (out, weight, sem) = rest[:count], rest[count:]

    @pl.when(pl.program_id(0) == 0)
    def _():
        place_pieces(pieces, weight, sem, axis)
        await_whole(weight, sem)

    step = min(out.shape[1], 512)
    for start in range(0, out.shape[1], step):
        if transposed:
            part = lax.dot_general(
                left[...], weight[start : start + step, :], (((1,), (1,)), ((), ())), preferred_element_type=F32
            )
        else:
            part = jnp.dot(left[...], weight[:, start : start + step], preferred_element_type=F32)
        out[:, start : start + step] = part.astype(out.dtype)


def gathered_matmul(left, pieces, axis, transposed, name):
    rows = left.shape[0]
    shape = list(pieces[0].shape)
    shape[axis] *= len(pieces)
    outer = shape[0] if transposed else shape[1]
    tile = min(rows, 256)
    return pl.pallas_call(
        functools.partial(gathered_body, len(pieces), axis, transposed),
        grid=(rows // tile,),
        in_specs=[pl.BlockSpec((tile, left.shape[1]), lambda i: (i, 0))] + [ANYWHERE] * len(pieces),
        out_specs=pl.BlockSpec((tile, outer), lambda i: (i, 0)),
        out_shape=jax.ShapeDtypeStruct((rows, outer), BF16),
        scratch_shapes=[pltpu.VMEM(tuple(shape), BF16), pltpu.SemaphoreType.DMA],
        compiler_params=params(1),
        cost_estimate=pl.CostEstimate(
            flops=2 * rows * shape[0] * shape[1],
            bytes_accessed=2 * (rows * sum(shape) + shape[0] * shape[1]),
            transcendentals=0,
        ),
        name=name,
    )(left, *pieces)


def ffn_body(count, narrow, tile, normed, d_ffn, *rest):
    gate_pieces, up_pieces, rest = rest[:count], rest[count : 2 * count], rest[2 * count :]
    low_pieces, high_pieces, rest = rest[:narrow], rest[narrow : 2 * narrow], rest[2 * narrow :]
    active, d_gate, d_up, out, d_normed, gate, up, down, out_sum, d_sum, sems = rest
    f_step = pl.program_id(1)
    half = down.shape[0] // 2

    @pl.when((pl.program_id(0) == 0) & (f_step == 0))
    def _():
        place_pieces(gate_pieces, gate, sems.at[0], 0)
        place_pieces(up_pieces, up, sems.at[1], 0)
        place_pieces(low_pieces, down.at[pl.ds(0, half)], sems.at[2], 1)
        place_pieces(high_pieces, down.at[pl.ds(half, half)], sems.at[3], 1)
        await_whole(gate, sems.at[0])
        await_whole(up, sems.at[1])
        await_whole(down.at[pl.ds(0, half)], sems.at[2])
        await_whole(down.at[pl.ds(half, half)], sems.at[3])

    units = pl.ds(pl.multiple_of(f_step * tile, tile), tile)
    gate_tile, up_tile, down_tile = gate[:, units], up[:, units], down[units, :]
    gate_in = jnp.dot(normed[...], gate_tile, preferred_element_type=F32)
    upward = jnp.dot(normed[...], up_tile, preferred_element_type=F32)
    d_active = lax.dot_general(d_ffn[...], down_tile, (((1,), (1,)), ((), ())), preferred_element_type=F32)
    sigma = 1.0 / (1.0 + jnp.exp(-gate_in))
    silu = gate_in * sigma
    active_low = (silu * upward).astype(BF16)
    gate_low = (d_active * upward * (sigma * (1.0 + gate_in * (1.0 - sigma)))).astype(BF16)
    up_low = (d_active * silu).astype(BF16)
    active[...] = active_low
    d_gate[...] = gate_low
    d_up[...] = up_low
    part = jnp.dot(active_low, down_tile, preferred_element_type=F32)
    d_part = lax.dot_general(gate_low, gate_tile, (((1,), (1,)), ((), ())), preferred_element_type=F32)
    d_part += lax.dot_general(up_low, up_tile, (((1,), (1,)), ((), ())), preferred_element_type=F32)

    @pl.when(f_step == 0)
    def _():
        out_sum[...] = part
        d_sum[...] = d_part

    @pl.when(f_step > 0)
    def _():
        out_sum[...] += part
        d_sum[...] += d_part

    @pl.when(f_step == pl.num_programs(1) - 1)
    def _():
        out[...] = out_sum[...].astype(BF16)
        d_normed[...] = d_sum[...].astype(BF16)


def ffn(normed, d_ffn, gate_pieces, up_pieces, low_pieces, high_pieces):
    rows, width = normed.shape
    units = gate_pieces[0].shape[1]
    count = len(gate_pieces)
    tile = 256
    row_tile = min(rows, 512)
    once = pl.Buffered(1)
    row_spec = pl.BlockSpec((row_tile, width), lambda i, f: (i, 0), pipeline_mode=once)
    unit_spec = pl.BlockSpec((row_tile, tile), lambda i, f: (i, f))
    unit_shape = jax.ShapeDtypeStruct((rows, units), BF16)
    row_shape = jax.ShapeDtypeStruct((rows, width), BF16)
    return pl.pallas_call(
        functools.partial(ffn_body, count, len(low_pieces), tile),
        grid=(rows // row_tile, units // tile),
        in_specs=[row_spec, row_spec] + [ANYWHERE] * (2 * count + 2 * len(low_pieces)),
        out_specs=[unit_spec, unit_spec, unit_spec, row_spec, row_spec],
        out_shape=[unit_shape, unit_shape, unit_shape, row_shape, row_shape],
        scratch_shapes=[
            pltpu.VMEM((width, units), BF16),
            pltpu.VMEM((width, units), BF16),
            pltpu.VMEM((units, width), BF16),
            pltpu.VMEM((row_tile, width), F32),
            pltpu.VMEM((row_tile, width), F32),
            pltpu.SemaphoreType.DMA((4,)),
        ],
        compiler_params=params(2),
        cost_estimate=pl.CostEstimate(
            flops=12 * rows * width * units, bytes_accessed=6 * width * units + 14 * rows * width, transcendentals=rows * units
        ),
        name="feed_forward",
    )(normed, d_ffn, *gate_pieces, *up_pieces, *low_pieces, *high_pieces)


def doubled(values, lane, head):
    rolled = pltpu.roll(values.astype(F32), HD, 1).astype(BF16)
    return jnp.where((lane < HD) == (head == 0), values, rolled)


def block_bias(order, seq, context_bits, r, block):
    per = order.shape[1] // lax.axis_size("context")
    own = order[seq, lax.axis_index("context") * per + pl.program_id(3)]
    other = order[seq, (lax.axis_index("context") ^ r) * per + block]
    return jnp.where(other <= own, 0.0, MASKED_SCORE).astype(F32)


def masked_scores(order, pieces_k, query):
    seq = pl.program_id(0)
    scores = []
    for r, key_rows in enumerate(pieces_k):
        part = lax.dot_general(key_rows, query, (((1,), (1,)), ((), ())), preferred_element_type=F32)
        for block in range(key_rows.shape[0] // BLK):
            bias = block_bias(order, seq, None, r, block)
            scores.append(part[block * BLK : (block + 1) * BLK] + bias)
    return scores


def attend_body(count, order, query_ref, *rest):
    pieces, (mixture, logs) = rest[:count], rest[count:]
    head = pl.program_id(1)
    lane = lax.broadcasted_iota(jnp.int32, (1, LANES), 1)
    keys = [doubled(piece[:, :LANES], lane, head) for piece in pieces]
    values = [doubled(piece[:, LANES:], lane, head) for piece in pieces]
    query = query_ref[...]
    parts = []
    for side in range(2):
        chosen = (lane < HD) if side == 0 else (lane >= HD)
        scores = masked_scores(order, keys, jnp.where(chosen, query, jnp.zeros_like(query)))
        top = functools.reduce(jnp.maximum, [jnp.max(s, axis=0, keepdims=True) for s in scores])
        powers = [jnp.exp(s - top) for s in scores]
        total = sum(jnp.sum(p, axis=0, keepdims=True) for p in powers)
        low = jnp.concatenate([p.astype(BF16) for p in powers], axis=0)
        whole = jnp.concatenate(values, axis=0)
        mixed = lax.dot_general(whole, low, (((0,), (0,)), ((), ())), preferred_element_type=F32)
        parts.append(mixed / total)
        logs[side : side + 1, :] = top + jnp.log(total)
    row = lax.broadcasted_iota(jnp.int32, (LANES, 1), 0)
    mixture[...] = jnp.where(row < HD, parts[0], parts[1]).T.astype(BF16)


def attend_specs(order, queries, pieces, group_pairs):
    seqs = order.shape[0]
    rows = queries.shape[0] // seqs
    tiles = rows // BLK
    grid = (seqs, 2, group_pairs, tiles)
    q_spec = pl.BlockSpec((BLK, LANES), lambda s, h, g, t: (s * tiles + t, h * group_pairs + g))
    kv_spec = pl.BlockSpec((rows, 2 * LANES), lambda s, h, g, t: (s, 0))
    log_spec = pl.BlockSpec((None, 2, BLK), lambda s, h, g, t: (h * group_pairs + g, 0, s * tiles + t))
    return grid, q_spec, kv_spec, log_spec


def attend(order, queries, pieces):
    rows, q_width = queries.shape
    pairs = q_width // LANES
    grid, q_spec, kv_spec, log_spec = attend_specs(order, queries, pieces, pairs // 2)
    keys = rows * len(pieces) // order.shape[0]
    return pl.pallas_call(
        functools.partial(attend_body, len(pieces)),
        grid=grid,
        in_specs=[pl.BlockSpec(memory_space=pltpu.SMEM), q_spec] + [kv_spec] * len(pieces),
        out_specs=[q_spec, log_spec],
        out_shape=[jax.ShapeDtypeStruct((rows, q_width), BF16), jax.ShapeDtypeStruct((pairs, 2, rows), F32)],
        compiler_params=params(4),
        cost_estimate=pl.CostEstimate(
            flops=8 * rows * keys * q_width * 2, bytes_accessed=8 * rows * q_width, transcendentals=rows * keys * q_width // HD
        ),
        name="attend",
    )(order, queries, *pieces)


def attend_back_body(count, order, query_ref, grad_ref, logs, *rest):
    pieces, rest = rest[:count], rest[count:]
    d_query, outs, (d_key_sum, d_value_sum) = rest[0], rest[1 : 1 + count], rest[1 + count :]
    head, pair, tile = pl.program_id(1), pl.program_id(2), pl.program_id(3)
    lane = lax.broadcasted_iota(jnp.int32, (1, LANES), 1)
    keys = [doubled(piece[:, :LANES], lane, head) for piece in pieces]
    values = jnp.concatenate([doubled(piece[:, LANES:], lane, head) for piece in pieces], axis=0)
    whole_keys = jnp.concatenate(keys, axis=0)
    parts, d_keys, d_values = [], 0.0, 0.0
    for side in range(2):
        chosen = (lane < HD) if side == 0 else (lane >= HD)
        query = jnp.where(chosen, query_ref[...], jnp.zeros_like(query_ref[...]))
        grad = jnp.where(chosen, grad_ref[...], jnp.zeros_like(grad_ref[...]))
        scores = jnp.concatenate(masked_scores(order, keys, query), axis=0)
        soft = jnp.exp(scores - logs[side : side + 1, :])
        d_soft = lax.dot_general(values, grad, (((1,), (1,)), ((), ())), preferred_element_type=F32)
        inner = jnp.sum(soft * d_soft, axis=0, keepdims=True)
        d_scores = (soft * (d_soft - inner)).astype(BF16)
        d_values += jnp.dot(soft.astype(BF16), grad, preferred_element_type=F32)
        d_keys += jnp.dot(d_scores, query, preferred_element_type=F32)
        parts.append(lax.dot_general(whole_keys, d_scores, (((0,), (0,)), ((), ())), preferred_element_type=F32))
    row = lax.broadcasted_iota(jnp.int32, (LANES, 1), 0)
    d_query[...] = jnp.where(row < HD, parts[0], parts[1]).T * SCORE_SCALE

    first = (pair == 0) & (tile == 0)
    last = (pair == pl.num_programs(2) - 1) & (tile == pl.num_programs(3) - 1)

    @pl.when(first)
    def _():
        d_key_sum[...] = d_keys
        d_value_sum[...] = d_values

    @pl.when(jnp.logical_not(first))
    def _():
        d_key_sum[...] += d_keys
        d_value_sum[...] += d_values

    @pl.when(last)
    def _():
        wanted = (lane < HD) == (head == 0)
        rows = outs[0].shape[0]
        for r, out in enumerate(outs):
            for base, total in ((0, d_key_sum), (LANES, d_value_sum)):
                part = total[r * rows : (r + 1) * rows, :]
                both = (part + pltpu.roll(part, HD, 1)).astype(out.dtype)
                spot = pl.ds(base, LANES)

                @pl.when(head == 0)
                def _():
                    out[:, spot] = both

                @pl.when(head == 1)
                def _():
                    out[:, spot] = jnp.where(wanted, both.astype(F32), out[:, spot].astype(F32)).astype(out.dtype)


def attend_back(order, queries, grads, logs, pieces):
    rows, q_width = queries.shape
    pairs = q_width // LANES
    grid, q_spec, kv_spec, log_spec = attend_specs(order, queries, pieces, pairs // 2)
    keys = rows * len(pieces) // order.shape[0]
    return pl.pallas_call(
        functools.partial(attend_back_body, len(pieces)),
        grid=grid,
        in_specs=[pl.BlockSpec(memory_space=pltpu.SMEM), q_spec, q_spec, log_spec] + [kv_spec] * len(pieces),
        out_specs=[q_spec] + [kv_spec] * len(pieces),
        out_shape=[jax.ShapeDtypeStruct((rows, q_width), F32)]
        + [jax.ShapeDtypeStruct((rows, 2 * LANES), F32 if r % 2 == 0 else BF16) for r in range(len(pieces))],
        scratch_shapes=[pltpu.VMEM((keys, LANES), F32), pltpu.VMEM((keys, LANES), F32)],
        compiler_params=params(4),
        cost_estimate=pl.CostEstimate(
            flops=20 * rows * keys * q_width * 2, bytes_accessed=12 * rows * q_width, transcendentals=rows * keys * q_width // HD
        ),
        name="attend_back",
    )(order, queries, grads, logs, *pieces)


def gather_context(piece):
    size = lax.axis_size("context")
    held = {0: piece}
    bit = size // 2
    while bit:
        for r in list(held):
            held[r | bit] = swap(held[r], "context", size, bit)
        bit //= 2
    return [held[r] for r in range(size)]


def reduce_context(pieces):
    size = len(pieces)
    held = dict(enumerate(pieces))
    bit = 1
    while bit < size:
        held = {
            r: held[r].astype(F32) + swap(held[r | bit].astype(BF16), "context", size, bit).astype(F32)
            for r in held
            if not r & bit
        }
        bit *= 2
    return held[0]


def stored_places(order_row, first, count):
    stored = first + jnp.arange(count, dtype=jnp.int32)
    picks = (stored // BLK)[:, None] == jnp.arange(order_row.shape[0], dtype=jnp.int32)[None, :]
    return jnp.sum(jnp.where(picks, order_row[None, :], 0), axis=1) * BLK + stored % BLK


def rope_tables(order, local_len):
    first = lax.axis_index("context") * local_len
    places = jnp.concatenate([stored_places(order[s], first, local_len) for s in range(order.shape[0])])
    half = HD // 2
    inverse = jnp.exp(jnp.arange(half, dtype=F32) * (-2.0 * math.log(ROPE_BASE) / HD))
    angles = places.astype(F32)[:, None] * jnp.tile(inverse, LANES // half)[None, :]
    return jnp.cos(angles), jnp.sin(angles)


def norm_back(d_normed, values, gain):
    inverse = lax.rsqrt(jnp.mean(values * values, axis=1, keepdims=True) + EPSILON)
    scaled = gain * d_normed
    d_gain = jnp.sum(d_normed * values * inverse, axis=0)
    inner = jnp.mean(scaled * values, axis=1, keepdims=True)
    return inverse * scaled - values * inverse * inverse * inverse * inner, d_gain


def weight_grad(left, right):
    return lax.dot_general(left, right, (((0,), (0,)), ((), ())), preferred_element_type=F32)


def local(
    tokens, block_order, w_query, w_key, w_value, w_output, w_gate, w_up, w_down, norm_attn, norm_ffn, grad_out
):
    seqs, local_len, width = tokens.shape
    rows = seqs * local_len
    size = plane_size()
    me = plane_index()
    z = lax.axis_index("tensor")
    z_rows = rows // lax.axis_size("tensor")
    token_rows = tokens.reshape(rows, width)
    grad_rows = grad_out.reshape(rows, width)
    q_width, kv_width = w_query.shape[1], w_key.shape[1]
    units = w_down.shape[0]
    half = units // 2

    gains = gather_small(jnp.stack([norm_attn, norm_ffn])).reshape(2, width)
    gain_attn, gain_ffn = gains[0:1], gains[1:2]
    w_qkv = jnp.concatenate([w_query, w_key, w_value], axis=1)
    qkv_pieces, output_pieces = gather_pair(w_qkv, w_output)
    gate_pieces, up_pieces = gather_pair(w_gate, w_up)
    low_pieces, high_pieces = gather_pair(w_down[:half], w_down[half:])
    output_pieces, low_pieces, high_pieces = widened(output_pieces), widened(low_pieces), widened(high_pieces)

    cosine, sine = rope_tables(block_order, local_len)
    normed, queries, keys_values = project_qkv(token_rows, gain_attn, cosine, sine, qkv_pieces, q_width)
    kv_pieces = gather_context(keys_values)
    mixture, logs = attend(block_order, queries, kv_pieces)
    branch = rows_sum(gathered_matmul(mixture, output_pieces, 1, False, "project_output"))
    tokens_own = chunk_of(token_rows, z, z_rows).astype(F32)
    grads_own = chunk_of(grad_rows, z, z_rows).astype(F32)
    hidden = tokens_own + RESIDUAL_SCALE * branch
    inverse = lax.rsqrt(jnp.mean(hidden * hidden, axis=1, keepdims=True) + EPSILON)
    normed_ffn = rows_gather((hidden * inverse * gain_ffn).astype(BF16))
    d_ffn = (RESIDUAL_SCALE * grad_rows.astype(F32)).astype(BF16)
    active, d_gate, d_up, ffn_out, d_normed_ffn = ffn(
        normed_ffn, d_ffn, gate_pieces, up_pieces, low_pieces, high_pieces
    )

    d_ffn_in, ffn_gain = norm_back(rows_sum(d_normed_ffn), hidden, gain_ffn)
    d_hidden = grads_own + d_ffn_in
    d_branch = rows_gather((RESIDUAL_SCALE * d_hidden).astype(BF16))
    layer_out = rows_gather((hidden + RESIDUAL_SCALE * rows_sum(ffn_out)).astype(BF16))

    def columns(values, r):
        extent = width // size
        return lax.dynamic_slice_in_dim(values, (me ^ r) * extent, extent, 1)

    grad_gate, grad_up = reduce_pair(
        [weight_grad(columns(normed_ffn, r), d_gate).astype(BF16) for r in range(size)],
        [weight_grad(columns(normed_ffn, r), d_up).astype(BF16) for r in range(size)],
    )
    grad_low, grad_high = reduce_pair(
        [weight_grad(active[:, :half], columns(d_ffn, r)).astype(BF16) for r in range(size)],
        [weight_grad(active[:, half:], columns(d_ffn, r)).astype(BF16) for r in range(size)],
    )

    d_mixture = gathered_matmul(d_branch, output_pieces, 1, True, "project_output_back")
    d_queries, *d_pieces = attend_back(block_order, queries, d_mixture, logs, kv_pieces)
    d_keys_values = reduce_context(d_pieces)
    d_qkv, d_normed = project_qkv_back(d_queries, d_keys_values, cosine, sine, qkv_pieces)
    d_attn_in, attn_gain = norm_back(rows_sum(d_normed), tokens_own, gain_attn)
    grad_tokens = rows_gather((d_hidden + d_attn_in).astype(BF16)).astype(F32)

    grad_qkv, grad_output = reduce_pair(
        [weight_grad(columns(normed, r), d_qkv).astype(BF16) for r in range(size)],
        [weight_grad(mixture, columns(d_branch, r)).astype(BF16) for r in range(size)],
    )
    gain_grads = jnp.stack([attn_gain, ffn_gain])
    everyone = ("shard", "context", "tensor")
    world = size * lax.axis_size("tensor")
    bit = 1
    while bit < world:
        gain_grads = gain_grads + swap(gain_grads, everyone, world, bit)
        bit *= 2
    gain_grads = lax.dynamic_slice_in_dim(gain_grads, me * (width // size), width // size, 1)
    return (
        layer_out.reshape(seqs, local_len, width),
        grad_tokens.reshape(seqs, local_len, width),
        grad_qkv[:, :q_width],
        grad_qkv[:, q_width : q_width + kv_width],
        grad_qkv[:, q_width + kv_width :],
        grad_output,
        grad_gate,
        grad_up,
        jnp.concatenate([grad_low, grad_high], axis=0),
        gain_grads[0],
        gain_grads[1],
    )


def solution(mesh):
    split = P("shard", "context", None)
    inward, outward = P(PLANE, "tensor"), P("tensor", PLANE)
    gain = P(PLANE)
    return jax.shard_map(
        local,
        mesh=mesh,
        in_specs=(split, P("shard", None), inward, inward, inward, outward, inward, inward, outward, gain, gain, split),
        out_specs=(split, split, inward, inward, inward, outward, inward, inward, outward, gain, gain),
        check_vma=False,
    )
```

```python
import functools
import math

import jax
import jax.numpy as jnp
from jax import lax
from jax.experimental import pallas as pl
from jax.experimental.pallas import tpu as pltpu
from jax.sharding import PartitionSpec as P

HD = 64
BLK = 256
LANES = 128
EPSILON = 1e-05
SCORE_SCALE = 0.015625
RESIDUAL_SCALE = 0.22
ROPE_BASE = 10000000.0
MASKED_SCORE = -1e30
PLANE = ("shard", "context")
VMEM_BYTES = 64000 * 1024


F32 = jnp.float32
BF16 = jnp.bfloat16


def plane_size():
    return lax.axis_size("shard") * lax.axis_size("context")


def plane_index():
    return lax.axis_index("shard") * lax.axis_size("context") + lax.axis_index("context")


def swap(value, axes, size, bit):
    return lax.ppermute(value, axes, [(i, i ^ bit) for i in range(size)])


def gather_pair(first, second, far_after=None, near_after=None):
    size = plane_size()
    bits = [1 << b for b in range(1, size.bit_length() - 1)]
    sides = [{0: first}, {0: second}]
    if len(bits) == 2:
        near, far = bits
        for side in sides:
            early = side[0] if far_after is None else after(side[0], far_after)
            late = side[0] if near_after is None else after(side[0], near_after)
            side[far] = swap(early, PLANE, size, far)
            side[near] = swap(late, PLANE, size, near)
        sides[0][near | far] = swap(sides[0][far], PLANE, size, near)
        sides[1][near | far] = swap(sides[1][near], PLANE, size, far)
    else:
        for side in sides:
            for bit in bits:
                for r in list(side):
                    side[r | bit] = swap(side[r], PLANE, size, bit)
    for side in sides:
        for r in list(side):
            side[r | 1] = swap(side[r], PLANE, size, 1)
    return [[side[r] for r in range(size)] for side in sides]


def widened(pieces):
    level = 1
    while pieces[0].shape[1] < LANES:
        upper = (plane_index() // level) % 2 == 1
        pairs = zip(pieces[0::2], pieces[1::2])
        pieces = [jnp.where(upper, jnp.concatenate([b, a], 1), jnp.concatenate([a, b], 1)) for a, b in pairs]
        level *= 2
    return pieces


def reduce_pair(first, second):
    size = plane_size()
    bits = [1 << b for b in range(1, size.bit_length() - 1)]
    sides = [dict(enumerate(first)), dict(enumerate(second))]

    def take(side, bit, kept):
        total = side[kept].astype(F32) + swap(side[kept | bit].astype(BF16), PLANE, size, bit).astype(F32)
        return total if kept == 0 else total.astype(BF16)

    sides = [{r: take(side, 1, r) for r in range(0, size, 2)} for side in sides]
    if len(bits) == 2:
        near, far = bits
        sides[0][near] = take(sides[0], far, near)
        sides[1][far] = take(sides[1], near, far)
        done = []
        for side in sides:
            a = swap(side[near].astype(BF16), PLANE, size, near).astype(F32)
            b = swap(side[far].astype(BF16), PLANE, size, far).astype(F32)
            done.append(side[0] + a + b)
        return done
    done = []
    for side in sides:
        for bit in reversed(bits):
            side = {r: take(side, bit, r) for r in side if not r & bit}
        done.append(side[0])
    return done


def gather_small(values):
    size = plane_size()
    stacked = values[None]
    bit = 1
    while bit < size:
        stacked = jnp.concatenate([stacked, swap(stacked, PLANE, size, bit)], axis=0)
        bit *= 2
    picks = jnp.arange(size, dtype=jnp.int32)[:, None] ^ plane_index()
    chosen = (picks == jnp.arange(size, dtype=jnp.int32)[None, :]).astype(F32)
    return jnp.einsum("ij,jkw->kiw", chosen, stacked.astype(F32), precision=lax.Precision.HIGHEST)


def chunk_of(rows, index, count):
    return lax.dynamic_slice_in_dim(rows, index * count, count, 0)


def rows_sum(partial):
    size = lax.axis_size("tensor")
    me = lax.axis_index("tensor")
    count = partial.shape[0] // size
    total = chunk_of(partial, me, count).astype(F32)
    for shift in range(1, size):
        sent = chunk_of(partial, lax.rem(me + shift, size), count)
        pairs = [(i, (i + shift) % size) for i in range(size)]
        total = total + lax.ppermute(sent, "tensor", pairs).astype(F32)
    return total


def rows_gather(chunk):
    size = lax.axis_size("tensor")
    me = lax.axis_index("tensor")
    count = chunk.shape[0]
    parts = [chunk]
    for shift in range(1, size):
        pairs = [(i, (i + shift) % size) for i in range(size)]
        parts.append(lax.ppermute(chunk, "tensor", pairs))
    whole = jnp.zeros((size * count,) + chunk.shape[1:], chunk.dtype)
    for shift in range(size):
        place = lax.rem(me - shift + size, size) * count
        whole = lax.dynamic_update_slice_in_dim(whole, parts[shift], place, 0)
    return whole


def params(steps):
    return pltpu.CompilerParams(
        dimension_semantics=("arbitrary",) * steps, vmem_limit_bytes=VMEM_BYTES
    )


def place_pieces(pieces, whole, sem, axis):
    size = len(pieces)
    me = plane_index() // (plane_size() // size)
    extent = whole.shape[axis] // size
    for r, piece in enumerate(pieces):
        start = pl.multiple_of((me ^ r) * extent, extent)
        target = whole.at[pl.ds(start, extent)] if axis == 0 else whole.at[:, pl.ds(start, extent)]
        pltpu.make_async_copy(piece, target, sem).start()


def await_whole(whole, sem):
    pltpu.make_async_copy(whole, whole, sem).wait()


ANYWHERE = pl.BlockSpec(memory_space=pl.ANY)


def turned(values, lane, sign):
    half = HD // 2
    upper = pltpu.roll(values, LANES - half, 1)
    lower = pltpu.roll(values, half, 1)
    return jnp.where(lane % HD < half, -sign * upper, sign * lower)


def qkv_body(count, scale_lanes, tokens, gain, cosine, sine, *rest):
    pieces, (normed, queries, keys_values, weight, sem) = rest[:count], rest[count:]

    @pl.when(pl.program_id(0) == 0)
    def _():
        place_pieces(pieces, weight, sem, 0)

    values = tokens[...].astype(F32)
    inverse = lax.rsqrt(jnp.mean(values * values, axis=1, keepdims=True) + EPSILON)
    low = (values * inverse * gain[...]).astype(BF16)
    normed[...] = low

    @pl.when(pl.program_id(0) == 0)
    def _():
        await_whole(weight, sem)

    cos, sin = cosine[...], sine[...]
    lane = lax.broadcasted_iota(jnp.int32, cos.shape, 1)
    q_width = queries.shape[1]
    k_width = keys_values.shape[1] // 2
    for start in range(0, weight.shape[1], LANES):
        part = jnp.dot(low, weight[:, start : start + LANES * 1], preferred_element_type=F32)
        if start < q_width + k_width:
            part = part * cos + turned(part, lane, 1.0) * sin
        if start < q_width:
            queries[:, start : start + LANES] = (part.astype(BF16) * SCORE_SCALE).astype(BF16)
        else:
            keys_values[:, start - q_width : start - q_width + LANES] = part.astype(BF16)


def project_qkv(tokens, gain, cosine, sine, pieces, q_width):
    rows, width = tokens.shape
    total = pieces[0].shape[1]
    tile = min(rows, 256)
    row_spec = lambda w: pl.BlockSpec((tile, w), lambda i: (i, 0))
    return pl.pallas_call(
        functools.partial(qkv_body, len(pieces), q_width),
        grid=(rows // tile,),
        in_specs=[row_spec(width), pl.BlockSpec((1, width), lambda i: (0, 0)), row_spec(LANES), row_spec(LANES)]
        + [ANYWHERE] * len(pieces),
        out_specs=[row_spec(width), row_spec(q_width), row_spec(total - q_width)],
        out_shape=[
            jax.ShapeDtypeStruct((rows, width), BF16),
            jax.ShapeDtypeStruct((rows, q_width), BF16),
            jax.ShapeDtypeStruct((rows, total - q_width), BF16),
        ],
        scratch_shapes=[pltpu.VMEM((width, total), BF16), pltpu.SemaphoreType.DMA],
        compiler_params=params(1),
        cost_estimate=pl.CostEstimate(
            flops=2 * rows * width * total, bytes_accessed=2 * (2 * rows * width + width * total), transcendentals=0
        ),
        name="project_qkv",
    )(tokens, gain, cosine, sine, *pieces)


def qkv_back_body(count, d_queries, d_keys_values, cosine, sine, *rest):
    pieces, (d_all, d_normed, weight, sem) = rest[:count], rest[count:]

    @pl.when(pl.program_id(0) == 0)
    def _():
        place_pieces(pieces, weight, sem, 0)

    cos, sin = cosine[...], sine[...]
    lane = lax.broadcasted_iota(jnp.int32, cos.shape, 1)
    q_width = d_queries.shape[1]
    k_width = d_keys_values.shape[1] // 2
    for start in range(0, d_all.shape[1], LANES):
        if start < q_width:
            part = d_queries[:, start : start + LANES]
        else:
            part = d_keys_values[:, start - q_width : start - q_width + LANES]
        if start < q_width + k_width:
            part = part * cos + turned(part * sin, lane, -1.0)
        d_all[:, start : start + LANES] = part.astype(BF16)

    @pl.when(pl.program_id(0) == 0)
    def _():
        await_whole(weight, sem)

    step = 512
    for start in range(0, weight.shape[0], step):
        d_normed[:, start : start + step] = lax.dot_general(
            d_all[...], weight[start : start + step, :], (((1,), (1,)), ((), ())), preferred_element_type=F32
        ).astype(BF16)


def project_qkv_back(d_queries, d_keys_values, cosine, sine, pieces):
    rows, q_width = d_queries.shape
    total = pieces[0].shape[1]
    width = pieces[0].shape[0] * len(pieces)
    tile = min(rows, 256)
    row_spec = lambda w: pl.BlockSpec((tile, w), lambda i: (i, 0))
    return pl.pallas_call(
        functools.partial(qkv_back_body, len(pieces)),
        grid=(rows // tile,),
        in_specs=[row_spec(q_width), row_spec(total - q_width), row_spec(LANES), row_spec(LANES)]
        + [ANYWHERE] * len(pieces),
        out_specs=[row_spec(total), row_spec(width)],
        out_shape=[jax.ShapeDtypeStruct((rows, total), BF16), jax.ShapeDtypeStruct((rows, width), BF16)],
        scratch_shapes=[pltpu.VMEM((width, total), BF16), pltpu.SemaphoreType.DMA],
        compiler_params=params(1),
        cost_estimate=pl.CostEstimate(
            flops=2 * rows * width * total, bytes_accessed=2 * (2 * rows * width + width * total), transcendentals=0
        ),
        name="project_qkv_back",
    )(d_queries, d_keys_values, cosine, sine, *pieces)


def gathered_body(count, axis, transposed, left, *rest):
    pieces, (out, weight, sem) = rest[:count], rest[count:]

    @pl.when(pl.program_id(0) == 0)
    def _():
        place_pieces(pieces, weight, sem, axis)
        await_whole(weight, sem)

    step = min(out.shape[1], 512)
    for start in range(0, out.shape[1], step):
        if transposed:
            part = lax.dot_general(
                left[...], weight[start : start + step, :], (((1,), (1,)), ((), ())), preferred_element_type=F32
            )
        else:
            part = jnp.dot(left[...], weight[:, start : start + step], preferred_element_type=F32)
        out[:, start : start + step] = part.astype(out.dtype)


def gathered_matmul(left, pieces, axis, transposed, name):
    rows = left.shape[0]
    shape = list(pieces[0].shape)
    shape[axis] *= len(pieces)
    outer = shape[0] if transposed else shape[1]
    tile = min(rows, 256)
    return pl.pallas_call(
        functools.partial(gathered_body, len(pieces), axis, transposed),
        grid=(rows // tile,),
        in_specs=[pl.BlockSpec((tile, left.shape[1]), lambda i: (i, 0))] + [ANYWHERE] * len(pieces),
        out_specs=pl.BlockSpec((tile, outer), lambda i: (i, 0)),
        out_shape=jax.ShapeDtypeStruct((rows, outer), BF16),
        scratch_shapes=[pltpu.VMEM(tuple(shape), BF16), pltpu.SemaphoreType.DMA],
        compiler_params=params(1),
        cost_estimate=pl.CostEstimate(
            flops=2 * rows * shape[0] * shape[1],
            bytes_accessed=2 * (rows * sum(shape) + shape[0] * shape[1]),
            transcendentals=0,
        ),
        name=name,
    )(left, *pieces)


def ffn_body(count, narrow, tile, normed, d_ffn, *rest):
    gate_pieces, up_pieces, rest = rest[:count], rest[count : 2 * count], rest[2 * count :]
    low_pieces, high_pieces, rest = rest[:narrow], rest[narrow : 2 * narrow], rest[2 * narrow :]
    active, d_gate, d_up, out, d_normed, gate, up, down, out_sum, d_sum, sems = rest
    f_step = pl.program_id(1)
    half = down.shape[0] // 2

    @pl.when((pl.program_id(0) == 0) & (f_step == 0))
    def _():
        place_pieces(gate_pieces, gate, sems.at[0], 0)
        place_pieces(up_pieces, up, sems.at[1], 0)
        place_pieces(low_pieces, down.at[pl.ds(0, half)], sems.at[2], 1)
        place_pieces(high_pieces, down.at[pl.ds(half, half)], sems.at[3], 1)
        await_whole(gate, sems.at[0])
        await_whole(up, sems.at[1])
        await_whole(down.at[pl.ds(0, half)], sems.at[2])
        await_whole(down.at[pl.ds(half, half)], sems.at[3])

    units = pl.ds(pl.multiple_of(f_step * tile, tile), tile)
    gate_tile, up_tile, down_tile = gate[:, units], up[:, units], down[units, :]
    gate_in = jnp.dot(normed[...], gate_tile, preferred_element_type=F32)
    upward = jnp.dot(normed[...], up_tile, preferred_element_type=F32)
    d_active = lax.dot_general(d_ffn[...], down_tile, (((1,), (1,)), ((), ())), preferred_element_type=F32)
    sigma = 1.0 / (1.0 + jnp.exp(-gate_in))
    silu = gate_in * sigma
    active_low = (silu * upward).astype(BF16)
    gate_low = (d_active * upward * (sigma * (1.0 + gate_in * (1.0 - sigma)))).astype(BF16)
    up_low = (d_active * silu).astype(BF16)
    active[...] = active_low
    d_gate[...] = gate_low
    d_up[...] = up_low
    part = jnp.dot(active_low, down_tile, preferred_element_type=F32)
    d_part = lax.dot_general(gate_low, gate_tile, (((1,), (1,)), ((), ())), preferred_element_type=F32)
    d_part += lax.dot_general(up_low, up_tile, (((1,), (1,)), ((), ())), preferred_element_type=F32)

    @pl.when(f_step == 0)
    def _():
        out_sum[...] = part
        d_sum[...] = d_part

    @pl.when(f_step > 0)
    def _():
        out_sum[...] += part
        d_sum[...] += d_part

    @pl.when(f_step == pl.num_programs(1) - 1)
    def _():
        out[...] = out_sum[...].astype(BF16)
        d_normed[...] = d_sum[...].astype(BF16)


def ffn(normed, d_ffn, gate_pieces, up_pieces, low_pieces, high_pieces):
    rows, width = normed.shape
    units = gate_pieces[0].shape[1]
    count = len(gate_pieces)
    tile = 256
    row_tile = min(rows, 512)
    once = pl.Buffered(1)
    row_spec = pl.BlockSpec((row_tile, width), lambda i, f: (i, 0), pipeline_mode=once)
    unit_spec = pl.BlockSpec((row_tile, tile), lambda i, f: (i, f))
    unit_shape = jax.ShapeDtypeStruct((rows, units), BF16)
    row_shape = jax.ShapeDtypeStruct((rows, width), BF16)
    return pl.pallas_call(
        functools.partial(ffn_body, count, len(low_pieces), tile),
        grid=(rows // row_tile, units // tile),
        in_specs=[row_spec, row_spec] + [ANYWHERE] * (2 * count + 2 * len(low_pieces)),
        out_specs=[unit_spec, unit_spec, unit_spec, row_spec, row_spec],
        out_shape=[unit_shape, unit_shape, unit_shape, row_shape, row_shape],
        scratch_shapes=[
            pltpu.VMEM((width, units), BF16),
            pltpu.VMEM((width, units), BF16),
            pltpu.VMEM((units, width), BF16),
            pltpu.VMEM((row_tile, width), F32),
            pltpu.VMEM((row_tile, width), F32),
            pltpu.SemaphoreType.DMA((4,)),
        ],
        compiler_params=params(2),
        cost_estimate=pl.CostEstimate(
            flops=12 * rows * width * units, bytes_accessed=6 * width * units + 14 * rows * width, transcendentals=rows * units
        ),
        name="feed_forward",
    )(normed, d_ffn, *gate_pieces, *up_pieces, *low_pieces, *high_pieces)


def doubled(values, lane, head):
    rolled = pltpu.roll(values.astype(F32), HD, 1).astype(BF16)
    return jnp.where((lane < HD) == (head == 0), values, rolled)


def block_bias(order, seq, context_bits, r, block):
    per = order.shape[1] // lax.axis_size("context")
    own = order[seq, lax.axis_index("context") * per + pl.program_id(3)]
    other = order[seq, (lax.axis_index("context") ^ r) * per + block]
    return jnp.where(other <= own, 0.0, MASKED_SCORE).astype(F32)


def masked_scores(order, pieces_k, query):
    seq = pl.program_id(0)
    scores = []
    for r, key_rows in enumerate(pieces_k):
        part = lax.dot_general(key_rows, query, (((1,), (1,)), ((), ())), preferred_element_type=F32)
        for block in range(key_rows.shape[0] // BLK):
            bias = block_bias(order, seq, None, r, block)
            scores.append(part[block * BLK : (block + 1) * BLK] + bias)
    return scores


def attend_body(count, order, query_ref, *rest):
    pieces, (mixture, logs) = rest[:count], rest[count:]
    head = pl.program_id(1)
    lane = lax.broadcasted_iota(jnp.int32, (1, LANES), 1)
    keys = [doubled(piece[:, :LANES], lane, head) for piece in pieces]
    values = [doubled(piece[:, LANES:], lane, head) for piece in pieces]
    query = query_ref[...]
    parts = []
    for side in range(2):
        chosen = (lane < HD) if side == 0 else (lane >= HD)
        scores = masked_scores(order, keys, jnp.where(chosen, query, jnp.zeros_like(query)))
        top = functools.reduce(jnp.maximum, [jnp.max(s, axis=0, keepdims=True) for s in scores])
        powers = [jnp.exp(s - top) for s in scores]
        total = sum(jnp.sum(p, axis=0, keepdims=True) for p in powers)
        low = jnp.concatenate([p.astype(BF16) for p in powers], axis=0)
        whole = jnp.concatenate(values, axis=0)
        mixed = lax.dot_general(whole, low, (((0,), (0,)), ((), ())), preferred_element_type=F32)
        parts.append(mixed / total)
        logs[side : side + 1, :] = top + jnp.log(total)
    row = lax.broadcasted_iota(jnp.int32, (LANES, 1), 0)
    mixture[...] = jnp.where(row < HD, parts[0], parts[1]).T.astype(BF16)


def attend_specs(order, queries, pieces, group_pairs):
    seqs = order.shape[0]
    rows = queries.shape[0] // seqs
    tiles = rows // BLK
    grid = (seqs, 2, group_pairs, tiles)
    q_spec = pl.BlockSpec((BLK, LANES), lambda s, h, g, t: (s * tiles + t, h * group_pairs + g))
    kv_spec = pl.BlockSpec((rows, 2 * LANES), lambda s, h, g, t: (s, 0))
    log_spec = pl.BlockSpec((None, 2, BLK), lambda s, h, g, t: (h * group_pairs + g, 0, s * tiles + t))
    return grid, q_spec, kv_spec, log_spec


def attend(order, queries, pieces):
    rows, q_width = queries.shape
    pairs = q_width // LANES
    grid, q_spec, kv_spec, log_spec = attend_specs(order, queries, pieces, pairs // 2)
    keys = rows * len(pieces) // order.shape[0]
    return pl.pallas_call(
        functools.partial(attend_body, len(pieces)),
        grid=grid,
        in_specs=[pl.BlockSpec(memory_space=pltpu.SMEM), q_spec] + [kv_spec] * len(pieces),
        out_specs=[q_spec, log_spec],
        out_shape=[jax.ShapeDtypeStruct((rows, q_width), BF16), jax.ShapeDtypeStruct((pairs, 2, rows), F32)],
        compiler_params=params(4),
        cost_estimate=pl.CostEstimate(
            flops=8 * rows * keys * q_width * 2, bytes_accessed=8 * rows * q_width, transcendentals=rows * keys * q_width // HD
        ),
        name="attend",
    )(order, queries, *pieces)


def attend_back_body(count, order, query_ref, grad_ref, logs, *rest):
    pieces, rest = rest[:count], rest[count:]
    d_query, outs, (d_key_sum, d_value_sum) = rest[0], rest[1 : 1 + count], rest[1 + count :]
    head, pair, tile = pl.program_id(1), pl.program_id(2), pl.program_id(3)
    lane = lax.broadcasted_iota(jnp.int32, (1, LANES), 1)
    keys = [doubled(piece[:, :LANES], lane, head) for piece in pieces]
    values = jnp.concatenate([doubled(piece[:, LANES:], lane, head) for piece in pieces], axis=0)
    whole_keys = jnp.concatenate(keys, axis=0)
    parts, d_keys, d_values = [], 0.0, 0.0
    for side in range(2):
        chosen = (lane < HD) if side == 0 else (lane >= HD)
        query = jnp.where(chosen, query_ref[...], jnp.zeros_like(query_ref[...]))
        grad = jnp.where(chosen, grad_ref[...], jnp.zeros_like(grad_ref[...]))
        scores = jnp.concatenate(masked_scores(order, keys, query), axis=0)
        soft = jnp.exp(scores - logs[side : side + 1, :])
        d_soft = lax.dot_general(values, grad, (((1,), (1,)), ((), ())), preferred_element_type=F32)
        inner = jnp.sum(soft * d_soft, axis=0, keepdims=True)
        d_scores = (soft * (d_soft - inner)).astype(BF16)
        d_values += jnp.dot(soft.astype(BF16), grad, preferred_element_type=F32)
        d_keys += jnp.dot(d_scores, query, preferred_element_type=F32)
        parts.append(lax.dot_general(whole_keys, d_scores, (((0,), (0,)), ((), ())), preferred_element_type=F32))
    row = lax.broadcasted_iota(jnp.int32, (LANES, 1), 0)
    d_query[...] = jnp.where(row < HD, parts[0], parts[1]).T * SCORE_SCALE

    first = (pair == 0) & (tile == 0)
    last = (pair == pl.num_programs(2) - 1) & (tile == pl.num_programs(3) - 1)

    @pl.when(first)
    def _():
        d_key_sum[...] = d_keys
        d_value_sum[...] = d_values

    @pl.when(jnp.logical_not(first))
    def _():
        d_key_sum[...] += d_keys
        d_value_sum[...] += d_values

    @pl.when(last)
    def _():
        wanted = (lane < HD) == (head == 0)
        rows = outs[0].shape[0]
        for r, out in enumerate(outs):
            for base, total in ((0, d_key_sum), (LANES, d_value_sum)):
                part = total[r * rows : (r + 1) * rows, :]
                both = (part + pltpu.roll(part, HD, 1)).astype(out.dtype)
                spot = pl.ds(base, LANES)

                @pl.when(head == 0)
                def _():
                    out[:, spot] = both

                @pl.when(head == 1)
                def _():
                    out[:, spot] = jnp.where(wanted, both.astype(F32), out[:, spot].astype(F32)).astype(out.dtype)


def attend_back(order, queries, grads, logs, pieces):
    rows, q_width = queries.shape
    pairs = q_width // LANES
    grid, q_spec, kv_spec, log_spec = attend_specs(order, queries, pieces, pairs // 2)
    keys = rows * len(pieces) // order.shape[0]
    return pl.pallas_call(
        functools.partial(attend_back_body, len(pieces)),
        grid=grid,
        in_specs=[pl.BlockSpec(memory_space=pltpu.SMEM), q_spec, q_spec, log_spec] + [kv_spec] * len(pieces),
        out_specs=[q_spec] + [kv_spec] * len(pieces),
        out_shape=[jax.ShapeDtypeStruct((rows, q_width), F32)]
        + [jax.ShapeDtypeStruct((rows, 2 * LANES), F32 if r % 2 == 0 else BF16) for r in range(len(pieces))],
        scratch_shapes=[pltpu.VMEM((keys, LANES), F32), pltpu.VMEM((keys, LANES), F32)],
        compiler_params=params(4),
        cost_estimate=pl.CostEstimate(
            flops=20 * rows * keys * q_width * 2, bytes_accessed=12 * rows * q_width, transcendentals=rows * keys * q_width // HD
        ),
        name="attend_back",
    )(order, queries, grads, logs, *pieces)


def line_steps(rows):
    half = rows // 2
    sub = 32
    return half, sub, half // sub


def line_body(finish, keep_state, gain_sum, n_in, *refs):
    partial, ins, rest = refs[0], refs[1 : 1 + n_in], refs[1 + n_in :]
    result, rest = rest[0], rest[1:]
    state_out, rest = (rest[0], rest[1:]) if keep_state else (None, rest)
    gain_out, rest = (rest[0], rest[1:]) if gain_sum else (None, rest)
    from_outer, from_peer, staged, send, recv = rest
    half, sub, count = line_steps(partial.shape[0])
    me = lax.axis_index("tensor")
    side = me // 2
    inner = lax.rem(me, 3) != 0
    to_outer, to_inner, to_peer = side * 3, 1 + side, 3 - me
    near, far = side * half, (1 - side) * half

    def rows(base, k):
        return pl.ds(pl.multiple_of(base + k * sub, sub), sub)

    def remote(source, target, s, r, k, where):
        return pltpu.make_async_remote_copy(
            src_ref=source,
            dst_ref=target,
            send_sem=send.at[s, k],
            recv_sem=recv.at[r, k],
            device_id={"tensor": where},
            device_id_type=pl.DeviceIdType.MESH,
        )

    def up_far(k):
        return remote(partial.at[rows(far, k)], from_outer.at[0, rows(0, k)], 0, 0, k, to_inner)

    def up_near(k):
        return remote(partial.at[rows(near, k)], from_outer.at[1, rows(0, k)], 1, 1, k, to_inner)

    def across(k):
        return remote(staged.at[rows(0, k)], from_peer.at[rows(0, k)], 0, 2, k, to_peer)

    def over(k, base):
        return remote(result.at[rows(base, k)], result.at[rows(base, k)], 2, 4, k, to_peer)

    def down_near(k):
        return remote(result.at[rows(near, k)], result.at[rows(near, k)], 1, 3, k, to_outer)

    def down_far(k):
        return remote(result.at[rows(far, k)], result.at[rows(far, k)], 3, 4, k, to_outer)

    barrier = pltpu.get_barrier_semaphore()

    def greet(where):
        pl.semaphore_signal(barrier, inc=1, device_id={"tensor": where}, device_id_type=pl.DeviceIdType.MESH)

    if gain_sum:
        gain_out[...] = jnp.zeros_like(gain_out)

    @pl.when(inner)
    def _():
        greet(to_outer)
        greet(to_peer)
        pl.semaphore_wait(barrier, 2)

        def step(k, carry):
            @pl.when(k < count)
            def _():
                up_far(k).wait_recv()
                total = partial[rows(far, k), :].astype(F32) + from_outer[0, rows(0, k), :].astype(F32)
                staged[rows(0, k), :] = total.astype(BF16)
                across(k).start()

            @pl.when((k >= 1) & (k <= count))
            def _():
                j = k - 1
                up_near(j).wait_recv()
                across(j).wait_recv()
                total = partial[rows(near, j), :].astype(F32) + from_outer[1, rows(0, j), :].astype(F32)
                total = total + from_peer[rows(0, j), :].astype(F32)
                low, state, gains = finish(total, rows(near, j), rows(0, j), ins)
                result[rows(near, j), :] = low
                if keep_state:
                    state_out[rows(0, j), :] = state
                if gain_sum:
                    gain_out[...] += jnp.sum(gains.reshape(sub // 8, 8, gains.shape[1]), axis=0)
                down_near(j).start()
                over(j, near).start()

            @pl.when(k >= 3)
            def _():
                over(k - 3, far).wait_recv()
                down_far(k - 3).start()

            return carry

        lax.fori_loop(0, count + 3, step, 0)

        def drain(k, carry):
            across(k).wait_send()
            down_near(k).wait_send()
            over(k, near).wait_send()
            down_far(k).wait_send()
            return carry

        lax.fori_loop(0, count, drain, 0)

    @pl.when(jnp.logical_not(inner))
    def _():
        greet(to_inner)
        pl.semaphore_wait(barrier, 1)

        def step(k, carry):
            up_far(k).start()
            up_near(k).start()
            return carry

        lax.fori_loop(0, count, step, 0)

        def drain(k, carry):
            down_near(k).wait_recv()
            down_far(k).wait_recv()
            up_far(k).wait_send()
            up_near(k).wait_send()
            return carry

        lax.fori_loop(0, count, drain, 0)


def line_sum(partial, ins, finish, keep_state, gain_sum, identity, name):
    rows, width = partial.shape
    half, sub, count = line_steps(rows)
    vmem = pl.BlockSpec(memory_space=pltpu.VMEM)
    shapes = [jax.ShapeDtypeStruct((rows, width), BF16)]
    if keep_state:
        shapes.append(jax.ShapeDtypeStruct((half, width), F32))
    if gain_sum:
        shapes.append(jax.ShapeDtypeStruct((8, width), F32))
    return pl.pallas_call(
        functools.partial(line_body, finish, keep_state, gain_sum, len(ins)),
        in_specs=[vmem] * (1 + len(ins)),
        out_specs=[vmem] * len(shapes),
        out_shape=shapes,
        scratch_shapes=[
            pltpu.VMEM((2, half, width), BF16),
            pltpu.VMEM((half, width), BF16),
            pltpu.VMEM((half, width), BF16),
            pltpu.SemaphoreType.DMA((4, count)),
            pltpu.SemaphoreType.DMA((5, count)),
        ],
        compiler_params=pltpu.CompilerParams(
            collective_id=identity, has_side_effects=True, vmem_limit_bytes=VMEM_BYTES
        ),
        cost_estimate=pl.CostEstimate(flops=0, bytes_accessed=100 * rows * width, transcendentals=0),
        name=name,
    )(partial, *ins)


def mean_square(values):
    return lax.rsqrt(jnp.mean(values * values, axis=1, keepdims=True) + EPSILON)


def finish_attention(total, whole, own, ins):
    tokens, gain = ins
    hidden = tokens[whole, :].astype(F32) + RESIDUAL_SCALE * total
    return (hidden * mean_square(hidden) * gain[...]).astype(BF16), hidden, None


def norm_pull(d_normed, values, gain):
    inverse = mean_square(values)
    scaled = gain * d_normed
    inner = jnp.mean(scaled * values, axis=1, keepdims=True)
    return inverse * scaled - values * inverse * inverse * inverse * inner, d_normed * values * inverse


def finish_ffn_back(total, whole, own, ins):
    hidden, grads, gain = ins
    pulled, gains = norm_pull(total, hidden[own, :], gain[...])
    d_hidden = grads[whole, :].astype(F32) + pulled
    return (RESIDUAL_SCALE * d_hidden).astype(BF16), d_hidden, gains


def finish_attention_back(total, whole, own, ins):
    tokens, d_hidden, gain = ins
    pulled, gains = norm_pull(total, tokens[whole, :].astype(F32), gain[...])
    return (d_hidden[own, :] + pulled).astype(BF16), None, gains


def grads_body(count, jobs, *refs):
    ins, rest = refs[: 2 * jobs], refs[2 * jobs :]
    outs, rest = rest[: count * jobs], rest[count * jobs :]
    stages, sems = rest[:jobs], rest[jobs]
    me = plane_index()

    def copies(slot, r):
        return [pltpu.make_async_copy(stages[j].at[slot], outs[r * jobs + j], sems.at[slot, j]) for j in range(jobs)]

    def step(i, carry):
        slot = lax.rem(i, 2)
        r = jnp.where(i < count // 2, 2 * i + 1, 2 * i - count)

        @pl.when(i >= 2)
        def _():
            for copy in copies(slot, 0):
                copy.wait()

        for j in range(jobs):
            left, right = ins[2 * j], ins[2 * j + 1]
            extent = left.shape[1] // count
            columns = pl.ds(pl.multiple_of((me ^ r) * extent, extent), extent)
            stages[j][slot] = lax.dot_general(
                left[:, columns], right[...], (((0,), (0,)), ((), ())), preferred_element_type=F32
            ).astype(BF16)
        for known in range(count):

            @pl.when(r == known)
            def _():
                for copy in copies(slot, known):
                    copy.start()

        return carry

    lax.fori_loop(0, count, step, 0)
    for slot in range(2):
        for copy in copies(slot, 0):
            copy.wait()


def grad_pieces(pairs, name):
    count = plane_size()
    jobs = len(pairs)
    extents = [left.shape[1] // count for left, _ in pairs]
    if any(extent % LANES for extent in extents):
        me = plane_index()
        return [
            [
                weight_grad(lax.dynamic_slice_in_dim(left, (me ^ r) * e, e, 1), right).astype(BF16)
                for r in range(count)
            ]
            for (left, right), e in zip(pairs, extents)
        ]
    piece_shapes = [(e, right.shape[1]) for e, (_, right) in zip(extents, pairs)]
    flat = pl.pallas_call(
        functools.partial(grads_body, count, jobs),
        in_specs=[pl.BlockSpec(memory_space=pltpu.VMEM)] * (2 * jobs),
        out_specs=[ANYWHERE] * (count * jobs),
        out_shape=[jax.ShapeDtypeStruct(shape, BF16) for _ in range(count) for shape in piece_shapes],
        scratch_shapes=[pltpu.VMEM((2,) + shape, BF16) for shape in piece_shapes]
        + [pltpu.SemaphoreType.DMA((2, jobs))],
        compiler_params=pltpu.CompilerParams(vmem_limit_bytes=VMEM_BYTES),
        cost_estimate=pl.CostEstimate(
            flops=sum(2 * left.shape[0] * left.shape[1] * right.shape[1] for left, right in pairs),
            bytes_accessed=sum(2 * left.shape[1] * right.shape[1] for left, right in pairs),
            transcendentals=0,
        ),
        name=name,
    )(*[value for pair in pairs for value in pair])
    return [flat[j::jobs] for j in range(jobs)]


def after(value, *others):
    return lax.optimization_barrier((value,) + others)[0]


def gather_context(piece):
    size = lax.axis_size("context")
    held = {0: piece}
    bit = size // 2
    while bit:
        for r in list(held):
            held[r | bit] = swap(held[r], "context", size, bit)
        bit //= 2
    return [held[r] for r in range(size)]


def reduce_context(pieces):
    size = len(pieces)
    held = dict(enumerate(pieces))
    bit = 1
    while bit < size:
        held = {
            r: held[r].astype(F32) + swap(held[r | bit].astype(BF16), "context", size, bit).astype(F32)
            for r in held
            if not r & bit
        }
        bit *= 2
    return held[0]


def stored_places(order_row, first, count):
    stored = first + jnp.arange(count, dtype=jnp.int32)
    picks = (stored // BLK)[:, None] == jnp.arange(order_row.shape[0], dtype=jnp.int32)[None, :]
    return jnp.sum(jnp.where(picks, order_row[None, :], 0), axis=1) * BLK + stored % BLK


def rope_tables(order, local_len):
    first = lax.axis_index("context") * local_len
    places = jnp.concatenate([stored_places(order[s], first, local_len) for s in range(order.shape[0])])
    half = HD // 2
    inverse = jnp.exp(jnp.arange(half, dtype=F32) * (-2.0 * math.log(ROPE_BASE) / HD))
    angles = places.astype(F32)[:, None] * jnp.tile(inverse, LANES // half)[None, :]
    return jnp.cos(angles), jnp.sin(angles)


def weight_grad(left, right):
    return lax.dot_general(left, right, (((0,), (0,)), ((), ())), preferred_element_type=F32)


def local(
    tokens, block_order, w_query, w_key, w_value, w_output, w_gate, w_up, w_down, norm_attn, norm_ffn, grad_out
):
    seqs, local_len, width = tokens.shape
    rows = seqs * local_len
    size = plane_size()
    me = plane_index()
    z = lax.axis_index("tensor")
    token_rows = tokens.reshape(rows, width)
    grad_rows = grad_out.reshape(rows, width)
    q_width, kv_width = w_query.shape[1], w_key.shape[1]
    units = w_down.shape[0]
    half = units // 2

    gains = gather_small(jnp.stack([norm_attn, norm_ffn])).reshape(2, width)
    gain_attn, gain_ffn = gains[0:1], gains[1:2]
    w_qkv = jnp.concatenate([w_query, w_key, w_value], axis=1)
    qkv_pieces, output_pieces = gather_pair(w_qkv, w_output)
    cosine, sine = rope_tables(block_order, local_len)
    normed, queries, keys_values = project_qkv(token_rows, gain_attn, cosine, sine, qkv_pieces, q_width)
    kv_pieces = gather_context(keys_values)
    early, late = qkv_pieces[-2], kv_pieces[-2]
    gate_pieces, up_pieces = gather_pair(w_gate, w_up, early, late)
    low_pieces, high_pieces = gather_pair(w_down[:half], w_down[half:], early, late)
    output_pieces, low_pieces, high_pieces = widened(output_pieces), widened(low_pieces), widened(high_pieces)

    mixture, logs = attend(block_order, queries, kv_pieces)
    branch = gathered_matmul(mixture, output_pieces, 1, False, "project_output")
    normed_ffn, hidden = line_sum(
        branch, [token_rows, gain_ffn], finish_attention, True, False, 0, "attention_sum"
    )
    d_ffn = (RESIDUAL_SCALE * grad_rows.astype(F32)).astype(BF16)
    active, d_gate, d_up, ffn_out, d_normed_ffn = ffn(
        normed_ffn, d_ffn, gate_pieces, up_pieces, low_pieces, high_pieces
    )
    d_branch, d_hidden, ffn_gain = line_sum(
        d_normed_ffn, [hidden, grad_rows, gain_ffn], finish_ffn_back, True, True, 1, "ffn_back_sum"
    )

    owner = lax.rem(z, 3) != 0
    padded = lax.dynamic_update_slice_in_dim(jnp.zeros((rows, width), F32), hidden, (z // 2) * (rows // 2), 0)
    out_part = RESIDUAL_SCALE * after(ffn_out, d_branch).astype(F32) + jnp.where(owner, padded, 0.0)
    layer_out = rows_gather(rows_sum(out_part.astype(BF16)).astype(BF16))

    grad_gate, grad_up, grad_low, grad_high = grad_pieces(
        [(normed_ffn, d_gate), (normed_ffn, d_up), (d_ffn, active[:, :half]), (d_ffn, active[:, half:])], "ffn_grads"
    )
    grad_gate, grad_up = reduce_pair(grad_gate, grad_up)
    grad_low, grad_high = reduce_pair(grad_low, grad_high)

    d_mixture = gathered_matmul(d_branch, output_pieces, 1, True, "project_output_back")
    d_queries, *d_pieces = attend_back(block_order, queries, d_mixture, logs, kv_pieces)
    d_keys_values = reduce_context(d_pieces)
    d_qkv, d_normed = project_qkv_back(d_queries, d_keys_values, cosine, sine, qkv_pieces)
    grad_qkv, grad_output = grad_pieces([(normed, d_qkv), (d_branch, mixture)], "attention_grads")
    grad_tokens, attn_gain = line_sum(
        d_normed, [token_rows, d_hidden, gain_attn], finish_attention_back, False, True, 2, "attention_back_sum"
    )
    grad_tokens = grad_tokens.astype(F32)
    grad_qkv, grad_output = reduce_pair(grad_qkv, grad_output)
    attn_gain, ffn_gain = jnp.sum(attn_gain, axis=0), jnp.sum(ffn_gain, axis=0)
    gain_grads = jnp.stack([attn_gain, ffn_gain])
    everyone = ("shard", "context", "tensor")
    world = size * lax.axis_size("tensor")
    bit = 1
    while bit < world:
        gain_grads = gain_grads + swap(gain_grads, everyone, world, bit)
        bit *= 2
    gain_grads = lax.dynamic_slice_in_dim(gain_grads, me * (width // size), width // size, 1)
    return (
        layer_out.reshape(seqs, local_len, width),
        grad_tokens.reshape(seqs, local_len, width),
        grad_qkv[:, :q_width],
        grad_qkv[:, q_width : q_width + kv_width],
        grad_qkv[:, q_width + kv_width :],
        grad_output.T,
        grad_gate,
        grad_up,
        jnp.concatenate([grad_low.T, grad_high.T], axis=0),
        gain_grads[0],
        gain_grads[1],
    )


def solution(mesh):
    split = P("shard", "context", None)
    inward, outward = P(PLANE, "tensor"), P("tensor", PLANE)
    gain = P(PLANE)
    return jax.shard_map(
        local,
        mesh=mesh,
        in_specs=(split, P("shard", None), inward, inward, inward, outward, inward, inward, outward, gain, gain, split),
        out_specs=(split, split, inward, inward, inward, outward, inward, inward, outward, gain, gain),
        check_vma=False,
    )
```

```python
import functools
import math

import jax
import jax.numpy as jnp
from jax import lax
from jax.experimental import pallas as pl
from jax.experimental.pallas import tpu as pltpu
from jax.sharding import PartitionSpec as P


HD = 64
BLK = 256
LANES = 128
EPSILON = 1e-05
SCORE_SCALE = 0.015625
RESIDUAL_SCALE = 0.22
ROPE_BASE = 10000000.0
MASKED_SCORE = -1e30
PLANE = ("shard", "context")
VMEM_BYTES = 64000 * 1024


F32 = jnp.float32
BF16 = jnp.bfloat16


def plane_size():
    return lax.axis_size("shard") * lax.axis_size("context")


def plane_index():
    return lax.axis_index("shard") * lax.axis_size("context") + lax.axis_index("context")


def swap(value, axes, size, bit):
    return lax.ppermute(value, axes, [(i, i ^ bit) for i in range(size)])


def gather_pair(first, second, far_after=(), near_after=(), cross_after=(), core_after=()):
    size = plane_size()
    bits = [1 << b for b in range(1, size.bit_length() - 1)]
    sides = [{0: first}, {0: second}]
    if len(bits) == 2:
        near, far = bits
        for side in sides:
            side[far] = swap(after(side[0], *far_after), PLANE, size, far)
        for side in reversed(sides):
            side[near] = swap(after(side[0], *near_after), PLANE, size, near)
        sides[0][near | far] = swap(after(sides[0][far], *cross_after), PLANE, size, near)
        sides[1][near | far] = swap(after(sides[1][near], *cross_after), PLANE, size, far)
    else:
        for side in sides:
            for bit in bits:
                for r in list(side):
                    side[r | bit] = swap(side[r], PLANE, size, bit)
    for side in sides:
        for r in list(side):
            side[r | 1] = swap(after(side[r], *core_after), PLANE, size, 1)
    return [[side[r] for r in range(size)] for side in sides]


def widened(pieces):
    level = 1
    while pieces[0].shape[1] < LANES:
        upper = (plane_index() // level) % 2 == 1
        pairs = zip(pieces[0::2], pieces[1::2])
        pieces = [jnp.where(upper, jnp.concatenate([b, a], 1), jnp.concatenate([a, b], 1)) for a, b in pairs]
        level *= 2
    return pieces


def take_sum(side, bit, kept):
    sent = side[kept | bit].astype(BF16)
    total = side[kept].astype(F32) + swap(sent, PLANE, plane_size(), bit).astype(F32)
    return total if kept == 0 else total.astype(BF16)


def reduce_pair(first, second):
    size = plane_size()
    bits = [1 << b for b in range(1, size.bit_length() - 1)]
    sides = [dict(first), dict(second)]
    if len(bits) == 2:
        near, far = bits
        sides[0][near] = take_sum(sides[0], far, near)
        sides[1][far] = take_sum(sides[1], near, far)
        done = []
        for side in sides:
            a = swap(side[near].astype(BF16), PLANE, size, near).astype(F32)
            b = swap(side[far].astype(BF16), PLANE, size, far).astype(F32)
            done.append(side[0] + a + b)
        return done
    done = []
    for side in sides:
        for bit in reversed(bits):
            side = {r: take_sum(side, bit, r) for r in side if not r & bit}
        done.append(side[0])
    return done


def gather_small(values):
    size = plane_size()
    stacked = values[None]
    bit = 1
    while bit < size:
        stacked = jnp.concatenate([stacked, swap(stacked, PLANE, size, bit)], axis=0)
        bit *= 2
    picks = jnp.arange(size, dtype=jnp.int32)[:, None] ^ plane_index()
    chosen = (picks == jnp.arange(size, dtype=jnp.int32)[None, :]).astype(F32)
    return jnp.einsum("ij,jkw->kiw", chosen, stacked.astype(F32), precision=lax.Precision.HIGHEST)


def chunk_of(rows, index, count):
    return lax.dynamic_slice_in_dim(rows, index * count, count, 0)


def rows_sum(partial):
    size = lax.axis_size("tensor")
    me = lax.axis_index("tensor")
    count = partial.shape[0] // size
    total = chunk_of(partial, me, count).astype(F32)
    for shift in range(1, size):
        sent = chunk_of(partial, lax.rem(me + shift, size), count)
        pairs = [(i, (i + shift) % size) for i in range(size)]
        total = total + lax.ppermute(sent, "tensor", pairs).astype(F32)
    return total


def rows_gather(chunk):
    size = lax.axis_size("tensor")
    me = lax.axis_index("tensor")
    count = chunk.shape[0]
    parts = [chunk]
    for shift in range(1, size):
        pairs = [(i, (i + shift) % size) for i in range(size)]
        parts.append(lax.ppermute(chunk, "tensor", pairs))
    whole = jnp.zeros((size * count,) + chunk.shape[1:], chunk.dtype)
    for shift in range(size):
        place = lax.rem(me - shift + size, size) * count
        whole = lax.dynamic_update_slice_in_dim(whole, parts[shift], place, 0)
    return whole


def params(steps):
    return pltpu.CompilerParams(
        dimension_semantics=("arbitrary",) * steps, vmem_limit_bytes=VMEM_BYTES
    )


def place_pieces(pieces, whole, sem, axis):
    size = len(pieces)
    me = plane_index() // (plane_size() // size)
    extent = whole.shape[axis] // size
    for r, piece in enumerate(pieces):
        start = pl.multiple_of((me ^ r) * extent, extent)
        target = whole.at[pl.ds(start, extent)] if axis == 0 else whole.at[:, pl.ds(start, extent)]
        pltpu.make_async_copy(piece, target, sem).start()


def await_whole(whole, sem):
    pltpu.make_async_copy(whole, whole, sem).wait()


ANYWHERE = pl.BlockSpec(memory_space=pl.ANY)


def turned(values, lane, sign):
    half = HD // 2
    upper = pltpu.roll(values, LANES - half, 1)
    lower = pltpu.roll(values, half, 1)
    return jnp.where(lane % HD < half, -sign * upper, sign * lower)


def qkv_body(count, tokens, gain, cosine, sine, *rest):
    pieces, (normed, queries, keys_values, weight, sem) = rest[:count], rest[count:]

    @pl.when(pl.program_id(0) == 0)
    def _():
        place_pieces(pieces, weight, sem, 0)

    values = tokens[...].astype(F32)
    inverse = lax.rsqrt(jnp.mean(values * values, axis=1, keepdims=True) + EPSILON)
    low = (values * inverse * gain[...]).astype(BF16)
    normed[...] = low

    @pl.when(pl.program_id(0) == 0)
    def _():
        await_whole(weight, sem)

    cos, sin = cosine[...], sine[...]
    lane = lax.broadcasted_iota(jnp.int32, cos.shape, 1)
    q_width = queries.shape[1]
    k_width = keys_values.shape[1] // 2
    for start in range(0, weight.shape[1], LANES):
        part = jnp.dot(low, weight[:, start : start + LANES * 1], preferred_element_type=F32)
        if start < q_width + k_width:
            part = part * cos + turned(part, lane, 1.0) * sin
        if start < q_width:
            queries[:, start : start + LANES] = (part.astype(BF16) * SCORE_SCALE).astype(BF16)
        else:
            keys_values[:, start - q_width : start - q_width + LANES] = part.astype(BF16)


def project_qkv(tokens, gain, cosine, sine, pieces, q_width):
    rows, width = tokens.shape
    total = pieces[0].shape[1]
    tile = min(rows, 256)
    row_spec = lambda w: pl.BlockSpec((tile, w), lambda i: (i, 0))
    return pl.pallas_call(
        functools.partial(qkv_body, len(pieces)),
        grid=(rows // tile,),
        in_specs=[row_spec(width), pl.BlockSpec((1, width), lambda i: (0, 0)), row_spec(LANES), row_spec(LANES)]
        + [ANYWHERE] * len(pieces),
        out_specs=[row_spec(width), row_spec(q_width), row_spec(total - q_width)],
        out_shape=[
            jax.ShapeDtypeStruct((rows, width), BF16),
            jax.ShapeDtypeStruct((rows, q_width), BF16),
            jax.ShapeDtypeStruct((rows, total - q_width), BF16),
        ],
        scratch_shapes=[pltpu.VMEM((width, total), BF16), pltpu.SemaphoreType.DMA],
        compiler_params=params(1),
        cost_estimate=pl.CostEstimate(
            flops=2 * rows * width * total, bytes_accessed=2 * (2 * rows * width + width * total), transcendentals=0
        ),
        name="project_qkv",
    )(tokens, gain, cosine, sine, *pieces)


def qkv_back_body(count, d_queries, d_keys_values, cosine, sine, *rest):
    pieces, (d_all, d_normed, weight, sem) = rest[:count], rest[count:]

    @pl.when(pl.program_id(0) == 0)
    def _():
        place_pieces(pieces, weight, sem, 0)

    cos, sin = cosine[...], sine[...]
    lane = lax.broadcasted_iota(jnp.int32, cos.shape, 1)
    q_width = d_queries.shape[1]
    k_width = d_keys_values.shape[1] // 2
    for start in range(0, d_all.shape[1], LANES):
        if start < q_width:
            part = d_queries[:, start : start + LANES]
        else:
            part = d_keys_values[:, start - q_width : start - q_width + LANES]
        if start < q_width + k_width:
            part = part * cos + turned(part * sin, lane, -1.0)
        d_all[:, start : start + LANES] = part.astype(BF16)

    @pl.when(pl.program_id(0) == 0)
    def _():
        await_whole(weight, sem)

    step = 512
    for start in range(0, weight.shape[0], step):
        d_normed[:, start : start + step] = lax.dot_general(
            d_all[...], weight[start : start + step, :], (((1,), (1,)), ((), ())), preferred_element_type=F32
        ).astype(BF16)


def project_qkv_back(d_queries, d_keys_values, cosine, sine, pieces):
    rows, q_width = d_queries.shape
    total = pieces[0].shape[1]
    width = pieces[0].shape[0] * len(pieces)
    tile = min(rows, 256)
    row_spec = lambda w: pl.BlockSpec((tile, w), lambda i: (i, 0))
    return pl.pallas_call(
        functools.partial(qkv_back_body, len(pieces)),
        grid=(rows // tile,),
        in_specs=[row_spec(q_width), row_spec(total - q_width), row_spec(LANES), row_spec(LANES)]
        + [ANYWHERE] * len(pieces),
        out_specs=[row_spec(total), row_spec(width)],
        out_shape=[jax.ShapeDtypeStruct((rows, total), BF16), jax.ShapeDtypeStruct((rows, width), BF16)],
        scratch_shapes=[pltpu.VMEM((width, total), BF16), pltpu.SemaphoreType.DMA],
        compiler_params=params(1),
        cost_estimate=pl.CostEstimate(
            flops=2 * rows * width * total, bytes_accessed=2 * (2 * rows * width + width * total), transcendentals=0
        ),
        name="project_qkv_back",
    )(d_queries, d_keys_values, cosine, sine, *pieces)


def gathered_body(count, axis, transposed, left, *rest):
    pieces, (out, weight, sem) = rest[:count], rest[count:]

    @pl.when(pl.program_id(0) == 0)
    def _():
        place_pieces(pieces, weight, sem, axis)
        await_whole(weight, sem)

    step = min(out.shape[1], 512)
    for start in range(0, out.shape[1], step):
        if transposed:
            part = lax.dot_general(
                left[...], weight[start : start + step, :], (((1,), (1,)), ((), ())), preferred_element_type=F32
            )
        else:
            part = jnp.dot(left[...], weight[:, start : start + step], preferred_element_type=F32)
        out[:, start : start + step] = part.astype(out.dtype)


def gathered_matmul(left, pieces, axis, transposed):
    rows = left.shape[0]
    shape = list(pieces[0].shape)
    shape[axis] *= len(pieces)
    outer = shape[0] if transposed else shape[1]
    tile = min(rows, 256)
    return pl.pallas_call(
        functools.partial(gathered_body, len(pieces), axis, transposed),
        grid=(rows // tile,),
        in_specs=[pl.BlockSpec((tile, left.shape[1]), lambda i: (i, 0))] + [ANYWHERE] * len(pieces),
        out_specs=pl.BlockSpec((tile, outer), lambda i: (i, 0)),
        out_shape=jax.ShapeDtypeStruct((rows, outer), BF16),
        scratch_shapes=[pltpu.VMEM(tuple(shape), BF16), pltpu.SemaphoreType.DMA],
        compiler_params=params(1),
        cost_estimate=pl.CostEstimate(
            flops=2 * rows * shape[0] * shape[1],
            bytes_accessed=2 * (rows * sum(shape) + shape[0] * shape[1]),
            transcendentals=0,
        ),
    )(left, *pieces)


def ffn_body(count, narrow, tile, normed, d_ffn, *rest):
    gate_pieces, up_pieces, rest = rest[:count], rest[count : 2 * count], rest[2 * count :]
    low_pieces, high_pieces, rest = rest[:narrow], rest[narrow : 2 * narrow], rest[2 * narrow :]
    active, d_gate, d_up, out, d_normed, gate, up, down, out_sum, d_sum, sems = rest
    f_step = pl.program_id(1)
    half = down.shape[0] // 2

    @pl.when((pl.program_id(0) == 0) & (f_step == 0))
    def _():
        place_pieces(gate_pieces, gate, sems.at[0], 0)
        place_pieces(up_pieces, up, sems.at[1], 0)
        place_pieces(low_pieces, down.at[pl.ds(0, half)], sems.at[2], 1)
        place_pieces(high_pieces, down.at[pl.ds(half, half)], sems.at[3], 1)
        await_whole(gate, sems.at[0])
        await_whole(up, sems.at[1])
        await_whole(down.at[pl.ds(0, half)], sems.at[2])
        await_whole(down.at[pl.ds(half, half)], sems.at[3])

    units = pl.ds(pl.multiple_of(f_step * tile, tile), tile)
    gate_tile, up_tile, down_tile = gate[:, units], up[:, units], down[units, :]
    gate_in = jnp.dot(normed[...], gate_tile, preferred_element_type=F32)
    upward = jnp.dot(normed[...], up_tile, preferred_element_type=F32)
    d_active = lax.dot_general(d_ffn[...], down_tile, (((1,), (1,)), ((), ())), preferred_element_type=F32)
    sigma = 1.0 / (1.0 + jnp.exp(-gate_in))
    silu = gate_in * sigma
    active_low = (silu * upward).astype(BF16)
    gate_low = (d_active * upward * (sigma * (1.0 + gate_in * (1.0 - sigma)))).astype(BF16)
    up_low = (d_active * silu).astype(BF16)
    active[...] = active_low
    d_gate[...] = gate_low
    d_up[...] = up_low
    part = jnp.dot(active_low, down_tile, preferred_element_type=F32)
    d_part = lax.dot_general(gate_low, gate_tile, (((1,), (1,)), ((), ())), preferred_element_type=F32)
    d_part += lax.dot_general(up_low, up_tile, (((1,), (1,)), ((), ())), preferred_element_type=F32)

    @pl.when(f_step == 0)
    def _():
        out_sum[...] = part
        d_sum[...] = d_part

    @pl.when(f_step > 0)
    def _():
        out_sum[...] += part
        d_sum[...] += d_part

    @pl.when(f_step == pl.num_programs(1) - 1)
    def _():
        out[...] = out_sum[...].astype(BF16)
        d_normed[...] = d_sum[...].astype(BF16)


def ffn(normed, d_ffn, gate_pieces, up_pieces, low_pieces, high_pieces):
    rows, width = normed.shape
    units = gate_pieces[0].shape[1]
    count = len(gate_pieces)
    tile = 256
    row_tile = min(rows, 512)
    once = pl.Buffered(1)
    row_spec = pl.BlockSpec((row_tile, width), lambda i, f: (i, 0), pipeline_mode=once)
    unit_spec = pl.BlockSpec((row_tile, tile), lambda i, f: (i, f))
    unit_shape = jax.ShapeDtypeStruct((rows, units), BF16)
    row_shape = jax.ShapeDtypeStruct((rows, width), BF16)
    return pl.pallas_call(
        functools.partial(ffn_body, count, len(low_pieces), tile),
        grid=(rows // row_tile, units // tile),
        in_specs=[row_spec, row_spec] + [ANYWHERE] * (2 * count + 2 * len(low_pieces)),
        out_specs=[unit_spec, unit_spec, unit_spec, row_spec, row_spec],
        out_shape=[unit_shape, unit_shape, unit_shape, row_shape, row_shape],
        scratch_shapes=[
            pltpu.VMEM((width, units), BF16),
            pltpu.VMEM((width, units), BF16),
            pltpu.VMEM((units, width), BF16),
            pltpu.VMEM((row_tile, width), F32),
            pltpu.VMEM((row_tile, width), F32),
            pltpu.SemaphoreType.DMA((4,)),
        ],
        compiler_params=params(2),
        cost_estimate=pl.CostEstimate(
            flops=12 * rows * width * units, bytes_accessed=6 * width * units + 14 * rows * width, transcendentals=rows * units
        ),
        name="feed_forward",
    )(normed, d_ffn, *gate_pieces, *up_pieces, *low_pieces, *high_pieces)


def doubled(values, lane, head):
    rolled = pltpu.roll(values.astype(F32), HD, 1).astype(BF16)
    return jnp.where((lane < HD) == (head == 0), values, rolled)


def block_bias(order, seq, r, block):
    per = order.shape[1] // lax.axis_size("context")
    own = order[seq, lax.axis_index("context") * per + pl.program_id(3)]
    other = order[seq, (lax.axis_index("context") ^ r) * per + block]
    return jnp.where(other <= own, 0.0, MASKED_SCORE).astype(F32)


def masked_scores(order, pieces_k, query):
    seq = pl.program_id(0)
    scores = []
    for r, key_rows in enumerate(pieces_k):
        part = lax.dot_general(key_rows, query, (((1,), (1,)), ((), ())), preferred_element_type=F32)
        for block in range(key_rows.shape[0] // BLK):
            bias = block_bias(order, seq, r, block)
            scores.append(part[block * BLK : (block + 1) * BLK] + bias)
    return scores


def attend_body(count, order, query_ref, *rest):
    pieces, (mixture, logs) = rest[:count], rest[count:]
    head = pl.program_id(1)
    lane = lax.broadcasted_iota(jnp.int32, (1, LANES), 1)
    keys = [doubled(piece[:, :LANES], lane, head) for piece in pieces]
    values = [doubled(piece[:, LANES:], lane, head) for piece in pieces]
    query = query_ref[...]
    parts = []
    for side in range(2):
        chosen = (lane < HD) if side == 0 else (lane >= HD)
        scores = masked_scores(order, keys, jnp.where(chosen, query, jnp.zeros_like(query)))
        top = functools.reduce(jnp.maximum, [jnp.max(s, axis=0, keepdims=True) for s in scores])
        powers = [jnp.exp(s - top) for s in scores]
        total = sum(jnp.sum(p, axis=0, keepdims=True) for p in powers)
        low = jnp.concatenate([p.astype(BF16) for p in powers], axis=0)
        whole = jnp.concatenate(values, axis=0)
        mixed = lax.dot_general(whole, low, (((0,), (0,)), ((), ())), preferred_element_type=F32)
        parts.append(mixed / total)
        logs[side : side + 1, :] = top + jnp.log(total)
    row = lax.broadcasted_iota(jnp.int32, (LANES, 1), 0)
    mixture[...] = jnp.where(row < HD, parts[0], parts[1]).T.astype(BF16)


def attend_specs(order, queries, group_pairs):
    seqs = order.shape[0]
    rows = queries.shape[0] // seqs
    tiles = rows // BLK
    grid = (seqs, 2, group_pairs, tiles)
    q_spec = pl.BlockSpec((BLK, LANES), lambda s, h, g, t: (s * tiles + t, h * group_pairs + g))
    kv_spec = pl.BlockSpec((rows, 2 * LANES), lambda s, h, g, t: (s, 0))
    log_spec = pl.BlockSpec((None, 2, BLK), lambda s, h, g, t: (h * group_pairs + g, 0, s * tiles + t))
    return grid, q_spec, kv_spec, log_spec


def attend(order, queries, pieces):
    rows, q_width = queries.shape
    pairs = q_width // LANES
    grid, q_spec, kv_spec, log_spec = attend_specs(order, queries, pairs // 2)
    keys = rows * len(pieces) // order.shape[0]
    return pl.pallas_call(
        functools.partial(attend_body, len(pieces)),
        grid=grid,
        in_specs=[pl.BlockSpec(memory_space=pltpu.SMEM), q_spec] + [kv_spec] * len(pieces),
        out_specs=[q_spec, log_spec],
        out_shape=[jax.ShapeDtypeStruct((rows, q_width), BF16), jax.ShapeDtypeStruct((pairs, 2, rows), F32)],
        compiler_params=params(4),
        cost_estimate=pl.CostEstimate(
            flops=8 * rows * keys * q_width * 2, bytes_accessed=8 * rows * q_width, transcendentals=rows * keys * q_width // HD
        ),
        name="attend",
    )(order, queries, *pieces)


def attend_back_body(count, order, query_ref, grad_ref, logs, *rest):
    pieces, rest = rest[:count], rest[count:]
    d_query, outs, (d_key_sum, d_value_sum) = rest[0], rest[1 : 1 + count], rest[1 + count :]
    head, pair, tile = pl.program_id(1), pl.program_id(2), pl.program_id(3)
    lane = lax.broadcasted_iota(jnp.int32, (1, LANES), 1)
    keys = [doubled(piece[:, :LANES], lane, head) for piece in pieces]
    values = jnp.concatenate([doubled(piece[:, LANES:], lane, head) for piece in pieces], axis=0)
    whole_keys = jnp.concatenate(keys, axis=0)
    parts, d_keys, d_values = [], 0.0, 0.0
    for side in range(2):
        chosen = (lane < HD) if side == 0 else (lane >= HD)
        query = jnp.where(chosen, query_ref[...], jnp.zeros_like(query_ref[...]))
        grad = jnp.where(chosen, grad_ref[...], jnp.zeros_like(grad_ref[...]))
        scores = jnp.concatenate(masked_scores(order, keys, query), axis=0)
        soft = jnp.exp(scores - logs[side : side + 1, :])
        d_soft = lax.dot_general(values, grad, (((1,), (1,)), ((), ())), preferred_element_type=F32)
        inner = jnp.sum(soft * d_soft, axis=0, keepdims=True)
        d_scores = (soft * (d_soft - inner)).astype(BF16)
        d_values += jnp.dot(soft.astype(BF16), grad, preferred_element_type=F32)
        d_keys += jnp.dot(d_scores, query, preferred_element_type=F32)
        parts.append(lax.dot_general(whole_keys, d_scores, (((0,), (0,)), ((), ())), preferred_element_type=F32))
    row = lax.broadcasted_iota(jnp.int32, (LANES, 1), 0)
    d_query[...] = jnp.where(row < HD, parts[0], parts[1]).T * SCORE_SCALE

    first = (pair == 0) & (tile == 0)
    last = (pair == pl.num_programs(2) - 1) & (tile == pl.num_programs(3) - 1)

    @pl.when(first)
    def _():
        d_key_sum[...] = d_keys
        d_value_sum[...] = d_values

    @pl.when(jnp.logical_not(first))
    def _():
        d_key_sum[...] += d_keys
        d_value_sum[...] += d_values

    @pl.when(last)
    def _():
        wanted = (lane < HD) == (head == 0)
        rows = outs[0].shape[0]
        for r, out in enumerate(outs):
            for base, total in ((0, d_key_sum), (LANES, d_value_sum)):
                part = total[r * rows : (r + 1) * rows, :]
                both = (part + pltpu.roll(part, HD, 1)).astype(out.dtype)
                spot = pl.ds(base, LANES)

                @pl.when(head == 0)
                def _():
                    out[:, spot] = both

                @pl.when(head == 1)
                def _():
                    out[:, spot] = jnp.where(wanted, both.astype(F32), out[:, spot].astype(F32)).astype(out.dtype)


def attend_back(order, queries, grads, logs, pieces):
    rows, q_width = queries.shape
    pairs = q_width // LANES
    grid, q_spec, kv_spec, log_spec = attend_specs(order, queries, pairs // 2)
    keys = rows * len(pieces) // order.shape[0]
    return pl.pallas_call(
        functools.partial(attend_back_body, len(pieces)),
        grid=grid,
        in_specs=[pl.BlockSpec(memory_space=pltpu.SMEM), q_spec, q_spec, log_spec] + [kv_spec] * len(pieces),
        out_specs=[q_spec] + [kv_spec] * len(pieces),
        out_shape=[jax.ShapeDtypeStruct((rows, q_width), F32)]
        + [jax.ShapeDtypeStruct((rows, 2 * LANES), F32 if r % 2 == 0 else BF16) for r in range(len(pieces))],
        scratch_shapes=[pltpu.VMEM((keys, LANES), F32), pltpu.VMEM((keys, LANES), F32)],
        compiler_params=params(4),
        cost_estimate=pl.CostEstimate(
            flops=20 * rows * keys * q_width * 2, bytes_accessed=12 * rows * q_width, transcendentals=rows * keys * q_width // HD
        ),
        name="attend_back",
    )(order, queries, grads, logs, *pieces)


def line_steps(rows):
    half = rows // 2
    sub = 16
    return half, sub, half // sub


def line_body(finish, keep_state, gain_sum, n_in, *refs):
    partial, ins, rest = refs[0], refs[1 : 1 + n_in], refs[1 + n_in :]
    result, rest = rest[0], rest[1:]
    state_out, rest = (rest[0], rest[1:]) if keep_state else (None, rest)
    gain_out, rest = (rest[0], rest[1:]) if gain_sum else (None, rest)
    from_outer, from_peer, staged, send, recv = rest
    half, sub, count = line_steps(partial.shape[0])
    me = lax.axis_index("tensor")
    side = me // 2
    inner = lax.rem(me, 3) != 0
    to_outer, to_inner, to_peer = side * 3, 1 + side, 3 - me
    near, far = side * half, (1 - side) * half

    def rows(base, k):
        return pl.ds(pl.multiple_of(base + k * sub, sub), sub)

    def remote(source, target, s, r, k, where):
        return pltpu.make_async_remote_copy(
            src_ref=source,
            dst_ref=target,
            send_sem=send.at[s, k],
            recv_sem=recv.at[r, k],
            device_id={"tensor": where},
            device_id_type=pl.DeviceIdType.MESH,
        )

    def up_far(k):
        return remote(partial.at[rows(far, k)], from_outer.at[0, rows(0, k)], 0, 0, k, to_inner)

    def up_near(k):
        return remote(partial.at[rows(near, k)], from_outer.at[1, rows(0, k)], 1, 1, k, to_inner)

    def across(k):
        return remote(staged.at[rows(0, k)], from_peer.at[rows(0, k)], 0, 2, k, to_peer)

    def over(k, base):
        return remote(result.at[rows(base, k)], result.at[rows(base, k)], 2, 4, k, to_peer)

    def down_near(k):
        return remote(result.at[rows(near, k)], result.at[rows(near, k)], 1, 3, k, to_outer)

    def down_far(k):
        return remote(result.at[rows(far, k)], result.at[rows(far, k)], 3, 4, k, to_outer)

    barrier = pltpu.get_barrier_semaphore()

    def greet(where):
        pl.semaphore_signal(barrier, inc=1, device_id={"tensor": where}, device_id_type=pl.DeviceIdType.MESH)

    if gain_sum:
        gain_out[...] = jnp.zeros_like(gain_out)

    @pl.when(inner)
    def _():
        greet(to_outer)
        greet(to_peer)
        pl.semaphore_wait(barrier, 2)

        def step(k, carry):
            @pl.when(k < count)
            def _():
                up_far(k).wait_recv()
                total = partial[rows(far, k), :].astype(F32) + from_outer[0, rows(0, k), :].astype(F32)
                staged[rows(0, k), :] = total.astype(BF16)
                across(k).start()

            @pl.when((k >= 1) & (k <= count))
            def _():
                j = k - 1
                up_near(j).wait_recv()
                across(j).wait_recv()
                total = partial[rows(near, j), :].astype(F32) + from_outer[1, rows(0, j), :].astype(F32)
                total = total + from_peer[rows(0, j), :].astype(F32)
                low, state, gains = finish(total, rows(near, j), rows(0, j), ins)
                result[rows(near, j), :] = low
                if keep_state:
                    state_out[rows(0, j), :] = state
                if gain_sum:
                    gain_out[...] += jnp.sum(gains.reshape(sub // 8, 8, gains.shape[1]), axis=0)
                down_near(j).start()
                over(j, near).start()

            @pl.when(k >= 3)
            def _():
                over(k - 3, far).wait_recv()
                down_far(k - 3).start()

            return carry

        lax.fori_loop(0, count + 3, step, 0)

        def drain(k, carry):
            across(k).wait_send()
            down_near(k).wait_send()
            over(k, near).wait_send()
            down_far(k).wait_send()
            return carry

        lax.fori_loop(0, count, drain, 0)

    @pl.when(jnp.logical_not(inner))
    def _():
        greet(to_inner)
        pl.semaphore_wait(barrier, 1)

        def step(k, carry):
            up_far(k).start()
            up_near(k).start()
            return carry

        lax.fori_loop(0, count, step, 0)

        def drain(k, carry):
            down_near(k).wait_recv()
            down_far(k).wait_recv()
            up_far(k).wait_send()
            up_near(k).wait_send()
            return carry

        lax.fori_loop(0, count, drain, 0)


def line_sum(partial, ins, finish, keep_state, gain_sum, identity):
    rows, width = partial.shape
    half, _, count = line_steps(rows)
    vmem = pl.BlockSpec(memory_space=pltpu.VMEM)
    shapes = [jax.ShapeDtypeStruct((rows, width), BF16)]
    if keep_state:
        shapes.append(jax.ShapeDtypeStruct((half, width), F32))
    if gain_sum:
        shapes.append(jax.ShapeDtypeStruct((8, width), F32))
    return pl.pallas_call(
        functools.partial(line_body, finish, keep_state, gain_sum, len(ins)),
        in_specs=[vmem] * (1 + len(ins)),
        out_specs=[vmem] * len(shapes),
        out_shape=shapes,
        scratch_shapes=[
            pltpu.VMEM((2, half, width), BF16),
            pltpu.VMEM((half, width), BF16),
            pltpu.VMEM((half, width), BF16),
            pltpu.SemaphoreType.DMA((4, count)),
            pltpu.SemaphoreType.DMA((5, count)),
        ],
        compiler_params=pltpu.CompilerParams(
            collective_id=identity, has_side_effects=True, vmem_limit_bytes=VMEM_BYTES
        ),
        cost_estimate=pl.CostEstimate(flops=0, bytes_accessed=100 * rows * width, transcendentals=0),
    )(partial, *ins)


def mean_square(values):
    return lax.rsqrt(jnp.mean(values * values, axis=1, keepdims=True) + EPSILON)


def finish_attention(total, whole, own, ins):
    tokens, gain = ins
    hidden = tokens[whole, :].astype(F32) + RESIDUAL_SCALE * total
    return (hidden * mean_square(hidden) * gain[...]).astype(BF16), hidden, None


def norm_pull(d_normed, values, gain):
    inverse = mean_square(values)
    scaled = gain * d_normed
    inner = jnp.mean(scaled * values, axis=1, keepdims=True)
    return inverse * scaled - values * inverse * inverse * inverse * inner, d_normed * values * inverse


def finish_ffn_back(total, whole, own, ins):
    hidden, grads, gain = ins
    pulled, gains = norm_pull(total, hidden[own, :], gain[...])
    d_hidden = grads[whole, :].astype(F32) + pulled
    return (RESIDUAL_SCALE * d_hidden).astype(BF16), d_hidden, gains


def finish_attention_back(total, whole, own, ins):
    tokens, d_hidden, gain = ins
    pulled, gains = norm_pull(total, tokens[whole, :].astype(F32), gain[...])
    return (d_hidden[own, :] + pulled).astype(BF16), None, gains


def grads_body(count, jobs, *refs):
    ins, rest = refs[: 2 * jobs], refs[2 * jobs :]
    halves = count // 2
    outs, rest = rest[: halves * jobs], rest[halves * jobs :]
    sent, got, own = rest[:jobs], rest[jobs : 2 * jobs], rest[2 * jobs : 3 * jobs]
    send, recv, done = rest[3 * jobs :]
    me = plane_index()
    mate = {"context": lax.axis_index("context") ^ 1}
    mesh_ids = pl.DeviceIdType.MESH

    def piece(j, r):
        left, right = ins[2 * j], ins[2 * j + 1]
        extent = left.shape[1] // count
        columns = pl.ds(pl.multiple_of((me ^ r) * extent, extent), extent)
        return lax.dot_general(left[:, columns], right[...], (((0,), (0,)), ((), ())), preferred_element_type=F32)

    def across(j, i):
        return pltpu.make_async_remote_copy(
            src_ref=sent[j].at[i],
            dst_ref=got[j].at[i],
            send_sem=send.at[j, i],
            recv_sem=recv.at[j, i],
            device_id=mate,
            device_id_type=mesh_ids,
        )

    barrier = pltpu.get_barrier_semaphore()
    pl.semaphore_signal(barrier, inc=1, device_id=mate, device_id_type=mesh_ids)
    pl.semaphore_wait(barrier, 1)

    def odd(step, carry):
        i = halves - 1 - step
        for j in range(jobs):
            sent[j][i] = piece(j, 2 * i + 1).astype(BF16)
            across(j, i).start()
        return carry

    lax.fori_loop(0, halves, odd, 0)

    def even(step, carry):
        i = halves - 1 - step
        for j in range(jobs):
            value = piece(j, 2 * i)
            across(j, i).wait_recv()
            value = value + got[j][i].astype(F32)

            @pl.when(i > 0)
            def _():
                got[j][i] = value.astype(BF16)

            @pl.when(i == 0)
            def _():
                own[j][...] = value

        for known in range(halves):

            @pl.when(i == known)
            def _():
                for j in range(jobs):
                    source = got[j].at[known] if known else own[j]
                    pltpu.make_async_copy(source, outs[known * jobs + j], done.at[known, j]).start()

        return carry

    lax.fori_loop(0, halves, even, 0)
    for known in range(halves):
        for j in range(jobs):
            source = got[j].at[known] if known else own[j]
            pltpu.make_async_copy(source, outs[known * jobs + j], done.at[known, j]).wait()
            across(j, known).wait_send()


def plane_grads(pairs, identity):
    count = plane_size()
    halves = count // 2
    jobs = len(pairs)
    extents = [left.shape[1] // count for left, _ in pairs]
    if any(extent % LANES for extent in extents):
        me = plane_index()
        sides = []
        for (left, right), e in zip(pairs, extents):
            columns = lambda r: lax.dynamic_slice_in_dim(left, (me ^ r) * e, e, 1)
            whole = {r: weight_grad(columns(r), right).astype(BF16) for r in range(count)}
            sides.append({r: take_sum(whole, 1, r) for r in range(0, count, 2)})
        return sides
    shapes = [(e, right.shape[1]) for e, (_, right) in zip(extents, pairs)]
    flat = pl.pallas_call(
        functools.partial(grads_body, count, jobs),
        in_specs=[pl.BlockSpec(memory_space=pltpu.VMEM)] * (2 * jobs),
        out_specs=[ANYWHERE] * (halves * jobs),
        out_shape=[jax.ShapeDtypeStruct(shape, BF16 if i else F32) for i in range(halves) for shape in shapes],
        scratch_shapes=[pltpu.VMEM((halves,) + shape, BF16) for shape in shapes] * 2
        + [pltpu.VMEM(shape, F32) for shape in shapes]
        + [
            pltpu.SemaphoreType.DMA((jobs, halves)),
            pltpu.SemaphoreType.DMA((jobs, halves)),
            pltpu.SemaphoreType.DMA((halves, jobs)),
        ],
        compiler_params=pltpu.CompilerParams(
            collective_id=identity, has_side_effects=True, vmem_limit_bytes=VMEM_BYTES
        ),
        cost_estimate=pl.CostEstimate(
            flops=sum(2 * left.shape[0] * left.shape[1] * right.shape[1] for left, right in pairs),
            bytes_accessed=sum(2 * left.shape[1] * right.shape[1] for left, right in pairs),
            transcendentals=0,
        ),
    )(*[value for pair in pairs for value in pair])
    return [{2 * i: flat[i * jobs + j] for i in range(halves)} for j in range(jobs)]


def after(value, *others):
    return lax.optimization_barrier((value,) + others)[0] if others else value


def gather_context(piece):
    size = lax.axis_size("context")
    held = {0: piece}
    bit = size // 2
    while bit:
        for r in list(held):
            held[r | bit] = swap(held[r], "context", size, bit)
        bit //= 2
    return [held[r] for r in range(size)]


def reduce_context(pieces):
    size = len(pieces)
    held = dict(enumerate(pieces))
    bit = 1
    while bit < size:
        held = {
            r: held[r].astype(F32) + swap(held[r | bit].astype(BF16), "context", size, bit).astype(F32)
            for r in held
            if not r & bit
        }
        bit *= 2
    return held[0]


def stored_places(order_row, first, count):
    stored = first + jnp.arange(count, dtype=jnp.int32)
    picks = (stored // BLK)[:, None] == jnp.arange(order_row.shape[0], dtype=jnp.int32)[None, :]
    return jnp.sum(jnp.where(picks, order_row[None, :], 0), axis=1) * BLK + stored % BLK


def rope_tables(order, local_len):
    first = lax.axis_index("context") * local_len
    places = jnp.concatenate([stored_places(order[s], first, local_len) for s in range(order.shape[0])])
    half = HD // 2
    inverse = jnp.exp(jnp.arange(half, dtype=F32) * (-2.0 * math.log(ROPE_BASE) / HD))
    angles = places.astype(F32)[:, None] * jnp.tile(inverse, LANES // half)[None, :]
    return jnp.cos(angles), jnp.sin(angles)


def weight_grad(left, right):
    return lax.dot_general(left, right, (((0,), (0,)), ((), ())), preferred_element_type=F32)


def local(
    tokens, block_order, w_query, w_key, w_value, w_output, w_gate, w_up, w_down, norm_attn, norm_ffn, grad_out
):
    seqs, local_len, width = tokens.shape
    rows = seqs * local_len
    size = plane_size()
    me = plane_index()
    z = lax.axis_index("tensor")
    token_rows = tokens.reshape(rows, width)
    grad_rows = grad_out.reshape(rows, width)
    q_width, kv_width = w_query.shape[1], w_key.shape[1]
    units = w_down.shape[0]
    half = units // 2

    gains = gather_small(jnp.stack([norm_attn, norm_ffn])).reshape(2, width)
    gain_attn, gain_ffn = gains[0:1], gains[1:2]
    w_qkv = jnp.concatenate([w_query, w_key, w_value], axis=1)
    qkv_pieces, output_pieces = gather_pair(w_qkv, w_output)
    cosine, sine = rope_tables(block_order, local_len)
    normed, queries, keys_values = project_qkv(token_rows, gain_attn, cosine, sine, qkv_pieces, q_width)
    kv_pieces = gather_context(keys_values)
    early, late = [qkv_pieces[-2], output_pieces[-2], output_pieces[size // 2]], [kv_pieces[-2]]
    mixture, logs = attend(block_order, queries, kv_pieces)
    output_pieces = widened(output_pieces)
    branch = gathered_matmul(mixture, output_pieces, 1, False)
    normed_ffn, hidden = line_sum(branch, [token_rows, gain_ffn], finish_attention, True, False, 0)
    gate_pieces, up_pieces = gather_pair(w_gate, w_up, early, late, [mixture], [normed_ffn])
    low_pieces, high_pieces = gather_pair(w_down[:half], w_down[half:], early, late, [normed_ffn], [normed_ffn])
    low_pieces, high_pieces = widened(low_pieces), widened(high_pieces)
    d_ffn = (RESIDUAL_SCALE * grad_rows.astype(F32)).astype(BF16)
    active, d_gate, d_up, ffn_out, d_normed_ffn = ffn(
        normed_ffn, d_ffn, gate_pieces, up_pieces, low_pieces, high_pieces
    )
    grad_gate, grad_up, grad_low, grad_high = plane_grads(
        [(normed_ffn, d_gate), (normed_ffn, d_up), (d_ffn, active[:, :half]), (d_ffn, active[:, half:])], 3
    )
    d_normed_ffn = after(d_normed_ffn, grad_gate[0])
    d_branch, d_hidden, ffn_gain = line_sum(d_normed_ffn, [hidden, grad_rows, gain_ffn], finish_ffn_back, True, True, 1)

    grad_gate, grad_up = reduce_pair(grad_gate, grad_up)
    grad_low, grad_high = reduce_pair(grad_low, grad_high)

    owner = lax.rem(z, 3) != 0
    padded = lax.dynamic_update_slice_in_dim(jnp.zeros((rows, width), F32), hidden, (z // 2) * (rows // 2), 0)
    out_part = RESIDUAL_SCALE * after(ffn_out, d_branch).astype(F32) + jnp.where(owner, padded, 0.0)
    layer_out = rows_gather(rows_sum(out_part.astype(BF16)).astype(BF16))

    d_mixture = gathered_matmul(d_branch, output_pieces, 1, True)
    d_queries, *d_pieces = attend_back(block_order, queries, d_mixture, logs, kv_pieces)
    d_keys_values = reduce_context(d_pieces)
    d_qkv, d_normed = project_qkv_back(d_queries, d_keys_values, cosine, sine, qkv_pieces)
    grad_qkv, grad_output = plane_grads([(normed, d_qkv), (d_branch, mixture)], 4)
    d_normed = after(d_normed, grad_qkv[0])
    grad_tokens, attn_gain = line_sum(
        d_normed, [token_rows, d_hidden, gain_attn], finish_attention_back, False, True, 2
    )
    grad_tokens = grad_tokens.astype(F32)
    grad_qkv, grad_output = reduce_pair(grad_qkv, grad_output)
    attn_gain, ffn_gain = jnp.sum(attn_gain, axis=0), jnp.sum(ffn_gain, axis=0)
    gain_grads = jnp.stack([attn_gain, ffn_gain])
    everyone = ("shard", "context", "tensor")
    world = size * lax.axis_size("tensor")
    bit = 1
    while bit < world:
        gain_grads = gain_grads + swap(gain_grads, everyone, world, bit)
        bit *= 2
    gain_grads = lax.dynamic_slice_in_dim(gain_grads, me * (width // size), width // size, 1)
    return (
        layer_out.reshape(seqs, local_len, width),
        grad_tokens.reshape(seqs, local_len, width),
        grad_qkv[:, :q_width],
        grad_qkv[:, q_width : q_width + kv_width],
        grad_qkv[:, q_width + kv_width :],
        grad_output.T,
        grad_gate,
        grad_up,
        jnp.concatenate([grad_low.T, grad_high.T], axis=0),
        gain_grads[0],
        gain_grads[1],
    )


def solution(mesh):
    split = P("shard", "context", None)
    inward, outward = P(PLANE, "tensor"), P("tensor", PLANE)
    gain = P(PLANE)
    return jax.shard_map(
        local,
        mesh=mesh,
        in_specs=(split, P("shard", None), inward, inward, inward, outward, inward, inward, outward, gain, gain, split),
        out_specs=(split, split, inward, inward, inward, outward, inward, inward, outward, gain, gain),
        check_vma=False,
    )
```

```python
import functools
import math

import jax
import jax.numpy as jnp
from jax import lax
from jax.experimental import pallas as pl
from jax.experimental.pallas import tpu as pltpu
from jax.sharding import PartitionSpec as P


HD = 64
BLK = 256
LANES = 128
EPSILON = 1e-05
SCORE_SCALE = 0.015625
RESIDUAL_SCALE = 0.22
ROPE_BASE = 10000000.0
MASKED_SCORE = -1e30
PLANE = ("shard", "context")
VMEM_BYTES = 64000 * 1024


F32 = jnp.float32
BF16 = jnp.bfloat16


def plane_size():
    return lax.axis_size("shard") * lax.axis_size("context")


def plane_index():
    return lax.axis_index("shard") * lax.axis_size("context") + lax.axis_index("context")


def swap(value, axes, size, bit):
    return lax.ppermute(value, axes, [(i, i ^ bit) for i in range(size)])


def gather_pair(first, second, far_after=(), near_after=(), cross_after=(), core_after=(), core=True):
    size = plane_size()
    bits = [1 << b for b in range(1, size.bit_length() - 1)]
    sides = [{0: first}, {0: second}]
    if len(bits) == 2:
        near, far = bits
        for side in sides:
            side[far] = swap(after(side[0], *far_after), PLANE, size, far)
        for side in reversed(sides):
            side[near] = swap(after(side[0], *near_after), PLANE, size, near)
        sides[0][near | far] = swap(after(sides[0][far], *cross_after), PLANE, size, near)
        sides[1][near | far] = swap(after(sides[1][near], *cross_after), PLANE, size, far)
    else:
        for side in sides:
            for bit in bits:
                for r in list(side):
                    side[r | bit] = swap(side[r], PLANE, size, bit)
    if not core:
        return [[side[r] for r in range(0, size, 2)] for side in sides]
    for side in sides:
        for r in list(side):
            side[r | 1] = swap(after(side[r], *core_after), PLANE, size, 1)
    return [[side[r] for r in range(size)] for side in sides]


def widened(pieces):
    level = 1
    while pieces[0].shape[1] < LANES:
        upper = (plane_index() // level) % 2 == 1
        pairs = zip(pieces[0::2], pieces[1::2])
        pieces = [jnp.where(upper, jnp.concatenate([b, a], 1), jnp.concatenate([a, b], 1)) for a, b in pairs]
        level *= 2
    return pieces


def take_sum(side, bit, kept):
    sent = side[kept | bit].astype(BF16)
    total = side[kept].astype(F32) + swap(sent, PLANE, plane_size(), bit).astype(F32)
    return total if kept == 0 else total.astype(BF16)


def reduce_pair(first, second):
    size = plane_size()
    bits = [1 << b for b in range(1, size.bit_length() - 1)]
    sides = [dict(first), dict(second)]
    if len(bits) == 2:
        near, far = bits
        sides[0][near] = take_sum(sides[0], far, near)
        sides[1][far] = take_sum(sides[1], near, far)
        done = []
        for side in sides:
            a = swap(side[near].astype(BF16), PLANE, size, near).astype(F32)
            b = swap(side[far].astype(BF16), PLANE, size, far).astype(F32)
            done.append(side[0] + a + b)
        return done
    done = []
    for side in sides:
        for bit in reversed(bits):
            side = {r: take_sum(side, bit, r) for r in side if not r & bit}
        done.append(side[0])
    return done


def gather_small(values):
    size = plane_size()
    stacked = values[None]
    bit = 1
    while bit < size:
        stacked = jnp.concatenate([stacked, swap(stacked, PLANE, size, bit)], axis=0)
        bit *= 2
    picks = jnp.arange(size, dtype=jnp.int32)[:, None] ^ plane_index()
    chosen = (picks == jnp.arange(size, dtype=jnp.int32)[None, :]).astype(F32)
    return jnp.einsum("ij,jkw->kiw", chosen, stacked.astype(F32), precision=lax.Precision.HIGHEST)


def chunk_of(rows, index, count):
    return lax.dynamic_slice_in_dim(rows, index * count, count, 0)


def rows_sum(partial):
    size = lax.axis_size("tensor")
    me = lax.axis_index("tensor")
    count = partial.shape[0] // size
    total = chunk_of(partial, me, count).astype(F32)
    for shift in range(1, size):
        sent = chunk_of(partial, lax.rem(me + shift, size), count)
        pairs = [(i, (i + shift) % size) for i in range(size)]
        total = total + lax.ppermute(sent, "tensor", pairs).astype(F32)
    return total


def rows_gather(chunk):
    size = lax.axis_size("tensor")
    me = lax.axis_index("tensor")
    count = chunk.shape[0]
    parts = [chunk]
    for shift in range(1, size):
        pairs = [(i, (i + shift) % size) for i in range(size)]
        parts.append(lax.ppermute(chunk, "tensor", pairs))
    whole = jnp.zeros((size * count,) + chunk.shape[1:], chunk.dtype)
    for shift in range(size):
        place = lax.rem(me - shift + size, size) * count
        whole = lax.dynamic_update_slice_in_dim(whole, parts[shift], place, 0)
    return whole


def params(steps):
    return pltpu.CompilerParams(
        dimension_semantics=("arbitrary",) * steps, vmem_limit_bytes=VMEM_BYTES
    )


def place_pieces(pieces, whole, sem, axis):
    size = len(pieces)
    me = plane_index() // (plane_size() // size)
    extent = whole.shape[axis] // size
    for r, piece in enumerate(pieces):
        start = pl.multiple_of((me ^ r) * extent, extent)
        target = whole.at[pl.ds(start, extent)] if axis == 0 else whole.at[:, pl.ds(start, extent)]
        pltpu.make_async_copy(piece, target, sem).start()


def await_whole(whole, sem):
    pltpu.make_async_copy(whole, whole, sem).wait()


ANYWHERE = pl.BlockSpec(memory_space=pl.ANY)


def turned(values, lane, sign):
    half = HD // 2
    upper = pltpu.roll(values, LANES - half, 1)
    lower = pltpu.roll(values, half, 1)
    return jnp.where(lane % HD < half, -sign * upper, sign * lower)


def qkv_body(count, tokens, gain, cosine, sine, *rest):
    pieces, (normed, queries, keys_values, weight, sem) = rest[:count], rest[count:]

    @pl.when(pl.program_id(0) == 0)
    def _():
        place_pieces(pieces, weight, sem, 0)

    values = tokens[...].astype(F32)
    inverse = lax.rsqrt(jnp.mean(values * values, axis=1, keepdims=True) + EPSILON)
    low = (values * inverse * gain[...]).astype(BF16)
    normed[...] = low

    @pl.when(pl.program_id(0) == 0)
    def _():
        await_whole(weight, sem)

    cos, sin = cosine[...], sine[...]
    lane = lax.broadcasted_iota(jnp.int32, cos.shape, 1)
    q_width = queries.shape[1]
    k_width = keys_values.shape[1] // 2
    for start in range(0, weight.shape[1], LANES):
        part = jnp.dot(low, weight[:, start : start + LANES * 1], preferred_element_type=F32)
        if start < q_width + k_width:
            part = part * cos + turned(part, lane, 1.0) * sin
        if start < q_width:
            queries[:, start : start + LANES] = (part.astype(BF16) * SCORE_SCALE).astype(BF16)
        else:
            keys_values[:, start - q_width : start - q_width + LANES] = part.astype(BF16)


def project_qkv(tokens, gain, cosine, sine, pieces, q_width):
    rows, width = tokens.shape
    total = pieces[0].shape[1]
    tile = min(rows, 256)
    row_spec = lambda w: pl.BlockSpec((tile, w), lambda i: (i, 0))
    return pl.pallas_call(
        functools.partial(qkv_body, len(pieces)),
        grid=(rows // tile,),
        in_specs=[row_spec(width), pl.BlockSpec((1, width), lambda i: (0, 0)), row_spec(LANES), row_spec(LANES)]
        + [ANYWHERE] * len(pieces),
        out_specs=[row_spec(width), row_spec(q_width), row_spec(total - q_width)],
        out_shape=[
            jax.ShapeDtypeStruct((rows, width), BF16),
            jax.ShapeDtypeStruct((rows, q_width), BF16),
            jax.ShapeDtypeStruct((rows, total - q_width), BF16),
        ],
        scratch_shapes=[pltpu.VMEM((width, total), BF16), pltpu.SemaphoreType.DMA],
        compiler_params=params(1),
        cost_estimate=pl.CostEstimate(
            flops=2 * rows * width * total, bytes_accessed=2 * (2 * rows * width + width * total), transcendentals=0
        ),
        name="project_qkv",
    )(tokens, gain, cosine, sine, *pieces)


def qkv_back_body(count, d_queries, d_keys_values, cosine, sine, *rest):
    pieces, (d_all, d_normed, weight, sem) = rest[:count], rest[count:]

    @pl.when(pl.program_id(0) == 0)
    def _():
        place_pieces(pieces, weight, sem, 0)

    cos, sin = cosine[...], sine[...]
    lane = lax.broadcasted_iota(jnp.int32, cos.shape, 1)
    q_width = d_queries.shape[1]
    k_width = d_keys_values.shape[1] // 2
    for start in range(0, d_all.shape[1], LANES):
        if start < q_width:
            part = d_queries[:, start : start + LANES]
        else:
            part = d_keys_values[:, start - q_width : start - q_width + LANES]
        if start < q_width + k_width:
            part = part * cos + turned(part * sin, lane, -1.0)
        d_all[:, start : start + LANES] = part.astype(BF16)

    @pl.when(pl.program_id(0) == 0)
    def _():
        await_whole(weight, sem)

    step = 512
    for start in range(0, weight.shape[0], step):
        d_normed[:, start : start + step] = lax.dot_general(
            d_all[...], weight[start : start + step, :], (((1,), (1,)), ((), ())), preferred_element_type=F32
        ).astype(BF16)


def project_qkv_back(d_queries, d_keys_values, cosine, sine, pieces):
    rows, q_width = d_queries.shape
    total = pieces[0].shape[1]
    width = pieces[0].shape[0] * len(pieces)
    tile = min(rows, 256)
    row_spec = lambda w: pl.BlockSpec((tile, w), lambda i: (i, 0))
    return pl.pallas_call(
        functools.partial(qkv_back_body, len(pieces)),
        grid=(rows // tile,),
        in_specs=[row_spec(q_width), row_spec(total - q_width), row_spec(LANES), row_spec(LANES)]
        + [ANYWHERE] * len(pieces),
        out_specs=[row_spec(total), row_spec(width)],
        out_shape=[jax.ShapeDtypeStruct((rows, total), BF16), jax.ShapeDtypeStruct((rows, width), BF16)],
        scratch_shapes=[pltpu.VMEM((width, total), BF16), pltpu.SemaphoreType.DMA],
        compiler_params=params(1),
        cost_estimate=pl.CostEstimate(
            flops=2 * rows * width * total, bytes_accessed=2 * (2 * rows * width + width * total), transcendentals=0
        ),
        name="project_qkv_back",
    )(d_queries, d_keys_values, cosine, sine, *pieces)


def gathered_body(count, axis, transposed, left, *rest):
    pieces, (out, weight, sem) = rest[:count], rest[count:]

    @pl.when(pl.program_id(0) == 0)
    def _():
        place_pieces(pieces, weight, sem, axis)
        await_whole(weight, sem)

    step = min(out.shape[1], 512)
    for start in range(0, out.shape[1], step):
        if transposed:
            part = lax.dot_general(
                left[...], weight[start : start + step, :], (((1,), (1,)), ((), ())), preferred_element_type=F32
            )
        else:
            part = jnp.dot(left[...], weight[:, start : start + step], preferred_element_type=F32)
        out[:, start : start + step] = part.astype(out.dtype)


def gathered_matmul(left, pieces, axis, transposed):
    rows = left.shape[0]
    shape = list(pieces[0].shape)
    shape[axis] *= len(pieces)
    outer = shape[0] if transposed else shape[1]
    tile = min(rows, 256)
    return pl.pallas_call(
        functools.partial(gathered_body, len(pieces), axis, transposed),
        grid=(rows // tile,),
        in_specs=[pl.BlockSpec((tile, left.shape[1]), lambda i: (i, 0))] + [ANYWHERE] * len(pieces),
        out_specs=pl.BlockSpec((tile, outer), lambda i: (i, 0)),
        out_shape=jax.ShapeDtypeStruct((rows, outer), BF16),
        scratch_shapes=[pltpu.VMEM(tuple(shape), BF16), pltpu.SemaphoreType.DMA],
        compiler_params=params(1),
        cost_estimate=pl.CostEstimate(
            flops=2 * rows * shape[0] * shape[1],
            bytes_accessed=2 * (rows * sum(shape) + shape[0] * shape[1]),
            transcendentals=0,
        ),
    )(left, *pieces)


def ffn_tile(f_step, tile, normed, d_ffn, gate, up, down, active, d_gate, d_up, out, d_normed, out_sum, d_sum):
    units = pl.ds(pl.multiple_of(f_step * tile, tile), tile)
    gate_tile, up_tile, down_tile = gate[:, units], up[:, units], down[units, :]
    gate_in = jnp.dot(normed[...], gate_tile, preferred_element_type=F32)
    upward = jnp.dot(normed[...], up_tile, preferred_element_type=F32)
    d_active = lax.dot_general(d_ffn[...], down_tile, (((1,), (1,)), ((), ())), preferred_element_type=F32)
    sigma = 1.0 / (1.0 + jnp.exp(-gate_in))
    silu = gate_in * sigma
    active_low = (silu * upward).astype(BF16)
    gate_low = (d_active * upward * (sigma * (1.0 + gate_in * (1.0 - sigma)))).astype(BF16)
    up_low = (d_active * silu).astype(BF16)
    active[...] = active_low
    d_gate[...] = gate_low
    d_up[...] = up_low
    part = jnp.dot(active_low, down_tile, preferred_element_type=F32)
    d_part = lax.dot_general(gate_low, gate_tile, (((1,), (1,)), ((), ())), preferred_element_type=F32)
    d_part += lax.dot_general(up_low, up_tile, (((1,), (1,)), ((), ())), preferred_element_type=F32)

    @pl.when(f_step == 0)
    def _():
        out_sum[...] = part
        d_sum[...] = d_part

    @pl.when(f_step > 0)
    def _():
        out_sum[...] += part
        d_sum[...] += d_part

    @pl.when(f_step == pl.num_programs(1) - 1)
    def _():
        out[...] = out_sum[...].astype(BF16)
        d_normed[...] = d_sum[...].astype(BF16)


def ffn_body(count, narrow, tile, normed, d_ffn, *rest):
    gate_pieces, up_pieces, rest = rest[:count], rest[count : 2 * count], rest[2 * count :]
    low_pieces, high_pieces, rest = rest[:narrow], rest[narrow : 2 * narrow], rest[2 * narrow :]
    active, d_gate, d_up, out, d_normed, gate, up, down, out_sum, d_sum, sems = rest
    f_step = pl.program_id(1)
    half = down.shape[0] // 2

    @pl.when((pl.program_id(0) == 0) & (f_step == 0))
    def _():
        place_pieces(gate_pieces, gate, sems.at[0], 0)
        place_pieces(up_pieces, up, sems.at[1], 0)
        place_pieces(low_pieces, down.at[pl.ds(0, half)], sems.at[2], 1)
        place_pieces(high_pieces, down.at[pl.ds(half, half)], sems.at[3], 1)
        await_whole(gate, sems.at[0])
        await_whole(up, sems.at[1])
        await_whole(down.at[pl.ds(0, half)], sems.at[2])
        await_whole(down.at[pl.ds(half, half)], sems.at[3])

    ffn_tile(f_step, tile, normed, d_ffn, gate, up, down, active, d_gate, d_up, out, d_normed, out_sum, d_sum)


def ffn(normed, d_ffn, gate_pieces, up_pieces, low_pieces, high_pieces, pushed):
    rows, width = normed.shape
    units = gate_pieces[0].shape[1]
    count = len(gate_pieces)
    tile = 256
    row_tile = min(rows, 512)
    once = pl.Buffered(1)
    row_spec = pl.BlockSpec((row_tile, width), lambda i, f: (i, 0), pipeline_mode=once)
    unit_spec = pl.BlockSpec((row_tile, tile), lambda i, f: (i, f))
    unit_shape = jax.ShapeDtypeStruct((rows, units), BF16)
    row_shape = jax.ShapeDtypeStruct((rows, width), BF16)
    body = functools.partial(ffn_body, count, len(low_pieces), tile)
    settings, sems = params(2), [pltpu.SemaphoreType.DMA((4,))]
    if pushed:
        body = functools.partial(pushed_body, count, tile)
        sems = [pltpu.SemaphoreType.DMA((3, units // tile))] * 3
        settings = pltpu.CompilerParams(
            dimension_semantics=("arbitrary",) * 2,
            vmem_limit_bytes=VMEM_BYTES,
            collective_id=5,
            has_side_effects=True,
        )
    return pl.pallas_call(
        body,
        grid=(rows // row_tile, units // tile),
        in_specs=[row_spec, row_spec] + [ANYWHERE] * (2 * count + 2 * len(low_pieces)),
        out_specs=[unit_spec, unit_spec, unit_spec, row_spec, row_spec],
        out_shape=[unit_shape, unit_shape, unit_shape, row_shape, row_shape],
        scratch_shapes=[
            pltpu.VMEM((width, units), BF16),
            pltpu.VMEM((width, units), BF16),
            pltpu.VMEM((units, width), BF16),
            pltpu.VMEM((row_tile, width), F32),
            pltpu.VMEM((row_tile, width), F32),
        ]
        + sems,
        compiler_params=settings,
        cost_estimate=pl.CostEstimate(
            flops=12 * rows * width * units, bytes_accessed=6 * width * units + 14 * rows * width, transcendentals=rows * units
        ),
        name="feed_forward",
    )(normed, d_ffn, *gate_pieces, *up_pieces, *low_pieces, *high_pieces)


def pushed_body(count, tile, normed, d_ffn, *refs):
    groups, rest = [refs[k * count : (k + 1) * count] for k in range(4)], refs[4 * count :]
    active, d_gate, d_up, out, d_normed, gate, up, down, out_sum, d_sum, near, send, recv = rest
    f_step = pl.program_id(1)
    first = (pl.program_id(0) == 0) & (f_step == 0)
    last = (pl.program_id(0) == pl.num_programs(0) - 1) & (f_step == pl.num_programs(1) - 1)
    steps = down.shape[0] // tile
    width = down.shape[1]
    extent = width // (2 * count)
    me = plane_index()
    mate = {"context": lax.axis_index("context") ^ 1}
    mesh_ids = pl.DeviceIdType.MESH

    def push(source, target, w, t):
        return pltpu.make_async_remote_copy(
            src_ref=source,
            dst_ref=target,
            send_sem=send.at[w, t],
            recv_sem=recv.at[w, t],
            device_id=mate,
            device_id_type=mesh_ids,
        )

    def halves(t):
        units = pl.ds(pl.multiple_of(t * tile, tile), tile)
        half = pl.ds(0, width // 2)
        return [gate.at[half, units], up.at[half, units], down.at[units, half]]

    @pl.when(first)
    def _():
        barrier = pltpu.get_barrier_semaphore()
        pl.semaphore_signal(barrier, inc=1, device_id=mate, device_id_type=mesh_ids)
        pl.semaphore_wait(barrier, 1)

        def start(t, carry):
            units = pl.ds(pl.multiple_of(t * tile, tile), tile)
            for i in range(count):
                base = pl.multiple_of((me ^ (2 * i)) * extent, extent)
                rows = pl.ds(base, extent)
                left = pl.ds(base, extent // 2)
                right = pl.ds(pl.multiple_of(base + extent // 2, extent // 2), extent // 2)
                moves = (
                    (0, groups[0][i].at[:, units], gate.at[rows, units]),
                    (1, groups[1][i].at[:, units], up.at[rows, units]),
                    (2, groups[2][i].at[units, :], down.at[units, left]),
                    (2, groups[3][i].at[units, :], down.at[units, right]),
                )
                for w, source, target in moves:
                    push(source, target, w, t).start()
                    pltpu.make_async_copy(source, target, near.at[w, t]).start()
            return carry

        lax.fori_loop(0, steps, start, 0)

    @pl.when(pl.program_id(0) == 0)
    def _():
        for w, half in enumerate(halves(f_step)):
            pltpu.make_async_copy(half, half, near.at[w, f_step]).wait()
            push(half, half, w, f_step).wait_recv()

    ffn_tile(f_step, tile, normed, d_ffn, gate, up, down, active, d_gate, d_up, out, d_normed, out_sum, d_sum)

    @pl.when(last)
    def _():
        def drain(t, carry):
            for w, half in enumerate(halves(t)):
                push(half, half, w, t).wait_send()
            return carry

        lax.fori_loop(0, steps, drain, 0)


def doubled(values, lane, head):
    rolled = pltpu.roll(values.astype(F32), HD, 1).astype(BF16)
    return jnp.where((lane < HD) == (head == 0), values, rolled)


def block_bias(order, seq, r, block):
    per = order.shape[1] // lax.axis_size("context")
    own = order[seq, lax.axis_index("context") * per + pl.program_id(3)]
    other = order[seq, (lax.axis_index("context") ^ r) * per + block]
    return jnp.where(other <= own, 0.0, MASKED_SCORE).astype(F32)


def masked_scores(order, pieces_k, query):
    seq = pl.program_id(0)
    scores = []
    for r, key_rows in enumerate(pieces_k):
        part = lax.dot_general(key_rows, query, (((1,), (1,)), ((), ())), preferred_element_type=F32)
        for block in range(key_rows.shape[0] // BLK):
            bias = block_bias(order, seq, r, block)
            scores.append(part[block * BLK : (block + 1) * BLK] + bias)
    return scores


def attend_body(count, order, query_ref, *rest):
    pieces, (mixture, logs) = rest[:count], rest[count:]
    head = pl.program_id(1)
    lane = lax.broadcasted_iota(jnp.int32, (1, LANES), 1)
    keys = [doubled(piece[:, :LANES], lane, head) for piece in pieces]
    values = [doubled(piece[:, LANES:], lane, head) for piece in pieces]
    query = query_ref[...]
    parts = []
    for side in range(2):
        chosen = (lane < HD) if side == 0 else (lane >= HD)
        scores = masked_scores(order, keys, jnp.where(chosen, query, jnp.zeros_like(query)))
        top = functools.reduce(jnp.maximum, [jnp.max(s, axis=0, keepdims=True) for s in scores])
        powers = [jnp.exp(s - top) for s in scores]
        total = sum(jnp.sum(p, axis=0, keepdims=True) for p in powers)
        low = jnp.concatenate([p.astype(BF16) for p in powers], axis=0)
        whole = jnp.concatenate(values, axis=0)
        mixed = lax.dot_general(whole, low, (((0,), (0,)), ((), ())), preferred_element_type=F32)
        parts.append(mixed / total)
        logs[side : side + 1, :] = top + jnp.log(total)
    row = lax.broadcasted_iota(jnp.int32, (LANES, 1), 0)
    mixture[...] = jnp.where(row < HD, parts[0], parts[1]).T.astype(BF16)


def attend_specs(order, queries, group_pairs):
    seqs = order.shape[0]
    rows = queries.shape[0] // seqs
    tiles = rows // BLK
    grid = (seqs, 2, group_pairs, tiles)
    q_spec = pl.BlockSpec((BLK, LANES), lambda s, h, g, t: (s * tiles + t, h * group_pairs + g))
    kv_spec = pl.BlockSpec((rows, 2 * LANES), lambda s, h, g, t: (s, 0))
    log_spec = pl.BlockSpec((None, 2, BLK), lambda s, h, g, t: (h * group_pairs + g, 0, s * tiles + t))
    return grid, q_spec, kv_spec, log_spec


def attend(order, queries, pieces):
    rows, q_width = queries.shape
    pairs = q_width // LANES
    grid, q_spec, kv_spec, log_spec = attend_specs(order, queries, pairs // 2)
    keys = rows * len(pieces) // order.shape[0]
    return pl.pallas_call(
        functools.partial(attend_body, len(pieces)),
        grid=grid,
        in_specs=[pl.BlockSpec(memory_space=pltpu.SMEM), q_spec] + [kv_spec] * len(pieces),
        out_specs=[q_spec, log_spec],
        out_shape=[jax.ShapeDtypeStruct((rows, q_width), BF16), jax.ShapeDtypeStruct((pairs, 2, rows), F32)],
        compiler_params=params(4),
        cost_estimate=pl.CostEstimate(
            flops=8 * rows * keys * q_width * 2, bytes_accessed=8 * rows * q_width, transcendentals=rows * keys * q_width // HD
        ),
        name="attend",
    )(order, queries, *pieces)


def attend_back_body(count, order, query_ref, grad_ref, logs, *rest):
    pieces, rest = rest[:count], rest[count:]
    d_query, outs, (d_key_sum, d_value_sum) = rest[0], rest[1 : 1 + count], rest[1 + count :]
    head, pair, tile = pl.program_id(1), pl.program_id(2), pl.program_id(3)
    lane = lax.broadcasted_iota(jnp.int32, (1, LANES), 1)
    keys = [doubled(piece[:, :LANES], lane, head) for piece in pieces]
    values = jnp.concatenate([doubled(piece[:, LANES:], lane, head) for piece in pieces], axis=0)
    whole_keys = jnp.concatenate(keys, axis=0)
    parts, d_keys, d_values = [], 0.0, 0.0
    for side in range(2):
        chosen = (lane < HD) if side == 0 else (lane >= HD)
        query = jnp.where(chosen, query_ref[...], jnp.zeros_like(query_ref[...]))
        grad = jnp.where(chosen, grad_ref[...], jnp.zeros_like(grad_ref[...]))
        scores = jnp.concatenate(masked_scores(order, keys, query), axis=0)
        soft = jnp.exp(scores - logs[side : side + 1, :])
        d_soft = lax.dot_general(values, grad, (((1,), (1,)), ((), ())), preferred_element_type=F32)
        inner = jnp.sum(soft * d_soft, axis=0, keepdims=True)
        d_scores = (soft * (d_soft - inner)).astype(BF16)
        d_values += jnp.dot(soft.astype(BF16), grad, preferred_element_type=F32)
        d_keys += jnp.dot(d_scores, query, preferred_element_type=F32)
        parts.append(lax.dot_general(whole_keys, d_scores, (((0,), (0,)), ((), ())), preferred_element_type=F32))
    row = lax.broadcasted_iota(jnp.int32, (LANES, 1), 0)
    d_query[...] = jnp.where(row < HD, parts[0], parts[1]).T * SCORE_SCALE

    first = (pair == 0) & (tile == 0)
    last = (pair == pl.num_programs(2) - 1) & (tile == pl.num_programs(3) - 1)

    @pl.when(first)
    def _():
        d_key_sum[...] = d_keys
        d_value_sum[...] = d_values

    @pl.when(jnp.logical_not(first))
    def _():
        d_key_sum[...] += d_keys
        d_value_sum[...] += d_values

    @pl.when(last)
    def _():
        wanted = (lane < HD) == (head == 0)
        rows = outs[0].shape[0]
        for r, out in enumerate(outs):
            for base, total in ((0, d_key_sum), (LANES, d_value_sum)):
                part = total[r * rows : (r + 1) * rows, :]
                both = (part + pltpu.roll(part, HD, 1)).astype(out.dtype)
                spot = pl.ds(base, LANES)

                @pl.when(head == 0)
                def _():
                    out[:, spot] = both

                @pl.when(head == 1)
                def _():
                    out[:, spot] = jnp.where(wanted, both.astype(F32), out[:, spot].astype(F32)).astype(out.dtype)


def attend_back(order, queries, grads, logs, pieces):
    rows, q_width = queries.shape
    pairs = q_width // LANES
    grid, q_spec, kv_spec, log_spec = attend_specs(order, queries, pairs // 2)
    keys = rows * len(pieces) // order.shape[0]
    return pl.pallas_call(
        functools.partial(attend_back_body, len(pieces)),
        grid=grid,
        in_specs=[pl.BlockSpec(memory_space=pltpu.SMEM), q_spec, q_spec, log_spec] + [kv_spec] * len(pieces),
        out_specs=[q_spec] + [kv_spec] * len(pieces),
        out_shape=[jax.ShapeDtypeStruct((rows, q_width), F32)]
        + [jax.ShapeDtypeStruct((rows, 2 * LANES), F32 if r % 2 == 0 else BF16) for r in range(len(pieces))],
        scratch_shapes=[pltpu.VMEM((keys, LANES), F32), pltpu.VMEM((keys, LANES), F32)],
        compiler_params=params(4),
        cost_estimate=pl.CostEstimate(
            flops=20 * rows * keys * q_width * 2, bytes_accessed=12 * rows * q_width, transcendentals=rows * keys * q_width // HD
        ),
        name="attend_back",
    )(order, queries, grads, logs, *pieces)


def line_steps(rows):
    half = rows // 2
    sub = 16
    return half, sub, half // sub


def line_body(finish, keep_state, gain_sum, n_in, *refs):
    partial, ins, rest = refs[0], refs[1 : 1 + n_in], refs[1 + n_in :]
    result, rest = rest[0], rest[1:]
    state_out, rest = (rest[0], rest[1:]) if keep_state else (None, rest)
    gain_out, rest = (rest[0], rest[1:]) if gain_sum else (None, rest)
    from_outer, from_peer, staged, send, recv = rest
    half, sub, count = line_steps(partial.shape[0])
    me = lax.axis_index("tensor")
    side = me // 2
    inner = lax.rem(me, 3) != 0
    to_outer, to_inner, to_peer = side * 3, 1 + side, 3 - me
    near, far = side * half, (1 - side) * half

    def rows(base, k):
        return pl.ds(pl.multiple_of(base + k * sub, sub), sub)

    def remote(source, target, s, r, k, where):
        return pltpu.make_async_remote_copy(
            src_ref=source,
            dst_ref=target,
            send_sem=send.at[s, k],
            recv_sem=recv.at[r, k],
            device_id={"tensor": where},
            device_id_type=pl.DeviceIdType.MESH,
        )

    def up_far(k):
        return remote(partial.at[rows(far, k)], from_outer.at[0, rows(0, k)], 0, 0, k, to_inner)

    def up_near(k):
        return remote(partial.at[rows(near, k)], from_outer.at[1, rows(0, k)], 1, 1, k, to_inner)

    def across(k):
        return remote(staged.at[rows(0, k)], from_peer.at[rows(0, k)], 0, 2, k, to_peer)

    def over(k, base):
        return remote(result.at[rows(base, k)], result.at[rows(base, k)], 2, 4, k, to_peer)

    def down_near(k):
        return remote(result.at[rows(near, k)], result.at[rows(near, k)], 1, 3, k, to_outer)

    def down_far(k):
        return remote(result.at[rows(far, k)], result.at[rows(far, k)], 3, 4, k, to_outer)

    barrier = pltpu.get_barrier_semaphore()

    def greet(where):
        pl.semaphore_signal(barrier, inc=1, device_id={"tensor": where}, device_id_type=pl.DeviceIdType.MESH)

    if gain_sum:
        gain_out[...] = jnp.zeros_like(gain_out)

    @pl.when(inner)
    def _():
        greet(to_outer)
        greet(to_peer)
        pl.semaphore_wait(barrier, 2)

        def step(k, carry):
            @pl.when(k < count)
            def _():
                up_far(k).wait_recv()
                total = partial[rows(far, k), :].astype(F32) + from_outer[0, rows(0, k), :].astype(F32)
                staged[rows(0, k), :] = total.astype(BF16)
                across(k).start()

            @pl.when((k >= 1) & (k <= count))
            def _():
                j = k - 1
                up_near(j).wait_recv()
                across(j).wait_recv()
                total = partial[rows(near, j), :].astype(F32) + from_outer[1, rows(0, j), :].astype(F32)
                total = total + from_peer[rows(0, j), :].astype(F32)
                low, state, gains = finish(total, rows(near, j), rows(0, j), ins)
                result[rows(near, j), :] = low
                if keep_state:
                    state_out[rows(0, j), :] = state
                if gain_sum:
                    gain_out[...] += jnp.sum(gains.reshape(sub // 8, 8, gains.shape[1]), axis=0)
                down_near(j).start()
                over(j, near).start()

            @pl.when(k >= 3)
            def _():
                over(k - 3, far).wait_recv()
                down_far(k - 3).start()

            return carry

        lax.fori_loop(0, count + 3, step, 0)

        def drain(k, carry):
            across(k).wait_send()
            down_near(k).wait_send()
            over(k, near).wait_send()
            down_far(k).wait_send()
            return carry

        lax.fori_loop(0, count, drain, 0)

    @pl.when(jnp.logical_not(inner))
    def _():
        greet(to_inner)
        pl.semaphore_wait(barrier, 1)

        def step(k, carry):
            up_far(k).start()
            up_near(k).start()
            return carry

        lax.fori_loop(0, count, step, 0)

        def drain(k, carry):
            down_near(k).wait_recv()
            down_far(k).wait_recv()
            up_far(k).wait_send()
            up_near(k).wait_send()
            return carry

        lax.fori_loop(0, count, drain, 0)


def line_sum(partial, ins, finish, keep_state, gain_sum, identity):
    rows, width = partial.shape
    half, _, count = line_steps(rows)
    vmem = pl.BlockSpec(memory_space=pltpu.VMEM)
    shapes = [jax.ShapeDtypeStruct((rows, width), BF16)]
    if keep_state:
        shapes.append(jax.ShapeDtypeStruct((half, width), F32))
    if gain_sum:
        shapes.append(jax.ShapeDtypeStruct((8, width), F32))
    return pl.pallas_call(
        functools.partial(line_body, finish, keep_state, gain_sum, len(ins)),
        in_specs=[vmem] * (1 + len(ins)),
        out_specs=[vmem] * len(shapes),
        out_shape=shapes,
        scratch_shapes=[
            pltpu.VMEM((2, half, width), BF16),
            pltpu.VMEM((half, width), BF16),
            pltpu.VMEM((half, width), BF16),
            pltpu.SemaphoreType.DMA((4, count)),
            pltpu.SemaphoreType.DMA((5, count)),
        ],
        compiler_params=pltpu.CompilerParams(
            collective_id=identity, has_side_effects=True, vmem_limit_bytes=VMEM_BYTES
        ),
        cost_estimate=pl.CostEstimate(flops=0, bytes_accessed=100 * rows * width, transcendentals=0),
    )(partial, *ins)


def mean_square(values):
    return lax.rsqrt(jnp.mean(values * values, axis=1, keepdims=True) + EPSILON)


def finish_attention(total, whole, own, ins):
    tokens, gain = ins
    hidden = tokens[whole, :].astype(F32) + RESIDUAL_SCALE * total
    return (hidden * mean_square(hidden) * gain[...]).astype(BF16), hidden, None


def norm_pull(d_normed, values, gain):
    inverse = mean_square(values)
    scaled = gain * d_normed
    inner = jnp.mean(scaled * values, axis=1, keepdims=True)
    return inverse * scaled - values * inverse * inverse * inverse * inner, d_normed * values * inverse


def finish_ffn_back(total, whole, own, ins):
    hidden, grads, gain = ins
    pulled, gains = norm_pull(total, hidden[own, :], gain[...])
    d_hidden = grads[whole, :].astype(F32) + pulled
    return (RESIDUAL_SCALE * d_hidden).astype(BF16), d_hidden, gains


def finish_attention_back(total, whole, own, ins):
    tokens, d_hidden, gain = ins
    pulled, gains = norm_pull(total, tokens[whole, :].astype(F32), gain[...])
    return (d_hidden[own, :] + pulled).astype(BF16), None, gains


def grads_body(count, jobs, *refs):
    ins, rest = refs[: 2 * jobs], refs[2 * jobs :]
    halves = count // 2
    outs, rest = rest[: halves * jobs], rest[halves * jobs :]
    sent, got, own = rest[:jobs], rest[jobs : 2 * jobs], rest[2 * jobs : 3 * jobs]
    send, recv, done = rest[3 * jobs :]
    me = plane_index()
    mate = {"context": lax.axis_index("context") ^ 1}
    mesh_ids = pl.DeviceIdType.MESH

    def piece(j, r):
        left, right = ins[2 * j], ins[2 * j + 1]
        extent = left.shape[1] // count
        columns = pl.ds(pl.multiple_of((me ^ r) * extent, extent), extent)
        return lax.dot_general(left[:, columns], right[...], (((0,), (0,)), ((), ())), preferred_element_type=F32)

    def across(j, i):
        return pltpu.make_async_remote_copy(
            src_ref=sent[j].at[i],
            dst_ref=got[j].at[i],
            send_sem=send.at[j, i],
            recv_sem=recv.at[j, i],
            device_id=mate,
            device_id_type=mesh_ids,
        )

    barrier = pltpu.get_barrier_semaphore()
    pl.semaphore_signal(barrier, inc=1, device_id=mate, device_id_type=mesh_ids)
    pl.semaphore_wait(barrier, 1)

    def odd(step, carry):
        i = halves - 1 - step
        for j in range(jobs):
            sent[j][i] = piece(j, 2 * i + 1).astype(BF16)
            across(j, i).start()
        return carry

    lax.fori_loop(0, halves, odd, 0)

    def even(step, carry):
        i = halves - 1 - step
        for j in range(jobs):
            value = piece(j, 2 * i)
            across(j, i).wait_recv()
            value = value + got[j][i].astype(F32)

            @pl.when(i > 0)
            def _():
                got[j][i] = value.astype(BF16)

            @pl.when(i == 0)
            def _():
                own[j][...] = value

        for known in range(halves):

            @pl.when(i == known)
            def _():
                for j in range(jobs):
                    source = got[j].at[known] if known else own[j]
                    pltpu.make_async_copy(source, outs[known * jobs + j], done.at[known, j]).start()

        return carry

    lax.fori_loop(0, halves, even, 0)
    for known in range(halves):
        for j in range(jobs):
            source = got[j].at[known] if known else own[j]
            pltpu.make_async_copy(source, outs[known * jobs + j], done.at[known, j]).wait()
            across(j, known).wait_send()


def plane_grads(pairs, identity):
    count = plane_size()
    halves = count // 2
    jobs = len(pairs)
    extents = [left.shape[1] // count for left, _ in pairs]
    if any(extent % LANES for extent in extents):
        me = plane_index()
        sides = []
        for (left, right), e in zip(pairs, extents):
            columns = lambda r: lax.dynamic_slice_in_dim(left, (me ^ r) * e, e, 1)
            whole = {r: weight_grad(columns(r), right).astype(BF16) for r in range(count)}
            sides.append({r: take_sum(whole, 1, r) for r in range(0, count, 2)})
        return sides
    shapes = [(e, right.shape[1]) for e, (_, right) in zip(extents, pairs)]
    flat = pl.pallas_call(
        functools.partial(grads_body, count, jobs),
        in_specs=[pl.BlockSpec(memory_space=pltpu.VMEM)] * (2 * jobs),
        out_specs=[ANYWHERE] * (halves * jobs),
        out_shape=[jax.ShapeDtypeStruct(shape, BF16 if i else F32) for i in range(halves) for shape in shapes],
        scratch_shapes=[pltpu.VMEM((halves,) + shape, BF16) for shape in shapes] * 2
        + [pltpu.VMEM(shape, F32) for shape in shapes]
        + [
            pltpu.SemaphoreType.DMA((jobs, halves)),
            pltpu.SemaphoreType.DMA((jobs, halves)),
            pltpu.SemaphoreType.DMA((halves, jobs)),
        ],
        compiler_params=pltpu.CompilerParams(
            collective_id=identity, has_side_effects=True, vmem_limit_bytes=VMEM_BYTES
        ),
        cost_estimate=pl.CostEstimate(
            flops=sum(2 * left.shape[0] * left.shape[1] * right.shape[1] for left, right in pairs),
            bytes_accessed=sum(2 * left.shape[1] * right.shape[1] for left, right in pairs),
            transcendentals=0,
        ),
    )(*[value for pair in pairs for value in pair])
    return [{2 * i: flat[i * jobs + j] for i in range(halves)} for j in range(jobs)]


def after(value, *others):
    return lax.optimization_barrier((value,) + others)[0] if others else value


def gather_context(piece):
    size = lax.axis_size("context")
    held = {0: piece}
    bit = size // 2
    while bit:
        for r in list(held):
            held[r | bit] = swap(held[r], "context", size, bit)
        bit //= 2
    return [held[r] for r in range(size)]


def reduce_context(pieces):
    size = len(pieces)
    held = dict(enumerate(pieces))
    bit = 1
    while bit < size:
        held = {
            r: held[r].astype(F32) + swap(held[r | bit].astype(BF16), "context", size, bit).astype(F32)
            for r in held
            if not r & bit
        }
        bit *= 2
    return held[0]


def stored_places(order_row, first, count):
    stored = first + jnp.arange(count, dtype=jnp.int32)
    picks = (stored // BLK)[:, None] == jnp.arange(order_row.shape[0], dtype=jnp.int32)[None, :]
    return jnp.sum(jnp.where(picks, order_row[None, :], 0), axis=1) * BLK + stored % BLK


def rope_tables(order, local_len):
    first = lax.axis_index("context") * local_len
    places = jnp.concatenate([stored_places(order[s], first, local_len) for s in range(order.shape[0])])
    half = HD // 2
    inverse = jnp.exp(jnp.arange(half, dtype=F32) * (-2.0 * math.log(ROPE_BASE) / HD))
    angles = places.astype(F32)[:, None] * jnp.tile(inverse, LANES // half)[None, :]
    return jnp.cos(angles), jnp.sin(angles)


def weight_grad(left, right):
    return lax.dot_general(left, right, (((0,), (0,)), ((), ())), preferred_element_type=F32)


def local(
    tokens, block_order, w_query, w_key, w_value, w_output, w_gate, w_up, w_down, norm_attn, norm_ffn, grad_out
):
    seqs, local_len, width = tokens.shape
    rows = seqs * local_len
    size = plane_size()
    me = plane_index()
    z = lax.axis_index("tensor")
    token_rows = tokens.reshape(rows, width)
    grad_rows = grad_out.reshape(rows, width)
    q_width, kv_width = w_query.shape[1], w_key.shape[1]
    units = w_down.shape[0]
    half = units // 2

    gains = gather_small(jnp.stack([norm_attn, norm_ffn])).reshape(2, width)
    gain_attn, gain_ffn = gains[0:1], gains[1:2]
    w_qkv = jnp.concatenate([w_query, w_key, w_value], axis=1)
    qkv_pieces, output_pieces = gather_pair(w_qkv, w_output)
    cosine, sine = rope_tables(block_order, local_len)
    normed, queries, keys_values = project_qkv(token_rows, gain_attn, cosine, sine, qkv_pieces, q_width)
    kv_pieces = gather_context(keys_values)
    early, late = [qkv_pieces[-2], output_pieces[-2], output_pieces[size // 2]], [kv_pieces[-2]]
    mixture, logs = attend(block_order, queries, kv_pieces)
    output_pieces = widened(output_pieces)
    branch = gathered_matmul(mixture, output_pieces, 1, False)
    normed_ffn, hidden = line_sum(branch, [token_rows, gain_ffn], finish_attention, True, False, 0)
    extent = width // size
    pushed = extent % (2 * LANES) == 0
    order = (early, late, [mixture], [normed_ffn], not pushed)
    gate_pieces, up_pieces = gather_pair(w_gate, w_up, *order)
    order = (early, late, [normed_ffn], [normed_ffn], not pushed)
    if pushed:
        low_pieces, high_pieces = gather_pair(w_down[:, : extent // 2], w_down[:, extent // 2 :], *order)
    else:
        low_pieces, high_pieces = gather_pair(w_down[:half], w_down[half:], *order)
        low_pieces, high_pieces = widened(low_pieces), widened(high_pieces)
    d_ffn = (RESIDUAL_SCALE * grad_rows.astype(F32)).astype(BF16)
    active, d_gate, d_up, ffn_out, d_normed_ffn = ffn(
        normed_ffn, d_ffn, gate_pieces, up_pieces, low_pieces, high_pieces, pushed
    )
    grad_gate, grad_up, grad_low, grad_high = plane_grads(
        [(normed_ffn, d_gate), (normed_ffn, d_up), (d_ffn, active[:, :half]), (d_ffn, active[:, half:])], 3
    )
    d_normed_ffn = after(d_normed_ffn, grad_gate[0])
    d_branch, d_hidden, ffn_gain = line_sum(d_normed_ffn, [hidden, grad_rows, gain_ffn], finish_ffn_back, True, True, 1)

    grad_gate, grad_up = reduce_pair(grad_gate, grad_up)
    grad_low, grad_high = reduce_pair(grad_low, grad_high)

    owner = lax.rem(z, 3) != 0
    padded = lax.dynamic_update_slice_in_dim(jnp.zeros((rows, width), F32), hidden, (z // 2) * (rows // 2), 0)
    out_part = RESIDUAL_SCALE * after(ffn_out, d_branch).astype(F32) + jnp.where(owner, padded, 0.0)
    layer_out = rows_gather(rows_sum(out_part.astype(BF16)).astype(BF16))

    d_mixture = gathered_matmul(d_branch, output_pieces, 1, True)
    d_queries, *d_pieces = attend_back(block_order, queries, d_mixture, logs, kv_pieces)
    d_keys_values = reduce_context(d_pieces)
    d_qkv, d_normed = project_qkv_back(d_queries, d_keys_values, cosine, sine, qkv_pieces)
    grad_qkv, grad_output = plane_grads([(normed, d_qkv), (d_branch, mixture)], 4)
    d_normed = after(d_normed, grad_qkv[0])
    grad_tokens, attn_gain = line_sum(
        d_normed, [token_rows, d_hidden, gain_attn], finish_attention_back, False, True, 2
    )
    grad_tokens = grad_tokens.astype(F32)
    grad_qkv, grad_output = reduce_pair(grad_qkv, grad_output)
    attn_gain, ffn_gain = jnp.sum(attn_gain, axis=0), jnp.sum(ffn_gain, axis=0)
    gain_grads = jnp.stack([attn_gain, ffn_gain])
    everyone = ("shard", "context", "tensor")
    world = size * lax.axis_size("tensor")
    bit = 1
    while bit < world:
        gain_grads = gain_grads + swap(gain_grads, everyone, world, bit)
        bit *= 2
    gain_grads = lax.dynamic_slice_in_dim(gain_grads, me * (width // size), width // size, 1)
    return (
        layer_out.reshape(seqs, local_len, width),
        grad_tokens.reshape(seqs, local_len, width),
        grad_qkv[:, :q_width],
        grad_qkv[:, q_width : q_width + kv_width],
        grad_qkv[:, q_width + kv_width :],
        grad_output.T,
        grad_gate,
        grad_up,
        jnp.concatenate([grad_low.T, grad_high.T], axis=0),
        gain_grads[0],
        gain_grads[1],
    )


def solution(mesh):
    split = P("shard", "context", None)
    inward, outward = P(PLANE, "tensor"), P("tensor", PLANE)
    gain = P(PLANE)
    return jax.shard_map(
        local,
        mesh=mesh,
        in_specs=(split, P("shard", None), inward, inward, inward, outward, inward, inward, outward, gain, gain, split),
        out_specs=(split, split, inward, inward, inward, outward, inward, inward, outward, gain, gain),
        check_vma=False,
    )
```

```python
import functools
import math

import jax
import jax.numpy as jnp
from jax import lax
from jax.experimental import pallas as pl
from jax.experimental.pallas import tpu as pltpu
from jax.sharding import PartitionSpec as P


HD = 64
BLK = 256
LANES = 128
EPSILON = 1e-05
SCORE_SCALE = 0.015625
RESIDUAL_SCALE = 0.22
ROPE_BASE = 10000000.0
MASKED_SCORE = -1e30
PLANE = ("shard", "context")
VMEM_BYTES = 64000 * 1024


F32 = jnp.float32
BF16 = jnp.bfloat16


def plane_size():
    return lax.axis_size("shard") * lax.axis_size("context")


def plane_index():
    return lax.axis_index("shard") * lax.axis_size("context") + lax.axis_index("context")


def swap(value, axes, size, bit):
    return lax.ppermute(value, axes, [(i, i ^ bit) for i in range(size)])


def gather_pair(first, second, far_after=(), near_after=(), cross_after=(), core_after=(), core=True):
    size = plane_size()
    bits = [1 << b for b in range(1, size.bit_length() - 1)]
    sides = [{0: first}, {0: second}]
    if len(bits) == 2:
        near, far = bits
        for side in sides:
            side[far] = swap(after(side[0], *far_after), PLANE, size, far)
        for side in reversed(sides):
            side[near] = swap(after(side[0], *near_after), PLANE, size, near)
        sides[0][near | far] = swap(after(sides[0][far], *cross_after), PLANE, size, near)
        sides[1][near | far] = swap(after(sides[1][near], *cross_after), PLANE, size, far)
    else:
        for side in sides:
            for bit in bits:
                for r in list(side):
                    side[r | bit] = swap(side[r], PLANE, size, bit)
    if not core:
        return [[side[r] for r in range(0, size, 2)] for side in sides]
    for side in sides:
        for r in list(side):
            side[r | 1] = swap(after(side[r], *core_after), PLANE, size, 1)
    return [[side[r] for r in range(size)] for side in sides]


def widened(pieces):
    level = 1
    while pieces[0].shape[1] < LANES:
        upper = (plane_index() // level) % 2 == 1
        pairs = zip(pieces[0::2], pieces[1::2])
        pieces = [jnp.where(upper, jnp.concatenate([b, a], 1), jnp.concatenate([a, b], 1)) for a, b in pairs]
        level *= 2
    return pieces


def take_sum(side, bit, kept):
    sent = side[kept | bit].astype(BF16)
    total = side[kept].astype(F32) + swap(sent, PLANE, plane_size(), bit).astype(F32)
    return total if kept == 0 else total.astype(BF16)


def reduce_pair(first, second, last_after=()):
    size = plane_size()
    bits = [1 << b for b in range(1, size.bit_length() - 1)]
    sides = [dict(first), dict(second)]
    if len(bits) == 2:
        near, far = bits
        sides[0][near] = take_sum(sides[0], far, near)
        sides[1][far] = take_sum(sides[1], near, far)
        done = []
        for side in sides:
            sent = [after(side[bit].astype(BF16), *last_after) for bit in bits]
            a = swap(sent[0], PLANE, size, near).astype(F32)
            b = swap(sent[1], PLANE, size, far).astype(F32)
            done.append(side[0] + a + b)
        return done
    done = []
    for side in sides:
        for bit in reversed(bits):
            side = {r: take_sum(side, bit, r) for r in side if not r & bit}
        done.append(side[0])
    return done


def gather_small(values):
    size = plane_size()
    stacked = values[None]
    bit = 1
    while bit < size:
        stacked = jnp.concatenate([stacked, swap(stacked, PLANE, size, bit)], axis=0)
        bit *= 2
    picks = jnp.arange(size, dtype=jnp.int32)[:, None] ^ plane_index()
    chosen = (picks == jnp.arange(size, dtype=jnp.int32)[None, :]).astype(F32)
    return jnp.einsum("ij,jkw->kiw", chosen, stacked.astype(F32), precision=lax.Precision.HIGHEST)


def chunk_of(rows, index, count):
    return lax.dynamic_slice_in_dim(rows, index * count, count, 0)


def rows_sum(chunks):
    size = lax.axis_size("tensor")
    total = chunks[0].astype(F32)
    for shift in range(1, size):
        pairs = [(i, (i + shift) % size) for i in range(size)]
        total = total + lax.ppermute(chunks[shift], "tensor", pairs).astype(F32)
    return total


def rows_gather(chunk):
    size = lax.axis_size("tensor")
    me = lax.axis_index("tensor")
    count = chunk.shape[0]
    parts = [chunk]
    for shift in range(1, size):
        pairs = [(i, (i + shift) % size) for i in range(size)]
        parts.append(lax.ppermute(chunk, "tensor", pairs))
    whole = jnp.zeros((size * count,) + chunk.shape[1:], chunk.dtype)
    for shift in range(size):
        place = lax.rem(me - shift + size, size) * count
        whole = lax.dynamic_update_slice_in_dim(whole, parts[shift], place, 0)
    return whole


def gains_sum(values):
    size, tensor, me = plane_size(), lax.axis_size("tensor"), plane_index()
    extent = values.shape[1] // size
    total = values
    for shift in range(1, tensor):
        total = total + lax.ppermute(values, "tensor", [(i, (i + shift) % tensor) for i in range(tensor)])
    own = 0.0
    for r in range(size):
        sent = lax.dynamic_slice_in_dim(total, (me ^ r) * extent, extent, 1)
        own = own + (swap(sent, PLANE, size, r) if r else sent)
    return own


def params(steps):
    return pltpu.CompilerParams(
        dimension_semantics=("arbitrary",) * steps, vmem_limit_bytes=VMEM_BYTES
    )


def place_pieces(pieces, whole, sem, axis):
    size = len(pieces)
    me = plane_index() // (plane_size() // size)
    extent = whole.shape[axis] // size
    for r, piece in enumerate(pieces):
        start = pl.multiple_of((me ^ r) * extent, extent)
        target = whole.at[pl.ds(start, extent)] if axis == 0 else whole.at[:, pl.ds(start, extent)]
        pltpu.make_async_copy(piece, target, sem).start()


def await_whole(whole, sem):
    pltpu.make_async_copy(whole, whole, sem).wait()


ANYWHERE = pl.BlockSpec(memory_space=pl.ANY)


def turned(values, lane, sign):
    half = HD // 2
    upper = pltpu.roll(values, LANES - half, 1)
    lower = pltpu.roll(values, half, 1)
    return jnp.where(lane % HD < half, -sign * upper, sign * lower)


def qkv_body(count, tokens, gain, cosine, sine, *rest):
    pieces, (normed, queries, keys_values, weight, sem) = rest[:count], rest[count:]

    @pl.when(pl.program_id(0) == 0)
    def _():
        place_pieces(pieces, weight, sem, 0)

    values = tokens[...].astype(F32)
    inverse = lax.rsqrt(jnp.mean(values * values, axis=1, keepdims=True) + EPSILON)
    low = (values * inverse * gain[...]).astype(BF16)
    normed[...] = low

    @pl.when(pl.program_id(0) == 0)
    def _():
        await_whole(weight, sem)

    cos, sin = cosine[...], sine[...]
    lane = lax.broadcasted_iota(jnp.int32, cos.shape, 1)
    q_width = queries.shape[1]
    k_width = keys_values.shape[1] // 2
    for start in range(0, weight.shape[1], LANES):
        part = jnp.dot(low, weight[:, start : start + LANES * 1], preferred_element_type=F32)
        if start < q_width + k_width:
            part = part * cos + turned(part, lane, 1.0) * sin
        if start < q_width:
            queries[:, start : start + LANES] = (part.astype(BF16) * SCORE_SCALE).astype(BF16)
        else:
            keys_values[:, start - q_width : start - q_width + LANES] = part.astype(BF16)


def project_qkv(tokens, gain, cosine, sine, pieces, q_width):
    rows, width = tokens.shape
    total = pieces[0].shape[1]
    tile = min(rows, 256)
    row_spec = lambda w: pl.BlockSpec((tile, w), lambda i: (i, 0))
    return pl.pallas_call(
        functools.partial(qkv_body, len(pieces)),
        grid=(rows // tile,),
        in_specs=[row_spec(width), pl.BlockSpec((1, width), lambda i: (0, 0)), row_spec(LANES), row_spec(LANES)]
        + [ANYWHERE] * len(pieces),
        out_specs=[row_spec(width), row_spec(q_width), row_spec(total - q_width)],
        out_shape=[
            jax.ShapeDtypeStruct((rows, width), BF16),
            jax.ShapeDtypeStruct((rows, q_width), BF16),
            jax.ShapeDtypeStruct((rows, total - q_width), BF16),
        ],
        scratch_shapes=[pltpu.VMEM((width, total), BF16), pltpu.SemaphoreType.DMA],
        compiler_params=params(1),
        cost_estimate=pl.CostEstimate(
            flops=2 * rows * width * total, bytes_accessed=2 * (2 * rows * width + width * total), transcendentals=0
        ),
        name="project_qkv",
    )(tokens, gain, cosine, sine, *pieces)


def qkv_back_body(count, d_queries, d_keys_values, cosine, sine, *rest):
    pieces, (d_all, d_normed, weight, sem) = rest[:count], rest[count:]

    @pl.when(pl.program_id(0) == 0)
    def _():
        place_pieces(pieces, weight, sem, 0)

    cos, sin = cosine[...], sine[...]
    lane = lax.broadcasted_iota(jnp.int32, cos.shape, 1)
    q_width = d_queries.shape[1]
    k_width = d_keys_values.shape[1] // 2
    for start in range(0, d_all.shape[1], LANES):
        if start < q_width:
            part = d_queries[:, start : start + LANES]
        else:
            part = d_keys_values[:, start - q_width : start - q_width + LANES]
        if start < q_width + k_width:
            part = part * cos + turned(part * sin, lane, -1.0)
        d_all[:, start : start + LANES] = part.astype(BF16)

    @pl.when(pl.program_id(0) == 0)
    def _():
        await_whole(weight, sem)

    step = 512
    for start in range(0, weight.shape[0], step):
        d_normed[:, start : start + step] = lax.dot_general(
            d_all[...], weight[start : start + step, :], (((1,), (1,)), ((), ())), preferred_element_type=F32
        ).astype(BF16)


def project_qkv_back(d_queries, d_keys_values, cosine, sine, pieces):
    rows, q_width = d_queries.shape
    total = pieces[0].shape[1]
    width = pieces[0].shape[0] * len(pieces)
    tile = min(rows, 256)
    row_spec = lambda w: pl.BlockSpec((tile, w), lambda i: (i, 0))
    return pl.pallas_call(
        functools.partial(qkv_back_body, len(pieces)),
        grid=(rows // tile,),
        in_specs=[row_spec(q_width), row_spec(total - q_width), row_spec(LANES), row_spec(LANES)]
        + [ANYWHERE] * len(pieces),
        out_specs=[row_spec(total), row_spec(width)],
        out_shape=[jax.ShapeDtypeStruct((rows, total), BF16), jax.ShapeDtypeStruct((rows, width), BF16)],
        scratch_shapes=[pltpu.VMEM((width, total), BF16), pltpu.SemaphoreType.DMA],
        compiler_params=params(1),
        cost_estimate=pl.CostEstimate(
            flops=2 * rows * width * total, bytes_accessed=2 * (2 * rows * width + width * total), transcendentals=0
        ),
        name="project_qkv_back",
    )(d_queries, d_keys_values, cosine, sine, *pieces)


def gathered_body(count, axis, transposed, left, *rest):
    pieces, (out, weight, sem) = rest[:count], rest[count:]

    @pl.when(pl.program_id(0) == 0)
    def _():
        place_pieces(pieces, weight, sem, axis)
        await_whole(weight, sem)

    step = min(out.shape[1], 512)
    for start in range(0, out.shape[1], step):
        if transposed:
            part = lax.dot_general(
                left[...], weight[start : start + step, :], (((1,), (1,)), ((), ())), preferred_element_type=F32
            )
        else:
            part = jnp.dot(left[...], weight[:, start : start + step], preferred_element_type=F32)
        out[:, start : start + step] = part.astype(out.dtype)


def gathered_matmul(left, pieces, axis, transposed):
    rows = left.shape[0]
    shape = list(pieces[0].shape)
    shape[axis] *= len(pieces)
    outer = shape[0] if transposed else shape[1]
    tile = min(rows, 256)
    return pl.pallas_call(
        functools.partial(gathered_body, len(pieces), axis, transposed),
        grid=(rows // tile,),
        in_specs=[pl.BlockSpec((tile, left.shape[1]), lambda i: (i, 0))] + [ANYWHERE] * len(pieces),
        out_specs=pl.BlockSpec((tile, outer), lambda i: (i, 0)),
        out_shape=jax.ShapeDtypeStruct((rows, outer), BF16),
        scratch_shapes=[pltpu.VMEM(tuple(shape), BF16), pltpu.SemaphoreType.DMA],
        compiler_params=params(1),
        cost_estimate=pl.CostEstimate(
            flops=2 * rows * shape[0] * shape[1],
            bytes_accessed=2 * (rows * sum(shape) + shape[0] * shape[1]),
            transcendentals=0,
        ),
    )(left, *pieces)


def ffn_tile(f_step, tile, normed, d_ffn, gate, up, down, active, d_gate, d_up, out, d_normed, out_sum, d_sum):
    units = pl.ds(pl.multiple_of(f_step * tile, tile), tile)
    gate_tile, up_tile, down_tile = gate[:, units], up[:, units], down[units, :]
    gate_in = jnp.dot(normed[...], gate_tile, preferred_element_type=F32)
    upward = jnp.dot(normed[...], up_tile, preferred_element_type=F32)
    d_active = lax.dot_general(d_ffn[...], down_tile, (((1,), (1,)), ((), ())), preferred_element_type=F32)
    sigma = 1.0 / (1.0 + jnp.exp(-gate_in))
    silu = gate_in * sigma
    active_low = (silu * upward).astype(BF16)
    gate_low = (d_active * upward * (sigma * (1.0 + gate_in * (1.0 - sigma)))).astype(BF16)
    up_low = (d_active * silu).astype(BF16)
    active[...] = active_low
    d_gate[...] = gate_low
    d_up[...] = up_low
    part = jnp.dot(active_low, down_tile, preferred_element_type=F32)
    d_part = lax.dot_general(gate_low, gate_tile, (((1,), (1,)), ((), ())), preferred_element_type=F32)
    d_part += lax.dot_general(up_low, up_tile, (((1,), (1,)), ((), ())), preferred_element_type=F32)

    @pl.when(f_step == 0)
    def _():
        out_sum[...] = part
        d_sum[...] = d_part

    @pl.when(f_step > 0)
    def _():
        out_sum[...] += part
        d_sum[...] += d_part

    @pl.when(f_step == pl.num_programs(1) - 1)
    def _():
        out[...] = out_sum[...].astype(BF16)
        d_normed[...] = d_sum[...].astype(BF16)


def ffn_body(count, narrow, tile, normed, d_ffn, *rest):
    gate_pieces, up_pieces, rest = rest[:count], rest[count : 2 * count], rest[2 * count :]
    low_pieces, high_pieces, rest = rest[:narrow], rest[narrow : 2 * narrow], rest[2 * narrow :]
    active, d_gate, d_up, out, d_normed, gate, up, down, out_sum, d_sum, sems = rest
    f_step = pl.program_id(1)
    half = down.shape[0] // 2

    @pl.when((pl.program_id(0) == 0) & (f_step == 0))
    def _():
        place_pieces(gate_pieces, gate, sems.at[0], 0)
        place_pieces(up_pieces, up, sems.at[1], 0)
        place_pieces(low_pieces, down.at[pl.ds(0, half)], sems.at[2], 1)
        place_pieces(high_pieces, down.at[pl.ds(half, half)], sems.at[3], 1)
        await_whole(gate, sems.at[0])
        await_whole(up, sems.at[1])
        await_whole(down.at[pl.ds(0, half)], sems.at[2])
        await_whole(down.at[pl.ds(half, half)], sems.at[3])

    ffn_tile(f_step, tile, normed, d_ffn, gate, up, down, active, d_gate, d_up, out, d_normed, out_sum, d_sum)


def ffn(normed, d_ffn, gate_pieces, up_pieces, low_pieces, high_pieces, pushed):
    rows, width = normed.shape
    units = gate_pieces[0].shape[1]
    count = len(gate_pieces)
    tile = 256
    row_tile = min(rows, 512)
    once = pl.Buffered(1)
    row_spec = pl.BlockSpec((row_tile, width), lambda i, f: (i, 0), pipeline_mode=once)
    unit_spec = pl.BlockSpec((row_tile, tile), lambda i, f: (i, f))
    unit_shape = jax.ShapeDtypeStruct((rows, units), BF16)
    row_shape = jax.ShapeDtypeStruct((rows, width), BF16)
    body = functools.partial(ffn_body, count, len(low_pieces), tile)
    settings, sems = params(2), [pltpu.SemaphoreType.DMA((4,))]
    if pushed:
        body = functools.partial(pushed_body, count, tile)
        sems = [pltpu.SemaphoreType.DMA((3, units // tile))] * 3
        settings = pltpu.CompilerParams(
            dimension_semantics=("arbitrary",) * 2,
            vmem_limit_bytes=VMEM_BYTES,
            collective_id=5,
            has_side_effects=True,
        )
    return pl.pallas_call(
        body,
        grid=(rows // row_tile, units // tile),
        in_specs=[row_spec, row_spec] + [ANYWHERE] * (2 * count + 2 * len(low_pieces)),
        out_specs=[unit_spec, unit_spec, unit_spec, row_spec, row_spec],
        out_shape=[unit_shape, unit_shape, unit_shape, row_shape, row_shape],
        scratch_shapes=[
            pltpu.VMEM((width, units), BF16),
            pltpu.VMEM((width, units), BF16),
            pltpu.VMEM((units, width), BF16),
            pltpu.VMEM((row_tile, width), F32),
            pltpu.VMEM((row_tile, width), F32),
        ]
        + sems,
        compiler_params=settings,
        cost_estimate=pl.CostEstimate(
            flops=12 * rows * width * units, bytes_accessed=6 * width * units + 14 * rows * width, transcendentals=rows * units
        ),
        name="feed_forward",
    )(normed, d_ffn, *gate_pieces, *up_pieces, *low_pieces, *high_pieces)


def pushed_body(count, tile, normed, d_ffn, *refs):
    groups, rest = [refs[k * count : (k + 1) * count] for k in range(4)], refs[4 * count :]
    active, d_gate, d_up, out, d_normed, gate, up, down, out_sum, d_sum, near, send, recv = rest
    f_step = pl.program_id(1)
    first = (pl.program_id(0) == 0) & (f_step == 0)
    last = (pl.program_id(0) == pl.num_programs(0) - 1) & (f_step == pl.num_programs(1) - 1)
    steps = down.shape[0] // tile
    width = down.shape[1]
    extent = width // (2 * count)
    me = plane_index()
    mate = {"context": lax.axis_index("context") ^ 1}
    mesh_ids = pl.DeviceIdType.MESH

    def push(source, target, w, t):
        return pltpu.make_async_remote_copy(
            src_ref=source,
            dst_ref=target,
            send_sem=send.at[w, t],
            recv_sem=recv.at[w, t],
            device_id=mate,
            device_id_type=mesh_ids,
        )

    def halves(t):
        units = pl.ds(pl.multiple_of(t * tile, tile), tile)
        half = pl.ds(0, width // 2)
        return [gate.at[half, units], up.at[half, units], down.at[units, half]]

    @pl.when(first)
    def _():
        barrier = pltpu.get_barrier_semaphore()
        pl.semaphore_signal(barrier, inc=1, device_id=mate, device_id_type=mesh_ids)
        pl.semaphore_wait(barrier, 1)

        def start(t, carry):
            units = pl.ds(pl.multiple_of(t * tile, tile), tile)
            for i in range(count):
                base = pl.multiple_of((me ^ (2 * i)) * extent, extent)
                rows = pl.ds(base, extent)
                left = pl.ds(base, extent // 2)
                right = pl.ds(pl.multiple_of(base + extent // 2, extent // 2), extent // 2)
                moves = (
                    (0, groups[0][i].at[:, units], gate.at[rows, units]),
                    (1, groups[1][i].at[:, units], up.at[rows, units]),
                    (2, groups[2][i].at[units, :], down.at[units, left]),
                    (2, groups[3][i].at[units, :], down.at[units, right]),
                )
                for w, source, target in moves:
                    push(source, target, w, t).start()
                    pltpu.make_async_copy(source, target, near.at[w, t]).start()
            return carry

        lax.fori_loop(0, steps, start, 0)

    @pl.when(pl.program_id(0) == 0)
    def _():
        for w, half in enumerate(halves(f_step)):
            pltpu.make_async_copy(half, half, near.at[w, f_step]).wait()
            push(half, half, w, f_step).wait_recv()

    ffn_tile(f_step, tile, normed, d_ffn, gate, up, down, active, d_gate, d_up, out, d_normed, out_sum, d_sum)

    @pl.when(last)
    def _():
        def drain(t, carry):
            for w, half in enumerate(halves(t)):
                push(half, half, w, t).wait_send()
            return carry

        lax.fori_loop(0, steps, drain, 0)


def doubled(values, lane, head):
    rolled = pltpu.roll(values.astype(F32), HD, 1).astype(BF16)
    return jnp.where((lane < HD) == (head == 0), values, rolled)


def block_bias(order, seq, r, block):
    per = order.shape[1] // lax.axis_size("context")
    own = order[seq, lax.axis_index("context") * per + pl.program_id(3)]
    other = order[seq, (lax.axis_index("context") ^ r) * per + block]
    return jnp.where(other <= own, 0.0, MASKED_SCORE).astype(F32)


def masked_scores(order, pieces_k, query):
    seq = pl.program_id(0)
    scores = []
    for r, key_rows in enumerate(pieces_k):
        part = lax.dot_general(key_rows, query, (((1,), (1,)), ((), ())), preferred_element_type=F32)
        for block in range(key_rows.shape[0] // BLK):
            bias = block_bias(order, seq, r, block)
            scores.append(part[block * BLK : (block + 1) * BLK] + bias)
    return scores


def attend_body(count, order, query_ref, *rest):
    pieces, (mixture, logs) = rest[:count], rest[count:]
    head = pl.program_id(1)
    lane = lax.broadcasted_iota(jnp.int32, (1, LANES), 1)
    keys = [doubled(piece[:, :LANES], lane, head) for piece in pieces]
    values = [doubled(piece[:, LANES:], lane, head) for piece in pieces]
    query = query_ref[...]
    parts = []
    for side in range(2):
        chosen = (lane < HD) if side == 0 else (lane >= HD)
        scores = masked_scores(order, keys, jnp.where(chosen, query, jnp.zeros_like(query)))
        top = functools.reduce(jnp.maximum, [jnp.max(s, axis=0, keepdims=True) for s in scores])
        powers = [jnp.exp(s - top) for s in scores]
        total = sum(jnp.sum(p, axis=0, keepdims=True) for p in powers)
        low = jnp.concatenate([p.astype(BF16) for p in powers], axis=0)
        whole = jnp.concatenate(values, axis=0)
        mixed = lax.dot_general(whole, low, (((0,), (0,)), ((), ())), preferred_element_type=F32)
        parts.append(mixed / total)
        logs[side : side + 1, :] = top + jnp.log(total)
    row = lax.broadcasted_iota(jnp.int32, (LANES, 1), 0)
    mixture[...] = jnp.where(row < HD, parts[0], parts[1]).T.astype(BF16)


def attend_specs(order, queries, group_pairs):
    seqs = order.shape[0]
    rows = queries.shape[0] // seqs
    tiles = rows // BLK
    grid = (seqs, 2, group_pairs, tiles)
    q_spec = pl.BlockSpec((BLK, LANES), lambda s, h, g, t: (s * tiles + t, h * group_pairs + g))
    kv_spec = pl.BlockSpec((rows, 2 * LANES), lambda s, h, g, t: (s, 0))
    log_spec = pl.BlockSpec((None, 2, BLK), lambda s, h, g, t: (h * group_pairs + g, 0, s * tiles + t))
    return grid, q_spec, kv_spec, log_spec


def attend(order, queries, pieces):
    rows, q_width = queries.shape
    pairs = q_width // LANES
    grid, q_spec, kv_spec, log_spec = attend_specs(order, queries, pairs // 2)
    keys = rows * len(pieces) // order.shape[0]
    return pl.pallas_call(
        functools.partial(attend_body, len(pieces)),
        grid=grid,
        in_specs=[pl.BlockSpec(memory_space=pltpu.SMEM), q_spec] + [kv_spec] * len(pieces),
        out_specs=[q_spec, log_spec],
        out_shape=[jax.ShapeDtypeStruct((rows, q_width), BF16), jax.ShapeDtypeStruct((pairs, 2, rows), F32)],
        compiler_params=params(4),
        cost_estimate=pl.CostEstimate(
            flops=8 * rows * keys * q_width * 2, bytes_accessed=8 * rows * q_width, transcendentals=rows * keys * q_width // HD
        ),
        name="attend",
    )(order, queries, *pieces)


def attend_back_body(count, order, query_ref, grad_ref, logs, *rest):
    pieces, rest = rest[:count], rest[count:]
    d_query, outs, (d_key_sum, d_value_sum) = rest[0], rest[1 : 1 + count], rest[1 + count :]
    head, pair, tile = pl.program_id(1), pl.program_id(2), pl.program_id(3)
    lane = lax.broadcasted_iota(jnp.int32, (1, LANES), 1)
    keys = [doubled(piece[:, :LANES], lane, head) for piece in pieces]
    values = jnp.concatenate([doubled(piece[:, LANES:], lane, head) for piece in pieces], axis=0)
    whole_keys = jnp.concatenate(keys, axis=0)
    parts, d_keys, d_values = [], 0.0, 0.0
    for side in range(2):
        chosen = (lane < HD) if side == 0 else (lane >= HD)
        query = jnp.where(chosen, query_ref[...], jnp.zeros_like(query_ref[...]))
        grad = jnp.where(chosen, grad_ref[...], jnp.zeros_like(grad_ref[...]))
        scores = jnp.concatenate(masked_scores(order, keys, query), axis=0)
        soft = jnp.exp(scores - logs[side : side + 1, :])
        d_soft = lax.dot_general(values, grad, (((1,), (1,)), ((), ())), preferred_element_type=F32)
        inner = jnp.sum(soft * d_soft, axis=0, keepdims=True)
        d_scores = (soft * (d_soft - inner)).astype(BF16)
        d_values += jnp.dot(soft.astype(BF16), grad, preferred_element_type=F32)
        d_keys += jnp.dot(d_scores, query, preferred_element_type=F32)
        parts.append(lax.dot_general(whole_keys, d_scores, (((0,), (0,)), ((), ())), preferred_element_type=F32))
    row = lax.broadcasted_iota(jnp.int32, (LANES, 1), 0)
    d_query[...] = jnp.where(row < HD, parts[0], parts[1]).T * SCORE_SCALE

    first = (pair == 0) & (tile == 0)
    last = (pair == pl.num_programs(2) - 1) & (tile == pl.num_programs(3) - 1)

    @pl.when(first)
    def _():
        d_key_sum[...] = d_keys
        d_value_sum[...] = d_values

    @pl.when(jnp.logical_not(first))
    def _():
        d_key_sum[...] += d_keys
        d_value_sum[...] += d_values

    @pl.when(last)
    def _():
        wanted = (lane < HD) == (head == 0)
        rows = outs[0].shape[0]
        for r, out in enumerate(outs):
            for base, total in ((0, d_key_sum), (LANES, d_value_sum)):
                part = total[r * rows : (r + 1) * rows, :]
                both = (part + pltpu.roll(part, HD, 1)).astype(out.dtype)
                spot = pl.ds(base, LANES)

                @pl.when(head == 0)
                def _():
                    out[:, spot] = both

                @pl.when(head == 1)
                def _():
                    out[:, spot] = jnp.where(wanted, both.astype(F32), out[:, spot].astype(F32)).astype(out.dtype)


def attend_back(order, queries, grads, logs, pieces):
    rows, q_width = queries.shape
    pairs = q_width // LANES
    grid, q_spec, kv_spec, log_spec = attend_specs(order, queries, pairs // 2)
    keys = rows * len(pieces) // order.shape[0]
    return pl.pallas_call(
        functools.partial(attend_back_body, len(pieces)),
        grid=grid,
        in_specs=[pl.BlockSpec(memory_space=pltpu.SMEM), q_spec, q_spec, log_spec] + [kv_spec] * len(pieces),
        out_specs=[q_spec] + [kv_spec] * len(pieces),
        out_shape=[jax.ShapeDtypeStruct((rows, q_width), F32)]
        + [jax.ShapeDtypeStruct((rows, 2 * LANES), F32 if r % 2 == 0 else BF16) for r in range(len(pieces))],
        scratch_shapes=[pltpu.VMEM((keys, LANES), F32), pltpu.VMEM((keys, LANES), F32)],
        compiler_params=params(4),
        cost_estimate=pl.CostEstimate(
            flops=20 * rows * keys * q_width * 2, bytes_accessed=12 * rows * q_width, transcendentals=rows * keys * q_width // HD
        ),
        name="attend_back",
    )(order, queries, grads, logs, *pieces)


def line_steps(rows):
    half = rows // 2
    sub = 16
    return half, sub, half // sub


def line_body(finish, keep_state, gain_sum, n_in, extra, *refs):
    partial, ins, rest = refs[0], refs[1 : 1 + n_in], refs[1 + n_in :]
    if extra:
        world, n_grad, plan = extra
        ffn_out, grad_ins, rest = rest[0], rest[1 : 1 + n_grad], rest[1 + n_grad :]
    result, rest = rest[0], rest[1:]
    state_out, rest = (rest[0], rest[1:]) if keep_state else (None, rest)
    gain_out, rest = (rest[0], rest[1:]) if gain_sum else (None, rest)
    if extra:
        spread = world // 2 * len(plan)
        out_parts, grad_outs, rest = rest[0], rest[1 : 1 + spread], rest[1 + spread :]
    from_outer, from_peer, staged, send, recv = rest[:5]
    half, sub, count = line_steps(partial.shape[0])
    me = lax.axis_index("tensor")
    side = me // 2
    inner = lax.rem(me, 3) != 0
    to_outer, to_inner, to_peer = side * 3, 1 + side, 3 - me
    near, far = side * half, (1 - side) * half

    def rows(base, k):
        return pl.ds(pl.multiple_of(base + k * sub, sub), sub)

    def remote(source, target, s, r, k, where):
        return pltpu.make_async_remote_copy(
            src_ref=source,
            dst_ref=target,
            send_sem=send.at[s, k],
            recv_sem=recv.at[r, k],
            device_id={"tensor": where},
            device_id_type=pl.DeviceIdType.MESH,
        )

    def up_far(k):
        return remote(partial.at[rows(far, k)], from_outer.at[0, rows(0, k)], 0, 0, k, to_inner)

    def up_near(k):
        return remote(partial.at[rows(near, k)], from_outer.at[1, rows(0, k)], 1, 1, k, to_inner)

    def across(k):
        return remote(staged.at[rows(0, k)], from_peer.at[rows(0, k)], 0, 2, k, to_peer)

    def over(k, base):
        return remote(result.at[rows(base, k)], result.at[rows(base, k)], 2, 4, k, to_peer)

    def down_near(k):
        return remote(result.at[rows(near, k)], result.at[rows(near, k)], 1, 3, k, to_outer)

    def down_far(k):
        return remote(result.at[rows(far, k)], result.at[rows(far, k)], 3, 4, k, to_outer)

    barrier = pltpu.get_barrier_semaphore()

    def greet(where):
        pl.semaphore_signal(barrier, inc=1, device_id={"tensor": where}, device_id_type=pl.DeviceIdType.MESH)

    if extra:
        mate = {"context": lax.axis_index("context") ^ 1}
        pl.semaphore_signal(barrier, inc=1, device_id=mate, device_id_type=pl.DeviceIdType.MESH)
        grad_work, grad_finish = grads_parts(world, plan, grad_ins, grad_outs, rest[5:])
    block = partial.shape[0] // world if extra else 0

    def work(q):
        grad_work(q)
        rows_q = pl.ds(pl.multiple_of(q * block, block), block)
        value = RESIDUAL_SCALE * ffn_out[rows_q, :].astype(F32)
        quarter = 2 * block * world // 8
        chunk = lax.rem(q * 4 // world - me + 4, 4)
        place = pl.ds(pl.multiple_of(lax.rem(q * block, quarter), block), block)
        owned = inner & (q * 2 // world == side)

        @pl.when(owned)
        def _():
            mine = pl.ds(pl.multiple_of(lax.rem(q * block, half), block), block)
            out_parts[chunk, place, :] = (value + ins[0][mine, :]).astype(BF16)

        @pl.when(jnp.logical_not(owned))
        def _():
            out_parts[chunk, place, :] = value.astype(BF16)

    if gain_sum:
        gain_out[...] = jnp.zeros_like(gain_out)

    @pl.when(inner)
    def _():
        greet(to_outer)
        greet(to_peer)
        pl.semaphore_wait(barrier, 3 if extra else 2)

        def step(k, carry):
            @pl.when(k < count)
            def _():
                up_far(k).wait_recv()
                total = partial[rows(far, k), :].astype(F32) + from_outer[0, rows(0, k), :].astype(F32)
                staged[rows(0, k), :] = total.astype(BF16)
                across(k).start()

            @pl.when((k >= 1) & (k <= count))
            def _():
                j = k - 1
                up_near(j).wait_recv()
                across(j).wait_recv()
                total = partial[rows(near, j), :].astype(F32) + from_outer[1, rows(0, j), :].astype(F32)
                total = total + from_peer[rows(0, j), :].astype(F32)
                low, state, gains = finish(total, rows(near, j), rows(0, j), ins)
                result[rows(near, j), :] = low
                if keep_state:
                    state_out[rows(0, j), :] = state
                if gain_sum:
                    gain_out[...] += jnp.sum(gains.reshape(sub // 8, 8, gains.shape[1]), axis=0)
                down_near(j).start()
                over(j, near).start()

            @pl.when(k >= 3)
            def _():
                over(k - 3, far).wait_recv()
                down_far(k - 3).start()

            if extra:

                @pl.when((lax.rem(k, count // world) == 0) & (k < count))
                def _():
                    work(k // (count // world))

            return carry

        lax.fori_loop(0, count + 3, step, 0)

        def drain(k, carry):
            across(k).wait_send()
            down_near(k).wait_send()
            over(k, near).wait_send()
            down_far(k).wait_send()
            return carry

        lax.fori_loop(0, count, drain, 0)

    @pl.when(jnp.logical_not(inner))
    def _():
        greet(to_inner)
        pl.semaphore_wait(barrier, 2 if extra else 1)

        def step(k, carry):
            up_far(k).start()
            up_near(k).start()
            return carry

        lax.fori_loop(0, count, step, 0)
        if extra:

            def busy(q, carry):
                work(q)
                return carry

            lax.fori_loop(0, world, busy, 0)

        def drain(k, carry):
            down_near(k).wait_recv()
            down_far(k).wait_recv()
            up_far(k).wait_send()
            up_near(k).wait_send()
            return carry

        lax.fori_loop(0, count, drain, 0)

    if extra:
        grad_finish()


def line_sum(partial, ins, finish, keep_state, gain_sum, identity, ffn_out=None, pairs=()):
    rows, width = partial.shape
    half, _, count = line_steps(rows)
    vmem = pl.BlockSpec(memory_space=pltpu.VMEM)
    shapes = [jax.ShapeDtypeStruct((rows, width), BF16)]
    if keep_state:
        shapes.append(jax.ShapeDtypeStruct((half, width), F32))
    if gain_sum:
        shapes.append(jax.ShapeDtypeStruct((8, width), F32))
    specs, more, scratch, extra = [vmem] * len(shapes), [], [], None
    if pairs:
        arrays, plan = unique_arrays(pairs)
        extra = (plane_size(), len(arrays), plan)
        more = [ffn_out] + arrays
        outs, scratch = grads_shapes(pairs)
        shapes += [jax.ShapeDtypeStruct((4, rows // 4, width), BF16)] + outs
        specs += [vmem] + [ANYWHERE] * len(outs)
    return pl.pallas_call(
        functools.partial(line_body, finish, keep_state, gain_sum, len(ins), extra),
        in_specs=[vmem] * (1 + len(ins) + len(more)),
        out_specs=specs,
        out_shape=shapes,
        scratch_shapes=[
            pltpu.VMEM((2, half, width), BF16),
            pltpu.VMEM((half, width), BF16),
            pltpu.VMEM((half, width), BF16),
            pltpu.SemaphoreType.DMA((4, count)),
            pltpu.SemaphoreType.DMA((5, count)),
        ]
        + scratch,
        compiler_params=pltpu.CompilerParams(
            collective_id=identity, has_side_effects=True, vmem_limit_bytes=VMEM_BYTES
        ),
        cost_estimate=pl.CostEstimate(flops=0, bytes_accessed=100 * rows * width, transcendentals=0),
    )(partial, *ins, *more)


def mean_square(values):
    return lax.rsqrt(jnp.mean(values * values, axis=1, keepdims=True) + EPSILON)


def finish_attention(total, whole, own, ins):
    tokens, gain = ins
    hidden = tokens[whole, :].astype(F32) + RESIDUAL_SCALE * total
    return (hidden * mean_square(hidden) * gain[...]).astype(BF16), hidden, None


def norm_pull(d_normed, values, gain):
    inverse = mean_square(values)
    scaled = gain * d_normed
    inner = jnp.mean(scaled * values, axis=1, keepdims=True)
    return inverse * scaled - values * inverse * inverse * inverse * inner, d_normed * values * inverse


def finish_ffn_back(total, whole, own, ins):
    hidden, grads, gain = ins
    pulled, gains = norm_pull(total, hidden[own, :], gain[...])
    d_hidden = grads[whole, :].astype(F32) + pulled
    return (RESIDUAL_SCALE * d_hidden).astype(BF16), d_hidden, gains


def finish_attention_back(total, whole, own, ins):
    tokens, d_hidden, gain = ins
    pulled, gains = norm_pull(total, tokens[whole, :].astype(F32), gain[...])
    return (d_hidden[own, :] + pulled).astype(BF16), None, gains


def unique_arrays(pairs):
    arrays, plan = [], []
    for left, right, low, high in pairs:
        spots = []
        for value in (left, right):
            known = [i for i, array in enumerate(arrays) if array is value]
            if not known:
                arrays.append(value)
            spots.append(known[0] if known else len(arrays) - 1)
        plan.append((spots[0], spots[1], low, high))
    return arrays, tuple(plan)


def grads_parts(count, plan, ins, outs, scratch):
    halves, jobs = count // 2, len(plan)
    sent, got, own = scratch[:jobs], scratch[jobs : 2 * jobs], scratch[2 * jobs : 3 * jobs]
    send, recv, done = scratch[3 * jobs :]
    me = plane_index()
    mate = {"context": lax.axis_index("context") ^ 1}

    def piece(j, r):
        left, right, low, high = plan[j]
        extent = ins[left].shape[1] // count
        columns = pl.ds(pl.multiple_of((me ^ r) * extent, extent), extent)
        return lax.dot_general(
            ins[left][:, columns], ins[right][:, low:high], (((0,), (0,)), ((), ())), preferred_element_type=F32
        )

    def across(j, i):
        return pltpu.make_async_remote_copy(
            src_ref=sent[j].at[i],
            dst_ref=got[j].at[i],
            send_sem=send.at[j, i],
            recv_sem=recv.at[j, i],
            device_id=mate,
            device_id_type=pl.DeviceIdType.MESH,
        )

    def odd(i):
        for j in range(jobs):
            sent[j][i] = piece(j, 2 * i + 1).astype(BF16)
            across(j, i).start()

    def even(i):
        for j in range(jobs):
            value = piece(j, 2 * i)
            across(j, i).wait_recv()
            value = value + got[j][i].astype(F32)

            @pl.when(i > 0)
            def _():
                got[j][i] = value.astype(BF16)

            @pl.when(i == 0)
            def _():
                own[j][...] = value

        for known in range(halves):

            @pl.when(i == known)
            def _():
                for j in range(jobs):
                    source = got[j].at[known] if known else own[j]
                    pltpu.make_async_copy(source, outs[known * jobs + j], done.at[known, j]).start()

    def work(q):
        @pl.when(q < halves)
        def _():
            odd(halves - 1 - q)

        @pl.when(q >= halves)
        def _():
            even(count - 1 - q)

    def finish():
        for known in range(halves):
            for j in range(jobs):
                source = got[j].at[known] if known else own[j]
                pltpu.make_async_copy(source, outs[known * jobs + j], done.at[known, j]).wait()
                across(j, known).wait_send()

    return work, finish


def grads_body(count, n_in, plan, *refs):
    ins, rest = refs[:n_in], refs[n_in:]
    spread = count // 2 * len(plan)
    outs, scratch = rest[:spread], rest[spread:]
    work, finish = grads_parts(count, plan, ins, outs, scratch)
    barrier = pltpu.get_barrier_semaphore()
    mate = {"context": lax.axis_index("context") ^ 1}
    pl.semaphore_signal(barrier, inc=1, device_id=mate, device_id_type=pl.DeviceIdType.MESH)
    pl.semaphore_wait(barrier, 1)

    def step(q, carry):
        work(q)
        return carry

    lax.fori_loop(0, count, step, 0)
    finish()


def grads_shapes(pairs):
    count = plane_size()
    halves = count // 2
    shapes = [(left.shape[1] // count, high - low) for left, right, low, high in pairs]
    outs = [jax.ShapeDtypeStruct(shape, BF16 if i else F32) for i in range(halves) for shape in shapes]
    scratch = [pltpu.VMEM((halves,) + shape, BF16) for shape in shapes] * 2
    scratch += [pltpu.VMEM(shape, F32) for shape in shapes]
    sems = [(len(pairs), halves), (len(pairs), halves), (halves, len(pairs))]
    return outs, scratch + [pltpu.SemaphoreType.DMA(shape) for shape in sems]


def grads_named(flat, jobs):
    return [{2 * i: flat[i * jobs + j] for i in range(len(flat) // jobs)} for j in range(jobs)]


def grads_fit(pairs):
    return all((pair[0].shape[1] // plane_size()) % LANES == 0 for pair in pairs)


def plane_grads(pairs, identity):
    count = plane_size()
    jobs = len(pairs)
    extents = [pair[0].shape[1] // count for pair in pairs]
    arrays, plan = unique_arrays(pairs)
    if not grads_fit(pairs):
        me = plane_index()
        sides = []
        for (left, right, low, high), e in zip(pairs, extents):
            columns = lambda r: lax.dynamic_slice_in_dim(left, (me ^ r) * e, e, 1)
            whole = {r: weight_grad(columns(r), right[:, low:high]).astype(BF16) for r in range(count)}
            sides.append({r: take_sum(whole, 1, r) for r in range(0, count, 2)})
        return sides
    outs, scratch = grads_shapes(pairs)
    flat = pl.pallas_call(
        functools.partial(grads_body, count, len(arrays), plan),
        in_specs=[pl.BlockSpec(memory_space=pltpu.VMEM)] * len(arrays),
        out_specs=[ANYWHERE] * len(outs),
        out_shape=outs,
        scratch_shapes=scratch,
        compiler_params=pltpu.CompilerParams(
            collective_id=identity, has_side_effects=True, vmem_limit_bytes=VMEM_BYTES
        ),
        cost_estimate=pl.CostEstimate(
            flops=sum(2 * left.shape[0] * left.shape[1] * (high - low) for left, _, low, high in pairs),
            bytes_accessed=sum(2 * left.shape[1] * (high - low) for left, _, low, high in pairs),
            transcendentals=0,
        ),
    )(*arrays)
    return grads_named(flat, jobs)


def after(value, *others):
    return lax.optimization_barrier((value,) + others)[0] if others else value


def gather_context(piece):
    size = lax.axis_size("context")
    held = {0: piece}
    bit = size // 2
    while bit:
        for r in list(held):
            held[r | bit] = swap(held[r], "context", size, bit)
        bit //= 2
    return [held[r] for r in range(size)]


def reduce_context(pieces):
    size = len(pieces)
    held = dict(enumerate(pieces))
    bit = 1
    while bit < size:
        held = {
            r: held[r].astype(F32) + swap(held[r | bit].astype(BF16), "context", size, bit).astype(F32)
            for r in held
            if not r & bit
        }
        bit *= 2
    return held[0]


def stored_places(order_row, first, count):
    stored = first + jnp.arange(count, dtype=jnp.int32)
    picks = (stored // BLK)[:, None] == jnp.arange(order_row.shape[0], dtype=jnp.int32)[None, :]
    return jnp.sum(jnp.where(picks, order_row[None, :], 0), axis=1) * BLK + stored % BLK


def rope_tables(order, local_len):
    first = lax.axis_index("context") * local_len
    places = jnp.concatenate([stored_places(order[s], first, local_len) for s in range(order.shape[0])])
    half = HD // 2
    inverse = jnp.exp(jnp.arange(half, dtype=F32) * (-2.0 * math.log(ROPE_BASE) / HD))
    angles = places.astype(F32)[:, None] * jnp.tile(inverse, LANES // half)[None, :]
    return jnp.cos(angles), jnp.sin(angles)


def weight_grad(left, right):
    return lax.dot_general(left, right, (((0,), (0,)), ((), ())), preferred_element_type=F32)


def local(
    tokens, block_order, w_query, w_key, w_value, w_output, w_gate, w_up, w_down, norm_attn, norm_ffn, grad_out
):
    seqs, local_len, width = tokens.shape
    rows = seqs * local_len
    size = plane_size()
    z = lax.axis_index("tensor")
    token_rows = tokens.reshape(rows, width)
    grad_rows = grad_out.reshape(rows, width)
    q_width, kv_width = w_query.shape[1], w_key.shape[1]
    units = w_down.shape[0]
    half = units // 2

    gains = gather_small(jnp.stack([norm_attn, norm_ffn])).reshape(2, width)
    gain_attn, gain_ffn = gains[0:1], gains[1:2]
    w_qkv = jnp.concatenate([w_query, w_key, w_value], axis=1)
    qkv_pieces, output_pieces = gather_pair(w_qkv, w_output)
    cosine, sine = rope_tables(block_order, local_len)
    normed, queries, keys_values = project_qkv(token_rows, gain_attn, cosine, sine, qkv_pieces, q_width)
    kv_pieces = gather_context(keys_values)
    early, late = [qkv_pieces[-2], output_pieces[-2], output_pieces[size // 2]], [kv_pieces[-2]]
    mixture, logs = attend(block_order, queries, kv_pieces)
    output_pieces = widened(output_pieces)
    branch = gathered_matmul(mixture, output_pieces, 1, False)
    normed_ffn, hidden = line_sum(branch, [token_rows, gain_ffn], finish_attention, True, False, 0)
    extent = width // size
    pushed = extent % (2 * LANES) == 0
    order = (early, late, [mixture], [normed_ffn], not pushed)
    gate_pieces, up_pieces = gather_pair(w_gate, w_up, *order)
    order = (early, late, [normed_ffn], [normed_ffn], not pushed)
    if pushed:
        low_pieces, high_pieces = gather_pair(w_down[:, : extent // 2], w_down[:, extent // 2 :], *order)
    else:
        low_pieces, high_pieces = gather_pair(w_down[:half], w_down[half:], *order)
        low_pieces, high_pieces = widened(low_pieces), widened(high_pieces)
    d_ffn = (RESIDUAL_SCALE * grad_rows.astype(F32)).astype(BF16)
    active, d_gate, d_up, ffn_out, d_normed_ffn = ffn(
        normed_ffn, d_ffn, gate_pieces, up_pieces, low_pieces, high_pieces, pushed
    )
    pairs = [
        (normed_ffn, d_gate, 0, units),
        (normed_ffn, d_up, 0, units),
        (d_ffn, active, 0, half),
        (d_ffn, active, half, units),
    ]
    sum_ins = [hidden, grad_rows, gain_ffn]
    if grads_fit(pairs):
        d_branch, d_hidden, ffn_gain, out_parts, *flat = line_sum(
            d_normed_ffn, sum_ins, finish_ffn_back, True, True, 1, ffn_out, pairs
        )
        grad_gate, grad_up, grad_low, grad_high = grads_named(flat, len(pairs))
        out_chunks = [out_parts[shift] for shift in range(4)]
    else:
        grad_gate, grad_up, grad_low, grad_high = plane_grads(pairs, 3)
        d_branch, d_hidden, ffn_gain = line_sum(
            after(d_normed_ffn, grad_gate[0]), sum_ins, finish_ffn_back, True, True, 1
        )
        padded = lax.dynamic_update_slice_in_dim(jnp.zeros((rows, width), F32), hidden, (z // 2) * (rows // 2), 0)
        out_part = RESIDUAL_SCALE * ffn_out.astype(F32) + jnp.where(lax.rem(z, 3) != 0, padded, 0.0)
        out_chunks = [chunk_of(out_part.astype(BF16), lax.rem(z + shift, 4), rows // 4) for shift in range(4)]
    layer_out = rows_gather(rows_sum(out_chunks).astype(BF16))

    d_mixture = gathered_matmul(d_branch, output_pieces, 1, True)
    d_queries, *d_pieces = attend_back(block_order, queries, d_mixture, logs, kv_pieces)
    d_keys_values = reduce_context(d_pieces)
    grad_gate, grad_up = reduce_pair(grad_gate, grad_up, [d_keys_values])
    grad_low, grad_high = reduce_pair(grad_low, grad_high, [d_keys_values])
    d_qkv, d_normed = project_qkv_back(d_queries, d_keys_values, cosine, sine, qkv_pieces)
    grad_qkv, grad_output = plane_grads([(normed, d_qkv, 0, d_qkv.shape[1]), (d_branch, mixture, 0, q_width)], 4)
    d_normed = after(d_normed, grad_qkv[0])
    grad_tokens, attn_gain = line_sum(
        d_normed, [token_rows, d_hidden, gain_attn], finish_attention_back, False, True, 2
    )
    grad_tokens = grad_tokens.astype(F32)
    grad_qkv, grad_output = reduce_pair(grad_qkv, grad_output)
    attn_gain, ffn_gain = jnp.sum(attn_gain, axis=0), jnp.sum(ffn_gain, axis=0)
    gain_grads = jnp.stack([attn_gain, ffn_gain])
    gain_grads = gains_sum(gain_grads)
    return (
        layer_out.reshape(seqs, local_len, width),
        grad_tokens.reshape(seqs, local_len, width),
        grad_qkv[:, :q_width],
        grad_qkv[:, q_width : q_width + kv_width],
        grad_qkv[:, q_width + kv_width :],
        grad_output.T,
        grad_gate,
        grad_up,
        jnp.concatenate([grad_low.T, grad_high.T], axis=0),
        gain_grads[0],
        gain_grads[1],
    )


def solution(mesh):
    split = P("shard", "context", None)
    inward, outward = P(PLANE, "tensor"), P("tensor", PLANE)
    gain = P(PLANE)
    return jax.shard_map(
        local,
        mesh=mesh,
        in_specs=(split, P("shard", None), inward, inward, inward, outward, inward, inward, outward, gain, gain, split),
        out_specs=(split, split, inward, inward, inward, outward, inward, inward, outward, gain, gain),
        check_vma=False,
    )
```

```python
import functools
import math

import jax
import jax.numpy as jnp
from jax import lax
from jax.experimental import pallas as pl
from jax.experimental.pallas import tpu as pltpu
from jax.sharding import PartitionSpec as P


HD = 64
BLK = 256
LANES = 128
EPSILON = 1e-05
SCORE_SCALE = 0.015625
RESIDUAL_SCALE = 0.22
ROPE_BASE = 10000000.0
MASKED_SCORE = -1e30
PLANE = ("shard", "context")
VMEM_BYTES = 64000 * 1024


F32 = jnp.float32
BF16 = jnp.bfloat16


def plane_size():
    return lax.axis_size("shard") * lax.axis_size("context")


def plane_index():
    return lax.axis_index("shard") * lax.axis_size("context") + lax.axis_index("context")


def swap(value, axes, size, bit):
    return lax.ppermute(value, axes, [(i, i ^ bit) for i in range(size)])


def gather_pair(first, second, far_after=(), near_after=(), cross_after=(), core_after=(), core=True):
    size = plane_size()
    bits = [1 << b for b in range(1, size.bit_length() - 1)]
    sides = [{0: first}, {0: second}]
    if len(bits) == 2:
        near, far = bits
        for side in sides:
            side[far] = swap(after(side[0], *far_after), PLANE, size, far)
        for side in reversed(sides):
            side[near] = swap(after(side[0], *near_after), PLANE, size, near)
        sides[0][near | far] = swap(after(sides[0][far], *cross_after), PLANE, size, near)
        sides[1][near | far] = swap(after(sides[1][near], *cross_after), PLANE, size, far)
    else:
        for side in sides:
            for bit in bits:
                for r in list(side):
                    side[r | bit] = swap(side[r], PLANE, size, bit)
    if not core:
        return [[side[r] for r in range(0, size, 2)] for side in sides]
    for side in sides:
        for r in list(side):
            side[r | 1] = swap(after(side[r], *core_after), PLANE, size, 1)
    return [[side[r] for r in range(size)] for side in sides]


def widened(pieces):
    level = 1
    while pieces[0].shape[1] < LANES:
        upper = (plane_index() // level) % 2 == 1
        pairs = zip(pieces[0::2], pieces[1::2])
        pieces = [jnp.where(upper, jnp.concatenate([b, a], 1), jnp.concatenate([a, b], 1)) for a, b in pairs]
        level *= 2
    return pieces


def take_sum(side, bit, kept):
    sent = side[kept | bit].astype(BF16)
    total = side[kept].astype(F32) + swap(sent, PLANE, plane_size(), bit).astype(F32)
    return total if kept == 0 else total.astype(BF16)


def reduce_pair(first, second, last_after=()):
    size = plane_size()
    bits = [1 << b for b in range(1, size.bit_length() - 1)]
    sides = [dict(first), dict(second)]
    if len(bits) == 2:
        near, far = bits
        sides[0][near] = take_sum(sides[0], far, near)
        sides[1][far] = take_sum(sides[1], near, far)
        done = []
        for side in sides:
            sent = [after(side[bit].astype(BF16), *last_after) for bit in bits]
            a = swap(sent[0], PLANE, size, near).astype(F32)
            b = swap(sent[1], PLANE, size, far).astype(F32)
            done.append(side[0] + a + b)
        return done
    done = []
    for side in sides:
        for bit in reversed(bits):
            side = {r: take_sum(side, bit, r) for r in side if not r & bit}
        done.append(side[0])
    return done


def gather_small(values):
    size = plane_size()
    stacked = values[None]
    bit = 1
    while bit < size:
        stacked = jnp.concatenate([stacked, swap(stacked, PLANE, size, bit)], axis=0)
        bit *= 2
    picks = jnp.arange(size, dtype=jnp.int32)[:, None] ^ plane_index()
    chosen = (picks == jnp.arange(size, dtype=jnp.int32)[None, :]).astype(F32)
    return jnp.einsum("ij,jkw->kiw", chosen, stacked.astype(F32), precision=lax.Precision.HIGHEST)


def chunk_of(rows, index, count):
    return lax.dynamic_slice_in_dim(rows, index * count, count, 0)


def rows_sum(chunks):
    size = lax.axis_size("tensor")
    total = chunks[0].astype(F32)
    for shift in range(1, size):
        pairs = [(i, (i + shift) % size) for i in range(size)]
        total = total + lax.ppermute(chunks[shift], "tensor", pairs).astype(F32)
    return total


def rows_gather(chunk):
    size = lax.axis_size("tensor")
    me = lax.axis_index("tensor")
    count = chunk.shape[0]
    parts = [chunk]
    for shift in range(1, size):
        pairs = [(i, (i + shift) % size) for i in range(size)]
        parts.append(lax.ppermute(chunk, "tensor", pairs))
    whole = jnp.zeros((size * count,) + chunk.shape[1:], chunk.dtype)
    for shift in range(size):
        place = lax.rem(me - shift + size, size) * count
        whole = lax.dynamic_update_slice_in_dim(whole, parts[shift], place, 0)
    return whole


def gains_sum(values):
    size, tensor, me = plane_size(), lax.axis_size("tensor"), plane_index()
    extent = values.shape[1] // size
    total = values
    for shift in range(1, tensor):
        total = total + lax.ppermute(values, "tensor", [(i, (i + shift) % tensor) for i in range(tensor)])
    own = 0.0
    for r in range(size):
        sent = lax.dynamic_slice_in_dim(total, (me ^ r) * extent, extent, 1)
        own = own + (swap(sent, PLANE, size, r) if r else sent)
    return own


def params(steps):
    return pltpu.CompilerParams(
        dimension_semantics=("arbitrary",) * steps, vmem_limit_bytes=VMEM_BYTES
    )


def place_pieces(pieces, whole, sem, axis):
    size = len(pieces)
    me = plane_index() // (plane_size() // size)
    extent = whole.shape[axis] // size
    for r, piece in enumerate(pieces):
        start = pl.multiple_of((me ^ r) * extent, extent)
        target = whole.at[pl.ds(start, extent)] if axis == 0 else whole.at[:, pl.ds(start, extent)]
        pltpu.make_async_copy(piece, target, sem).start()


def await_whole(whole, sem):
    pltpu.make_async_copy(whole, whole, sem).wait()


ANYWHERE = pl.BlockSpec(memory_space=pl.ANY)


def turned(values, lane, sign):
    half = HD // 2
    upper = pltpu.roll(values, LANES - half, 1)
    lower = pltpu.roll(values, half, 1)
    return jnp.where(lane % HD < half, -sign * upper, sign * lower)


def qkv_body(count, tokens, gain, cosine, sine, *rest):
    pieces, (normed, queries, keys_values, weight, sem) = rest[:count], rest[count:]

    @pl.when(pl.program_id(0) == 0)
    def _():
        place_pieces(pieces, weight, sem, 0)

    values = tokens[...].astype(F32)
    inverse = lax.rsqrt(jnp.mean(values * values, axis=1, keepdims=True) + EPSILON)
    low = (values * inverse * gain[...]).astype(BF16)
    normed[...] = low

    @pl.when(pl.program_id(0) == 0)
    def _():
        await_whole(weight, sem)

    cos, sin = cosine[...], sine[...]
    lane = lax.broadcasted_iota(jnp.int32, cos.shape, 1)
    q_width = queries.shape[1]
    k_width = keys_values.shape[1] // 2
    for start in range(0, weight.shape[1], LANES):
        part = jnp.dot(low, weight[:, start : start + LANES * 1], preferred_element_type=F32)
        if start < q_width + k_width:
            part = part * cos + turned(part, lane, 1.0) * sin
        if start < q_width:
            queries[:, start : start + LANES] = (part.astype(BF16) * SCORE_SCALE).astype(BF16)
        else:
            keys_values[:, start - q_width : start - q_width + LANES] = part.astype(BF16)


def project_qkv(tokens, gain, cosine, sine, pieces, q_width):
    rows, width = tokens.shape
    total = pieces[0].shape[1]
    tile = min(rows, 256)
    row_spec = lambda w: pl.BlockSpec((tile, w), lambda i: (i, 0))
    return pl.pallas_call(
        functools.partial(qkv_body, len(pieces)),
        grid=(rows // tile,),
        in_specs=[row_spec(width), pl.BlockSpec((1, width), lambda i: (0, 0)), row_spec(LANES), row_spec(LANES)]
        + [ANYWHERE] * len(pieces),
        out_specs=[row_spec(width), row_spec(q_width), row_spec(total - q_width)],
        out_shape=[
            jax.ShapeDtypeStruct((rows, width), BF16),
            jax.ShapeDtypeStruct((rows, q_width), BF16),
            jax.ShapeDtypeStruct((rows, total - q_width), BF16),
        ],
        scratch_shapes=[pltpu.VMEM((width, total), BF16), pltpu.SemaphoreType.DMA],
        compiler_params=params(1),
        cost_estimate=pl.CostEstimate(
            flops=2 * rows * width * total, bytes_accessed=2 * (2 * rows * width + width * total), transcendentals=0
        ),
        name="project_qkv",
    )(tokens, gain, cosine, sine, *pieces)


def qkv_back_body(count, d_queries, d_keys_values, cosine, sine, *rest):
    pieces, (d_all, d_normed, weight, sem) = rest[:count], rest[count:]

    @pl.when(pl.program_id(0) == 0)
    def _():
        place_pieces(pieces, weight, sem, 0)

    cos, sin = cosine[...], sine[...]
    lane = lax.broadcasted_iota(jnp.int32, cos.shape, 1)
    q_width = d_queries.shape[1]
    k_width = d_keys_values.shape[1] // 2
    for start in range(0, d_all.shape[1], LANES):
        if start < q_width:
            part = d_queries[:, start : start + LANES]
        else:
            part = d_keys_values[:, start - q_width : start - q_width + LANES]
        if start < q_width + k_width:
            part = part * cos + turned(part * sin, lane, -1.0)
        d_all[:, start : start + LANES] = part.astype(BF16)

    @pl.when(pl.program_id(0) == 0)
    def _():
        await_whole(weight, sem)

    step = 512
    for start in range(0, weight.shape[0], step):
        d_normed[:, start : start + step] = lax.dot_general(
            d_all[...], weight[start : start + step, :], (((1,), (1,)), ((), ())), preferred_element_type=F32
        ).astype(BF16)


def project_qkv_back(d_queries, d_keys_values, cosine, sine, pieces):
    rows, q_width = d_queries.shape
    total = pieces[0].shape[1]
    width = pieces[0].shape[0] * len(pieces)
    tile = min(rows, 256)
    row_spec = lambda w: pl.BlockSpec((tile, w), lambda i: (i, 0))
    return pl.pallas_call(
        functools.partial(qkv_back_body, len(pieces)),
        grid=(rows // tile,),
        in_specs=[row_spec(q_width), row_spec(total - q_width), row_spec(LANES), row_spec(LANES)]
        + [ANYWHERE] * len(pieces),
        out_specs=[row_spec(total), row_spec(width)],
        out_shape=[jax.ShapeDtypeStruct((rows, total), BF16), jax.ShapeDtypeStruct((rows, width), BF16)],
        scratch_shapes=[pltpu.VMEM((width, total), BF16), pltpu.SemaphoreType.DMA],
        compiler_params=params(1),
        cost_estimate=pl.CostEstimate(
            flops=2 * rows * width * total, bytes_accessed=2 * (2 * rows * width + width * total), transcendentals=0
        ),
        name="project_qkv_back",
    )(d_queries, d_keys_values, cosine, sine, *pieces)


def gathered_body(count, axis, transposed, left, *rest):
    pieces, (out, weight, sem) = rest[:count], rest[count:]

    @pl.when(pl.program_id(0) == 0)
    def _():
        place_pieces(pieces, weight, sem, axis)
        await_whole(weight, sem)

    step = min(out.shape[1], 512)
    for start in range(0, out.shape[1], step):
        if transposed:
            part = lax.dot_general(
                left[...], weight[start : start + step, :], (((1,), (1,)), ((), ())), preferred_element_type=F32
            )
        else:
            part = jnp.dot(left[...], weight[:, start : start + step], preferred_element_type=F32)
        out[:, start : start + step] = part.astype(out.dtype)


def gathered_matmul(left, pieces, axis, transposed):
    rows = left.shape[0]
    shape = list(pieces[0].shape)
    shape[axis] *= len(pieces)
    outer = shape[0] if transposed else shape[1]
    tile = min(rows, 256)
    return pl.pallas_call(
        functools.partial(gathered_body, len(pieces), axis, transposed),
        grid=(rows // tile,),
        in_specs=[pl.BlockSpec((tile, left.shape[1]), lambda i: (i, 0))] + [ANYWHERE] * len(pieces),
        out_specs=pl.BlockSpec((tile, outer), lambda i: (i, 0)),
        out_shape=jax.ShapeDtypeStruct((rows, outer), BF16),
        scratch_shapes=[pltpu.VMEM(tuple(shape), BF16), pltpu.SemaphoreType.DMA],
        compiler_params=params(1),
        cost_estimate=pl.CostEstimate(
            flops=2 * rows * shape[0] * shape[1],
            bytes_accessed=2 * (rows * sum(shape) + shape[0] * shape[1]),
            transcendentals=0,
        ),
    )(left, *pieces)


def ffn_tile(f_step, tile, normed, d_ffn, gate, up, down, active, d_gate, d_up, out, d_normed, out_sum, d_sum):
    units = pl.ds(pl.multiple_of(f_step * tile, tile), tile)
    gate_tile, up_tile, down_tile = gate[:, units], up[:, units], down[units, :]
    gate_in = jnp.dot(normed[...], gate_tile, preferred_element_type=F32)
    upward = jnp.dot(normed[...], up_tile, preferred_element_type=F32)
    d_active = lax.dot_general(d_ffn[...], down_tile, (((1,), (1,)), ((), ())), preferred_element_type=F32)
    sigma = 1.0 / (1.0 + jnp.exp(-gate_in))
    silu = gate_in * sigma
    active_low = (silu * upward).astype(BF16)
    gate_low = (d_active * upward * (sigma * (1.0 + gate_in * (1.0 - sigma)))).astype(BF16)
    up_low = (d_active * silu).astype(BF16)
    active[...] = active_low
    d_gate[...] = gate_low
    d_up[...] = up_low
    part = jnp.dot(active_low, down_tile, preferred_element_type=F32)
    d_part = lax.dot_general(gate_low, gate_tile, (((1,), (1,)), ((), ())), preferred_element_type=F32)
    d_part += lax.dot_general(up_low, up_tile, (((1,), (1,)), ((), ())), preferred_element_type=F32)

    @pl.when(f_step == 0)
    def _():
        out_sum[...] = part
        d_sum[...] = d_part

    @pl.when(f_step > 0)
    def _():
        out_sum[...] += part
        d_sum[...] += d_part

    @pl.when(f_step == pl.num_programs(1) - 1)
    def _():
        out[...] = out_sum[...].astype(BF16)
        d_normed[...] = d_sum[...].astype(BF16)


def ffn_body(count, narrow, tile, normed, d_ffn, *rest):
    gate_pieces, up_pieces, rest = rest[:count], rest[count : 2 * count], rest[2 * count :]
    low_pieces, high_pieces, rest = rest[:narrow], rest[narrow : 2 * narrow], rest[2 * narrow :]
    active, d_gate, d_up, out, d_normed, gate, up, down, out_sum, d_sum, sems = rest
    f_step = pl.program_id(1)
    half = down.shape[0] // 2

    @pl.when((pl.program_id(0) == 0) & (f_step == 0))
    def _():
        place_pieces(gate_pieces, gate, sems.at[0], 0)
        place_pieces(up_pieces, up, sems.at[1], 0)
        place_pieces(low_pieces, down.at[pl.ds(0, half)], sems.at[2], 1)
        place_pieces(high_pieces, down.at[pl.ds(half, half)], sems.at[3], 1)
        await_whole(gate, sems.at[0])
        await_whole(up, sems.at[1])
        await_whole(down.at[pl.ds(0, half)], sems.at[2])
        await_whole(down.at[pl.ds(half, half)], sems.at[3])

    ffn_tile(f_step, tile, normed, d_ffn, gate, up, down, active, d_gate, d_up, out, d_normed, out_sum, d_sum)


def ffn(normed, d_ffn, gate_pieces, up_pieces, low_pieces, high_pieces, pushed):
    rows, width = normed.shape
    units = gate_pieces[0].shape[1]
    count = len(gate_pieces)
    tile = 256
    row_tile = min(rows, 512)
    once = pl.Buffered(1)
    row_spec = pl.BlockSpec((row_tile, width), lambda i, f: (i, 0), pipeline_mode=once)
    unit_spec = pl.BlockSpec((row_tile, tile), lambda i, f: (i, f))
    unit_shape = jax.ShapeDtypeStruct((rows, units), BF16)
    row_shape = jax.ShapeDtypeStruct((rows, width), BF16)
    body = functools.partial(ffn_body, count, len(low_pieces), tile)
    settings, sems = params(2), [pltpu.SemaphoreType.DMA((4,))]
    if pushed:
        body = functools.partial(pushed_body, count, tile)
        sems = [pltpu.SemaphoreType.DMA((3, units // tile))] * 3
        settings = pltpu.CompilerParams(
            dimension_semantics=("arbitrary",) * 2,
            vmem_limit_bytes=VMEM_BYTES,
            collective_id=5,
            has_side_effects=True,
        )
    return pl.pallas_call(
        body,
        grid=(rows // row_tile, units // tile),
        in_specs=[row_spec, row_spec] + [ANYWHERE] * (2 * count + 2 * len(low_pieces)),
        out_specs=[unit_spec, unit_spec, unit_spec, row_spec, row_spec],
        out_shape=[unit_shape, unit_shape, unit_shape, row_shape, row_shape],
        scratch_shapes=[
            pltpu.VMEM((width, units), BF16),
            pltpu.VMEM((width, units), BF16),
            pltpu.VMEM((units, width), BF16),
            pltpu.VMEM((row_tile, width), F32),
            pltpu.VMEM((row_tile, width), F32),
        ]
        + sems,
        compiler_params=settings,
        cost_estimate=pl.CostEstimate(
            flops=12 * rows * width * units, bytes_accessed=6 * width * units + 14 * rows * width, transcendentals=rows * units
        ),
        name="feed_forward",
    )(normed, d_ffn, *gate_pieces, *up_pieces, *low_pieces, *high_pieces)


def pushed_body(count, tile, normed, d_ffn, *refs):
    groups, rest = [refs[k * count : (k + 1) * count] for k in range(4)], refs[4 * count :]
    active, d_gate, d_up, out, d_normed, gate, up, down, out_sum, d_sum, near, send, recv = rest
    f_step = pl.program_id(1)
    first = (pl.program_id(0) == 0) & (f_step == 0)
    last = (pl.program_id(0) == pl.num_programs(0) - 1) & (f_step == pl.num_programs(1) - 1)
    steps = down.shape[0] // tile
    width = down.shape[1]
    extent = width // (2 * count)
    me = plane_index()
    mate = {"context": lax.axis_index("context") ^ 1}
    mesh_ids = pl.DeviceIdType.MESH

    def push(source, target, w, t):
        return pltpu.make_async_remote_copy(
            src_ref=source,
            dst_ref=target,
            send_sem=send.at[w, t],
            recv_sem=recv.at[w, t],
            device_id=mate,
            device_id_type=mesh_ids,
        )

    def halves(t):
        units = pl.ds(pl.multiple_of(t * tile, tile), tile)
        half = pl.ds(0, width // 2)
        return [gate.at[half, units], up.at[half, units], down.at[units, half]]

    @pl.when(first)
    def _():
        barrier = pltpu.get_barrier_semaphore()
        pl.semaphore_signal(barrier, inc=1, device_id=mate, device_id_type=mesh_ids)
        pl.semaphore_wait(barrier, 1)

        def start(t, carry):
            units = pl.ds(pl.multiple_of(t * tile, tile), tile)
            for i in range(count):
                base = pl.multiple_of((me ^ (2 * i)) * extent, extent)
                rows = pl.ds(base, extent)
                left = pl.ds(base, extent // 2)
                right = pl.ds(pl.multiple_of(base + extent // 2, extent // 2), extent // 2)
                moves = (
                    (0, groups[0][i].at[:, units], gate.at[rows, units]),
                    (1, groups[1][i].at[:, units], up.at[rows, units]),
                    (2, groups[2][i].at[units, :], down.at[units, left]),
                    (2, groups[3][i].at[units, :], down.at[units, right]),
                )
                for w, source, target in moves:
                    push(source, target, w, t).start()
                    pltpu.make_async_copy(source, target, near.at[w, t]).start()
            return carry

        lax.fori_loop(0, steps, start, 0)

    @pl.when(pl.program_id(0) == 0)
    def _():
        for w, half in enumerate(halves(f_step)):
            pltpu.make_async_copy(half, half, near.at[w, f_step]).wait()
            push(half, half, w, f_step).wait_recv()

    ffn_tile(f_step, tile, normed, d_ffn, gate, up, down, active, d_gate, d_up, out, d_normed, out_sum, d_sum)

    @pl.when(last)
    def _():
        def drain(t, carry):
            for w, half in enumerate(halves(t)):
                push(half, half, w, t).wait_send()
            return carry

        lax.fori_loop(0, steps, drain, 0)


def doubled(values, lane, head):
    rolled = pltpu.roll(values.astype(F32), HD, 1).astype(BF16)
    return jnp.where((lane < HD) == (head == 0), values, rolled)


def block_bias(order, seq, r, block):
    per = order.shape[1] // lax.axis_size("context")
    own = order[seq, lax.axis_index("context") * per + pl.program_id(3)]
    other = order[seq, (lax.axis_index("context") ^ r) * per + block]
    return jnp.where(other <= own, 0.0, MASKED_SCORE).astype(F32)


def masked_scores(order, pieces_k, query):
    seq = pl.program_id(0)
    scores = []
    for r, key_rows in enumerate(pieces_k):
        part = lax.dot_general(key_rows, query, (((1,), (1,)), ((), ())), preferred_element_type=F32)
        for block in range(key_rows.shape[0] // BLK):
            bias = block_bias(order, seq, r, block)
            scores.append(part[block * BLK : (block + 1) * BLK] + bias)
    return scores


def attend_body(count, order, query_ref, *rest):
    pieces, (mixture, logs) = rest[:count], rest[count:]
    head = pl.program_id(1)
    lane = lax.broadcasted_iota(jnp.int32, (1, LANES), 1)
    keys = [doubled(piece[:, :LANES], lane, head) for piece in pieces]
    values = [doubled(piece[:, LANES:], lane, head) for piece in pieces]
    query = query_ref[...]
    parts = []
    for side in range(2):
        chosen = (lane < HD) if side == 0 else (lane >= HD)
        scores = masked_scores(order, keys, jnp.where(chosen, query, jnp.zeros_like(query)))
        top = functools.reduce(jnp.maximum, [jnp.max(s, axis=0, keepdims=True) for s in scores])
        powers = [jnp.exp(s - top) for s in scores]
        total = sum(jnp.sum(p, axis=0, keepdims=True) for p in powers)
        low = jnp.concatenate([p.astype(BF16) for p in powers], axis=0)
        whole = jnp.concatenate(values, axis=0)
        mixed = lax.dot_general(whole, low, (((0,), (0,)), ((), ())), preferred_element_type=F32)
        parts.append(mixed / total)
        logs[side : side + 1, :] = top + jnp.log(total)
    row = lax.broadcasted_iota(jnp.int32, (LANES, 1), 0)
    mixture[...] = jnp.where(row < HD, parts[0], parts[1]).T.astype(BF16)


def attend_specs(order, queries, pieces, group_pairs):
    seqs = order.shape[0]
    rows = queries.shape[0] // seqs
    tiles = rows // BLK
    grid = (seqs, 2, group_pairs, tiles)
    q_spec = pl.BlockSpec((BLK, LANES), lambda s, h, g, t: (s * tiles + t, h * group_pairs + g))
    kv_spec = pl.BlockSpec((rows, 2 * LANES), lambda s, h, g, t: (s, 0))
    kv_ins = [pl.BlockSpec((None, rows, 2 * LANES), lambda s, h, g, t, r=r: (r, s, 0)) for r in range(pieces.shape[0])]
    log_spec = pl.BlockSpec((None, 2, BLK), lambda s, h, g, t: (h * group_pairs + g, 0, s * tiles + t))
    return grid, q_spec, kv_spec, kv_ins, log_spec


def attend(order, queries, pieces):
    rows, q_width = queries.shape
    pairs = q_width // LANES
    grid, q_spec, _, kv_ins, log_spec = attend_specs(order, queries, pieces, pairs // 2)
    keys = rows * pieces.shape[0] // order.shape[0]
    return pl.pallas_call(
        functools.partial(attend_body, pieces.shape[0]),
        grid=grid,
        in_specs=[pl.BlockSpec(memory_space=pltpu.SMEM), q_spec] + kv_ins,
        out_specs=[q_spec, log_spec],
        out_shape=[jax.ShapeDtypeStruct((rows, q_width), BF16), jax.ShapeDtypeStruct((pairs, 2, rows), F32)],
        compiler_params=params(4),
        cost_estimate=pl.CostEstimate(
            flops=8 * rows * keys * q_width * 2, bytes_accessed=8 * rows * q_width, transcendentals=rows * keys * q_width // HD
        ),
        name="attend",
    )(order, queries, *[pieces] * pieces.shape[0])


def attend_back_body(count, order, query_ref, grad_ref, logs, *rest):
    pieces, rest = rest[:count], rest[count:]
    d_query, outs, (d_key_sum, d_value_sum) = rest[0], rest[1 : 1 + count], rest[1 + count :]
    head, pair, tile = pl.program_id(1), pl.program_id(2), pl.program_id(3)
    lane = lax.broadcasted_iota(jnp.int32, (1, LANES), 1)
    keys = [doubled(piece[:, :LANES], lane, head) for piece in pieces]
    values = jnp.concatenate([doubled(piece[:, LANES:], lane, head) for piece in pieces], axis=0)
    whole_keys = jnp.concatenate(keys, axis=0)
    parts, d_keys, d_values = [], 0.0, 0.0
    for side in range(2):
        chosen = (lane < HD) if side == 0 else (lane >= HD)
        query = jnp.where(chosen, query_ref[...], jnp.zeros_like(query_ref[...]))
        grad = jnp.where(chosen, grad_ref[...], jnp.zeros_like(grad_ref[...]))
        scores = jnp.concatenate(masked_scores(order, keys, query), axis=0)
        soft = jnp.exp(scores - logs[side : side + 1, :])
        d_soft = lax.dot_general(values, grad, (((1,), (1,)), ((), ())), preferred_element_type=F32)
        inner = jnp.sum(soft * d_soft, axis=0, keepdims=True)
        d_scores = (soft * (d_soft - inner)).astype(BF16)
        d_values += jnp.dot(soft.astype(BF16), grad, preferred_element_type=F32)
        d_keys += jnp.dot(d_scores, query, preferred_element_type=F32)
        parts.append(lax.dot_general(whole_keys, d_scores, (((0,), (0,)), ((), ())), preferred_element_type=F32))
    row = lax.broadcasted_iota(jnp.int32, (LANES, 1), 0)
    d_query[...] = jnp.where(row < HD, parts[0], parts[1]).T * SCORE_SCALE

    first = (pair == 0) & (tile == 0)
    last = (pair == pl.num_programs(2) - 1) & (tile == pl.num_programs(3) - 1)

    @pl.when(first)
    def _():
        d_key_sum[...] = d_keys
        d_value_sum[...] = d_values

    @pl.when(jnp.logical_not(first))
    def _():
        d_key_sum[...] += d_keys
        d_value_sum[...] += d_values

    @pl.when(last)
    def _():
        wanted = (lane < HD) == (head == 0)
        rows = outs[0].shape[0]
        for r, out in enumerate(outs):
            for base, total in ((0, d_key_sum), (LANES, d_value_sum)):
                part = total[r * rows : (r + 1) * rows, :]
                both = (part + pltpu.roll(part, HD, 1)).astype(out.dtype)
                spot = pl.ds(base, LANES)

                @pl.when(head == 0)
                def _():
                    out[:, spot] = both

                @pl.when(head == 1)
                def _():
                    out[:, spot] = jnp.where(wanted, both.astype(F32), out[:, spot].astype(F32)).astype(out.dtype)


def attend_back(order, queries, grads, logs, pieces):
    rows, q_width = queries.shape
    pairs = q_width // LANES
    grid, q_spec, kv_spec, kv_ins, log_spec = attend_specs(order, queries, pieces, pairs // 2)
    keys = rows * pieces.shape[0] // order.shape[0]
    return pl.pallas_call(
        functools.partial(attend_back_body, pieces.shape[0]),
        grid=grid,
        in_specs=[pl.BlockSpec(memory_space=pltpu.SMEM), q_spec, q_spec, log_spec] + kv_ins,
        out_specs=[q_spec] + [kv_spec] * pieces.shape[0],
        out_shape=[jax.ShapeDtypeStruct((rows, q_width), F32)]
        + [jax.ShapeDtypeStruct((rows, 2 * LANES), F32 if r % 2 == 0 else BF16) for r in range(pieces.shape[0])],
        scratch_shapes=[pltpu.VMEM((keys, LANES), F32), pltpu.VMEM((keys, LANES), F32)],
        compiler_params=params(4),
        cost_estimate=pl.CostEstimate(
            flops=20 * rows * keys * q_width * 2, bytes_accessed=12 * rows * q_width, transcendentals=rows * keys * q_width // HD
        ),
        name="attend_back",
    )(order, queries, grads, logs, *[pieces] * pieces.shape[0])


def line_steps(rows):
    half = rows // 2
    sub = 16
    return half, sub, half // sub


def line_body(finish, keep_state, gain_sum, n_in, extra, *refs):
    partial, ins, rest = refs[0], refs[1 : 1 + n_in], refs[1 + n_in :]
    if extra:
        world, n_grad, plan = extra
        ffn_out, grad_ins, rest = rest[0], rest[1 : 1 + n_grad], rest[1 + n_grad :]
    result, rest = rest[0], rest[1:]
    state_out, rest = (rest[0], rest[1:]) if keep_state else (None, rest)
    gain_out, rest = (rest[0], rest[1:]) if gain_sum else (None, rest)
    if extra:
        spread = world // 2 * len(plan)
        out_parts, grad_outs, rest = rest[0], rest[1 : 1 + spread], rest[1 + spread :]
    from_outer, from_peer, staged, send, recv = rest[:5]
    half, sub, count = line_steps(partial.shape[0])
    me = lax.axis_index("tensor")
    side = me // 2
    inner = lax.rem(me, 3) != 0
    to_outer, to_inner, to_peer = side * 3, 1 + side, 3 - me
    near, far = side * half, (1 - side) * half

    def rows(base, k):
        return pl.ds(pl.multiple_of(base + k * sub, sub), sub)

    def remote(source, target, s, r, k, where):
        return pltpu.make_async_remote_copy(
            src_ref=source,
            dst_ref=target,
            send_sem=send.at[s, k],
            recv_sem=recv.at[r, k],
            device_id={"tensor": where},
            device_id_type=pl.DeviceIdType.MESH,
        )

    def up_far(k):
        return remote(partial.at[rows(far, k)], from_outer.at[0, rows(0, k)], 0, 0, k, to_inner)

    def up_near(k):
        return remote(partial.at[rows(near, k)], from_outer.at[1, rows(0, k)], 1, 1, k, to_inner)

    def across(k):
        return remote(staged.at[rows(0, k)], from_peer.at[rows(0, k)], 0, 2, k, to_peer)

    def over(k, base):
        return remote(result.at[rows(base, k)], result.at[rows(base, k)], 2, 4, k, to_peer)

    def down_near(k):
        return remote(result.at[rows(near, k)], result.at[rows(near, k)], 1, 3, k, to_outer)

    def down_far(k):
        return remote(result.at[rows(far, k)], result.at[rows(far, k)], 3, 4, k, to_outer)

    barrier = pltpu.get_barrier_semaphore()

    def greet(where):
        pl.semaphore_signal(barrier, inc=1, device_id={"tensor": where}, device_id_type=pl.DeviceIdType.MESH)

    if extra:
        mate = {"context": lax.axis_index("context") ^ 1}
        pl.semaphore_signal(barrier, inc=1, device_id=mate, device_id_type=pl.DeviceIdType.MESH)
        grad_work, grad_finish = grads_parts(world, plan, grad_ins, grad_outs, rest[5:])
    block = partial.shape[0] // world if extra else 0

    def work(q):
        grad_work(q)
        rows_q = pl.ds(pl.multiple_of(q * block, block), block)
        value = RESIDUAL_SCALE * ffn_out[rows_q, :].astype(F32)
        quarter = 2 * block * world // 8
        chunk = lax.rem(q * 4 // world - me + 4, 4)
        place = pl.ds(pl.multiple_of(lax.rem(q * block, quarter), block), block)
        owned = inner & (q * 2 // world == side)

        @pl.when(owned)
        def _():
            mine = pl.ds(pl.multiple_of(lax.rem(q * block, half), block), block)
            out_parts[chunk, place, :] = (value + ins[0][mine, :]).astype(BF16)

        @pl.when(jnp.logical_not(owned))
        def _():
            out_parts[chunk, place, :] = value.astype(BF16)

    if gain_sum:
        gain_out[...] = jnp.zeros_like(gain_out)

    @pl.when(inner)
    def _():
        greet(to_outer)
        greet(to_peer)
        pl.semaphore_wait(barrier, 3 if extra else 2)

        def step(k, carry):
            @pl.when(k < count)
            def _():
                up_far(k).wait_recv()
                total = partial[rows(far, k), :].astype(F32) + from_outer[0, rows(0, k), :].astype(F32)
                staged[rows(0, k), :] = total.astype(BF16)
                across(k).start()

            @pl.when((k >= 1) & (k <= count))
            def _():
                j = k - 1
                up_near(j).wait_recv()
                across(j).wait_recv()
                total = partial[rows(near, j), :].astype(F32) + from_outer[1, rows(0, j), :].astype(F32)
                total = total + from_peer[rows(0, j), :].astype(F32)
                low, state, gains = finish(total, rows(near, j), rows(0, j), ins)
                result[rows(near, j), :] = low
                if keep_state:
                    state_out[rows(0, j), :] = state
                if gain_sum:
                    gain_out[...] += jnp.sum(gains.reshape(sub // 8, 8, gains.shape[1]), axis=0)
                down_near(j).start()
                over(j, near).start()

            @pl.when(k >= 3)
            def _():
                over(k - 3, far).wait_recv()
                down_far(k - 3).start()

            if extra:

                @pl.when((lax.rem(k, count // world) == 0) & (k < count))
                def _():
                    work(k // (count // world))

            return carry

        lax.fori_loop(0, count + 3, step, 0)

        def drain(k, carry):
            across(k).wait_send()
            down_near(k).wait_send()
            over(k, near).wait_send()
            down_far(k).wait_send()
            return carry

        lax.fori_loop(0, count, drain, 0)

    @pl.when(jnp.logical_not(inner))
    def _():
        greet(to_inner)
        pl.semaphore_wait(barrier, 2 if extra else 1)

        def step(k, carry):
            up_far(k).start()
            up_near(k).start()
            return carry

        lax.fori_loop(0, count, step, 0)
        if extra:

            def busy(q, carry):
                work(q)
                return carry

            lax.fori_loop(0, world, busy, 0)

        def drain(k, carry):
            down_near(k).wait_recv()
            down_far(k).wait_recv()
            up_far(k).wait_send()
            up_near(k).wait_send()
            return carry

        lax.fori_loop(0, count, drain, 0)

    if extra:
        grad_finish()


def line_sum(partial, ins, finish, keep_state, gain_sum, identity, ffn_out=None, pairs=()):
    rows, width = partial.shape
    half, _, count = line_steps(rows)
    vmem = pl.BlockSpec(memory_space=pltpu.VMEM)
    shapes = [jax.ShapeDtypeStruct((rows, width), BF16)]
    if keep_state:
        shapes.append(jax.ShapeDtypeStruct((half, width), F32))
    if gain_sum:
        shapes.append(jax.ShapeDtypeStruct((8, width), F32))
    specs, more, scratch, extra = [vmem] * len(shapes), [], [], None
    if pairs:
        arrays, plan = unique_arrays(pairs)
        extra = (plane_size(), len(arrays), plan)
        more = [ffn_out] + arrays
        outs, scratch = grads_shapes(pairs)
        shapes += [jax.ShapeDtypeStruct((4, rows // 4, width), BF16)] + outs
        specs += [vmem] + [ANYWHERE] * len(outs)
    return pl.pallas_call(
        functools.partial(line_body, finish, keep_state, gain_sum, len(ins), extra),
        in_specs=[vmem] * (1 + len(ins) + len(more)),
        out_specs=specs,
        out_shape=shapes,
        scratch_shapes=[
            pltpu.VMEM((2, half, width), BF16),
            pltpu.VMEM((half, width), BF16),
            pltpu.VMEM((half, width), BF16),
            pltpu.SemaphoreType.DMA((4, count)),
            pltpu.SemaphoreType.DMA((5, count)),
        ]
        + scratch,
        compiler_params=pltpu.CompilerParams(
            collective_id=identity, has_side_effects=True, vmem_limit_bytes=VMEM_BYTES
        ),
        cost_estimate=pl.CostEstimate(flops=0, bytes_accessed=100 * rows * width, transcendentals=0),
    )(partial, *ins, *more)


def mean_square(values):
    return lax.rsqrt(jnp.mean(values * values, axis=1, keepdims=True) + EPSILON)


def finish_attention(total, whole, own, ins):
    tokens, gain = ins
    hidden = tokens[whole, :].astype(F32) + RESIDUAL_SCALE * total
    return (hidden * mean_square(hidden) * gain[...]).astype(BF16), hidden, None


def norm_pull(d_normed, values, gain):
    inverse = mean_square(values)
    scaled = gain * d_normed
    inner = jnp.mean(scaled * values, axis=1, keepdims=True)
    return inverse * scaled - values * inverse * inverse * inverse * inner, d_normed * values * inverse


def finish_ffn_back(total, whole, own, ins):
    hidden, grads, gain = ins
    pulled, gains = norm_pull(total, hidden[own, :], gain[...])
    d_hidden = grads[whole, :].astype(F32) + pulled
    return (RESIDUAL_SCALE * d_hidden).astype(BF16), d_hidden, gains


def finish_attention_back(total, whole, own, ins):
    tokens, d_hidden, gain = ins
    pulled, gains = norm_pull(total, tokens[whole, :].astype(F32), gain[...])
    return (d_hidden[own, :] + pulled).astype(BF16), None, gains


def front_fits():
    return lax.axis_size("shard") == 2 and lax.axis_size("context") == 4


def front_body(*refs):
    tokens, gain_piece, cosine, sine, w_query, w_key, w_value, w_output = refs[:8]
    normed, queries, kv, weight, output, gains = refs[8:14]
    local_sem, send, recv = refs[14:]
    me = plane_index()
    extent = weight.shape[0] // 8
    q_width = queries.shape[1]
    k_width = kv.shape[2] // 2
    context, shard = lax.axis_index("context"), lax.axis_index("shard")
    peers = {1: {"context": context ^ 1}, 2: {"context": context ^ 2}, 4: {"shard": shard ^ 1}}
    mesh_ids = pl.DeviceIdType.MESH
    barrier = pltpu.get_barrier_semaphore()
    for bit in (1, 2, 4):
        pl.semaphore_signal(barrier, inc=1, device_id=peers[bit], device_id_type=mesh_ids)

    def start(r):
        return pl.multiple_of((me ^ r) * extent, extent)

    def qkv_at(r, part=None):
        size = extent if part is None else extent // 2
        base = start(r) + (part or 0) * size
        return weight.at[pl.ds(pl.multiple_of(base, size), size)]

    def output_at(r, part=None):
        columns = pl.ds(start(r), extent)
        if part is None:
            return output.at[:, columns]
        size = output.shape[0] // 2
        return output.at[pl.ds(part * size, size), columns]

    def gains_at(r):
        return gains.at[:, pl.ds(start(r), extent)]

    spots = {}

    def remote(name, ref, bit, target=None):
        index = spots.setdefault(name, len(spots))
        return pltpu.make_async_remote_copy(
            src_ref=ref,
            dst_ref=ref if target is None else target,
            send_sem=send.at[index],
            recv_sem=recv.at[index],
            device_id=peers[bit],
            device_id_type=mesh_ids,
        )

    locals_ = [
        pltpu.make_async_copy(gain_piece, gains_at(0), local_sem.at[0]),
        pltpu.make_async_copy(w_query, weight.at[pl.ds(start(0), extent), pl.ds(0, q_width)], local_sem.at[1]),
        pltpu.make_async_copy(w_key, weight.at[pl.ds(start(0), extent), pl.ds(q_width, k_width)], local_sem.at[2]),
        pltpu.make_async_copy(
            w_value, weight.at[pl.ds(start(0), extent), pl.ds(q_width + k_width, k_width)], local_sem.at[3]
        ),
        pltpu.make_async_copy(w_output, output_at(0), local_sem.at[4]),
    ]
    for copy in locals_:
        copy.start()

    begun = []

    def begin(copy):
        copy.start()
        begun.append(copy)
        return copy

    pl.semaphore_wait(barrier, 3)
    locals_[0].wait()
    gain_in = [begin(remote("g2", gains_at(0), 2)), begin(remote("g4", gains_at(0), 4))]
    gain_core = [begin(remote("gc0", gains_at(0), 1))]
    for copy in locals_[1:4]:
        copy.wait()
    near, far = begin(remote("q2", qkv_at(0), 2)), begin(remote("q4", qkv_at(0), 4))
    core = [begin(remote("qc0", qkv_at(0), 1))]
    locals_[4].wait()
    out_near, out_far = begin(remote("o2", output_at(0), 2)), begin(remote("o4", output_at(0), 4))
    out_core = [begin(remote("oc0", output_at(0), 1))]

    gain_in[0].wait_recv()
    gain_in[1].wait_recv()
    diagonal = begin(remote("g6", gains_at(4), 2))
    gain_core += [begin(remote("gc2", gains_at(2), 1)), begin(remote("gc4", gains_at(4), 1))]
    diagonal.wait_recv()
    gain_core.append(begin(remote("gc6", gains_at(6), 1)))
    for copy in gain_core:
        copy.wait_recv()

    rows = tokens.shape[0]
    tile = 128

    def norm(i, carry):
        spot = pl.ds(pl.multiple_of(i * tile, tile), tile)
        values = tokens[spot, :].astype(F32)
        normed[spot, :] = (values * mean_square(values) * gains[0:1, :]).astype(BF16)
        return carry

    lax.fori_loop(0, rows // tile, norm, 0)

    far.wait_recv()
    cross = [begin(remote("q6a", qkv_at(4, 0), 2))]
    core.append(begin(remote("qc4", qkv_at(4), 1)))
    near.wait_recv()
    cross.append(begin(remote("q6b", qkv_at(2, 1), 4)))
    core.append(begin(remote("qc2", qkv_at(2), 1)))
    cross[0].wait_recv()
    cross[1].wait_recv()
    core.append(begin(remote("qc6", qkv_at(6), 1)))
    out_far.wait_recv()
    out_cross = [begin(remote("o6a", output_at(4, 0), 2))]
    out_core.append(begin(remote("oc4", output_at(4), 1)))
    out_near.wait_recv()
    out_cross.append(begin(remote("o6b", output_at(2, 1), 4)))
    out_core.append(begin(remote("oc2", output_at(2), 1)))
    for copy in core:
        copy.wait_recv()

    lane = lax.broadcasted_iota(jnp.int32, (1, LANES), 1)

    def rotated(part, spot):
        return part * cosine[spot, :] + turned(part, lane, 1.0) * sine[spot, :]

    def keys(i, carry):
        spot = pl.ds(pl.multiple_of(i * 256, 256), 256)
        part = jnp.dot(normed[spot, :], weight[:, q_width:], preferred_element_type=F32)
        kv[0, spot, :k_width] = rotated(part[:, :k_width], spot).astype(BF16)
        kv[0, spot, k_width:] = part[:, k_width:].astype(BF16)
        return carry

    lax.fori_loop(0, rows // 256, keys, 0)
    kv_near = begin(remote("k2", kv.at[0], 2, kv.at[2]))
    kv_core = begin(remote("k1", kv.at[0], 1, kv.at[1]))

    def query(i, carry):
        spot = pl.ds(pl.multiple_of(i * 256, 256), 256)
        part = jnp.dot(normed[spot, :], weight[:, :q_width], preferred_element_type=F32)
        for base in range(0, q_width, LANES):
            turned_part = rotated(part[:, base : base + LANES], spot).astype(BF16)
            queries[spot, base : base + LANES] = (turned_part * SCORE_SCALE).astype(BF16)
        return carry

    lax.fori_loop(0, rows // 256, query, 0)
    kv_near.wait_recv()
    kv_last = begin(remote("k3", kv.at[2], 1, kv.at[3]))
    out_cross[0].wait_recv()
    out_cross[1].wait_recv()
    out_core.append(begin(remote("oc6", output_at(6), 1)))
    for copy in out_core:
        copy.wait_recv()
    kv_core.wait_recv()
    kv_last.wait_recv()
    for copy in begun:
        copy.wait_send()


def front(tokens, gains, cosine, sine, w_query, w_key, w_value, w_output):
    rows, width = tokens.shape
    q_width, k_width = w_query.shape[1], w_key.shape[1]
    total = q_width + 2 * k_width
    vmem = pl.BlockSpec(memory_space=pltpu.VMEM)
    return pl.pallas_call(
        front_body,
        in_specs=[vmem] * 4 + [ANYWHERE] * 4,
        out_specs=[vmem] * 6,
        out_shape=[
            jax.ShapeDtypeStruct((rows, width), BF16),
            jax.ShapeDtypeStruct((rows, q_width), BF16),
            jax.ShapeDtypeStruct((4, rows, 2 * k_width), BF16),
            jax.ShapeDtypeStruct((width, total), BF16),
            jax.ShapeDtypeStruct((w_output.shape[0], width), BF16),
            jax.ShapeDtypeStruct((8, width), F32),
        ],
        scratch_shapes=[
            pltpu.SemaphoreType.DMA((5,)),
            pltpu.SemaphoreType.DMA((27,)),
            pltpu.SemaphoreType.DMA((27,)),
        ],
        compiler_params=pltpu.CompilerParams(collective_id=6, has_side_effects=True, vmem_limit_bytes=VMEM_BYTES),
        cost_estimate=pl.CostEstimate(
            flops=2 * rows * width * total, bytes_accessed=10 * rows * width, transcendentals=0
        ),
        name="front",
    )(tokens, gains, cosine, sine, w_query, w_key, w_value, w_output)


def unique_arrays(pairs):
    arrays, plan = [], []
    for left, right, low, high in pairs:
        spots = []
        for value in (left, right):
            known = [i for i, array in enumerate(arrays) if array is value]
            if not known:
                arrays.append(value)
            spots.append(known[0] if known else len(arrays) - 1)
        plan.append((spots[0], spots[1], low, high))
    return arrays, tuple(plan)


def grads_parts(count, plan, ins, outs, scratch):
    halves, jobs = count // 2, len(plan)
    sent, got, own = scratch[:jobs], scratch[jobs : 2 * jobs], scratch[2 * jobs : 3 * jobs]
    send, recv, done = scratch[3 * jobs :]
    me = plane_index()
    mate = {"context": lax.axis_index("context") ^ 1}

    def piece(j, r):
        left, right, low, high = plan[j]
        extent = ins[left].shape[1] // count
        columns = pl.ds(pl.multiple_of((me ^ r) * extent, extent), extent)
        return lax.dot_general(
            ins[left][:, columns], ins[right][:, low:high], (((0,), (0,)), ((), ())), preferred_element_type=F32
        )

    def across(j, i):
        return pltpu.make_async_remote_copy(
            src_ref=sent[j].at[i],
            dst_ref=got[j].at[i],
            send_sem=send.at[j, i],
            recv_sem=recv.at[j, i],
            device_id=mate,
            device_id_type=pl.DeviceIdType.MESH,
        )

    def odd(i):
        for j in range(jobs):
            sent[j][i] = piece(j, 2 * i + 1).astype(BF16)
            across(j, i).start()

    def even(i):
        for j in range(jobs):
            value = piece(j, 2 * i)
            across(j, i).wait_recv()
            value = value + got[j][i].astype(F32)

            @pl.when(i > 0)
            def _():
                got[j][i] = value.astype(BF16)

            @pl.when(i == 0)
            def _():
                own[j][...] = value

        for known in range(halves):

            @pl.when(i == known)
            def _():
                for j in range(jobs):
                    source = got[j].at[known] if known else own[j]
                    pltpu.make_async_copy(source, outs[known * jobs + j], done.at[known, j]).start()

    def work(q):
        @pl.when(q < halves)
        def _():
            odd(halves - 1 - q)

        @pl.when(q >= halves)
        def _():
            even(count - 1 - q)

    def finish():
        for known in range(halves):
            for j in range(jobs):
                source = got[j].at[known] if known else own[j]
                pltpu.make_async_copy(source, outs[known * jobs + j], done.at[known, j]).wait()
                across(j, known).wait_send()

    return work, finish


def grads_body(count, n_in, plan, *refs):
    ins, rest = refs[:n_in], refs[n_in:]
    spread = count // 2 * len(plan)
    outs, scratch = rest[:spread], rest[spread:]
    work, finish = grads_parts(count, plan, ins, outs, scratch)
    barrier = pltpu.get_barrier_semaphore()
    mate = {"context": lax.axis_index("context") ^ 1}
    pl.semaphore_signal(barrier, inc=1, device_id=mate, device_id_type=pl.DeviceIdType.MESH)
    pl.semaphore_wait(barrier, 1)

    def step(q, carry):
        work(q)
        return carry

    lax.fori_loop(0, count, step, 0)
    finish()


def grads_shapes(pairs):
    count = plane_size()
    halves = count // 2
    shapes = [(left.shape[1] // count, high - low) for left, right, low, high in pairs]
    outs = [jax.ShapeDtypeStruct(shape, BF16 if i else F32) for i in range(halves) for shape in shapes]
    scratch = [pltpu.VMEM((halves,) + shape, BF16) for shape in shapes] * 2
    scratch += [pltpu.VMEM(shape, F32) for shape in shapes]
    sems = [(len(pairs), halves), (len(pairs), halves), (halves, len(pairs))]
    return outs, scratch + [pltpu.SemaphoreType.DMA(shape) for shape in sems]


def grads_named(flat, jobs):
    return [{2 * i: flat[i * jobs + j] for i in range(len(flat) // jobs)} for j in range(jobs)]


def grads_fit(pairs):
    return all((pair[0].shape[1] // plane_size()) % LANES == 0 for pair in pairs)


def plane_grads(pairs, identity):
    count = plane_size()
    jobs = len(pairs)
    extents = [pair[0].shape[1] // count for pair in pairs]
    arrays, plan = unique_arrays(pairs)
    if not grads_fit(pairs):
        me = plane_index()
        sides = []
        for (left, right, low, high), e in zip(pairs, extents):
            columns = lambda r: lax.dynamic_slice_in_dim(left, (me ^ r) * e, e, 1)
            whole = {r: weight_grad(columns(r), right[:, low:high]).astype(BF16) for r in range(count)}
            sides.append({r: take_sum(whole, 1, r) for r in range(0, count, 2)})
        return sides
    outs, scratch = grads_shapes(pairs)
    flat = pl.pallas_call(
        functools.partial(grads_body, count, len(arrays), plan),
        in_specs=[pl.BlockSpec(memory_space=pltpu.VMEM)] * len(arrays),
        out_specs=[ANYWHERE] * len(outs),
        out_shape=outs,
        scratch_shapes=scratch,
        compiler_params=pltpu.CompilerParams(
            collective_id=identity, has_side_effects=True, vmem_limit_bytes=VMEM_BYTES
        ),
        cost_estimate=pl.CostEstimate(
            flops=sum(2 * left.shape[0] * left.shape[1] * (high - low) for left, _, low, high in pairs),
            bytes_accessed=sum(2 * left.shape[1] * (high - low) for left, _, low, high in pairs),
            transcendentals=0,
        ),
    )(*arrays)
    return grads_named(flat, jobs)


def after(value, *others):
    return lax.optimization_barrier((value,) + others)[0] if others else value


def gather_context(piece):
    size = lax.axis_size("context")
    held = {0: piece}
    bit = size // 2
    while bit:
        for r in list(held):
            held[r | bit] = swap(held[r], "context", size, bit)
        bit //= 2
    return [held[r] for r in range(size)]


def reduce_context(pieces):
    size = len(pieces)
    held = dict(enumerate(pieces))
    bit = 1
    while bit < size:
        held = {
            r: held[r].astype(F32) + swap(held[r | bit].astype(BF16), "context", size, bit).astype(F32)
            for r in held
            if not r & bit
        }
        bit *= 2
    return held[0]


def stored_places(order_row, first, count):
    stored = first + jnp.arange(count, dtype=jnp.int32)
    picks = (stored // BLK)[:, None] == jnp.arange(order_row.shape[0], dtype=jnp.int32)[None, :]
    return jnp.sum(jnp.where(picks, order_row[None, :], 0), axis=1) * BLK + stored % BLK


def rope_tables(order, local_len):
    first = lax.axis_index("context") * local_len
    places = jnp.concatenate([stored_places(order[s], first, local_len) for s in range(order.shape[0])])
    half = HD // 2
    inverse = jnp.exp(jnp.arange(half, dtype=F32) * (-2.0 * math.log(ROPE_BASE) / HD))
    angles = places.astype(F32)[:, None] * jnp.tile(inverse, LANES // half)[None, :]
    return jnp.cos(angles), jnp.sin(angles)


def weight_grad(left, right):
    return lax.dot_general(left, right, (((0,), (0,)), ((), ())), preferred_element_type=F32)


def local(
    tokens, block_order, w_query, w_key, w_value, w_output, w_gate, w_up, w_down, norm_attn, norm_ffn, grad_out
):
    seqs, local_len, width = tokens.shape
    rows = seqs * local_len
    size = plane_size()
    z = lax.axis_index("tensor")
    token_rows = tokens.reshape(rows, width)
    grad_rows = grad_out.reshape(rows, width)
    q_width, kv_width = w_query.shape[1], w_key.shape[1]
    units = w_down.shape[0]
    half = units // 2

    cosine, sine = rope_tables(block_order, local_len)
    if front_fits():
        gain_piece = jnp.pad(jnp.stack([norm_attn, norm_ffn]).astype(F32), ((0, 6), (0, 0)))
        normed, queries, kv_pieces, w_qkv, w_out, gains = front(
            token_rows, gain_piece, cosine, sine, w_query, w_key, w_value, w_output
        )
        qkv_pieces, output_pieces = [w_qkv], [w_out]
        early, late = [queries], [queries]
        gain_attn, gain_ffn = gains[0:1], gains[1:2]
    else:
        gains = gather_small(jnp.stack([norm_attn, norm_ffn])).reshape(2, width)
        gain_attn, gain_ffn = gains[0:1], gains[1:2]
        w_qkv = jnp.concatenate([w_query, w_key, w_value], axis=1)
        qkv_pieces, output_pieces = gather_pair(w_qkv, w_output)
        normed, queries, keys_values = project_qkv(token_rows, gain_attn, cosine, sine, qkv_pieces, q_width)
        kv_pieces = jnp.stack(gather_context(keys_values))
        early, late = [qkv_pieces[-2]], [kv_pieces]
        output_pieces = widened(output_pieces)
    mixture, logs = attend(block_order, queries, kv_pieces)
    branch = gathered_matmul(mixture, output_pieces, 1, False)
    normed_ffn, hidden = line_sum(branch, [token_rows, gain_ffn], finish_attention, True, False, 0)
    extent = width // size
    pushed = extent % (2 * LANES) == 0
    order = (early, late, [mixture], [normed_ffn], not pushed)
    gate_pieces, up_pieces = gather_pair(w_gate, w_up, *order)
    order = (early, late, [normed_ffn], [normed_ffn], not pushed)
    if pushed:
        low_pieces, high_pieces = gather_pair(w_down[:, : extent // 2], w_down[:, extent // 2 :], *order)
    else:
        low_pieces, high_pieces = gather_pair(w_down[:half], w_down[half:], *order)
        low_pieces, high_pieces = widened(low_pieces), widened(high_pieces)
    d_ffn = (RESIDUAL_SCALE * grad_rows.astype(F32)).astype(BF16)
    active, d_gate, d_up, ffn_out, d_normed_ffn = ffn(
        normed_ffn, d_ffn, gate_pieces, up_pieces, low_pieces, high_pieces, pushed
    )
    pairs = [
        (normed_ffn, d_gate, 0, units),
        (normed_ffn, d_up, 0, units),
        (d_ffn, active, 0, half),
        (d_ffn, active, half, units),
    ]
    sum_ins = [hidden, grad_rows, gain_ffn]
    if grads_fit(pairs):
        d_branch, d_hidden, ffn_gain, out_parts, *flat = line_sum(
            d_normed_ffn, sum_ins, finish_ffn_back, True, True, 1, ffn_out, pairs
        )
        grad_gate, grad_up, grad_low, grad_high = grads_named(flat, len(pairs))
        out_chunks = [out_parts[shift] for shift in range(4)]
    else:
        grad_gate, grad_up, grad_low, grad_high = plane_grads(pairs, 3)
        d_branch, d_hidden, ffn_gain = line_sum(
            after(d_normed_ffn, grad_gate[0]), sum_ins, finish_ffn_back, True, True, 1
        )
        padded = lax.dynamic_update_slice_in_dim(jnp.zeros((rows, width), F32), hidden, (z // 2) * (rows // 2), 0)
        out_part = RESIDUAL_SCALE * ffn_out.astype(F32) + jnp.where(lax.rem(z, 3) != 0, padded, 0.0)
        out_chunks = [chunk_of(out_part.astype(BF16), lax.rem(z + shift, 4), rows // 4) for shift in range(4)]
    layer_out = rows_gather(rows_sum(out_chunks).astype(BF16))

    d_mixture = gathered_matmul(d_branch, output_pieces, 1, True)
    d_queries, *d_pieces = attend_back(block_order, queries, d_mixture, logs, kv_pieces)
    d_keys_values = reduce_context(d_pieces)
    grad_gate, grad_up = reduce_pair(grad_gate, grad_up, [d_keys_values])
    grad_low, grad_high = reduce_pair(grad_low, grad_high, [d_keys_values])
    d_qkv, d_normed = project_qkv_back(d_queries, d_keys_values, cosine, sine, qkv_pieces)
    grad_qkv, grad_output = plane_grads([(normed, d_qkv, 0, d_qkv.shape[1]), (d_branch, mixture, 0, q_width)], 4)
    d_normed = after(d_normed, grad_qkv[0])
    grad_tokens, attn_gain = line_sum(
        d_normed, [token_rows, d_hidden, gain_attn], finish_attention_back, False, True, 2
    )
    grad_tokens = grad_tokens.astype(F32)
    grad_qkv, grad_output = reduce_pair(grad_qkv, grad_output)
    attn_gain, ffn_gain = jnp.sum(attn_gain, axis=0), jnp.sum(ffn_gain, axis=0)
    gain_grads = jnp.stack([attn_gain, ffn_gain])
    gain_grads = gains_sum(gain_grads)
    return (
        layer_out.reshape(seqs, local_len, width),
        grad_tokens.reshape(seqs, local_len, width),
        grad_qkv[:, :q_width],
        grad_qkv[:, q_width : q_width + kv_width],
        grad_qkv[:, q_width + kv_width :],
        grad_output.T,
        grad_gate,
        grad_up,
        jnp.concatenate([grad_low.T, grad_high.T], axis=0),
        gain_grads[0],
        gain_grads[1],
    )


def solution(mesh):
    split = P("shard", "context", None)
    inward, outward = P(PLANE, "tensor"), P("tensor", PLANE)
    gain = P(PLANE)
    return jax.shard_map(
        local,
        mesh=mesh,
        in_specs=(split, P("shard", None), inward, inward, inward, outward, inward, inward, outward, gain, gain, split),
        out_specs=(split, split, inward, inward, inward, outward, inward, inward, outward, gain, gain),
        check_vma=False,
    )
```

```python
import functools
import math

import jax
import jax.numpy as jnp
from jax import lax
from jax.experimental import pallas as pl
from jax.experimental.pallas import tpu as pltpu
from jax.sharding import PartitionSpec as P


HD = 64
BLK = 256
LANES = 128
EPSILON = 1e-05
SCORE_SCALE = 0.015625
RESIDUAL_SCALE = 0.22
ROPE_BASE = 10000000.0
MASKED_SCORE = -1e30
PLANE = ("shard", "context")
VMEM_BYTES = 64000 * 1024


F32 = jnp.float32
BF16 = jnp.bfloat16


def plane_size():
    return lax.axis_size("shard") * lax.axis_size("context")


def plane_index():
    return lax.axis_index("shard") * lax.axis_size("context") + lax.axis_index("context")


def swap(value, axes, size, bit):
    return lax.ppermute(value, axes, [(i, i ^ bit) for i in range(size)])


def gather_pair(first, second, far_after=(), near_after=(), cross_after=(), core_after=(), core=True):
    size = plane_size()
    bits = [1 << b for b in range(1, size.bit_length() - 1)]
    sides = [{0: first}, {0: second}]
    if len(bits) == 2:
        near, far = bits
        for side in sides:
            side[far] = swap(after(side[0], *far_after), PLANE, size, far)
        for side in reversed(sides):
            side[near] = swap(after(side[0], *near_after), PLANE, size, near)
        sides[0][near | far] = swap(after(sides[0][far], *cross_after), PLANE, size, near)
        sides[1][near | far] = swap(after(sides[1][near], *cross_after), PLANE, size, far)
    else:
        for side in sides:
            for bit in bits:
                for r in list(side):
                    side[r | bit] = swap(side[r], PLANE, size, bit)
    if not core:
        return [[side[r] for r in range(0, size, 2)] for side in sides]
    for side in sides:
        for r in list(side):
            side[r | 1] = swap(after(side[r], *core_after), PLANE, size, 1)
    return [[side[r] for r in range(size)] for side in sides]


def widened(pieces):
    level = 1
    while pieces[0].shape[1] < LANES:
        upper = (plane_index() // level) % 2 == 1
        pairs = zip(pieces[0::2], pieces[1::2])
        pieces = [jnp.where(upper, jnp.concatenate([b, a], 1), jnp.concatenate([a, b], 1)) for a, b in pairs]
        level *= 2
    return pieces


def take_sum(side, bit, kept):
    sent = side[kept | bit].astype(BF16)
    total = side[kept].astype(F32) + swap(sent, PLANE, plane_size(), bit).astype(F32)
    return total if kept == 0 else total.astype(BF16)


def reduce_pair(first, second, last_after=()):
    size = plane_size()
    bits = [1 << b for b in range(1, size.bit_length() - 1)]
    sides = [dict(first), dict(second)]
    if len(bits) == 2:
        near, far = bits
        sides[0][near] = take_sum(sides[0], far, near)
        sides[1][far] = take_sum(sides[1], near, far)
        done = []
        for side in sides:
            sent = [after(side[bit].astype(BF16), *last_after) for bit in bits]
            a = swap(sent[0], PLANE, size, near).astype(F32)
            b = swap(sent[1], PLANE, size, far).astype(F32)
            done.append(side[0] + a + b)
        return done
    done = []
    for side in sides:
        for bit in reversed(bits):
            side = {r: take_sum(side, bit, r) for r in side if not r & bit}
        done.append(side[0])
    return done


def gather_small(values):
    size = plane_size()
    stacked = values[None]
    bit = 1
    while bit < size:
        stacked = jnp.concatenate([stacked, swap(stacked, PLANE, size, bit)], axis=0)
        bit *= 2
    picks = jnp.arange(size, dtype=jnp.int32)[:, None] ^ plane_index()
    chosen = (picks == jnp.arange(size, dtype=jnp.int32)[None, :]).astype(F32)
    return jnp.einsum("ij,jkw->kiw", chosen, stacked.astype(F32), precision=lax.Precision.HIGHEST)


def chunk_of(rows, index, count):
    return lax.dynamic_slice_in_dim(rows, index * count, count, 0)


def rows_sum(chunks):
    size = lax.axis_size("tensor")
    total = chunks[0].astype(F32)
    for shift in range(1, size):
        pairs = [(i, (i + shift) % size) for i in range(size)]
        total = total + lax.ppermute(chunks[shift], "tensor", pairs).astype(F32)
    return total


def rows_gather(chunk):
    size = lax.axis_size("tensor")
    count = chunk.shape[0]
    parts = [chunk]
    for shift in range(1, size):
        pairs = [(i, (i + shift) % size) for i in range(size)]
        parts.append(lax.ppermute(chunk, "tensor", pairs))
    return pl.pallas_call(
        assemble_body,
        in_specs=[ANYWHERE] * size,
        out_specs=pl.BlockSpec(memory_space=pltpu.VMEM),
        out_shape=jax.ShapeDtypeStruct((size * count,) + chunk.shape[1:], chunk.dtype),
        scratch_shapes=[pltpu.SemaphoreType.DMA],
        compiler_params=pltpu.CompilerParams(vmem_limit_bytes=8 << 20),
        cost_estimate=pl.CostEstimate(flops=0, bytes_accessed=4 * size * chunk.size, transcendentals=0),
        name="assemble",
    )(*parts)


def assemble_body(*refs):
    parts, whole, sem = refs[:-2], refs[-2], refs[-1]
    count = parts[0].shape[0]
    me = lax.axis_index("tensor")
    for shift, part in enumerate(parts):
        place = pl.multiple_of(lax.rem(me - shift + len(parts), len(parts)) * count, count)
        pltpu.make_async_copy(part, whole.at[pl.ds(place, count)], sem).start()
    pltpu.make_async_copy(whole, whole, sem).wait()


def gains_sum(values):
    size, tensor, me = plane_size(), lax.axis_size("tensor"), plane_index()
    extent = values.shape[1] // size
    total = values
    for shift in range(1, tensor):
        total = total + lax.ppermute(values, "tensor", [(i, (i + shift) % tensor) for i in range(tensor)])
    own = 0.0
    for r in range(size):
        sent = lax.dynamic_slice_in_dim(total, (me ^ r) * extent, extent, 1)
        own = own + (swap(sent, PLANE, size, r) if r else sent)
    return own


def params(steps):
    return pltpu.CompilerParams(
        dimension_semantics=("arbitrary",) * steps, vmem_limit_bytes=VMEM_BYTES
    )


def place_pieces(pieces, whole, sem, axis):
    size = len(pieces)
    me = plane_index() // (plane_size() // size)
    extent = whole.shape[axis] // size
    for r, piece in enumerate(pieces):
        start = pl.multiple_of((me ^ r) * extent, extent)
        target = whole.at[pl.ds(start, extent)] if axis == 0 else whole.at[:, pl.ds(start, extent)]
        pltpu.make_async_copy(piece, target, sem).start()


def await_whole(whole, sem):
    pltpu.make_async_copy(whole, whole, sem).wait()


ANYWHERE = pl.BlockSpec(memory_space=pl.ANY)


def turned(values, lane, sign):
    half = HD // 2
    upper = pltpu.roll(values, LANES - half, 1)
    lower = pltpu.roll(values, half, 1)
    return jnp.where(lane % HD < half, -sign * upper, sign * lower)


def qkv_body(count, tokens, gain, cosine, sine, *rest):
    pieces, (normed, queries, keys_values, weight, sem) = rest[:count], rest[count:]

    @pl.when(pl.program_id(0) == 0)
    def _():
        place_pieces(pieces, weight, sem, 0)

    values = tokens[...].astype(F32)
    inverse = lax.rsqrt(jnp.mean(values * values, axis=1, keepdims=True) + EPSILON)
    low = (values * inverse * gain[...]).astype(BF16)
    normed[...] = low

    @pl.when(pl.program_id(0) == 0)
    def _():
        await_whole(weight, sem)

    cos, sin = cosine[...], sine[...]
    lane = lax.broadcasted_iota(jnp.int32, cos.shape, 1)
    q_width = queries.shape[1]
    k_width = keys_values.shape[1] // 2
    for start in range(0, weight.shape[1], LANES):
        part = jnp.dot(low, weight[:, start : start + LANES * 1], preferred_element_type=F32)
        if start < q_width + k_width:
            part = part * cos + turned(part, lane, 1.0) * sin
        if start < q_width:
            queries[:, start : start + LANES] = (part.astype(BF16) * SCORE_SCALE).astype(BF16)
        else:
            keys_values[:, start - q_width : start - q_width + LANES] = part.astype(BF16)


def project_qkv(tokens, gain, cosine, sine, pieces, q_width):
    rows, width = tokens.shape
    total = pieces[0].shape[1]
    tile = min(rows, 256)
    row_spec = lambda w: pl.BlockSpec((tile, w), lambda i: (i, 0))
    return pl.pallas_call(
        functools.partial(qkv_body, len(pieces)),
        grid=(rows // tile,),
        in_specs=[row_spec(width), pl.BlockSpec((1, width), lambda i: (0, 0)), row_spec(LANES), row_spec(LANES)]
        + [ANYWHERE] * len(pieces),
        out_specs=[row_spec(width), row_spec(q_width), row_spec(total - q_width)],
        out_shape=[
            jax.ShapeDtypeStruct((rows, width), BF16),
            jax.ShapeDtypeStruct((rows, q_width), BF16),
            jax.ShapeDtypeStruct((rows, total - q_width), BF16),
        ],
        scratch_shapes=[pltpu.VMEM((width, total), BF16), pltpu.SemaphoreType.DMA],
        compiler_params=params(1),
        cost_estimate=pl.CostEstimate(
            flops=2 * rows * width * total, bytes_accessed=2 * (2 * rows * width + width * total), transcendentals=0
        ),
        name="project_qkv",
    )(tokens, gain, cosine, sine, *pieces)


def qkv_back_body(count, d_queries, d_keys_values, cosine, sine, *rest):
    pieces, (d_all, d_normed, weight, sem) = rest[:count], rest[count:]

    @pl.when(pl.program_id(0) == 0)
    def _():
        place_pieces(pieces, weight, sem, 0)

    cos, sin = cosine[...], sine[...]
    lane = lax.broadcasted_iota(jnp.int32, cos.shape, 1)
    q_width = d_queries.shape[1]
    k_width = d_keys_values.shape[1] // 2
    for start in range(0, d_all.shape[1], LANES):
        if start < q_width:
            part = d_queries[:, start : start + LANES]
        else:
            part = d_keys_values[:, start - q_width : start - q_width + LANES]
        if start < q_width + k_width:
            part = part * cos + turned(part * sin, lane, -1.0)
        d_all[:, start : start + LANES] = part.astype(BF16)

    @pl.when(pl.program_id(0) == 0)
    def _():
        await_whole(weight, sem)

    step = 512
    for start in range(0, weight.shape[0], step):
        d_normed[:, start : start + step] = lax.dot_general(
            d_all[...], weight[start : start + step, :], (((1,), (1,)), ((), ())), preferred_element_type=F32
        ).astype(BF16)


def project_qkv_back(d_queries, d_keys_values, cosine, sine, pieces):
    rows, q_width = d_queries.shape
    total = pieces[0].shape[1]
    width = pieces[0].shape[0] * len(pieces)
    tile = min(rows, 256)
    row_spec = lambda w: pl.BlockSpec((tile, w), lambda i: (i, 0))
    return pl.pallas_call(
        functools.partial(qkv_back_body, len(pieces)),
        grid=(rows // tile,),
        in_specs=[row_spec(q_width), row_spec(total - q_width), row_spec(LANES), row_spec(LANES)]
        + [ANYWHERE] * len(pieces),
        out_specs=[row_spec(total), row_spec(width)],
        out_shape=[jax.ShapeDtypeStruct((rows, total), BF16), jax.ShapeDtypeStruct((rows, width), BF16)],
        scratch_shapes=[pltpu.VMEM((width, total), BF16), pltpu.SemaphoreType.DMA],
        compiler_params=params(1),
        cost_estimate=pl.CostEstimate(
            flops=2 * rows * width * total, bytes_accessed=2 * (2 * rows * width + width * total), transcendentals=0
        ),
        name="project_qkv_back",
    )(d_queries, d_keys_values, cosine, sine, *pieces)


def gathered_body(count, axis, transposed, left, *rest):
    pieces, (out, weight, sem) = rest[:count], rest[count:]

    @pl.when(pl.program_id(0) == 0)
    def _():
        place_pieces(pieces, weight, sem, axis)
        await_whole(weight, sem)

    step = min(out.shape[1], 512)
    for start in range(0, out.shape[1], step):
        if transposed:
            part = lax.dot_general(
                left[...], weight[start : start + step, :], (((1,), (1,)), ((), ())), preferred_element_type=F32
            )
        else:
            part = jnp.dot(left[...], weight[:, start : start + step], preferred_element_type=F32)
        out[:, start : start + step] = part.astype(out.dtype)


def gathered_matmul(left, pieces, axis, transposed):
    rows = left.shape[0]
    shape = list(pieces[0].shape)
    shape[axis] *= len(pieces)
    outer = shape[0] if transposed else shape[1]
    tile = min(rows, 256)
    return pl.pallas_call(
        functools.partial(gathered_body, len(pieces), axis, transposed),
        grid=(rows // tile,),
        in_specs=[pl.BlockSpec((tile, left.shape[1]), lambda i: (i, 0))] + [ANYWHERE] * len(pieces),
        out_specs=pl.BlockSpec((tile, outer), lambda i: (i, 0)),
        out_shape=jax.ShapeDtypeStruct((rows, outer), BF16),
        scratch_shapes=[pltpu.VMEM(tuple(shape), BF16), pltpu.SemaphoreType.DMA],
        compiler_params=params(1),
        cost_estimate=pl.CostEstimate(
            flops=2 * rows * shape[0] * shape[1],
            bytes_accessed=2 * (rows * sum(shape) + shape[0] * shape[1]),
            transcendentals=0,
        ),
    )(left, *pieces)


def ffn_tile(f_step, tile, normed, d_ffn, gate, up, down, active, d_gate, d_up, out, d_normed, out_sum, d_sum):
    units = pl.ds(pl.multiple_of(f_step * tile, tile), tile)
    gate_tile, up_tile, down_tile = gate[:, units], up[:, units], down[units, :]
    gate_in = jnp.dot(normed[...], gate_tile, preferred_element_type=F32)
    upward = jnp.dot(normed[...], up_tile, preferred_element_type=F32)
    d_active = lax.dot_general(d_ffn[...], down_tile, (((1,), (1,)), ((), ())), preferred_element_type=F32)
    sigma = 1.0 / (1.0 + jnp.exp(-gate_in))
    silu = gate_in * sigma
    active_low = (silu * upward).astype(BF16)
    gate_low = (d_active * upward * (sigma * (1.0 + gate_in * (1.0 - sigma)))).astype(BF16)
    up_low = (d_active * silu).astype(BF16)
    active[...] = active_low
    d_gate[...] = gate_low
    d_up[...] = up_low
    part = jnp.dot(active_low, down_tile, preferred_element_type=F32)
    d_part = lax.dot_general(gate_low, gate_tile, (((1,), (1,)), ((), ())), preferred_element_type=F32)
    d_part += lax.dot_general(up_low, up_tile, (((1,), (1,)), ((), ())), preferred_element_type=F32)

    @pl.when(f_step == 0)
    def _():
        out_sum[...] = part
        d_sum[...] = d_part

    @pl.when(f_step > 0)
    def _():
        out_sum[...] += part
        d_sum[...] += d_part

    @pl.when(f_step == pl.num_programs(1) - 1)
    def _():
        out[...] = out_sum[...].astype(BF16)
        d_normed[...] = d_sum[...].astype(BF16)


def ffn_body(count, narrow, tile, normed, d_ffn, *rest):
    gate_pieces, up_pieces, rest = rest[:count], rest[count : 2 * count], rest[2 * count :]
    low_pieces, high_pieces, rest = rest[:narrow], rest[narrow : 2 * narrow], rest[2 * narrow :]
    active, d_gate, d_up, out, d_normed, gate, up, down, out_sum, d_sum, sems = rest
    f_step = pl.program_id(1)
    half = down.shape[0] // 2

    @pl.when((pl.program_id(0) == 0) & (f_step == 0))
    def _():
        place_pieces(gate_pieces, gate, sems.at[0], 0)
        place_pieces(up_pieces, up, sems.at[1], 0)
        place_pieces(low_pieces, down.at[pl.ds(0, half)], sems.at[2], 1)
        place_pieces(high_pieces, down.at[pl.ds(half, half)], sems.at[3], 1)
        await_whole(gate, sems.at[0])
        await_whole(up, sems.at[1])
        await_whole(down.at[pl.ds(0, half)], sems.at[2])
        await_whole(down.at[pl.ds(half, half)], sems.at[3])

    ffn_tile(f_step, tile, normed, d_ffn, gate, up, down, active, d_gate, d_up, out, d_normed, out_sum, d_sum)


def ffn(normed, d_ffn, gate_pieces, up_pieces, low_pieces, high_pieces, pushed):
    rows, width = normed.shape
    units = gate_pieces[0].shape[1]
    count = len(gate_pieces)
    tile = 256
    row_tile = min(rows, 512)
    once = pl.Buffered(1)
    row_spec = pl.BlockSpec((row_tile, width), lambda i, f: (i, 0), pipeline_mode=once)
    unit_spec = pl.BlockSpec((row_tile, tile), lambda i, f: (i, f))
    unit_shape = jax.ShapeDtypeStruct((rows, units), BF16)
    row_shape = jax.ShapeDtypeStruct((rows, width), BF16)
    body = functools.partial(ffn_body, count, len(low_pieces), tile)
    settings, sems = params(2), [pltpu.SemaphoreType.DMA((4,))]
    if pushed:
        body = functools.partial(pushed_body, count, tile)
        sems = [pltpu.SemaphoreType.DMA((3, units // tile))] * 3
        settings = pltpu.CompilerParams(
            dimension_semantics=("arbitrary",) * 2,
            vmem_limit_bytes=VMEM_BYTES,
            collective_id=5,
            has_side_effects=True,
        )
    return pl.pallas_call(
        body,
        grid=(rows // row_tile, units // tile),
        in_specs=[row_spec, row_spec] + [ANYWHERE] * (2 * count + 2 * len(low_pieces)),
        out_specs=[unit_spec, unit_spec, unit_spec, row_spec, row_spec],
        out_shape=[unit_shape, unit_shape, unit_shape, row_shape, row_shape],
        scratch_shapes=[
            pltpu.VMEM((width, units), BF16),
            pltpu.VMEM((width, units), BF16),
            pltpu.VMEM((units, width), BF16),
            pltpu.VMEM((row_tile, width), F32),
            pltpu.VMEM((row_tile, width), F32),
        ]
        + sems,
        compiler_params=settings,
        cost_estimate=pl.CostEstimate(
            flops=12 * rows * width * units, bytes_accessed=6 * width * units + 14 * rows * width, transcendentals=rows * units
        ),
        name="feed_forward",
    )(normed, d_ffn, *gate_pieces, *up_pieces, *low_pieces, *high_pieces)


def pushed_body(count, tile, normed, d_ffn, *refs):
    groups, rest = [refs[k * count : (k + 1) * count] for k in range(4)], refs[4 * count :]
    active, d_gate, d_up, out, d_normed, gate, up, down, out_sum, d_sum, near, send, recv = rest
    f_step = pl.program_id(1)
    first = (pl.program_id(0) == 0) & (f_step == 0)
    last = (pl.program_id(0) == pl.num_programs(0) - 1) & (f_step == pl.num_programs(1) - 1)
    steps = down.shape[0] // tile
    width = down.shape[1]
    extent = width // (2 * count)
    me = plane_index()
    mate = {"context": lax.axis_index("context") ^ 1}
    mesh_ids = pl.DeviceIdType.MESH

    def push(source, target, w, t):
        return pltpu.make_async_remote_copy(
            src_ref=source,
            dst_ref=target,
            send_sem=send.at[w, t],
            recv_sem=recv.at[w, t],
            device_id=mate,
            device_id_type=mesh_ids,
        )

    def halves(t):
        units = pl.ds(pl.multiple_of(t * tile, tile), tile)
        half = pl.ds(0, width // 2)
        return [gate.at[half, units], up.at[half, units], down.at[units, half]]

    @pl.when(first)
    def _():
        barrier = pltpu.get_barrier_semaphore()
        pl.semaphore_signal(barrier, inc=1, device_id=mate, device_id_type=mesh_ids)
        pl.semaphore_wait(barrier, 1)

        def start(t, carry):
            units = pl.ds(pl.multiple_of(t * tile, tile), tile)
            for i in range(count):
                base = pl.multiple_of((me ^ (2 * i)) * extent, extent)
                rows = pl.ds(base, extent)
                left = pl.ds(base, extent // 2)
                right = pl.ds(pl.multiple_of(base + extent // 2, extent // 2), extent // 2)
                moves = (
                    (0, groups[0][i].at[:, units], gate.at[rows, units]),
                    (1, groups[1][i].at[:, units], up.at[rows, units]),
                    (2, groups[2][i].at[units, :], down.at[units, left]),
                    (2, groups[3][i].at[units, :], down.at[units, right]),
                )
                for w, source, target in moves:
                    push(source, target, w, t).start()
                    pltpu.make_async_copy(source, target, near.at[w, t]).start()
            return carry

        lax.fori_loop(0, steps, start, 0)

    @pl.when(pl.program_id(0) == 0)
    def _():
        for w, half in enumerate(halves(f_step)):
            pltpu.make_async_copy(half, half, near.at[w, f_step]).wait()
            push(half, half, w, f_step).wait_recv()

    ffn_tile(f_step, tile, normed, d_ffn, gate, up, down, active, d_gate, d_up, out, d_normed, out_sum, d_sum)

    @pl.when(last)
    def _():
        def drain(t, carry):
            for w, half in enumerate(halves(t)):
                push(half, half, w, t).wait_send()
            return carry

        lax.fori_loop(0, steps, drain, 0)


def doubled(values, lane, head):
    rolled = pltpu.roll(values.astype(F32), HD, 1).astype(BF16)
    return jnp.where((lane < HD) == (head == 0), values, rolled)


def block_bias(order, seq, r, block):
    per = order.shape[1] // lax.axis_size("context")
    own = order[seq, lax.axis_index("context") * per + pl.program_id(3)]
    other = order[seq, (lax.axis_index("context") ^ r) * per + block]
    return jnp.where(other <= own, 0.0, MASKED_SCORE).astype(F32)


def masked_scores(order, pieces_k, query):
    seq = pl.program_id(0)
    scores = []
    for r, key_rows in enumerate(pieces_k):
        part = lax.dot_general(key_rows, query, (((1,), (1,)), ((), ())), preferred_element_type=F32)
        for block in range(key_rows.shape[0] // BLK):
            bias = block_bias(order, seq, r, block)
            scores.append(part[block * BLK : (block + 1) * BLK] + bias)
    return scores


def attend_body(count, order, query_ref, *rest):
    pieces, (mixture, logs) = rest[:count], rest[count:]
    head = pl.program_id(1)
    lane = lax.broadcasted_iota(jnp.int32, (1, LANES), 1)
    keys = [doubled(piece[:, :LANES], lane, head) for piece in pieces]
    values = [doubled(piece[:, LANES:], lane, head) for piece in pieces]
    query = query_ref[...]
    parts = []
    for side in range(2):
        chosen = (lane < HD) if side == 0 else (lane >= HD)
        scores = masked_scores(order, keys, jnp.where(chosen, query, jnp.zeros_like(query)))
        top = functools.reduce(jnp.maximum, [jnp.max(s, axis=0, keepdims=True) for s in scores])
        powers = [jnp.exp(s - top) for s in scores]
        total = sum(jnp.sum(p, axis=0, keepdims=True) for p in powers)
        low = jnp.concatenate([p.astype(BF16) for p in powers], axis=0)
        whole = jnp.concatenate(values, axis=0)
        mixed = lax.dot_general(whole, low, (((0,), (0,)), ((), ())), preferred_element_type=F32)
        parts.append(mixed / total)
        logs[side : side + 1, :] = top + jnp.log(total)
    row = lax.broadcasted_iota(jnp.int32, (LANES, 1), 0)
    mixture[...] = jnp.where(row < HD, parts[0], parts[1]).T.astype(BF16)


def attend_specs(order, queries, pieces, group_pairs):
    seqs = order.shape[0]
    rows = queries.shape[0] // seqs
    tiles = rows // BLK
    grid = (seqs, 2, group_pairs, tiles)
    q_spec = pl.BlockSpec((BLK, LANES), lambda s, h, g, t: (s * tiles + t, h * group_pairs + g))
    kv_spec = pl.BlockSpec((rows, 2 * LANES), lambda s, h, g, t: (s, 0))
    kv_ins = [pl.BlockSpec((None, rows, 2 * LANES), lambda s, h, g, t, r=r: (r, s, 0)) for r in range(pieces.shape[0])]
    log_spec = pl.BlockSpec((None, 2, BLK), lambda s, h, g, t: (h * group_pairs + g, 0, s * tiles + t))
    return grid, q_spec, kv_spec, kv_ins, log_spec


def attend(order, queries, pieces):
    rows, q_width = queries.shape
    pairs = q_width // LANES
    grid, q_spec, _, kv_ins, log_spec = attend_specs(order, queries, pieces, pairs // 2)
    keys = rows * pieces.shape[0] // order.shape[0]
    return pl.pallas_call(
        functools.partial(attend_body, pieces.shape[0]),
        grid=grid,
        in_specs=[pl.BlockSpec(memory_space=pltpu.SMEM), q_spec] + kv_ins,
        out_specs=[q_spec, log_spec],
        out_shape=[jax.ShapeDtypeStruct((rows, q_width), BF16), jax.ShapeDtypeStruct((pairs, 2, rows), F32)],
        compiler_params=params(4),
        cost_estimate=pl.CostEstimate(
            flops=8 * rows * keys * q_width * 2, bytes_accessed=8 * rows * q_width, transcendentals=rows * keys * q_width // HD
        ),
        name="attend",
    )(order, queries, *[pieces] * pieces.shape[0])


def attend_back_body(count, order, query_ref, grad_ref, logs, *rest):
    pieces, rest = rest[:count], rest[count:]
    d_query, outs, (d_key_sum, d_value_sum) = rest[0], rest[1 : 1 + count], rest[1 + count :]
    head, pair, tile = pl.program_id(1), pl.program_id(2), pl.program_id(3)
    lane = lax.broadcasted_iota(jnp.int32, (1, LANES), 1)
    keys = [doubled(piece[:, :LANES], lane, head) for piece in pieces]
    values = jnp.concatenate([doubled(piece[:, LANES:], lane, head) for piece in pieces], axis=0)
    whole_keys = jnp.concatenate(keys, axis=0)
    parts, d_keys, d_values = [], 0.0, 0.0
    for side in range(2):
        chosen = (lane < HD) if side == 0 else (lane >= HD)
        query = jnp.where(chosen, query_ref[...], jnp.zeros_like(query_ref[...]))
        grad = jnp.where(chosen, grad_ref[...], jnp.zeros_like(grad_ref[...]))
        scores = jnp.concatenate(masked_scores(order, keys, query), axis=0)
        soft = jnp.exp(scores - logs[side : side + 1, :])
        d_soft = lax.dot_general(values, grad, (((1,), (1,)), ((), ())), preferred_element_type=F32)
        inner = jnp.sum(soft * d_soft, axis=0, keepdims=True)
        d_scores = (soft * (d_soft - inner)).astype(BF16)
        d_values += jnp.dot(soft.astype(BF16), grad, preferred_element_type=F32)
        d_keys += jnp.dot(d_scores, query, preferred_element_type=F32)
        parts.append(lax.dot_general(whole_keys, d_scores, (((0,), (0,)), ((), ())), preferred_element_type=F32))
    row = lax.broadcasted_iota(jnp.int32, (LANES, 1), 0)
    d_query[...] = jnp.where(row < HD, parts[0], parts[1]).T * SCORE_SCALE

    first = (pair == 0) & (tile == 0)
    last = (pair == pl.num_programs(2) - 1) & (tile == pl.num_programs(3) - 1)

    @pl.when(first)
    def _():
        d_key_sum[...] = d_keys
        d_value_sum[...] = d_values

    @pl.when(jnp.logical_not(first))
    def _():
        d_key_sum[...] += d_keys
        d_value_sum[...] += d_values

    @pl.when(last)
    def _():
        wanted = (lane < HD) == (head == 0)
        rows = outs[0].shape[0]
        for r, out in enumerate(outs):
            for base, total in ((0, d_key_sum), (LANES, d_value_sum)):
                part = total[r * rows : (r + 1) * rows, :]
                both = (part + pltpu.roll(part, HD, 1)).astype(out.dtype)
                spot = pl.ds(base, LANES)

                @pl.when(head == 0)
                def _():
                    out[:, spot] = both

                @pl.when(head == 1)
                def _():
                    out[:, spot] = jnp.where(wanted, both.astype(F32), out[:, spot].astype(F32)).astype(out.dtype)


def attend_back(order, queries, grads, logs, pieces):
    rows, q_width = queries.shape
    pairs = q_width // LANES
    grid, q_spec, kv_spec, kv_ins, log_spec = attend_specs(order, queries, pieces, pairs // 2)
    keys = rows * pieces.shape[0] // order.shape[0]
    return pl.pallas_call(
        functools.partial(attend_back_body, pieces.shape[0]),
        grid=grid,
        in_specs=[pl.BlockSpec(memory_space=pltpu.SMEM), q_spec, q_spec, log_spec] + kv_ins,
        out_specs=[q_spec] + [kv_spec] * pieces.shape[0],
        out_shape=[jax.ShapeDtypeStruct((rows, q_width), F32)]
        + [jax.ShapeDtypeStruct((rows, 2 * LANES), F32 if r % 2 == 0 else BF16) for r in range(pieces.shape[0])],
        scratch_shapes=[pltpu.VMEM((keys, LANES), F32), pltpu.VMEM((keys, LANES), F32)],
        compiler_params=params(4),
        cost_estimate=pl.CostEstimate(
            flops=20 * rows * keys * q_width * 2, bytes_accessed=12 * rows * q_width, transcendentals=rows * keys * q_width // HD
        ),
        name="attend_back",
    )(order, queries, grads, logs, *[pieces] * pieces.shape[0])


def line_steps(rows):
    half = rows // 2
    sub = 16
    return half, sub, half // sub


def line_body(finish, keep_state, gain_sum, n_in, extra, *refs):
    partial, ins, rest = refs[0], refs[1 : 1 + n_in], refs[1 + n_in :]
    if extra:
        world, n_grad, plan, whole_plane = extra
        ffn_out, rest = (None, rest) if whole_plane else (rest[0], rest[1:])
        grad_ins, rest = rest[:n_grad], rest[n_grad:]
    result, rest = rest[0], rest[1:]
    state_out, rest = (rest[0], rest[1:]) if keep_state else (None, rest)
    gain_out, rest = (rest[0], rest[1:]) if gain_sum else (None, rest)
    if extra:
        spread = len(plan) if whole_plane else world // 2 * len(plan)
        n_parts = 0 if whole_plane else 4
        out_parts, grad_outs, rest = rest[:n_parts], rest[n_parts : n_parts + spread], rest[n_parts + spread :]
    from_outer, from_peer, staged, send, recv = rest[:5]
    half, sub, count = line_steps(partial.shape[0])
    me = lax.axis_index("tensor")
    side = me // 2
    inner = lax.rem(me, 3) != 0
    to_outer, to_inner, to_peer = side * 3, 1 + side, 3 - me
    near, far = side * half, (1 - side) * half

    def rows(base, k):
        return pl.ds(pl.multiple_of(base + k * sub, sub), sub)

    def remote(source, target, s, r, k, where):
        return pltpu.make_async_remote_copy(
            src_ref=source,
            dst_ref=target,
            send_sem=send.at[s, k],
            recv_sem=recv.at[r, k],
            device_id={"tensor": where},
            device_id_type=pl.DeviceIdType.MESH,
        )

    def up_far(k):
        return remote(partial.at[rows(far, k)], from_outer.at[0, rows(0, k)], 0, 0, k, to_inner)

    def up_near(k):
        return remote(partial.at[rows(near, k)], from_outer.at[1, rows(0, k)], 1, 1, k, to_inner)

    def across(k):
        return remote(staged.at[rows(0, k)], from_peer.at[rows(0, k)], 0, 2, k, to_peer)

    def over(k, base):
        return remote(result.at[rows(base, k)], result.at[rows(base, k)], 2, 4, k, to_peer)

    def down_near(k):
        return remote(result.at[rows(near, k)], result.at[rows(near, k)], 1, 3, k, to_outer)

    def down_far(k):
        return remote(result.at[rows(far, k)], result.at[rows(far, k)], 3, 4, k, to_outer)

    barrier = pltpu.get_barrier_semaphore()

    def greet(where):
        pl.semaphore_signal(barrier, inc=1, device_id={"tensor": where}, device_id_type=pl.DeviceIdType.MESH)

    if extra:
        mate = {"context": lax.axis_index("context") ^ 1}
        pl.semaphore_signal(barrier, inc=1, device_id=mate, device_id_type=pl.DeviceIdType.MESH)
        if whole_plane:
            for where in ({"context": lax.axis_index("context") ^ 2}, {"shard": lax.axis_index("shard") ^ 1}):
                pl.semaphore_signal(barrier, inc=1, device_id=where, device_id_type=pl.DeviceIdType.MESH)
            grad_work, grad_rest, grad_finish = plane_parts(world, plan, grad_ins, grad_outs, rest[5:])
        else:
            grad_work, grad_finish = grads_parts(world, plan, grad_ins, grad_outs, rest[5:])
            grad_rest = lambda: None
    block = partial.shape[0] // world if extra else 0
    more_greetings = (3 if whole_plane else 1) if extra else 0

    def work(q):
        grad_work(q)
        if not whole_plane:
            out_work(q)

    def out_work(q):
        rows_q = pl.ds(pl.multiple_of(q * block, block), block)
        value = RESIDUAL_SCALE * ffn_out[rows_q, :].astype(F32)
        quarter = 2 * block * world // 8
        chunk = lax.rem(q * 4 // world - me + 4, 4)
        place = pl.ds(pl.multiple_of(lax.rem(q * block, quarter), block), block)
        owned = inner & (q * 2 // world == side)

        for part in range(4):

            @pl.when(owned & (chunk == part))
            def _():
                mine = pl.ds(pl.multiple_of(lax.rem(q * block, half), block), block)
                out_parts[part][place, :] = (value + ins[0][mine, :]).astype(BF16)

            @pl.when(jnp.logical_not(owned) & (chunk == part))
            def _():
                out_parts[part][place, :] = value.astype(BF16)

    if gain_sum:
        gain_out[...] = jnp.zeros_like(gain_out)

    @pl.when(inner)
    def _():
        greet(to_outer)
        greet(to_peer)
        pl.semaphore_wait(barrier, 2 + more_greetings)

        def step(k, carry):
            @pl.when(k < count)
            def _():
                up_far(k).wait_recv()
                total = partial[rows(far, k), :].astype(F32) + from_outer[0, rows(0, k), :].astype(F32)
                staged[rows(0, k), :] = total.astype(BF16)
                across(k).start()

            @pl.when((k >= 1) & (k <= count))
            def _():
                j = k - 1
                up_near(j).wait_recv()
                across(j).wait_recv()
                total = partial[rows(near, j), :].astype(F32) + from_outer[1, rows(0, j), :].astype(F32)
                total = total + from_peer[rows(0, j), :].astype(F32)
                low, state, gains = finish(total, rows(near, j), rows(0, j), ins)
                result[rows(near, j), :] = low
                if keep_state:
                    state_out[rows(0, j), :] = state
                if gain_sum:
                    gain_out[...] += jnp.sum(gains.reshape(sub // 8, 8, gains.shape[1]), axis=0)
                down_near(j).start()
                over(j, near).start()

            @pl.when(k >= 3)
            def _():
                over(k - 3, far).wait_recv()
                down_far(k - 3).start()

            if extra:

                @pl.when((lax.rem(k, count // world) == 0) & (k < count))
                def _():
                    work(k // (count // world))

            return carry

        lax.fori_loop(0, count + 3, step, 0)

        def drain(k, carry):
            across(k).wait_send()
            down_near(k).wait_send()
            over(k, near).wait_send()
            down_far(k).wait_send()
            return carry

        lax.fori_loop(0, count, drain, 0)

    @pl.when(jnp.logical_not(inner))
    def _():
        greet(to_inner)
        pl.semaphore_wait(barrier, 1 + more_greetings)

        def step(k, carry):
            up_far(k).start()
            up_near(k).start()
            return carry

        lax.fori_loop(0, count, step, 0)
        if extra:

            def busy(q, carry):
                work(q)
                return carry

            lax.fori_loop(0, world, busy, 0)

        def drain(k, carry):
            down_near(k).wait_recv()
            down_far(k).wait_recv()
            up_far(k).wait_send()
            up_near(k).wait_send()
            return carry

        lax.fori_loop(0, count, drain, 0)

    if extra:
        grad_rest()
        grad_finish()


def line_sum(partial, ins, finish, keep_state, gain_sum, identity, ffn_out=None, pairs=()):
    rows, width = partial.shape
    half, _, count = line_steps(rows)
    vmem = pl.BlockSpec(memory_space=pltpu.VMEM)
    shapes = [jax.ShapeDtypeStruct((rows, width), BF16)]
    if keep_state:
        shapes.append(jax.ShapeDtypeStruct((half, width), F32))
    if gain_sum:
        shapes.append(jax.ShapeDtypeStruct((8, width), F32))
    specs, more, scratch, extra = [vmem] * len(shapes), [], [], None
    if pairs:
        arrays, plan = unique_arrays(pairs)
        whole_plane = ffn_out is None
        extra = (plane_size(), len(arrays), plan, whole_plane)
        outs, scratch = grads_shapes(pairs)
        if whole_plane:
            more = arrays
            pieces = [(left.shape[1] // plane_size(), high - low) for left, right, low, high in pairs]
            shapes += [jax.ShapeDtypeStruct(shape, F32) for shape in pieces]
            specs += [vmem] * len(pieces)
            scratch = scratch[:-1] + [pltpu.VMEM((3,) + shape, BF16) for shape in pieces]
            scratch += [pltpu.SemaphoreType.DMA((3, len(pairs)))] * 2
        else:
            more = [ffn_out] + arrays
            shapes += [jax.ShapeDtypeStruct((rows // 4, width), BF16)] * 4 + outs
            specs += [vmem] * 4 + [ANYWHERE] * len(outs)
    return pl.pallas_call(
        functools.partial(line_body, finish, keep_state, gain_sum, len(ins), extra),
        in_specs=[vmem] * (1 + len(ins) + len(more)),
        out_specs=specs,
        out_shape=shapes,
        scratch_shapes=[
            pltpu.VMEM((2, half, width), BF16),
            pltpu.VMEM((half, width), BF16),
            pltpu.VMEM((half, width), BF16),
            pltpu.SemaphoreType.DMA((4, count)),
            pltpu.SemaphoreType.DMA((5, count)),
        ]
        + scratch,
        compiler_params=pltpu.CompilerParams(
            collective_id=identity, has_side_effects=True, vmem_limit_bytes=VMEM_BYTES
        ),
        cost_estimate=pl.CostEstimate(flops=0, bytes_accessed=100 * rows * width, transcendentals=0),
    )(partial, *ins, *more)


def mean_square(values):
    return lax.rsqrt(jnp.mean(values * values, axis=1, keepdims=True) + EPSILON)


def finish_attention(total, whole, own, ins):
    tokens, gain = ins
    hidden = tokens[whole, :].astype(F32) + RESIDUAL_SCALE * total
    return (hidden * mean_square(hidden) * gain[...]).astype(BF16), hidden, None


def norm_pull(d_normed, values, gain):
    inverse = mean_square(values)
    scaled = gain * d_normed
    inner = jnp.mean(scaled * values, axis=1, keepdims=True)
    return inverse * scaled - values * inverse * inverse * inverse * inner, d_normed * values * inverse


def finish_ffn_back(total, whole, own, ins):
    hidden, grads, gain = ins
    pulled, gains = norm_pull(total, hidden[own, :], gain[...])
    d_hidden = grads[whole, :].astype(F32) + pulled
    return (RESIDUAL_SCALE * d_hidden).astype(BF16), d_hidden, gains


def finish_attention_back(total, whole, own, ins):
    tokens, d_hidden, gain = ins
    pulled, gains = norm_pull(total, tokens[whole, :].astype(F32), gain[...])
    return (d_hidden[own, :] + pulled).astype(BF16), None, gains


def front_fits():
    return lax.axis_size("shard") == 2 and lax.axis_size("context") == 4


def front_body(*refs):
    tokens, gain_piece, cosine, sine, w_query, w_key, w_value, w_output = refs[:8]
    normed, queries, kv, weight, output, gains = refs[8:14]
    local_sem, send, recv = refs[14:]
    me = plane_index()
    extent = weight.shape[0] // 8
    q_width = queries.shape[1]
    k_width = kv.shape[2] // 2
    context, shard = lax.axis_index("context"), lax.axis_index("shard")
    peers = {1: {"context": context ^ 1}, 2: {"context": context ^ 2}, 4: {"shard": shard ^ 1}}
    mesh_ids = pl.DeviceIdType.MESH
    barrier = pltpu.get_barrier_semaphore()
    for bit in (1, 2, 4):
        pl.semaphore_signal(barrier, inc=1, device_id=peers[bit], device_id_type=mesh_ids)

    def start(r):
        return pl.multiple_of((me ^ r) * extent, extent)

    def qkv_at(r, part=None):
        size = extent if part is None else extent // 2
        base = start(r) + (part or 0) * size
        return weight.at[pl.ds(pl.multiple_of(base, size), size)]

    def output_at(r, part=None):
        columns = pl.ds(start(r), extent)
        if part is None:
            return output.at[:, columns]
        size = output.shape[0] // 2
        return output.at[pl.ds(part * size, size), columns]

    def gains_at(r):
        return gains.at[:, pl.ds(start(r), extent)]

    spots = {}

    def remote(name, ref, bit, target=None):
        index = spots.setdefault(name, len(spots))
        return pltpu.make_async_remote_copy(
            src_ref=ref,
            dst_ref=ref if target is None else target,
            send_sem=send.at[index],
            recv_sem=recv.at[index],
            device_id=peers[bit],
            device_id_type=mesh_ids,
        )

    locals_ = [
        pltpu.make_async_copy(gain_piece, gains_at(0), local_sem.at[0]),
        pltpu.make_async_copy(w_query, weight.at[pl.ds(start(0), extent), pl.ds(0, q_width)], local_sem.at[1]),
        pltpu.make_async_copy(w_key, weight.at[pl.ds(start(0), extent), pl.ds(q_width, k_width)], local_sem.at[2]),
        pltpu.make_async_copy(
            w_value, weight.at[pl.ds(start(0), extent), pl.ds(q_width + k_width, k_width)], local_sem.at[3]
        ),
        pltpu.make_async_copy(w_output, output_at(0), local_sem.at[4]),
    ]
    for copy in locals_:
        copy.start()

    begun = []

    def begin(copy):
        copy.start()
        begun.append(copy)
        return copy

    pl.semaphore_wait(barrier, 3)
    locals_[0].wait()
    gain_in = [begin(remote("g2", gains_at(0), 2)), begin(remote("g4", gains_at(0), 4))]
    gain_core = [begin(remote("gc0", gains_at(0), 1))]
    for copy in locals_[1:4]:
        copy.wait()
    near, far = begin(remote("q2", qkv_at(0), 2)), begin(remote("q4", qkv_at(0), 4))
    core = [begin(remote("qc0", qkv_at(0), 1))]
    locals_[4].wait()
    out_near, out_far = begin(remote("o2", output_at(0), 2)), begin(remote("o4", output_at(0), 4))
    out_core = [begin(remote("oc0", output_at(0), 1))]

    gain_in[0].wait_recv()
    gain_in[1].wait_recv()
    diagonal = begin(remote("g6", gains_at(4), 2))
    gain_core += [begin(remote("gc2", gains_at(2), 1)), begin(remote("gc4", gains_at(4), 1))]
    diagonal.wait_recv()
    gain_core.append(begin(remote("gc6", gains_at(6), 1)))
    for copy in gain_core:
        copy.wait_recv()

    rows = tokens.shape[0]
    tile = 128

    def norm(i, carry):
        spot = pl.ds(pl.multiple_of(i * tile, tile), tile)
        values = tokens[spot, :].astype(F32)
        normed[spot, :] = (values * mean_square(values) * gains[0:1, :]).astype(BF16)
        return carry

    lax.fori_loop(0, rows // tile, norm, 0)

    far.wait_recv()
    cross = [begin(remote("q6a", qkv_at(4, 0), 2))]
    core.append(begin(remote("qc4", qkv_at(4), 1)))
    near.wait_recv()
    cross.append(begin(remote("q6b", qkv_at(2, 1), 4)))
    core.append(begin(remote("qc2", qkv_at(2), 1)))
    cross[0].wait_recv()
    cross[1].wait_recv()
    core.append(begin(remote("qc6", qkv_at(6), 1)))
    out_far.wait_recv()
    out_cross = [begin(remote("o6a", output_at(4, 0), 2))]
    out_core.append(begin(remote("oc4", output_at(4), 1)))
    out_near.wait_recv()
    out_cross.append(begin(remote("o6b", output_at(2, 1), 4)))
    out_core.append(begin(remote("oc2", output_at(2), 1)))
    for copy in core:
        copy.wait_recv()

    lane = lax.broadcasted_iota(jnp.int32, (1, LANES), 1)

    def rotated(part, spot):
        return part * cosine[spot, :] + turned(part, lane, 1.0) * sine[spot, :]

    def keys(i, carry):
        spot = pl.ds(pl.multiple_of(i * 256, 256), 256)
        part = jnp.dot(normed[spot, :], weight[:, q_width:], preferred_element_type=F32)
        kv[0, spot, :k_width] = rotated(part[:, :k_width], spot).astype(BF16)
        kv[0, spot, k_width:] = part[:, k_width:].astype(BF16)
        return carry

    lax.fori_loop(0, rows // 256, keys, 0)
    kv_near = begin(remote("k2", kv.at[0], 2, kv.at[2]))
    kv_core = begin(remote("k1", kv.at[0], 1, kv.at[1]))

    def query(i, carry):
        spot = pl.ds(pl.multiple_of(i * 256, 256), 256)
        part = jnp.dot(normed[spot, :], weight[:, :q_width], preferred_element_type=F32)
        for base in range(0, q_width, LANES):
            turned_part = rotated(part[:, base : base + LANES], spot).astype(BF16)
            queries[spot, base : base + LANES] = (turned_part * SCORE_SCALE).astype(BF16)
        return carry

    lax.fori_loop(0, rows // 256, query, 0)
    kv_near.wait_recv()
    kv_last = begin(remote("k3", kv.at[2], 1, kv.at[3]))
    out_cross[0].wait_recv()
    out_cross[1].wait_recv()
    out_core.append(begin(remote("oc6", output_at(6), 1)))
    for copy in out_core:
        copy.wait_recv()
    kv_core.wait_recv()
    kv_last.wait_recv()
    for copy in begun:
        copy.wait_send()


def front(tokens, gains, cosine, sine, w_query, w_key, w_value, w_output):
    rows, width = tokens.shape
    q_width, k_width = w_query.shape[1], w_key.shape[1]
    total = q_width + 2 * k_width
    vmem = pl.BlockSpec(memory_space=pltpu.VMEM)
    return pl.pallas_call(
        front_body,
        in_specs=[vmem] * 4 + [ANYWHERE] * 4,
        out_specs=[vmem] * 6,
        out_shape=[
            jax.ShapeDtypeStruct((rows, width), BF16),
            jax.ShapeDtypeStruct((rows, q_width), BF16),
            jax.ShapeDtypeStruct((4, rows, 2 * k_width), BF16),
            jax.ShapeDtypeStruct((width, total), BF16),
            jax.ShapeDtypeStruct((w_output.shape[0], width), BF16),
            jax.ShapeDtypeStruct((8, width), F32),
        ],
        scratch_shapes=[
            pltpu.SemaphoreType.DMA((5,)),
            pltpu.SemaphoreType.DMA((27,)),
            pltpu.SemaphoreType.DMA((27,)),
        ],
        compiler_params=pltpu.CompilerParams(collective_id=6, has_side_effects=True, vmem_limit_bytes=VMEM_BYTES),
        cost_estimate=pl.CostEstimate(
            flops=2 * rows * width * total, bytes_accessed=10 * rows * width, transcendentals=0
        ),
        name="front",
    )(tokens, gains, cosine, sine, w_query, w_key, w_value, w_output)


def unique_arrays(pairs):
    arrays, plan = [], []
    for left, right, low, high in pairs:
        spots = []
        for value in (left, right):
            known = [i for i, array in enumerate(arrays) if array is value]
            if not known:
                arrays.append(value)
            spots.append(known[0] if known else len(arrays) - 1)
        plan.append((spots[0], spots[1], low, high))
    return arrays, tuple(plan)


def grads_parts(count, plan, ins, outs, scratch):
    halves, jobs = count // 2, len(plan)
    sent, got, own = scratch[:jobs], scratch[jobs : 2 * jobs], scratch[2 * jobs : 3 * jobs]
    send, recv, done = scratch[3 * jobs :]
    me = plane_index()
    mate = {"context": lax.axis_index("context") ^ 1}

    def piece(j, r):
        left, right, low, high = plan[j]
        extent = ins[left].shape[1] // count
        columns = pl.ds(pl.multiple_of((me ^ r) * extent, extent), extent)
        return lax.dot_general(
            ins[left][:, columns], ins[right][:, low:high], (((0,), (0,)), ((), ())), preferred_element_type=F32
        )

    def across(j, i):
        return pltpu.make_async_remote_copy(
            src_ref=sent[j].at[i],
            dst_ref=got[j].at[i],
            send_sem=send.at[j, i],
            recv_sem=recv.at[j, i],
            device_id=mate,
            device_id_type=pl.DeviceIdType.MESH,
        )

    def odd(i):
        for j in range(jobs):
            sent[j][i] = piece(j, 2 * i + 1).astype(BF16)
            across(j, i).start()

    def even(i):
        for j in range(jobs):
            value = piece(j, 2 * i)
            across(j, i).wait_recv()
            value = value + got[j][i].astype(F32)

            @pl.when(i > 0)
            def _():
                got[j][i] = value.astype(BF16)

            @pl.when(i == 0)
            def _():
                own[j][...] = value

        for known in range(halves):

            @pl.when(i == known)
            def _():
                for j in range(jobs):
                    source = got[j].at[known] if known else own[j]
                    pltpu.make_async_copy(source, outs[known * jobs + j], done.at[known, j]).start()

    def work(q):
        @pl.when(q < halves)
        def _():
            odd(halves - 1 - q)

        @pl.when(q >= halves)
        def _():
            even(count - 1 - q)

    def finish():
        for known in range(halves):
            for j in range(jobs):
                source = got[j].at[known] if known else own[j]
                pltpu.make_async_copy(source, outs[known * jobs + j], done.at[known, j]).wait()
                across(j, known).wait_send()

    return work, finish


def plane_parts(count, plan, ins, outs, scratch):
    jobs = len(plan)
    sent, got, own = scratch[:jobs], scratch[jobs : 2 * jobs], scratch[2 * jobs : 3 * jobs]
    send, recv = scratch[3 * jobs : 3 * jobs + 2]
    landed = scratch[3 * jobs + 2 : 4 * jobs + 2]
    plane_send, plane_recv = scratch[4 * jobs + 2 :]
    me = plane_index()
    core = {"context": lax.axis_index("context") ^ 1}
    peers = ({"context": lax.axis_index("context") ^ 2}, {"shard": lax.axis_index("shard") ^ 1})

    def piece(j, r):
        left, right, low, high = plan[j]
        extent = ins[left].shape[1] // count
        columns = pl.ds(pl.multiple_of((me ^ r) * extent, extent), extent)
        return lax.dot_general(
            ins[left][:, columns], ins[right][:, low:high], (((0,), (0,)), ((), ())), preferred_element_type=F32
        )

    def across(j, i):
        return pltpu.make_async_remote_copy(
            src_ref=sent[j].at[i],
            dst_ref=got[j].at[i],
            send_sem=send.at[j, i],
            recv_sem=recv.at[j, i],
            device_id=core,
            device_id_type=pl.DeviceIdType.MESH,
        )

    def move(j, i, slot, way):
        return pltpu.make_async_remote_copy(
            src_ref=got[j].at[i],
            dst_ref=landed[j].at[slot],
            send_sem=plane_send.at[slot, j],
            recv_sem=plane_recv.at[slot, j],
            device_id=peers[way],
            device_id_type=pl.DeviceIdType.MESH,
        )

    first = [(j + 1) % 2 for j in range(jobs)]
    cross = [move(j, 3, 2, first[j]) for j in range(jobs)]
    early = [move(j, 2 if first[j] else 1, 1 if first[j] else 0, first[j]) for j in range(jobs)]
    late = [move(j, 1 if first[j] else 2, 0 if first[j] else 1, 1 - first[j]) for j in range(jobs)]

    def work(q):
        @pl.when(q < 4)
        def _():
            i = 3 - q
            for j in range(jobs):
                sent[j][i] = piece(j, 2 * i + 1).astype(BF16)
                across(j, i).start()

        @pl.when(q >= 4)
        def _():
            i = 7 - q
            for j in range(jobs):
                value = piece(j, 2 * i)
                across(j, i).wait_recv()
                value = value + got[j][i].astype(F32)

                @pl.when(i > 0)
                def _():
                    got[j][i] = value.astype(BF16)

                @pl.when(i == 0)
                def _():
                    own[j][...] = value

        @pl.when(q == 4)
        def _():
            for j in range(jobs):
                cross[j].start()

        @pl.when(q == 7)
        def _():
            for j in range(jobs):
                early[j].start()

    def rest():
        for j in range(jobs):
            kept = 1 if first[j] else 2
            cross[j].wait_recv()
            got[j][kept] = (got[j][kept].astype(F32) + landed[j][2].astype(F32)).astype(BF16)
            late[j].start()
        for j in range(jobs):
            early[j].wait_recv()
            late[j].wait_recv()
            outs[j][...] = own[j][...] + landed[j][0].astype(F32) + landed[j][1].astype(F32)

    def finish():
        for j in range(jobs):
            for copy in (cross[j], early[j], late[j]):
                copy.wait_send()
            for i in range(4):
                across(j, i).wait_send()

    return work, rest, finish


def grads_body(count, n_in, plan, *refs):
    ins, rest = refs[:n_in], refs[n_in:]
    spread = count // 2 * len(plan)
    outs, scratch = rest[:spread], rest[spread:]
    work, finish = grads_parts(count, plan, ins, outs, scratch)
    barrier = pltpu.get_barrier_semaphore()
    mate = {"context": lax.axis_index("context") ^ 1}
    pl.semaphore_signal(barrier, inc=1, device_id=mate, device_id_type=pl.DeviceIdType.MESH)
    pl.semaphore_wait(barrier, 1)

    def step(q, carry):
        work(q)
        return carry

    lax.fori_loop(0, count, step, 0)
    finish()


def grads_shapes(pairs):
    count = plane_size()
    halves = count // 2
    shapes = [(left.shape[1] // count, high - low) for left, right, low, high in pairs]
    outs = [jax.ShapeDtypeStruct(shape, BF16 if i else F32) for i in range(halves) for shape in shapes]
    scratch = [pltpu.VMEM((halves,) + shape, BF16) for shape in shapes] * 2
    scratch += [pltpu.VMEM(shape, F32) for shape in shapes]
    sems = [(len(pairs), halves), (len(pairs), halves), (halves, len(pairs))]
    return outs, scratch + [pltpu.SemaphoreType.DMA(shape) for shape in sems]


def grads_named(flat, jobs):
    return [{2 * i: flat[i * jobs + j] for i in range(len(flat) // jobs)} for j in range(jobs)]


def grads_fit(pairs):
    return all((pair[0].shape[1] // plane_size()) % LANES == 0 for pair in pairs)


def plane_grads(pairs, identity):
    count = plane_size()
    jobs = len(pairs)
    extents = [pair[0].shape[1] // count for pair in pairs]
    arrays, plan = unique_arrays(pairs)
    if not grads_fit(pairs):
        me = plane_index()
        sides = []
        for (left, right, low, high), e in zip(pairs, extents):
            columns = lambda r: lax.dynamic_slice_in_dim(left, (me ^ r) * e, e, 1)
            whole = {r: weight_grad(columns(r), right[:, low:high]).astype(BF16) for r in range(count)}
            sides.append({r: take_sum(whole, 1, r) for r in range(0, count, 2)})
        return sides
    outs, scratch = grads_shapes(pairs)
    flat = pl.pallas_call(
        functools.partial(grads_body, count, len(arrays), plan),
        in_specs=[pl.BlockSpec(memory_space=pltpu.VMEM)] * len(arrays),
        out_specs=[ANYWHERE] * len(outs),
        out_shape=outs,
        scratch_shapes=scratch,
        compiler_params=pltpu.CompilerParams(
            collective_id=identity, has_side_effects=True, vmem_limit_bytes=VMEM_BYTES
        ),
        cost_estimate=pl.CostEstimate(
            flops=sum(2 * left.shape[0] * left.shape[1] * (high - low) for left, _, low, high in pairs),
            bytes_accessed=sum(2 * left.shape[1] * (high - low) for left, _, low, high in pairs),
            transcendentals=0,
        ),
    )(*arrays)
    return grads_named(flat, jobs)


def after(value, *others):
    return lax.optimization_barrier((value,) + others)[0] if others else value


def gather_context(piece):
    size = lax.axis_size("context")
    held = {0: piece}
    bit = size // 2
    while bit:
        for r in list(held):
            held[r | bit] = swap(held[r], "context", size, bit)
        bit //= 2
    return [held[r] for r in range(size)]


def reduce_context(pieces):
    size = len(pieces)
    held = dict(enumerate(pieces))
    bit = 1
    while bit < size:
        held = {
            r: held[r].astype(F32) + swap(held[r | bit].astype(BF16), "context", size, bit).astype(F32)
            for r in held
            if not r & bit
        }
        bit *= 2
    return held[0]


def stored_places(order_row, first, count):
    stored = first + jnp.arange(count, dtype=jnp.int32)
    picks = (stored // BLK)[:, None] == jnp.arange(order_row.shape[0], dtype=jnp.int32)[None, :]
    return jnp.sum(jnp.where(picks, order_row[None, :], 0), axis=1) * BLK + stored % BLK


def rope_tables(order, local_len):
    first = lax.axis_index("context") * local_len
    places = jnp.concatenate([stored_places(order[s], first, local_len) for s in range(order.shape[0])])
    half = HD // 2
    inverse = jnp.exp(jnp.arange(half, dtype=F32) * (-2.0 * math.log(ROPE_BASE) / HD))
    angles = places.astype(F32)[:, None] * jnp.tile(inverse, LANES // half)[None, :]
    return jnp.cos(angles), jnp.sin(angles)


def weight_grad(left, right):
    return lax.dot_general(left, right, (((0,), (0,)), ((), ())), preferred_element_type=F32)


def local(
    tokens, block_order, w_query, w_key, w_value, w_output, w_gate, w_up, w_down, norm_attn, norm_ffn, grad_out
):
    seqs, local_len, width = tokens.shape
    rows = seqs * local_len
    size = plane_size()
    z = lax.axis_index("tensor")
    token_rows = tokens.reshape(rows, width)
    grad_rows = grad_out.reshape(rows, width)
    q_width, kv_width = w_query.shape[1], w_key.shape[1]
    units = w_down.shape[0]
    half = units // 2

    cosine, sine = rope_tables(block_order, local_len)
    if front_fits():
        gain_piece = jnp.pad(jnp.stack([norm_attn, norm_ffn]).astype(F32), ((0, 6), (0, 0)))
        normed, queries, kv_pieces, w_qkv, w_out, gains = front(
            token_rows, gain_piece, cosine, sine, w_query, w_key, w_value, w_output
        )
        qkv_pieces, output_pieces = [w_qkv], [w_out]
        early, late = [queries], [queries]
        gain_attn, gain_ffn = gains[0:1], gains[1:2]
    else:
        gains = gather_small(jnp.stack([norm_attn, norm_ffn])).reshape(2, width)
        gain_attn, gain_ffn = gains[0:1], gains[1:2]
        w_qkv = jnp.concatenate([w_query, w_key, w_value], axis=1)
        qkv_pieces, output_pieces = gather_pair(w_qkv, w_output)
        normed, queries, keys_values = project_qkv(token_rows, gain_attn, cosine, sine, qkv_pieces, q_width)
        kv_pieces = jnp.stack(gather_context(keys_values))
        early, late = [qkv_pieces[-2]], [kv_pieces]
        output_pieces = widened(output_pieces)
    mixture, logs = attend(block_order, queries, kv_pieces)
    branch = gathered_matmul(mixture, output_pieces, 1, False)
    normed_ffn, hidden = line_sum(branch, [token_rows, gain_ffn], finish_attention, True, False, 0)
    extent = width // size
    pushed = extent % (2 * LANES) == 0
    order = (early, late, [mixture], [normed_ffn], not pushed)
    gate_pieces, up_pieces = gather_pair(w_gate, w_up, *order)
    order = (early, late, [normed_ffn], [normed_ffn], not pushed)
    if pushed:
        low_pieces, high_pieces = gather_pair(w_down[:, : extent // 2], w_down[:, extent // 2 :], *order)
    else:
        low_pieces, high_pieces = gather_pair(w_down[:half], w_down[half:], *order)
        low_pieces, high_pieces = widened(low_pieces), widened(high_pieces)
    d_ffn = (RESIDUAL_SCALE * grad_rows.astype(F32)).astype(BF16)
    active, d_gate, d_up, ffn_out, d_normed_ffn = ffn(
        normed_ffn, d_ffn, gate_pieces, up_pieces, low_pieces, high_pieces, pushed
    )
    pairs = [
        (normed_ffn, d_gate, 0, units),
        (normed_ffn, d_up, 0, units),
        (d_ffn, active, 0, half),
        (d_ffn, active, half, units),
    ]
    sum_ins = [hidden, grad_rows, gain_ffn]
    if grads_fit(pairs):
        d_branch, d_hidden, ffn_gain, *flat = line_sum(
            d_normed_ffn, sum_ins, finish_ffn_back, True, True, 1, ffn_out, pairs
        )
        out_chunks = flat[:4]
        grad_gate, grad_up, grad_low, grad_high = grads_named(flat[4:], len(pairs))
    else:
        grad_gate, grad_up, grad_low, grad_high = plane_grads(pairs, 3)
        d_branch, d_hidden, ffn_gain = line_sum(
            after(d_normed_ffn, grad_gate[0]), sum_ins, finish_ffn_back, True, True, 1
        )
        padded = lax.dynamic_update_slice_in_dim(jnp.zeros((rows, width), F32), hidden, (z // 2) * (rows // 2), 0)
        out_part = RESIDUAL_SCALE * ffn_out.astype(F32) + jnp.where(lax.rem(z, 3) != 0, padded, 0.0)
        out_chunks = [chunk_of(out_part.astype(BF16), lax.rem(z + shift, 4), rows // 4) for shift in range(4)]
    layer_out = rows_gather(rows_sum(out_chunks).astype(BF16))

    d_mixture = gathered_matmul(d_branch, output_pieces, 1, True)
    d_queries, *d_pieces = attend_back(block_order, queries, d_mixture, logs, kv_pieces)
    d_keys_values = reduce_context(d_pieces)
    grad_gate, grad_up = reduce_pair(grad_gate, grad_up, [d_keys_values])
    grad_low, grad_high = reduce_pair(grad_low, grad_high, [d_keys_values])
    d_qkv, d_normed = project_qkv_back(d_queries, d_keys_values, cosine, sine, qkv_pieces)
    pairs = [(normed, d_qkv, 0, d_qkv.shape[1]), (d_branch, mixture, 0, q_width)]
    sum_ins = [token_rows, d_hidden, gain_attn]
    if grads_fit(pairs) and front_fits():
        grad_tokens, attn_gain, grad_qkv, grad_output = line_sum(
            d_normed, sum_ins, finish_attention_back, False, True, 2, None, pairs
        )
    else:
        grad_qkv, grad_output = plane_grads(pairs, 4)
        grad_tokens, attn_gain = line_sum(after(d_normed, grad_qkv[0]), sum_ins, finish_attention_back, False, True, 2)
        grad_qkv, grad_output = reduce_pair(grad_qkv, grad_output)
    grad_tokens = grad_tokens.astype(F32)
    attn_gain, ffn_gain = jnp.sum(attn_gain, axis=0), jnp.sum(ffn_gain, axis=0)
    gain_grads = jnp.stack([attn_gain, ffn_gain])
    gain_grads = gains_sum(gain_grads)
    return (
        layer_out.reshape(seqs, local_len, width),
        grad_tokens.reshape(seqs, local_len, width),
        grad_qkv[:, :q_width],
        grad_qkv[:, q_width : q_width + kv_width],
        grad_qkv[:, q_width + kv_width :],
        grad_output.T,
        grad_gate,
        grad_up,
        jnp.concatenate([grad_low.T, grad_high.T], axis=0),
        gain_grads[0],
        gain_grads[1],
    )


def solution(mesh):
    split = P("shard", "context", None)
    inward, outward = P(PLANE, "tensor"), P("tensor", PLANE)
    gain = P(PLANE)
    return jax.shard_map(
        local,
        mesh=mesh,
        in_specs=(split, P("shard", None), inward, inward, inward, outward, inward, inward, outward, gain, gain, split),
        out_specs=(split, split, inward, inward, inward, outward, inward, inward, outward, gain, gain),
        check_vma=False,
    )
```

```python
import functools
import math

import jax
import jax.numpy as jnp
from jax import lax
from jax.experimental import pallas as pl
from jax.experimental.pallas import tpu as pltpu
from jax.sharding import PartitionSpec as P


HD = 64
BLK = 256
LANES = 128
EPSILON = 1e-05
SCORE_SCALE = 0.015625
RESIDUAL_SCALE = 0.22
ROPE_BASE = 10000000.0
MASKED_SCORE = -1e30
PLANE = ("shard", "context")
VMEM_BYTES = 64000 * 1024


F32 = jnp.float32
BF16 = jnp.bfloat16


def plane_size():
    return lax.axis_size("shard") * lax.axis_size("context")


def plane_index():
    return lax.axis_index("shard") * lax.axis_size("context") + lax.axis_index("context")


def swap(value, axes, size, bit):
    return lax.ppermute(value, axes, [(i, i ^ bit) for i in range(size)])


def gather_pair(first, second, far_after=(), near_after=(), cross_after=(), core_after=(), core=True):
    size = plane_size()
    bits = [1 << b for b in range(1, size.bit_length() - 1)]
    sides = [{0: first}, {0: second}]
    if len(bits) == 2:
        near, far = bits
        for side in sides:
            side[far] = swap(after(side[0], *far_after), PLANE, size, far)
        for side in reversed(sides):
            side[near] = swap(after(side[0], *near_after), PLANE, size, near)
        sides[0][near | far] = swap(after(sides[0][far], *cross_after), PLANE, size, near)
        sides[1][near | far] = swap(after(sides[1][near], *cross_after), PLANE, size, far)
    else:
        for side in sides:
            for bit in bits:
                for r in list(side):
                    side[r | bit] = swap(side[r], PLANE, size, bit)
    if not core:
        return [[side[r] for r in range(0, size, 2)] for side in sides]
    for side in sides:
        for r in list(side):
            side[r | 1] = swap(after(side[r], *core_after), PLANE, size, 1)
    return [[side[r] for r in range(size)] for side in sides]


def widened(pieces):
    level = 1
    while pieces[0].shape[1] < LANES:
        upper = (plane_index() // level) % 2 == 1
        pairs = zip(pieces[0::2], pieces[1::2])
        pieces = [jnp.where(upper, jnp.concatenate([b, a], 1), jnp.concatenate([a, b], 1)) for a, b in pairs]
        level *= 2
    return pieces


def take_sum(side, bit, kept):
    sent = side[kept | bit].astype(BF16)
    total = side[kept].astype(F32) + swap(sent, PLANE, plane_size(), bit).astype(F32)
    return total if kept == 0 else total.astype(BF16)


def crossed_pair(first, second, second_after):
    size, near, far = plane_size(), 2, 4
    first, second = dict(first), dict(second)
    first[near] = (first[near].astype(F32) + first[6].astype(F32)).astype(BF16)
    second[far] = (second[far].astype(F32) + second[6].astype(F32)).astype(BF16)
    done = []
    for side, waits in ((first, ()), (second, second_after)):
        a = swap(after(side[near], *waits), PLANE, size, near).astype(F32)
        b = swap(side[far], PLANE, size, far).astype(F32)
        done.append(side[0] + a + b)
    return done


def reduce_pair(first, second, last_after=()):
    size = plane_size()
    bits = [1 << b for b in range(1, size.bit_length() - 1)]
    sides = [dict(first), dict(second)]
    if len(bits) == 2:
        near, far = bits
        sides[0][near] = take_sum(sides[0], far, near)
        sides[1][far] = take_sum(sides[1], near, far)
        done = []
        for side in sides:
            sent = [after(side[bit].astype(BF16), *last_after) for bit in bits]
            a = swap(sent[0], PLANE, size, near).astype(F32)
            b = swap(sent[1], PLANE, size, far).astype(F32)
            done.append(side[0] + a + b)
        return done
    done = []
    for side in sides:
        for bit in reversed(bits):
            side = {r: take_sum(side, bit, r) for r in side if not r & bit}
        done.append(side[0])
    return done


def gather_small(values):
    size = plane_size()
    stacked = values[None]
    bit = 1
    while bit < size:
        stacked = jnp.concatenate([stacked, swap(stacked, PLANE, size, bit)], axis=0)
        bit *= 2
    picks = jnp.arange(size, dtype=jnp.int32)[:, None] ^ plane_index()
    chosen = (picks == jnp.arange(size, dtype=jnp.int32)[None, :]).astype(F32)
    return jnp.einsum("ij,jkw->kiw", chosen, stacked.astype(F32), precision=lax.Precision.HIGHEST)


def chunk_of(rows, index, count):
    return lax.dynamic_slice_in_dim(rows, index * count, count, 0)


def rows_sum(chunks):
    size = lax.axis_size("tensor")
    total = chunks[0].astype(F32)
    for shift in range(1, size):
        pairs = [(i, (i + shift) % size) for i in range(size)]
        total = total + lax.ppermute(chunks[shift], "tensor", pairs).astype(F32)
    return total


def rows_gather(chunk):
    size = lax.axis_size("tensor")
    count = chunk.shape[0]
    parts = [chunk]
    for shift in range(1, size):
        pairs = [(i, (i + shift) % size) for i in range(size)]
        parts.append(lax.ppermute(chunk, "tensor", pairs))
    return pl.pallas_call(
        assemble_body,
        in_specs=[ANYWHERE] * size,
        out_specs=pl.BlockSpec(memory_space=pltpu.VMEM),
        out_shape=jax.ShapeDtypeStruct((size * count,) + chunk.shape[1:], chunk.dtype),
        scratch_shapes=[pltpu.SemaphoreType.DMA],
        compiler_params=pltpu.CompilerParams(vmem_limit_bytes=8 << 20),
        cost_estimate=pl.CostEstimate(flops=0, bytes_accessed=4 * size * chunk.size, transcendentals=0),
        name="assemble",
    )(*parts)


def assemble_body(*refs):
    parts, whole, sem = refs[:-2], refs[-2], refs[-1]
    count = parts[0].shape[0]
    me = lax.axis_index("tensor")
    for shift, part in enumerate(parts):
        place = pl.multiple_of(lax.rem(me - shift + len(parts), len(parts)) * count, count)
        pltpu.make_async_copy(part, whole.at[pl.ds(place, count)], sem).start()
    pltpu.make_async_copy(whole, whole, sem).wait()


def gains_sum(values):
    size, tensor, me = plane_size(), lax.axis_size("tensor"), plane_index()
    extent = values.shape[1] // size
    total = values
    for shift in range(1, tensor):
        total = total + lax.ppermute(values, "tensor", [(i, (i + shift) % tensor) for i in range(tensor)])
    own = 0.0
    for r in range(size):
        sent = lax.dynamic_slice_in_dim(total, (me ^ r) * extent, extent, 1)
        own = own + (swap(sent, PLANE, size, r) if r else sent)
    return own


def params(steps):
    return pltpu.CompilerParams(
        dimension_semantics=("arbitrary",) * steps, vmem_limit_bytes=VMEM_BYTES
    )


def place_pieces(pieces, whole, sem, axis):
    size = len(pieces)
    me = plane_index() // (plane_size() // size)
    extent = whole.shape[axis] // size
    for r, piece in enumerate(pieces):
        start = pl.multiple_of((me ^ r) * extent, extent)
        target = whole.at[pl.ds(start, extent)] if axis == 0 else whole.at[:, pl.ds(start, extent)]
        pltpu.make_async_copy(piece, target, sem).start()


def await_whole(whole, sem):
    pltpu.make_async_copy(whole, whole, sem).wait()


ANYWHERE = pl.BlockSpec(memory_space=pl.ANY)


def turned(values, lane, sign):
    half = HD // 2
    upper = pltpu.roll(values, LANES - half, 1)
    lower = pltpu.roll(values, half, 1)
    return jnp.where(lane % HD < half, -sign * upper, sign * lower)


def qkv_body(count, tokens, gain, cosine, sine, *rest):
    pieces, (normed, queries, keys_values, weight, sem) = rest[:count], rest[count:]

    @pl.when(pl.program_id(0) == 0)
    def _():
        place_pieces(pieces, weight, sem, 0)

    values = tokens[...].astype(F32)
    inverse = lax.rsqrt(jnp.mean(values * values, axis=1, keepdims=True) + EPSILON)
    low = (values * inverse * gain[...]).astype(BF16)
    normed[...] = low

    @pl.when(pl.program_id(0) == 0)
    def _():
        await_whole(weight, sem)

    cos, sin = cosine[...], sine[...]
    lane = lax.broadcasted_iota(jnp.int32, cos.shape, 1)
    q_width = queries.shape[1]
    k_width = keys_values.shape[1] // 2
    for start in range(0, weight.shape[1], LANES):
        part = jnp.dot(low, weight[:, start : start + LANES * 1], preferred_element_type=F32)
        if start < q_width + k_width:
            part = part * cos + turned(part, lane, 1.0) * sin
        if start < q_width:
            queries[:, start : start + LANES] = (part.astype(BF16) * SCORE_SCALE).astype(BF16)
        else:
            keys_values[:, start - q_width : start - q_width + LANES] = part.astype(BF16)


def project_qkv(tokens, gain, cosine, sine, pieces, q_width):
    rows, width = tokens.shape
    total = pieces[0].shape[1]
    tile = min(rows, 256)
    row_spec = lambda w: pl.BlockSpec((tile, w), lambda i: (i, 0))
    return pl.pallas_call(
        functools.partial(qkv_body, len(pieces)),
        grid=(rows // tile,),
        in_specs=[row_spec(width), pl.BlockSpec((1, width), lambda i: (0, 0)), row_spec(LANES), row_spec(LANES)]
        + [ANYWHERE] * len(pieces),
        out_specs=[row_spec(width), row_spec(q_width), row_spec(total - q_width)],
        out_shape=[
            jax.ShapeDtypeStruct((rows, width), BF16),
            jax.ShapeDtypeStruct((rows, q_width), BF16),
            jax.ShapeDtypeStruct((rows, total - q_width), BF16),
        ],
        scratch_shapes=[pltpu.VMEM((width, total), BF16), pltpu.SemaphoreType.DMA],
        compiler_params=params(1),
        cost_estimate=pl.CostEstimate(
            flops=2 * rows * width * total, bytes_accessed=2 * (2 * rows * width + width * total), transcendentals=0
        ),
        name="project_qkv",
    )(tokens, gain, cosine, sine, *pieces)


def qkv_back_body(count, d_queries, d_keys_values, cosine, sine, *rest):
    pieces, (d_all, d_normed, weight, sem) = rest[:count], rest[count:]

    @pl.when(pl.program_id(0) == 0)
    def _():
        place_pieces(pieces, weight, sem, 0)

    cos, sin = cosine[...], sine[...]
    lane = lax.broadcasted_iota(jnp.int32, cos.shape, 1)
    q_width = d_queries.shape[1]
    k_width = d_keys_values.shape[1] // 2
    for start in range(0, d_all.shape[1], LANES):
        if start < q_width:
            part = d_queries[:, start : start + LANES]
        else:
            part = d_keys_values[:, start - q_width : start - q_width + LANES]
        if start < q_width + k_width:
            part = part * cos + turned(part * sin, lane, -1.0)
        d_all[:, start : start + LANES] = part.astype(BF16)

    @pl.when(pl.program_id(0) == 0)
    def _():
        await_whole(weight, sem)

    step = 512
    for start in range(0, weight.shape[0], step):
        d_normed[:, start : start + step] = lax.dot_general(
            d_all[...], weight[start : start + step, :], (((1,), (1,)), ((), ())), preferred_element_type=F32
        ).astype(BF16)


def project_qkv_back(d_queries, d_keys_values, cosine, sine, pieces):
    rows, q_width = d_queries.shape
    total = pieces[0].shape[1]
    width = pieces[0].shape[0] * len(pieces)
    tile = min(rows, 256)
    row_spec = lambda w: pl.BlockSpec((tile, w), lambda i: (i, 0))
    return pl.pallas_call(
        functools.partial(qkv_back_body, len(pieces)),
        grid=(rows // tile,),
        in_specs=[row_spec(q_width), row_spec(total - q_width), row_spec(LANES), row_spec(LANES)]
        + [ANYWHERE] * len(pieces),
        out_specs=[row_spec(total), row_spec(width)],
        out_shape=[jax.ShapeDtypeStruct((rows, total), BF16), jax.ShapeDtypeStruct((rows, width), BF16)],
        scratch_shapes=[pltpu.VMEM((width, total), BF16), pltpu.SemaphoreType.DMA],
        compiler_params=params(1),
        cost_estimate=pl.CostEstimate(
            flops=2 * rows * width * total, bytes_accessed=2 * (2 * rows * width + width * total), transcendentals=0
        ),
        name="project_qkv_back",
    )(d_queries, d_keys_values, cosine, sine, *pieces)


def gathered_body(count, axis, transposed, left, *rest):
    pieces, (out, weight, sem) = rest[:count], rest[count:]

    @pl.when(pl.program_id(0) == 0)
    def _():
        place_pieces(pieces, weight, sem, axis)
        await_whole(weight, sem)

    step = min(out.shape[1], 512)
    for start in range(0, out.shape[1], step):
        if transposed:
            part = lax.dot_general(
                left[...], weight[start : start + step, :], (((1,), (1,)), ((), ())), preferred_element_type=F32
            )
        else:
            part = jnp.dot(left[...], weight[:, start : start + step], preferred_element_type=F32)
        out[:, start : start + step] = part.astype(out.dtype)


def gathered_matmul(left, pieces, axis, transposed):
    rows = left.shape[0]
    shape = list(pieces[0].shape)
    shape[axis] *= len(pieces)
    outer = shape[0] if transposed else shape[1]
    tile = min(rows, 256)
    return pl.pallas_call(
        functools.partial(gathered_body, len(pieces), axis, transposed),
        grid=(rows // tile,),
        in_specs=[pl.BlockSpec((tile, left.shape[1]), lambda i: (i, 0))] + [ANYWHERE] * len(pieces),
        out_specs=pl.BlockSpec((tile, outer), lambda i: (i, 0)),
        out_shape=jax.ShapeDtypeStruct((rows, outer), BF16),
        scratch_shapes=[pltpu.VMEM(tuple(shape), BF16), pltpu.SemaphoreType.DMA],
        compiler_params=params(1),
        cost_estimate=pl.CostEstimate(
            flops=2 * rows * shape[0] * shape[1],
            bytes_accessed=2 * (rows * sum(shape) + shape[0] * shape[1]),
            transcendentals=0,
        ),
    )(left, *pieces)


def ffn_tile(f_step, tile, normed, d_ffn, gate, up, down, active, d_gate, d_up, out, d_normed, out_sum, d_sum):
    units = pl.ds(pl.multiple_of(f_step * tile, tile), tile)
    gate_tile, up_tile, down_tile = gate[:, units], up[:, units], down[units, :]
    gate_in = jnp.dot(normed[...], gate_tile, preferred_element_type=F32)
    upward = jnp.dot(normed[...], up_tile, preferred_element_type=F32)
    d_active = lax.dot_general(d_ffn[...], down_tile, (((1,), (1,)), ((), ())), preferred_element_type=F32)
    sigma = 1.0 / (1.0 + jnp.exp(-gate_in))
    silu = gate_in * sigma
    active_low = (silu * upward).astype(BF16)
    gate_low = (d_active * upward * (sigma * (1.0 + gate_in * (1.0 - sigma)))).astype(BF16)
    up_low = (d_active * silu).astype(BF16)
    active[...] = active_low
    d_gate[...] = gate_low
    d_up[...] = up_low
    part = jnp.dot(active_low, down_tile, preferred_element_type=F32)
    d_part = lax.dot_general(gate_low, gate_tile, (((1,), (1,)), ((), ())), preferred_element_type=F32)
    d_part += lax.dot_general(up_low, up_tile, (((1,), (1,)), ((), ())), preferred_element_type=F32)

    @pl.when(f_step == 0)
    def _():
        out_sum[...] = part
        d_sum[...] = d_part

    @pl.when(f_step > 0)
    def _():
        out_sum[...] += part
        d_sum[...] += d_part

    @pl.when(f_step == pl.num_programs(1) - 1)
    def _():
        out[...] = out_sum[...].astype(BF16)
        d_normed[...] = d_sum[...].astype(BF16)


def ffn_body(count, narrow, tile, normed, d_ffn, *rest):
    gate_pieces, up_pieces, rest = rest[:count], rest[count : 2 * count], rest[2 * count :]
    low_pieces, high_pieces, rest = rest[:narrow], rest[narrow : 2 * narrow], rest[2 * narrow :]
    active, d_gate, d_up, out, d_normed, gate, up, down, out_sum, d_sum, sems = rest
    f_step = pl.program_id(1)
    half = down.shape[0] // 2

    @pl.when((pl.program_id(0) == 0) & (f_step == 0))
    def _():
        place_pieces(gate_pieces, gate, sems.at[0], 0)
        place_pieces(up_pieces, up, sems.at[1], 0)
        place_pieces(low_pieces, down.at[pl.ds(0, half)], sems.at[2], 1)
        place_pieces(high_pieces, down.at[pl.ds(half, half)], sems.at[3], 1)
        await_whole(gate, sems.at[0])
        await_whole(up, sems.at[1])
        await_whole(down.at[pl.ds(0, half)], sems.at[2])
        await_whole(down.at[pl.ds(half, half)], sems.at[3])

    ffn_tile(f_step, tile, normed, d_ffn, gate, up, down, active, d_gate, d_up, out, d_normed, out_sum, d_sum)


def ffn(normed, d_ffn, gate_pieces, up_pieces, low_pieces, high_pieces, pushed):
    rows, width = normed.shape
    units = gate_pieces[0].shape[1]
    count = len(gate_pieces)
    tile = 256
    row_tile = min(rows, 512)
    once = pl.Buffered(1)
    row_spec = pl.BlockSpec((row_tile, width), lambda i, f: (i, 0), pipeline_mode=once)
    unit_spec = pl.BlockSpec((row_tile, tile), lambda i, f: (i, f))
    unit_shape = jax.ShapeDtypeStruct((rows, units), BF16)
    row_shape = jax.ShapeDtypeStruct((rows, width), BF16)
    body = functools.partial(ffn_body, count, len(low_pieces), tile)
    settings, sems = params(2), [pltpu.SemaphoreType.DMA((4,))]
    if pushed:
        body = functools.partial(pushed_body, count, tile)
        sems = [pltpu.SemaphoreType.DMA((3, units // tile))] * 3
        settings = pltpu.CompilerParams(
            dimension_semantics=("arbitrary",) * 2,
            vmem_limit_bytes=VMEM_BYTES,
            collective_id=5,
            has_side_effects=True,
        )
    return pl.pallas_call(
        body,
        grid=(rows // row_tile, units // tile),
        in_specs=[row_spec, row_spec] + [ANYWHERE] * (2 * count + 2 * len(low_pieces)),
        out_specs=[unit_spec, unit_spec, unit_spec, row_spec, row_spec],
        out_shape=[unit_shape, unit_shape, unit_shape, row_shape, row_shape],
        scratch_shapes=[
            pltpu.VMEM((width, units), BF16),
            pltpu.VMEM((width, units), BF16),
            pltpu.VMEM((units, width), BF16),
            pltpu.VMEM((row_tile, width), F32),
            pltpu.VMEM((row_tile, width), F32),
        ]
        + sems,
        compiler_params=settings,
        cost_estimate=pl.CostEstimate(
            flops=12 * rows * width * units, bytes_accessed=6 * width * units + 14 * rows * width, transcendentals=rows * units
        ),
        name="feed_forward",
    )(normed, d_ffn, *gate_pieces, *up_pieces, *low_pieces, *high_pieces)


def pushed_body(count, tile, normed, d_ffn, *refs):
    groups, rest = [refs[k * count : (k + 1) * count] for k in range(4)], refs[4 * count :]
    active, d_gate, d_up, out, d_normed, gate, up, down, out_sum, d_sum, near, send, recv = rest
    f_step = pl.program_id(1)
    first = (pl.program_id(0) == 0) & (f_step == 0)
    last = (pl.program_id(0) == pl.num_programs(0) - 1) & (f_step == pl.num_programs(1) - 1)
    steps = down.shape[0] // tile
    width = down.shape[1]
    extent = width // (2 * count)
    me = plane_index()
    mate = {"context": lax.axis_index("context") ^ 1}
    mesh_ids = pl.DeviceIdType.MESH

    def push(source, target, w, t):
        return pltpu.make_async_remote_copy(
            src_ref=source,
            dst_ref=target,
            send_sem=send.at[w, t],
            recv_sem=recv.at[w, t],
            device_id=mate,
            device_id_type=mesh_ids,
        )

    def halves(t):
        units = pl.ds(pl.multiple_of(t * tile, tile), tile)
        half = pl.ds(0, width // 2)
        return [gate.at[half, units], up.at[half, units], down.at[units, half]]

    @pl.when(first)
    def _():
        barrier = pltpu.get_barrier_semaphore()
        pl.semaphore_signal(barrier, inc=1, device_id=mate, device_id_type=mesh_ids)
        pl.semaphore_wait(barrier, 1)

        def start(t, carry):
            units = pl.ds(pl.multiple_of(t * tile, tile), tile)
            for i in range(count):
                base = pl.multiple_of((me ^ (2 * i)) * extent, extent)
                rows = pl.ds(base, extent)
                left = pl.ds(base, extent // 2)
                right = pl.ds(pl.multiple_of(base + extent // 2, extent // 2), extent // 2)
                moves = (
                    (0, groups[0][i].at[:, units], gate.at[rows, units]),
                    (1, groups[1][i].at[:, units], up.at[rows, units]),
                    (2, groups[2][i].at[units, :], down.at[units, left]),
                    (2, groups[3][i].at[units, :], down.at[units, right]),
                )
                for w, source, target in moves:
                    push(source, target, w, t).start()
                    pltpu.make_async_copy(source, target, near.at[w, t]).start()
            return carry

        lax.fori_loop(0, steps, start, 0)

    @pl.when(pl.program_id(0) == 0)
    def _():
        for w, half in enumerate(halves(f_step)):
            pltpu.make_async_copy(half, half, near.at[w, f_step]).wait()
            push(half, half, w, f_step).wait_recv()

    ffn_tile(f_step, tile, normed, d_ffn, gate, up, down, active, d_gate, d_up, out, d_normed, out_sum, d_sum)

    @pl.when(last)
    def _():
        def drain(t, carry):
            for w, half in enumerate(halves(t)):
                push(half, half, w, t).wait_send()
            return carry

        lax.fori_loop(0, steps, drain, 0)


def doubled(values, lane, head):
    rolled = pltpu.roll(values.astype(F32), HD, 1).astype(BF16)
    return jnp.where((lane < HD) == (head == 0), values, rolled)


def block_bias(order, seq, r, block):
    per = order.shape[1] // lax.axis_size("context")
    own = order[seq, lax.axis_index("context") * per + pl.program_id(3)]
    other = order[seq, (lax.axis_index("context") ^ r) * per + block]
    return jnp.where(other <= own, 0.0, MASKED_SCORE).astype(F32)


def masked_scores(order, pieces_k, query):
    seq = pl.program_id(0)
    scores = []
    for r, key_rows in enumerate(pieces_k):
        part = lax.dot_general(key_rows, query, (((1,), (1,)), ((), ())), preferred_element_type=F32)
        for block in range(key_rows.shape[0] // BLK):
            bias = block_bias(order, seq, r, block)
            scores.append(part[block * BLK : (block + 1) * BLK] + bias)
    return scores


def attend_body(count, order, query_ref, *rest):
    pieces, (mixture, logs) = rest[:count], rest[count:]
    head = pl.program_id(1)
    lane = lax.broadcasted_iota(jnp.int32, (1, LANES), 1)
    keys = [doubled(piece[:, :LANES], lane, head) for piece in pieces]
    values = [doubled(piece[:, LANES:], lane, head) for piece in pieces]
    query = query_ref[...]
    parts = []
    for side in range(2):
        chosen = (lane < HD) if side == 0 else (lane >= HD)
        scores = masked_scores(order, keys, jnp.where(chosen, query, jnp.zeros_like(query)))
        top = functools.reduce(jnp.maximum, [jnp.max(s, axis=0, keepdims=True) for s in scores])
        powers = [jnp.exp(s - top) for s in scores]
        total = sum(jnp.sum(p, axis=0, keepdims=True) for p in powers)
        low = jnp.concatenate([p.astype(BF16) for p in powers], axis=0)
        whole = jnp.concatenate(values, axis=0)
        mixed = lax.dot_general(whole, low, (((0,), (0,)), ((), ())), preferred_element_type=F32)
        parts.append(mixed / total)
        logs[side : side + 1, :] = top + jnp.log(total)
    row = lax.broadcasted_iota(jnp.int32, (LANES, 1), 0)
    mixture[...] = jnp.where(row < HD, parts[0], parts[1]).T.astype(BF16)


def attend_specs(order, queries, pieces, group_pairs):
    seqs = order.shape[0]
    rows = queries.shape[0] // seqs
    tiles = rows // BLK
    grid = (seqs, 2, group_pairs, tiles)
    q_spec = pl.BlockSpec((BLK, LANES), lambda s, h, g, t: (s * tiles + t, h * group_pairs + g))
    kv_spec = pl.BlockSpec((rows, 2 * LANES), lambda s, h, g, t: (s, 0))
    kv_ins = [pl.BlockSpec((None, rows, 2 * LANES), lambda s, h, g, t, r=r: (r, s, 0)) for r in range(pieces.shape[0])]
    log_spec = pl.BlockSpec((None, 2, BLK), lambda s, h, g, t: (h * group_pairs + g, 0, s * tiles + t))
    return grid, q_spec, kv_spec, kv_ins, log_spec


def attend(order, queries, pieces):
    rows, q_width = queries.shape
    pairs = q_width // LANES
    grid, q_spec, _, kv_ins, log_spec = attend_specs(order, queries, pieces, pairs // 2)
    keys = rows * pieces.shape[0] // order.shape[0]
    return pl.pallas_call(
        functools.partial(attend_body, pieces.shape[0]),
        grid=grid,
        in_specs=[pl.BlockSpec(memory_space=pltpu.SMEM), q_spec] + kv_ins,
        out_specs=[q_spec, log_spec],
        out_shape=[jax.ShapeDtypeStruct((rows, q_width), BF16), jax.ShapeDtypeStruct((pairs, 2, rows), F32)],
        compiler_params=params(4),
        cost_estimate=pl.CostEstimate(
            flops=8 * rows * keys * q_width * 2, bytes_accessed=8 * rows * q_width, transcendentals=rows * keys * q_width // HD
        ),
        name="attend",
    )(order, queries, *[pieces] * pieces.shape[0])


def attend_back_body(count, order, query_ref, grad_ref, logs, *rest):
    pieces, rest = rest[:count], rest[count:]
    d_query, outs, (d_key_sum, d_value_sum) = rest[0], rest[1 : 1 + count], rest[1 + count :]
    head, pair, tile = pl.program_id(1), pl.program_id(2), pl.program_id(3)
    lane = lax.broadcasted_iota(jnp.int32, (1, LANES), 1)
    keys = [doubled(piece[:, :LANES], lane, head) for piece in pieces]
    values = jnp.concatenate([doubled(piece[:, LANES:], lane, head) for piece in pieces], axis=0)
    whole_keys = jnp.concatenate(keys, axis=0)
    parts, d_keys, d_values = [], 0.0, 0.0
    for side in range(2):
        chosen = (lane < HD) if side == 0 else (lane >= HD)
        query = jnp.where(chosen, query_ref[...], jnp.zeros_like(query_ref[...]))
        grad = jnp.where(chosen, grad_ref[...], jnp.zeros_like(grad_ref[...]))
        scores = jnp.concatenate(masked_scores(order, keys, query), axis=0)
        soft = jnp.exp(scores - logs[side : side + 1, :])
        d_soft = lax.dot_general(values, grad, (((1,), (1,)), ((), ())), preferred_element_type=F32)
        inner = jnp.sum(soft * d_soft, axis=0, keepdims=True)
        d_scores = (soft * (d_soft - inner)).astype(BF16)
        d_values += jnp.dot(soft.astype(BF16), grad, preferred_element_type=F32)
        d_keys += jnp.dot(d_scores, query, preferred_element_type=F32)
        parts.append(lax.dot_general(whole_keys, d_scores, (((0,), (0,)), ((), ())), preferred_element_type=F32))
    row = lax.broadcasted_iota(jnp.int32, (LANES, 1), 0)
    d_query[...] = jnp.where(row < HD, parts[0], parts[1]).T * SCORE_SCALE

    first = (pair == 0) & (tile == 0)
    last = (pair == pl.num_programs(2) - 1) & (tile == pl.num_programs(3) - 1)

    @pl.when(first)
    def _():
        d_key_sum[...] = d_keys
        d_value_sum[...] = d_values

    @pl.when(jnp.logical_not(first))
    def _():
        d_key_sum[...] += d_keys
        d_value_sum[...] += d_values

    @pl.when(last)
    def _():
        wanted = (lane < HD) == (head == 0)
        rows = outs[0].shape[0]
        for r, out in enumerate(outs):
            for base, total in ((0, d_key_sum), (LANES, d_value_sum)):
                part = total[r * rows : (r + 1) * rows, :]
                both = (part + pltpu.roll(part, HD, 1)).astype(out.dtype)
                spot = pl.ds(base, LANES)

                @pl.when(head == 0)
                def _():
                    out[:, spot] = both

                @pl.when(head == 1)
                def _():
                    out[:, spot] = jnp.where(wanted, both.astype(F32), out[:, spot].astype(F32)).astype(out.dtype)


def attend_back(order, queries, grads, logs, pieces):
    rows, q_width = queries.shape
    pairs = q_width // LANES
    grid, q_spec, kv_spec, kv_ins, log_spec = attend_specs(order, queries, pieces, pairs // 2)
    keys = rows * pieces.shape[0] // order.shape[0]
    return pl.pallas_call(
        functools.partial(attend_back_body, pieces.shape[0]),
        grid=grid,
        in_specs=[pl.BlockSpec(memory_space=pltpu.SMEM), q_spec, q_spec, log_spec] + kv_ins,
        out_specs=[q_spec] + [kv_spec] * pieces.shape[0],
        out_shape=[jax.ShapeDtypeStruct((rows, q_width), F32)]
        + [jax.ShapeDtypeStruct((rows, 2 * LANES), F32 if r % 2 == 0 else BF16) for r in range(pieces.shape[0])],
        scratch_shapes=[pltpu.VMEM((keys, LANES), F32), pltpu.VMEM((keys, LANES), F32)],
        compiler_params=params(4),
        cost_estimate=pl.CostEstimate(
            flops=20 * rows * keys * q_width * 2, bytes_accessed=12 * rows * q_width, transcendentals=rows * keys * q_width // HD
        ),
        name="attend_back",
    )(order, queries, grads, logs, *[pieces] * pieces.shape[0])


def line_steps(rows):
    half = rows // 2
    sub = 16
    return half, sub, half // sub


def line_body(finish, keep_state, gain_sum, n_in, extra, *refs):
    partial, ins, rest = refs[0], refs[1 : 1 + n_in], refs[1 + n_in :]
    if extra:
        world, n_grad, plan, whole_plane = extra
        ffn_out, rest = (None, rest) if whole_plane else (rest[0], rest[1:])
        grad_ins, rest = rest[:n_grad], rest[n_grad:]
    result, rest = rest[0], rest[1:]
    state_out, rest = (rest[0], rest[1:]) if keep_state else (None, rest)
    gain_out, rest = (rest[0], rest[1:]) if gain_sum else (None, rest)
    if extra:
        spread = len(plan) if whole_plane else world // 2 * len(plan)
        n_parts = 0 if whole_plane else 4
        out_parts, grad_outs, rest = rest[:n_parts], rest[n_parts : n_parts + spread], rest[n_parts + spread :]
    from_outer, from_peer, staged, send, recv = rest[:5]
    half, sub, count = line_steps(partial.shape[0])
    me = lax.axis_index("tensor")
    side = me // 2
    inner = lax.rem(me, 3) != 0
    to_outer, to_inner, to_peer = side * 3, 1 + side, 3 - me
    near, far = side * half, (1 - side) * half

    def rows(base, k):
        return pl.ds(pl.multiple_of(base + k * sub, sub), sub)

    def remote(source, target, s, r, k, where):
        return pltpu.make_async_remote_copy(
            src_ref=source,
            dst_ref=target,
            send_sem=send.at[s, k],
            recv_sem=recv.at[r, k],
            device_id={"tensor": where},
            device_id_type=pl.DeviceIdType.MESH,
        )

    def up_far(k):
        return remote(partial.at[rows(far, k)], from_outer.at[0, rows(0, k)], 0, 0, k, to_inner)

    def up_near(k):
        return remote(partial.at[rows(near, k)], from_outer.at[1, rows(0, k)], 1, 1, k, to_inner)

    def across(k):
        return remote(staged.at[rows(0, k)], from_peer.at[rows(0, k)], 0, 2, k, to_peer)

    def over(k, base):
        return remote(result.at[rows(base, k)], result.at[rows(base, k)], 2, 4, k, to_peer)

    def down_near(k):
        return remote(result.at[rows(near, k)], result.at[rows(near, k)], 1, 3, k, to_outer)

    def down_far(k):
        return remote(result.at[rows(far, k)], result.at[rows(far, k)], 3, 4, k, to_outer)

    barrier = pltpu.get_barrier_semaphore()

    def greet(where):
        pl.semaphore_signal(barrier, inc=1, device_id={"tensor": where}, device_id_type=pl.DeviceIdType.MESH)

    if extra:
        mate = {"context": lax.axis_index("context") ^ 1}
        pl.semaphore_signal(barrier, inc=1, device_id=mate, device_id_type=pl.DeviceIdType.MESH)
        for where in ({"context": lax.axis_index("context") ^ 2}, {"shard": lax.axis_index("shard") ^ 1}):
            pl.semaphore_signal(barrier, inc=1, device_id=where, device_id_type=pl.DeviceIdType.MESH)
        if whole_plane:
            grad_work, grad_rest, grad_finish = plane_parts(world, plan, grad_ins, grad_outs, rest[5:])
        else:
            jobs = len(plan)
            crossed, grad_outs = grad_outs[-jobs:], grad_outs[:-jobs]
            grad_work, grad_finish = grads_parts(
                world, plan, grad_ins, grad_outs, rest[5:-2], crossed, rest[-2:]
            )
            grad_rest = lambda: None
    block = partial.shape[0] // world if extra else 0
    more_greetings = 3 if extra else 0
    last_work = world + 1 if extra and whole_plane else world if extra else 0

    def work(q):
        grad_work(q)
        if not whole_plane:
            out_work(q)

    def out_work(q):
        rows_q = pl.ds(pl.multiple_of(q * block, block), block)
        value = RESIDUAL_SCALE * ffn_out[rows_q, :].astype(F32)
        quarter = 2 * block * world // 8
        chunk = lax.rem(q * 4 // world - me + 4, 4)
        place = pl.ds(pl.multiple_of(lax.rem(q * block, quarter), block), block)
        owned = inner & (q * 2 // world == side)

        for part in range(4):

            @pl.when(owned & (chunk == part))
            def _():
                mine = pl.ds(pl.multiple_of(lax.rem(q * block, half), block), block)
                out_parts[part][place, :] = (value + ins[0][mine, :]).astype(BF16)

            @pl.when(jnp.logical_not(owned) & (chunk == part))
            def _():
                out_parts[part][place, :] = value.astype(BF16)

    if gain_sum:
        gain_out[...] = jnp.zeros_like(gain_out)

    @pl.when(inner)
    def _():
        greet(to_outer)
        greet(to_peer)
        pl.semaphore_wait(barrier, 2 + more_greetings)

        def step(k, carry):
            @pl.when(k < count)
            def _():
                up_far(k).wait_recv()
                total = partial[rows(far, k), :].astype(F32) + from_outer[0, rows(0, k), :].astype(F32)
                staged[rows(0, k), :] = total.astype(BF16)
                across(k).start()

            @pl.when((k >= 1) & (k <= count))
            def _():
                j = k - 1
                up_near(j).wait_recv()
                across(j).wait_recv()
                total = partial[rows(near, j), :].astype(F32) + from_outer[1, rows(0, j), :].astype(F32)
                total = total + from_peer[rows(0, j), :].astype(F32)
                low, state, gains = finish(total, rows(near, j), rows(0, j), ins)
                result[rows(near, j), :] = low
                if keep_state:
                    state_out[rows(0, j), :] = state
                if gain_sum:
                    gain_out[...] += jnp.sum(gains.reshape(sub // 8, 8, gains.shape[1]), axis=0)
                down_near(j).start()
                over(j, near).start()

            @pl.when(k >= 3)
            def _():
                over(k - 3, far).wait_recv()
                down_far(k - 3).start()

            if extra:

                @pl.when((lax.rem(k, count // world) == 0) & (k < last_work * (count // world)))
                def _():
                    work(k // (count // world))

            return carry

        lax.fori_loop(0, count + 3, step, 0)

        def drain(k, carry):
            across(k).wait_send()
            down_near(k).wait_send()
            over(k, near).wait_send()
            down_far(k).wait_send()
            return carry

        lax.fori_loop(0, count, drain, 0)

    @pl.when(jnp.logical_not(inner))
    def _():
        greet(to_inner)
        pl.semaphore_wait(barrier, 1 + more_greetings)

        def step(k, carry):
            up_far(k).start()
            up_near(k).start()
            return carry

        lax.fori_loop(0, count, step, 0)
        if extra:

            def busy(q, carry):
                work(q)
                return carry

            lax.fori_loop(0, last_work, busy, 0)

        def drain(k, carry):
            down_near(k).wait_recv()
            down_far(k).wait_recv()
            up_far(k).wait_send()
            up_near(k).wait_send()
            return carry

        lax.fori_loop(0, count, drain, 0)

    if extra:
        grad_rest()
        grad_finish()


def line_sum(partial, ins, finish, keep_state, gain_sum, identity, ffn_out=None, pairs=()):
    rows, width = partial.shape
    half, _, count = line_steps(rows)
    vmem = pl.BlockSpec(memory_space=pltpu.VMEM)
    shapes = [jax.ShapeDtypeStruct((rows, width), BF16)]
    if keep_state:
        shapes.append(jax.ShapeDtypeStruct((half, width), F32))
    if gain_sum:
        shapes.append(jax.ShapeDtypeStruct((8, width), F32))
    specs, more, scratch, extra = [vmem] * len(shapes), [], [], None
    if pairs:
        arrays, plan = unique_arrays(pairs)
        whole_plane = ffn_out is None
        extra = (plane_size(), len(arrays), plan, whole_plane)
        outs, scratch = grads_shapes(pairs)
        if whole_plane:
            more = arrays
            pieces = [(left.shape[1] // plane_size(), high - low) for left, right, low, high in pairs]
            shapes += [jax.ShapeDtypeStruct(shape, F32) for shape in pieces]
            specs += [vmem] * len(pieces)
            scratch = scratch[:-1] + [pltpu.VMEM((3,) + shape, BF16) for shape in pieces]
            scratch += [pltpu.SemaphoreType.DMA((3, len(pairs)))] * 2
        else:
            more = [ffn_out] + arrays
            shapes += [jax.ShapeDtypeStruct((rows // 4, width), BF16)] * 4 + outs
            specs += [vmem] * 4 + [ANYWHERE] * len(outs)
            scratch = scratch + [pltpu.SemaphoreType.DMA((len(pairs),))] * 2
    return pl.pallas_call(
        functools.partial(line_body, finish, keep_state, gain_sum, len(ins), extra),
        in_specs=[vmem] * (1 + len(ins) + len(more)),
        out_specs=specs,
        out_shape=shapes,
        scratch_shapes=[
            pltpu.VMEM((2, half, width), BF16),
            pltpu.VMEM((half, width), BF16),
            pltpu.VMEM((half, width), BF16),
            pltpu.SemaphoreType.DMA((4, count)),
            pltpu.SemaphoreType.DMA((5, count)),
        ]
        + scratch,
        compiler_params=pltpu.CompilerParams(
            collective_id=identity, has_side_effects=True, vmem_limit_bytes=VMEM_BYTES
        ),
        cost_estimate=pl.CostEstimate(flops=0, bytes_accessed=100 * rows * width, transcendentals=0),
    )(partial, *ins, *more)


def mean_square(values):
    return lax.rsqrt(jnp.mean(values * values, axis=1, keepdims=True) + EPSILON)


def finish_attention(total, whole, own, ins):
    tokens, gain = ins
    hidden = tokens[whole, :].astype(F32) + RESIDUAL_SCALE * total
    return (hidden * mean_square(hidden) * gain[...]).astype(BF16), hidden, None


def norm_pull(d_normed, values, gain):
    inverse = mean_square(values)
    scaled = gain * d_normed
    inner = jnp.mean(scaled * values, axis=1, keepdims=True)
    return inverse * scaled - values * inverse * inverse * inverse * inner, d_normed * values * inverse


def finish_ffn_back(total, whole, own, ins):
    hidden, grads, gain = ins
    pulled, gains = norm_pull(total, hidden[own, :], gain[...])
    d_hidden = grads[whole, :].astype(F32) + pulled
    return (RESIDUAL_SCALE * d_hidden).astype(BF16), d_hidden, gains


def finish_attention_back(total, whole, own, ins):
    tokens, d_hidden, gain = ins
    pulled, gains = norm_pull(total, tokens[whole, :].astype(F32), gain[...])
    return (d_hidden[own, :] + pulled).astype(BF16), None, gains


def front_fits():
    return lax.axis_size("shard") == 2 and lax.axis_size("context") == 4


def front_body(*refs):
    tokens, gain_piece, cosine, sine, w_query, w_key, w_value, w_output = refs[:8]
    normed, queries, kv, weight, output, gains = refs[8:14]
    local_sem, send, recv = refs[14:]
    me = plane_index()
    extent = weight.shape[0] // 8
    q_width = queries.shape[1]
    k_width = kv.shape[2] // 2
    context, shard = lax.axis_index("context"), lax.axis_index("shard")
    peers = {1: {"context": context ^ 1}, 2: {"context": context ^ 2}, 4: {"shard": shard ^ 1}}
    mesh_ids = pl.DeviceIdType.MESH
    barrier = pltpu.get_barrier_semaphore()
    for bit in (1, 2, 4):
        pl.semaphore_signal(barrier, inc=1, device_id=peers[bit], device_id_type=mesh_ids)

    def start(r):
        return pl.multiple_of((me ^ r) * extent, extent)

    def qkv_at(r, part=None):
        size = extent if part is None else extent // 2
        base = start(r) + (part or 0) * size
        return weight.at[pl.ds(pl.multiple_of(base, size), size)]

    def output_at(r, part=None):
        columns = pl.ds(start(r), extent)
        if part is None:
            return output.at[:, columns]
        size = output.shape[0] // 2
        return output.at[pl.ds(part * size, size), columns]

    def gains_at(r):
        return gains.at[:, pl.ds(start(r), extent)]

    spots = {}

    def remote(name, ref, bit, target=None):
        index = spots.setdefault(name, len(spots))
        return pltpu.make_async_remote_copy(
            src_ref=ref,
            dst_ref=ref if target is None else target,
            send_sem=send.at[index],
            recv_sem=recv.at[index],
            device_id=peers[bit],
            device_id_type=mesh_ids,
        )

    locals_ = [
        pltpu.make_async_copy(gain_piece, gains_at(0), local_sem.at[0]),
        pltpu.make_async_copy(w_query, weight.at[pl.ds(start(0), extent), pl.ds(0, q_width)], local_sem.at[1]),
        pltpu.make_async_copy(w_key, weight.at[pl.ds(start(0), extent), pl.ds(q_width, k_width)], local_sem.at[2]),
        pltpu.make_async_copy(
            w_value, weight.at[pl.ds(start(0), extent), pl.ds(q_width + k_width, k_width)], local_sem.at[3]
        ),
        pltpu.make_async_copy(w_output, output_at(0), local_sem.at[4]),
    ]
    for copy in locals_:
        copy.start()

    begun = []

    def begin(copy):
        copy.start()
        begun.append(copy)
        return copy

    pl.semaphore_wait(barrier, 3)
    locals_[0].wait()
    gain_in = [begin(remote("g2", gains_at(0), 2)), begin(remote("g4", gains_at(0), 4))]
    gain_core = [begin(remote("gc0", gains_at(0), 1))]
    for copy in locals_[1:4]:
        copy.wait()
    near, far = begin(remote("q2", qkv_at(0), 2)), begin(remote("q4", qkv_at(0), 4))
    core = [begin(remote("qc0", qkv_at(0), 1))]
    locals_[4].wait()
    out_near, out_far = begin(remote("o2", output_at(0), 2)), begin(remote("o4", output_at(0), 4))
    out_core = [begin(remote("oc0", output_at(0), 1))]

    gain_in[0].wait_recv()
    gain_in[1].wait_recv()
    diagonal = begin(remote("g6", gains_at(4), 2))
    gain_core += [begin(remote("gc2", gains_at(2), 1)), begin(remote("gc4", gains_at(4), 1))]
    diagonal.wait_recv()
    gain_core.append(begin(remote("gc6", gains_at(6), 1)))
    for copy in gain_core:
        copy.wait_recv()

    rows = tokens.shape[0]
    tile = 128

    def norm(i, carry):
        spot = pl.ds(pl.multiple_of(i * tile, tile), tile)
        values = tokens[spot, :].astype(F32)
        normed[spot, :] = (values * mean_square(values) * gains[0:1, :]).astype(BF16)
        return carry

    lax.fori_loop(0, rows // tile, norm, 0)

    far.wait_recv()
    cross = [begin(remote("q6a", qkv_at(4, 0), 2))]
    core.append(begin(remote("qc4", qkv_at(4), 1)))
    near.wait_recv()
    cross.append(begin(remote("q6b", qkv_at(2, 1), 4)))
    core.append(begin(remote("qc2", qkv_at(2), 1)))
    cross[0].wait_recv()
    cross[1].wait_recv()
    core.append(begin(remote("qc6", qkv_at(6), 1)))
    out_far.wait_recv()
    out_cross = [begin(remote("o6a", output_at(4, 0), 2))]
    out_core.append(begin(remote("oc4", output_at(4), 1)))
    out_near.wait_recv()
    out_cross.append(begin(remote("o6b", output_at(2, 1), 4)))
    out_core.append(begin(remote("oc2", output_at(2), 1)))
    for copy in core:
        copy.wait_recv()

    lane = lax.broadcasted_iota(jnp.int32, (1, LANES), 1)

    def rotated(part, spot):
        return part * cosine[spot, :] + turned(part, lane, 1.0) * sine[spot, :]

    def keys(i, carry):
        spot = pl.ds(pl.multiple_of(i * 256, 256), 256)
        part = jnp.dot(normed[spot, :], weight[:, q_width:], preferred_element_type=F32)
        kv[0, spot, :k_width] = rotated(part[:, :k_width], spot).astype(BF16)
        kv[0, spot, k_width:] = part[:, k_width:].astype(BF16)
        return carry

    lax.fori_loop(0, rows // 256, keys, 0)
    kv_near = begin(remote("k2", kv.at[0], 2, kv.at[2]))
    kv_core = begin(remote("k1", kv.at[0], 1, kv.at[1]))

    def query(i, carry):
        spot = pl.ds(pl.multiple_of(i * 256, 256), 256)
        part = jnp.dot(normed[spot, :], weight[:, :q_width], preferred_element_type=F32)
        for base in range(0, q_width, LANES):
            turned_part = rotated(part[:, base : base + LANES], spot).astype(BF16)
            queries[spot, base : base + LANES] = (turned_part * SCORE_SCALE).astype(BF16)
        return carry

    lax.fori_loop(0, rows // 256, query, 0)
    kv_near.wait_recv()
    kv_last = begin(remote("k3", kv.at[2], 1, kv.at[3]))
    out_cross[0].wait_recv()
    out_cross[1].wait_recv()
    out_core.append(begin(remote("oc6", output_at(6), 1)))
    for copy in out_core:
        copy.wait_recv()
    kv_core.wait_recv()
    kv_last.wait_recv()
    for copy in begun:
        copy.wait_send()


def front(tokens, gains, cosine, sine, w_query, w_key, w_value, w_output):
    rows, width = tokens.shape
    q_width, k_width = w_query.shape[1], w_key.shape[1]
    total = q_width + 2 * k_width
    vmem = pl.BlockSpec(memory_space=pltpu.VMEM)
    return pl.pallas_call(
        front_body,
        in_specs=[vmem] * 4 + [ANYWHERE] * 4,
        out_specs=[vmem] * 6,
        out_shape=[
            jax.ShapeDtypeStruct((rows, width), BF16),
            jax.ShapeDtypeStruct((rows, q_width), BF16),
            jax.ShapeDtypeStruct((4, rows, 2 * k_width), BF16),
            jax.ShapeDtypeStruct((width, total), BF16),
            jax.ShapeDtypeStruct((w_output.shape[0], width), BF16),
            jax.ShapeDtypeStruct((8, width), F32),
        ],
        scratch_shapes=[
            pltpu.SemaphoreType.DMA((5,)),
            pltpu.SemaphoreType.DMA((27,)),
            pltpu.SemaphoreType.DMA((27,)),
        ],
        compiler_params=pltpu.CompilerParams(collective_id=6, has_side_effects=True, vmem_limit_bytes=VMEM_BYTES),
        cost_estimate=pl.CostEstimate(
            flops=2 * rows * width * total, bytes_accessed=10 * rows * width, transcendentals=0
        ),
        name="front",
    )(tokens, gains, cosine, sine, w_query, w_key, w_value, w_output)


def unique_arrays(pairs):
    arrays, plan = [], []
    for left, right, low, high in pairs:
        spots = []
        for value in (left, right):
            known = [i for i, array in enumerate(arrays) if array is value]
            if not known:
                arrays.append(value)
            spots.append(known[0] if known else len(arrays) - 1)
        plan.append((spots[0], spots[1], low, high))
    return arrays, tuple(plan)


def grads_parts(count, plan, ins, outs, scratch, crossed=(), cross_sems=()):
    halves, jobs = count // 2, len(plan)
    sent, got, own = scratch[:jobs], scratch[jobs : 2 * jobs], scratch[2 * jobs : 3 * jobs]
    send, recv, done = scratch[3 * jobs : 3 * jobs + 3]
    kept = halves - 1 if crossed else halves
    cross = []
    for j, landed in enumerate(crossed):
        ways = ({"shard": lax.axis_index("shard") ^ 1}, {"context": lax.axis_index("context") ^ 2})
        cross.append(
            pltpu.make_async_remote_copy(
                src_ref=got[j].at[halves - 1],
                dst_ref=landed,
                send_sem=cross_sems[0].at[j],
                recv_sem=cross_sems[1].at[j],
                device_id=ways[j % 2],
                device_id_type=pl.DeviceIdType.MESH,
            )
        )
    me = plane_index()
    mate = {"context": lax.axis_index("context") ^ 1}

    def piece(j, r):
        left, right, low, high = plan[j]
        extent = ins[left].shape[1] // count
        columns = pl.ds(pl.multiple_of((me ^ r) * extent, extent), extent)
        return lax.dot_general(
            ins[left][:, columns], ins[right][:, low:high], (((0,), (0,)), ((), ())), preferred_element_type=F32
        )

    def across(j, i):
        return pltpu.make_async_remote_copy(
            src_ref=sent[j].at[i],
            dst_ref=got[j].at[i],
            send_sem=send.at[j, i],
            recv_sem=recv.at[j, i],
            device_id=mate,
            device_id_type=pl.DeviceIdType.MESH,
        )

    def odd(i):
        for j in range(jobs):
            sent[j][i] = piece(j, 2 * i + 1).astype(BF16)
            across(j, i).start()

    def even(i):
        for j in range(jobs):
            value = piece(j, 2 * i)
            across(j, i).wait_recv()
            value = value + got[j][i].astype(F32)

            @pl.when(i > 0)
            def _():
                got[j][i] = value.astype(BF16)

            @pl.when(i == 0)
            def _():
                own[j][...] = value

        for known in range(kept):

            @pl.when(i == known)
            def _():
                for j in range(jobs):
                    source = got[j].at[known] if known else own[j]
                    pltpu.make_async_copy(source, outs[known * jobs + j], done.at[known, j]).start()

        if crossed:

            @pl.when(i == halves - 1)
            def _():
                for copy in cross:
                    copy.start()

    def work(q):
        @pl.when(q < halves)
        def _():
            odd(halves - 1 - q)

        @pl.when(q >= halves)
        def _():
            even(count - 1 - q)

    def finish():
        for known in range(halves):
            for j in range(jobs):
                source = got[j].at[known] if known else own[j]
                if known < kept:
                    pltpu.make_async_copy(source, outs[known * jobs + j], done.at[known, j]).wait()
                across(j, known).wait_send()
        for copy in cross:
            copy.wait()

    return work, finish


def plane_parts(count, plan, ins, outs, scratch):
    jobs = len(plan)
    sent, got, own = scratch[:jobs], scratch[jobs : 2 * jobs], scratch[2 * jobs : 3 * jobs]
    send, recv = scratch[3 * jobs : 3 * jobs + 2]
    landed = scratch[3 * jobs + 2 : 4 * jobs + 2]
    plane_send, plane_recv = scratch[4 * jobs + 2 :]
    me = plane_index()
    core = {"context": lax.axis_index("context") ^ 1}
    peers = ({"context": lax.axis_index("context") ^ 2}, {"shard": lax.axis_index("shard") ^ 1})

    def piece(j, r):
        left, right, low, high = plan[j]
        extent = ins[left].shape[1] // count
        columns = pl.ds(pl.multiple_of((me ^ r) * extent, extent), extent)
        return lax.dot_general(
            ins[left][:, columns], ins[right][:, low:high], (((0,), (0,)), ((), ())), preferred_element_type=F32
        )

    def across(j, i):
        return pltpu.make_async_remote_copy(
            src_ref=sent[j].at[i],
            dst_ref=got[j].at[i],
            send_sem=send.at[j, i],
            recv_sem=recv.at[j, i],
            device_id=core,
            device_id_type=pl.DeviceIdType.MESH,
        )

    def move(j, i, slot, way):
        return pltpu.make_async_remote_copy(
            src_ref=got[j].at[i],
            dst_ref=landed[j].at[slot],
            send_sem=plane_send.at[slot, j],
            recv_sem=plane_recv.at[slot, j],
            device_id=peers[way],
            device_id_type=pl.DeviceIdType.MESH,
        )

    first = [(j + 1) % 2 for j in range(jobs)]
    cross = [move(j, 3, 2, first[j]) for j in range(jobs)]
    early = [move(j, 2 if first[j] else 1, 1 if first[j] else 0, first[j]) for j in range(jobs)]
    late = [move(j, 1 if first[j] else 2, 0 if first[j] else 1, 1 - first[j]) for j in range(jobs)]

    def work(q):
        @pl.when(q < 4)
        def _():
            i = 3 - q
            for j in range(jobs):
                sent[j][i] = piece(j, 2 * i + 1).astype(BF16)
                across(j, i).start()

        @pl.when(q == 8)
        def _():
            for j in range(jobs):
                kept = 1 if first[j] else 2
                cross[j].wait_recv()
                got[j][kept] = (got[j][kept].astype(F32) + landed[j][2].astype(F32)).astype(BF16)
                late[j].start()

        @pl.when((q >= 4) & (q < 8))
        def _():
            i = 7 - q
            for j in range(jobs):
                value = piece(j, 2 * i)
                across(j, i).wait_recv()
                value = value + got[j][i].astype(F32)

                @pl.when(i > 0)
                def _():
                    got[j][i] = value.astype(BF16)

                @pl.when(i == 0)
                def _():
                    own[j][...] = value

        @pl.when(q == 4)
        def _():
            for j in range(jobs):
                cross[j].start()

        @pl.when(q == 7)
        def _():
            for j in range(jobs):
                early[j].start()

    def rest():
        for j in range(jobs):
            early[j].wait_recv()
            late[j].wait_recv()
            outs[j][...] = own[j][...] + landed[j][0].astype(F32) + landed[j][1].astype(F32)

    def finish():
        for j in range(jobs):
            for copy in (cross[j], early[j], late[j]):
                copy.wait_send()
            for i in range(4):
                across(j, i).wait_send()

    return work, rest, finish


def grads_body(count, n_in, plan, *refs):
    ins, rest = refs[:n_in], refs[n_in:]
    spread = count // 2 * len(plan)
    outs, scratch = rest[:spread], rest[spread:]
    work, finish = grads_parts(count, plan, ins, outs, scratch)
    barrier = pltpu.get_barrier_semaphore()
    mate = {"context": lax.axis_index("context") ^ 1}
    pl.semaphore_signal(barrier, inc=1, device_id=mate, device_id_type=pl.DeviceIdType.MESH)
    pl.semaphore_wait(barrier, 1)

    def step(q, carry):
        work(q)
        return carry

    lax.fori_loop(0, count, step, 0)
    finish()


def grads_shapes(pairs):
    count = plane_size()
    halves = count // 2
    shapes = [(left.shape[1] // count, high - low) for left, right, low, high in pairs]
    outs = [jax.ShapeDtypeStruct(shape, BF16 if i else F32) for i in range(halves) for shape in shapes]
    scratch = [pltpu.VMEM((halves,) + shape, BF16) for shape in shapes] * 2
    scratch += [pltpu.VMEM(shape, F32) for shape in shapes]
    sems = [(len(pairs), halves), (len(pairs), halves), (halves, len(pairs))]
    return outs, scratch + [pltpu.SemaphoreType.DMA(shape) for shape in sems]


def grads_named(flat, jobs):
    return [{2 * i: flat[i * jobs + j] for i in range(len(flat) // jobs)} for j in range(jobs)]


def grads_fit(pairs):
    return all((pair[0].shape[1] // plane_size()) % LANES == 0 for pair in pairs)


def plane_grads(pairs, identity):
    count = plane_size()
    jobs = len(pairs)
    extents = [pair[0].shape[1] // count for pair in pairs]
    arrays, plan = unique_arrays(pairs)
    if not grads_fit(pairs):
        me = plane_index()
        sides = []
        for (left, right, low, high), e in zip(pairs, extents):
            columns = lambda r: lax.dynamic_slice_in_dim(left, (me ^ r) * e, e, 1)
            whole = {r: weight_grad(columns(r), right[:, low:high]).astype(BF16) for r in range(count)}
            sides.append({r: take_sum(whole, 1, r) for r in range(0, count, 2)})
        return sides
    outs, scratch = grads_shapes(pairs)
    flat = pl.pallas_call(
        functools.partial(grads_body, count, len(arrays), plan),
        in_specs=[pl.BlockSpec(memory_space=pltpu.VMEM)] * len(arrays),
        out_specs=[ANYWHERE] * len(outs),
        out_shape=outs,
        scratch_shapes=scratch,
        compiler_params=pltpu.CompilerParams(
            collective_id=identity, has_side_effects=True, vmem_limit_bytes=VMEM_BYTES
        ),
        cost_estimate=pl.CostEstimate(
            flops=sum(2 * left.shape[0] * left.shape[1] * (high - low) for left, _, low, high in pairs),
            bytes_accessed=sum(2 * left.shape[1] * (high - low) for left, _, low, high in pairs),
            transcendentals=0,
        ),
    )(*arrays)
    return grads_named(flat, jobs)


def after(value, *others):
    return lax.optimization_barrier((value,) + others)[0] if others else value


def gather_context(piece):
    size = lax.axis_size("context")
    held = {0: piece}
    bit = size // 2
    while bit:
        for r in list(held):
            held[r | bit] = swap(held[r], "context", size, bit)
        bit //= 2
    return [held[r] for r in range(size)]


def reduce_context(pieces):
    size = len(pieces)
    held = dict(enumerate(pieces))
    bit = 1
    while bit < size:
        held = {
            r: held[r].astype(F32) + swap(held[r | bit].astype(BF16), "context", size, bit).astype(F32)
            for r in held
            if not r & bit
        }
        bit *= 2
    return held[0]


def stored_places(order_row, first, count):
    stored = first + jnp.arange(count, dtype=jnp.int32)
    picks = (stored // BLK)[:, None] == jnp.arange(order_row.shape[0], dtype=jnp.int32)[None, :]
    return jnp.sum(jnp.where(picks, order_row[None, :], 0), axis=1) * BLK + stored % BLK


def rope_tables(order, local_len):
    first = lax.axis_index("context") * local_len
    places = jnp.concatenate([stored_places(order[s], first, local_len) for s in range(order.shape[0])])
    half = HD // 2
    inverse = jnp.exp(jnp.arange(half, dtype=F32) * (-2.0 * math.log(ROPE_BASE) / HD))
    angles = places.astype(F32)[:, None] * jnp.tile(inverse, LANES // half)[None, :]
    return jnp.cos(angles), jnp.sin(angles)


def weight_grad(left, right):
    return lax.dot_general(left, right, (((0,), (0,)), ((), ())), preferred_element_type=F32)


def local(
    tokens, block_order, w_query, w_key, w_value, w_output, w_gate, w_up, w_down, norm_attn, norm_ffn, grad_out
):
    seqs, local_len, width = tokens.shape
    rows = seqs * local_len
    size = plane_size()
    z = lax.axis_index("tensor")
    token_rows = tokens.reshape(rows, width)
    grad_rows = grad_out.reshape(rows, width)
    q_width, kv_width = w_query.shape[1], w_key.shape[1]
    units = w_down.shape[0]
    half = units // 2

    cosine, sine = rope_tables(block_order, local_len)
    if front_fits():
        gain_piece = jnp.pad(jnp.stack([norm_attn, norm_ffn]).astype(F32), ((0, 6), (0, 0)))
        normed, queries, kv_pieces, w_qkv, w_out, gains = front(
            token_rows, gain_piece, cosine, sine, w_query, w_key, w_value, w_output
        )
        qkv_pieces, output_pieces = [w_qkv], [w_out]
        early, late = [queries], [queries]
        gain_attn, gain_ffn = gains[0:1], gains[1:2]
    else:
        gains = gather_small(jnp.stack([norm_attn, norm_ffn])).reshape(2, width)
        gain_attn, gain_ffn = gains[0:1], gains[1:2]
        w_qkv = jnp.concatenate([w_query, w_key, w_value], axis=1)
        qkv_pieces, output_pieces = gather_pair(w_qkv, w_output)
        normed, queries, keys_values = project_qkv(token_rows, gain_attn, cosine, sine, qkv_pieces, q_width)
        kv_pieces = jnp.stack(gather_context(keys_values))
        early, late = [qkv_pieces[-2]], [kv_pieces]
        output_pieces = widened(output_pieces)
    mixture, logs = attend(block_order, queries, kv_pieces)
    branch = gathered_matmul(mixture, output_pieces, 1, False)
    normed_ffn, hidden = line_sum(branch, [token_rows, gain_ffn], finish_attention, True, False, 0)
    extent = width // size
    pushed = extent % (2 * LANES) == 0
    order = (early, late, [mixture], [normed_ffn], not pushed)
    gate_pieces, up_pieces = gather_pair(w_gate, w_up, *order)
    order = (early, late, [normed_ffn], [normed_ffn], not pushed)
    if pushed:
        low_pieces, high_pieces = gather_pair(w_down[:, : extent // 2], w_down[:, extent // 2 :], *order)
    else:
        low_pieces, high_pieces = gather_pair(w_down[:half], w_down[half:], *order)
        low_pieces, high_pieces = widened(low_pieces), widened(high_pieces)
    d_ffn = (RESIDUAL_SCALE * grad_rows.astype(F32)).astype(BF16)
    active, d_gate, d_up, ffn_out, d_normed_ffn = ffn(
        normed_ffn, d_ffn, gate_pieces, up_pieces, low_pieces, high_pieces, pushed
    )
    pairs = [
        (normed_ffn, d_gate, 0, units),
        (normed_ffn, d_up, 0, units),
        (d_ffn, active, 0, half),
        (d_ffn, active, half, units),
    ]
    sum_ins = [hidden, grad_rows, gain_ffn]
    fused = grads_fit(pairs) and front_fits()
    if fused:
        d_branch, d_hidden, ffn_gain, *flat = line_sum(
            d_normed_ffn, sum_ins, finish_ffn_back, True, True, 1, ffn_out, pairs
        )
        out_chunks, jobs = flat[:4], len(pairs)
        grad_gate, grad_up, grad_low, grad_high = grads_named(flat[4:], jobs)
    else:
        grad_gate, grad_up, grad_low, grad_high = plane_grads(pairs, 3)
        d_branch, d_hidden, ffn_gain = line_sum(
            after(d_normed_ffn, grad_gate[0]), sum_ins, finish_ffn_back, True, True, 1
        )
        padded = lax.dynamic_update_slice_in_dim(jnp.zeros((rows, width), F32), hidden, (z // 2) * (rows // 2), 0)
        out_part = RESIDUAL_SCALE * ffn_out.astype(F32) + jnp.where(lax.rem(z, 3) != 0, padded, 0.0)
        out_chunks = [chunk_of(out_part.astype(BF16), lax.rem(z + shift, 4), rows // 4) for shift in range(4)]
    layer_out = rows_gather(rows_sum(out_chunks).astype(BF16))

    d_mixture = gathered_matmul(d_branch, output_pieces, 1, True)
    d_queries, *d_pieces = attend_back(block_order, queries, d_mixture, logs, kv_pieces)
    d_keys_values = reduce_context(d_pieces)
    if fused:
        grad_gate, grad_up = crossed_pair(grad_gate, grad_up, [d_keys_values])
        grad_low, grad_high = crossed_pair(grad_low, grad_high, [d_keys_values])
    else:
        grad_gate, grad_up = reduce_pair(grad_gate, grad_up, [d_keys_values])
        grad_low, grad_high = reduce_pair(grad_low, grad_high, [d_keys_values])
    d_qkv, d_normed = project_qkv_back(d_queries, d_keys_values, cosine, sine, qkv_pieces)
    pairs = [(normed, d_qkv, 0, d_qkv.shape[1]), (d_branch, mixture, 0, q_width)]
    sum_ins = [token_rows, d_hidden, gain_attn]
    if grads_fit(pairs) and front_fits():
        grad_tokens, attn_gain, grad_qkv, grad_output = line_sum(
            d_normed, sum_ins, finish_attention_back, False, True, 2, None, pairs
        )
    else:
        grad_qkv, grad_output = plane_grads(pairs, 4)
        grad_tokens, attn_gain = line_sum(after(d_normed, grad_qkv[0]), sum_ins, finish_attention_back, False, True, 2)
        grad_qkv, grad_output = reduce_pair(grad_qkv, grad_output)
    grad_tokens = grad_tokens.astype(F32)
    attn_gain, ffn_gain = jnp.sum(attn_gain, axis=0), jnp.sum(ffn_gain, axis=0)
    gain_grads = jnp.stack([attn_gain, ffn_gain])
    gain_grads = gains_sum(gain_grads)
    return (
        layer_out.reshape(seqs, local_len, width),
        grad_tokens.reshape(seqs, local_len, width),
        grad_qkv[:, :q_width],
        grad_qkv[:, q_width : q_width + kv_width],
        grad_qkv[:, q_width + kv_width :],
        grad_output.T,
        grad_gate,
        grad_up,
        jnp.concatenate([grad_low.T, grad_high.T], axis=0),
        gain_grads[0],
        gain_grads[1],
    )


def solution(mesh):
    split = P("shard", "context", None)
    inward, outward = P(PLANE, "tensor"), P("tensor", PLANE)
    gain = P(PLANE)
    return jax.shard_map(
        local,
        mesh=mesh,
        in_specs=(split, P("shard", None), inward, inward, inward, outward, inward, inward, outward, gain, gain, split),
        out_specs=(split, split, inward, inward, inward, outward, inward, inward, outward, gain, gain),
        check_vma=False,
    )
```

```python
import functools
import math

import jax
import jax.numpy as jnp
from jax import lax
from jax.experimental import pallas as pl
from jax.experimental.pallas import tpu as pltpu
from jax.sharding import PartitionSpec as P


HD = 64
BLK = 256
LANES = 128
EPSILON = 1e-05
SCORE_SCALE = 0.015625
RESIDUAL_SCALE = 0.22
ROPE_BASE = 10000000.0
MASKED_SCORE = -1e30
PLANE = ("shard", "context")
VMEM_BYTES = 64000 * 1024


F32 = jnp.float32
BF16 = jnp.bfloat16


def plane_size():
    return lax.axis_size("shard") * lax.axis_size("context")


def plane_index():
    return lax.axis_index("shard") * lax.axis_size("context") + lax.axis_index("context")


def swap(value, axes, size, bit):
    return lax.ppermute(value, axes, [(i, i ^ bit) for i in range(size)])


def gather_pair(first, second, far_after=(), near_after=(), cross_after=(), core_after=(), core=True):
    size = plane_size()
    bits = [1 << b for b in range(1, size.bit_length() - 1)]
    sides = [{0: first}, {0: second}]
    if len(bits) == 2:
        near, far = bits
        for side in sides:
            side[far] = swap(after(side[0], *far_after), PLANE, size, far)
        for side in reversed(sides):
            side[near] = swap(after(side[0], *near_after), PLANE, size, near)
        sides[0][near | far] = swap(after(sides[0][far], *cross_after), PLANE, size, near)
        sides[1][near | far] = swap(after(sides[1][near], *cross_after), PLANE, size, far)
    else:
        for side in sides:
            for bit in bits:
                for r in list(side):
                    side[r | bit] = swap(side[r], PLANE, size, bit)
    if not core:
        return [[side[r] for r in range(0, size, 2)] for side in sides]
    for side in sides:
        for r in list(side):
            side[r | 1] = swap(after(side[r], *core_after), PLANE, size, 1)
    return [[side[r] for r in range(size)] for side in sides]


def widened(pieces):
    level = 1
    while pieces[0].shape[1] < LANES:
        upper = (plane_index() // level) % 2 == 1
        pairs = zip(pieces[0::2], pieces[1::2])
        pieces = [jnp.where(upper, jnp.concatenate([b, a], 1), jnp.concatenate([a, b], 1)) for a, b in pairs]
        level *= 2
    return pieces


def take_sum(side, bit, kept):
    sent = side[kept | bit].astype(BF16)
    total = side[kept].astype(F32) + swap(sent, PLANE, plane_size(), bit).astype(F32)
    return total if kept == 0 else total.astype(BF16)


def crossed_sum(side, own_bit, wait, waits):
    size, near, far = plane_size(), 2, 4
    side = dict(side)
    side[own_bit] = (side[own_bit].astype(F32) + after(side[6], wait).astype(F32)).astype(BF16)
    a = swap(after(side[near], *waits), PLANE, size, near).astype(F32)
    b = swap(side[far], PLANE, size, far).astype(F32)
    return side[0] + a + b


def reduce_pair(first, second, last_after=()):
    size = plane_size()
    bits = [1 << b for b in range(1, size.bit_length() - 1)]
    sides = [dict(first), dict(second)]
    if len(bits) == 2:
        near, far = bits
        sides[0][near] = take_sum(sides[0], far, near)
        sides[1][far] = take_sum(sides[1], near, far)
        done = []
        for side in sides:
            sent = [after(side[bit].astype(BF16), *last_after) for bit in bits]
            a = swap(sent[0], PLANE, size, near).astype(F32)
            b = swap(sent[1], PLANE, size, far).astype(F32)
            done.append(side[0] + a + b)
        return done
    done = []
    for side in sides:
        for bit in reversed(bits):
            side = {r: take_sum(side, bit, r) for r in side if not r & bit}
        done.append(side[0])
    return done


def gather_small(values):
    size = plane_size()
    stacked = values[None]
    bit = 1
    while bit < size:
        stacked = jnp.concatenate([stacked, swap(stacked, PLANE, size, bit)], axis=0)
        bit *= 2
    picks = jnp.arange(size, dtype=jnp.int32)[:, None] ^ plane_index()
    chosen = (picks == jnp.arange(size, dtype=jnp.int32)[None, :]).astype(F32)
    return jnp.einsum("ij,jkw->kiw", chosen, stacked.astype(F32), precision=lax.Precision.HIGHEST)


def chunk_of(rows, index, count):
    return lax.dynamic_slice_in_dim(rows, index * count, count, 0)


def rows_sum(chunks):
    size = lax.axis_size("tensor")
    total = chunks[0].astype(F32)
    for shift in range(1, size):
        pairs = [(i, (i + shift) % size) for i in range(size)]
        total = total + lax.ppermute(chunks[shift], "tensor", pairs).astype(F32)
    return total


def rows_gather(chunk):
    size = lax.axis_size("tensor")
    count = chunk.shape[0]
    parts = [chunk]
    for shift in range(1, size):
        pairs = [(i, (i + shift) % size) for i in range(size)]
        parts.append(lax.ppermute(chunk, "tensor", pairs))
    return pl.pallas_call(
        assemble_body,
        in_specs=[ANYWHERE] * size,
        out_specs=pl.BlockSpec(memory_space=pltpu.VMEM),
        out_shape=jax.ShapeDtypeStruct((size * count,) + chunk.shape[1:], chunk.dtype),
        scratch_shapes=[pltpu.SemaphoreType.DMA],
        compiler_params=pltpu.CompilerParams(vmem_limit_bytes=8 << 20),
        cost_estimate=pl.CostEstimate(flops=0, bytes_accessed=4 * size * chunk.size, transcendentals=0),
        name="assemble",
    )(*parts)


def assemble_body(*refs):
    parts, whole, sem = refs[:-2], refs[-2], refs[-1]
    count = parts[0].shape[0]
    me = lax.axis_index("tensor")
    for shift, part in enumerate(parts):
        place = pl.multiple_of(lax.rem(me - shift + len(parts), len(parts)) * count, count)
        pltpu.make_async_copy(part, whole.at[pl.ds(place, count)], sem).start()
    pltpu.make_async_copy(whole, whole, sem).wait()


def gains_sum(values):
    size, tensor, me = plane_size(), lax.axis_size("tensor"), plane_index()
    extent = values.shape[1] // size
    total = values
    for shift in range(1, tensor):
        total = total + lax.ppermute(values, "tensor", [(i, (i + shift) % tensor) for i in range(tensor)])
    own = 0.0
    for r in range(size):
        sent = lax.dynamic_slice_in_dim(total, (me ^ r) * extent, extent, 1)
        own = own + (swap(sent, PLANE, size, r) if r else sent)
    return own


def params(steps):
    return pltpu.CompilerParams(
        dimension_semantics=("arbitrary",) * steps, vmem_limit_bytes=VMEM_BYTES
    )


def place_pieces(pieces, whole, sem, axis):
    size = len(pieces)
    me = plane_index() // (plane_size() // size)
    extent = whole.shape[axis] // size
    for r, piece in enumerate(pieces):
        start = pl.multiple_of((me ^ r) * extent, extent)
        target = whole.at[pl.ds(start, extent)] if axis == 0 else whole.at[:, pl.ds(start, extent)]
        pltpu.make_async_copy(piece, target, sem).start()


def await_whole(whole, sem):
    pltpu.make_async_copy(whole, whole, sem).wait()


ANYWHERE = pl.BlockSpec(memory_space=pl.ANY)


def turned(values, lane, sign):
    half = HD // 2
    upper = pltpu.roll(values, LANES - half, 1)
    lower = pltpu.roll(values, half, 1)
    return jnp.where(lane % HD < half, -sign * upper, sign * lower)


def qkv_body(count, tokens, gain, cosine, sine, *rest):
    pieces, (normed, queries, keys_values, weight, sem) = rest[:count], rest[count:]

    @pl.when(pl.program_id(0) == 0)
    def _():
        place_pieces(pieces, weight, sem, 0)

    values = tokens[...].astype(F32)
    inverse = lax.rsqrt(jnp.mean(values * values, axis=1, keepdims=True) + EPSILON)
    low = (values * inverse * gain[...]).astype(BF16)
    normed[...] = low

    @pl.when(pl.program_id(0) == 0)
    def _():
        await_whole(weight, sem)

    cos, sin = cosine[...], sine[...]
    lane = lax.broadcasted_iota(jnp.int32, cos.shape, 1)
    q_width = queries.shape[1]
    k_width = keys_values.shape[1] // 2
    for start in range(0, weight.shape[1], LANES):
        part = jnp.dot(low, weight[:, start : start + LANES * 1], preferred_element_type=F32)
        if start < q_width + k_width:
            part = part * cos + turned(part, lane, 1.0) * sin
        if start < q_width:
            queries[:, start : start + LANES] = (part.astype(BF16) * SCORE_SCALE).astype(BF16)
        else:
            keys_values[:, start - q_width : start - q_width + LANES] = part.astype(BF16)


def project_qkv(tokens, gain, cosine, sine, pieces, q_width):
    rows, width = tokens.shape
    total = pieces[0].shape[1]
    tile = min(rows, 256)
    row_spec = lambda w: pl.BlockSpec((tile, w), lambda i: (i, 0))
    return pl.pallas_call(
        functools.partial(qkv_body, len(pieces)),
        grid=(rows // tile,),
        in_specs=[row_spec(width), pl.BlockSpec((1, width), lambda i: (0, 0)), row_spec(LANES), row_spec(LANES)]
        + [ANYWHERE] * len(pieces),
        out_specs=[row_spec(width), row_spec(q_width), row_spec(total - q_width)],
        out_shape=[
            jax.ShapeDtypeStruct((rows, width), BF16),
            jax.ShapeDtypeStruct((rows, q_width), BF16),
            jax.ShapeDtypeStruct((rows, total - q_width), BF16),
        ],
        scratch_shapes=[pltpu.VMEM((width, total), BF16), pltpu.SemaphoreType.DMA],
        compiler_params=params(1),
        cost_estimate=pl.CostEstimate(
            flops=2 * rows * width * total, bytes_accessed=2 * (2 * rows * width + width * total), transcendentals=0
        ),
        name="project_qkv",
    )(tokens, gain, cosine, sine, *pieces)


def qkv_back_body(count, d_queries, d_keys_values, cosine, sine, *rest):
    pieces, (d_all, d_normed, weight, sem) = rest[:count], rest[count:]

    @pl.when(pl.program_id(0) == 0)
    def _():
        place_pieces(pieces, weight, sem, 0)

    cos, sin = cosine[...], sine[...]
    lane = lax.broadcasted_iota(jnp.int32, cos.shape, 1)
    q_width = d_queries.shape[1]
    k_width = d_keys_values.shape[1] // 2
    for start in range(0, d_all.shape[1], LANES):
        if start < q_width:
            part = d_queries[:, start : start + LANES]
        else:
            part = d_keys_values[:, start - q_width : start - q_width + LANES]
        if start < q_width + k_width:
            part = part * cos + turned(part * sin, lane, -1.0)
        d_all[:, start : start + LANES] = part.astype(BF16)

    @pl.when(pl.program_id(0) == 0)
    def _():
        await_whole(weight, sem)

    step = 512
    for start in range(0, weight.shape[0], step):
        d_normed[:, start : start + step] = lax.dot_general(
            d_all[...], weight[start : start + step, :], (((1,), (1,)), ((), ())), preferred_element_type=F32
        ).astype(BF16)


def project_qkv_back(d_queries, d_keys_values, cosine, sine, pieces):
    rows, q_width = d_queries.shape
    total = pieces[0].shape[1]
    width = pieces[0].shape[0] * len(pieces)
    tile = min(rows, 256)
    row_spec = lambda w: pl.BlockSpec((tile, w), lambda i: (i, 0))
    return pl.pallas_call(
        functools.partial(qkv_back_body, len(pieces)),
        grid=(rows // tile,),
        in_specs=[row_spec(q_width), row_spec(total - q_width), row_spec(LANES), row_spec(LANES)]
        + [ANYWHERE] * len(pieces),
        out_specs=[row_spec(total), row_spec(width)],
        out_shape=[jax.ShapeDtypeStruct((rows, total), BF16), jax.ShapeDtypeStruct((rows, width), BF16)],
        scratch_shapes=[pltpu.VMEM((width, total), BF16), pltpu.SemaphoreType.DMA],
        compiler_params=params(1),
        cost_estimate=pl.CostEstimate(
            flops=2 * rows * width * total, bytes_accessed=2 * (2 * rows * width + width * total), transcendentals=0
        ),
        name="project_qkv_back",
    )(d_queries, d_keys_values, cosine, sine, *pieces)


def gathered_body(count, axis, transposed, left, *rest):
    pieces, (out, weight, sem) = rest[:count], rest[count:]

    @pl.when(pl.program_id(0) == 0)
    def _():
        place_pieces(pieces, weight, sem, axis)
        await_whole(weight, sem)

    step = min(out.shape[1], 512)
    for start in range(0, out.shape[1], step):
        if transposed:
            part = lax.dot_general(
                left[...], weight[start : start + step, :], (((1,), (1,)), ((), ())), preferred_element_type=F32
            )
        else:
            part = jnp.dot(left[...], weight[:, start : start + step], preferred_element_type=F32)
        out[:, start : start + step] = part.astype(out.dtype)


def gathered_matmul(left, pieces, axis, transposed):
    rows = left.shape[0]
    shape = list(pieces[0].shape)
    shape[axis] *= len(pieces)
    outer = shape[0] if transposed else shape[1]
    tile = min(rows, 256)
    return pl.pallas_call(
        functools.partial(gathered_body, len(pieces), axis, transposed),
        grid=(rows // tile,),
        in_specs=[pl.BlockSpec((tile, left.shape[1]), lambda i: (i, 0))] + [ANYWHERE] * len(pieces),
        out_specs=pl.BlockSpec((tile, outer), lambda i: (i, 0)),
        out_shape=jax.ShapeDtypeStruct((rows, outer), BF16),
        scratch_shapes=[pltpu.VMEM(tuple(shape), BF16), pltpu.SemaphoreType.DMA],
        compiler_params=params(1),
        cost_estimate=pl.CostEstimate(
            flops=2 * rows * shape[0] * shape[1],
            bytes_accessed=2 * (rows * sum(shape) + shape[0] * shape[1]),
            transcendentals=0,
        ),
    )(left, *pieces)


def ffn_tile(f_step, tile, normed, d_ffn, gate, up, down, active, d_gate, d_up, out, d_normed, out_sum, d_sum):
    units = pl.ds(pl.multiple_of(f_step * tile, tile), tile)
    gate_tile, up_tile, down_tile = gate[:, units], up[:, units], down[units, :]
    gate_in = jnp.dot(normed[...], gate_tile, preferred_element_type=F32)
    upward = jnp.dot(normed[...], up_tile, preferred_element_type=F32)
    d_active = lax.dot_general(d_ffn[...], down_tile, (((1,), (1,)), ((), ())), preferred_element_type=F32)
    sigma = 1.0 / (1.0 + jnp.exp(-gate_in))
    silu = gate_in * sigma
    active_low = (silu * upward).astype(BF16)
    gate_low = (d_active * upward * (sigma * (1.0 + gate_in * (1.0 - sigma)))).astype(BF16)
    up_low = (d_active * silu).astype(BF16)
    active[...] = active_low
    d_gate[...] = gate_low
    d_up[...] = up_low
    part = jnp.dot(active_low, down_tile, preferred_element_type=F32)
    d_part = lax.dot_general(gate_low, gate_tile, (((1,), (1,)), ((), ())), preferred_element_type=F32)
    d_part += lax.dot_general(up_low, up_tile, (((1,), (1,)), ((), ())), preferred_element_type=F32)

    @pl.when(f_step == 0)
    def _():
        out_sum[...] = part
        d_sum[...] = d_part

    @pl.when(f_step > 0)
    def _():
        out_sum[...] += part
        d_sum[...] += d_part

    @pl.when(f_step == pl.num_programs(1) - 1)
    def _():
        out[...] = out_sum[...].astype(BF16)
        d_normed[...] = d_sum[...].astype(BF16)


def ffn_body(count, narrow, tile, normed, d_ffn, *rest):
    gate_pieces, up_pieces, rest = rest[:count], rest[count : 2 * count], rest[2 * count :]
    low_pieces, high_pieces, rest = rest[:narrow], rest[narrow : 2 * narrow], rest[2 * narrow :]
    active, d_gate, d_up, out, d_normed, gate, up, down, out_sum, d_sum, sems = rest
    f_step = pl.program_id(1)
    half = down.shape[0] // 2

    @pl.when((pl.program_id(0) == 0) & (f_step == 0))
    def _():
        place_pieces(gate_pieces, gate, sems.at[0], 0)
        place_pieces(up_pieces, up, sems.at[1], 0)
        place_pieces(low_pieces, down.at[pl.ds(0, half)], sems.at[2], 1)
        place_pieces(high_pieces, down.at[pl.ds(half, half)], sems.at[3], 1)
        await_whole(gate, sems.at[0])
        await_whole(up, sems.at[1])
        await_whole(down.at[pl.ds(0, half)], sems.at[2])
        await_whole(down.at[pl.ds(half, half)], sems.at[3])

    ffn_tile(f_step, tile, normed, d_ffn, gate, up, down, active, d_gate, d_up, out, d_normed, out_sum, d_sum)


def ffn(normed, d_ffn, gate_pieces, up_pieces, low_pieces, high_pieces, pushed):
    rows, width = normed.shape
    units = gate_pieces[0].shape[1]
    count = len(gate_pieces)
    tile = 256
    row_tile = min(rows, 512)
    once = pl.Buffered(1)
    row_spec = pl.BlockSpec((row_tile, width), lambda i, f: (i, 0), pipeline_mode=once)
    unit_spec = pl.BlockSpec((row_tile, tile), lambda i, f: (i, f))
    unit_shape = jax.ShapeDtypeStruct((rows, units), BF16)
    row_shape = jax.ShapeDtypeStruct((rows, width), BF16)
    body = functools.partial(ffn_body, count, len(low_pieces), tile)
    settings, sems = params(2), [pltpu.SemaphoreType.DMA((4,))]
    if pushed:
        body = functools.partial(pushed_body, count, tile)
        sems = [pltpu.SemaphoreType.DMA((3, units // tile))] * 3
        settings = pltpu.CompilerParams(
            dimension_semantics=("arbitrary",) * 2,
            vmem_limit_bytes=VMEM_BYTES,
            collective_id=5,
            has_side_effects=True,
        )
    return pl.pallas_call(
        body,
        grid=(rows // row_tile, units // tile),
        in_specs=[row_spec, row_spec] + [ANYWHERE] * (2 * count + 2 * len(low_pieces)),
        out_specs=[unit_spec, unit_spec, unit_spec, row_spec, row_spec],
        out_shape=[unit_shape, unit_shape, unit_shape, row_shape, row_shape],
        scratch_shapes=[
            pltpu.VMEM((width, units), BF16),
            pltpu.VMEM((width, units), BF16),
            pltpu.VMEM((units, width), BF16),
            pltpu.VMEM((row_tile, width), F32),
            pltpu.VMEM((row_tile, width), F32),
        ]
        + sems,
        compiler_params=settings,
        cost_estimate=pl.CostEstimate(
            flops=12 * rows * width * units, bytes_accessed=6 * width * units + 14 * rows * width, transcendentals=rows * units
        ),
        name="feed_forward",
    )(normed, d_ffn, *gate_pieces, *up_pieces, *low_pieces, *high_pieces)


def pushed_body(count, tile, normed, d_ffn, *refs):
    groups, rest = [refs[k * count : (k + 1) * count] for k in range(4)], refs[4 * count :]
    active, d_gate, d_up, out, d_normed, gate, up, down, out_sum, d_sum, near, send, recv = rest
    f_step = pl.program_id(1)
    first = (pl.program_id(0) == 0) & (f_step == 0)
    last = (pl.program_id(0) == pl.num_programs(0) - 1) & (f_step == pl.num_programs(1) - 1)
    steps = down.shape[0] // tile
    width = down.shape[1]
    extent = width // (2 * count)
    me = plane_index()
    mate = {"context": lax.axis_index("context") ^ 1}
    mesh_ids = pl.DeviceIdType.MESH

    def push(source, target, w, t):
        return pltpu.make_async_remote_copy(
            src_ref=source,
            dst_ref=target,
            send_sem=send.at[w, t],
            recv_sem=recv.at[w, t],
            device_id=mate,
            device_id_type=mesh_ids,
        )

    def halves(t):
        units = pl.ds(pl.multiple_of(t * tile, tile), tile)
        half = pl.ds(0, width // 2)
        return [gate.at[half, units], up.at[half, units], down.at[units, half]]

    @pl.when(first)
    def _():
        barrier = pltpu.get_barrier_semaphore()
        pl.semaphore_signal(barrier, inc=1, device_id=mate, device_id_type=mesh_ids)
        pl.semaphore_wait(barrier, 1)

        def start(t, carry):
            units = pl.ds(pl.multiple_of(t * tile, tile), tile)
            for i in range(count):
                base = pl.multiple_of((me ^ (2 * i)) * extent, extent)
                rows = pl.ds(base, extent)
                left = pl.ds(base, extent // 2)
                right = pl.ds(pl.multiple_of(base + extent // 2, extent // 2), extent // 2)
                moves = (
                    (0, groups[0][i].at[:, units], gate.at[rows, units]),
                    (1, groups[1][i].at[:, units], up.at[rows, units]),
                    (2, groups[2][i].at[units, :], down.at[units, left]),
                    (2, groups[3][i].at[units, :], down.at[units, right]),
                )
                for w, source, target in moves:
                    push(source, target, w, t).start()
                    pltpu.make_async_copy(source, target, near.at[w, t]).start()
            return carry

        lax.fori_loop(0, steps, start, 0)

    @pl.when(pl.program_id(0) == 0)
    def _():
        for w, half in enumerate(halves(f_step)):
            pltpu.make_async_copy(half, half, near.at[w, f_step]).wait()
            push(half, half, w, f_step).wait_recv()

    ffn_tile(f_step, tile, normed, d_ffn, gate, up, down, active, d_gate, d_up, out, d_normed, out_sum, d_sum)

    @pl.when(last)
    def _():
        def drain(t, carry):
            for w, half in enumerate(halves(t)):
                push(half, half, w, t).wait_send()
            return carry

        lax.fori_loop(0, steps, drain, 0)


def doubled(values, lane, head):
    rolled = pltpu.roll(values.astype(F32), HD, 1).astype(BF16)
    return jnp.where((lane < HD) == (head == 0), values, rolled)


def block_bias(order, seq, r, block):
    per = order.shape[1] // lax.axis_size("context")
    own = order[seq, lax.axis_index("context") * per + pl.program_id(3)]
    other = order[seq, (lax.axis_index("context") ^ r) * per + block]
    return jnp.where(other <= own, 0.0, MASKED_SCORE).astype(F32)


def masked_scores(order, pieces_k, query):
    seq = pl.program_id(0)
    scores = []
    for r, key_rows in enumerate(pieces_k):
        part = lax.dot_general(key_rows, query, (((1,), (1,)), ((), ())), preferred_element_type=F32)
        for block in range(key_rows.shape[0] // BLK):
            bias = block_bias(order, seq, r, block)
            scores.append(part[block * BLK : (block + 1) * BLK] + bias)
    return scores


def attend_body(count, order, query_ref, *rest):
    pieces, (mixture, logs) = rest[:count], rest[count:]
    head = pl.program_id(1)
    lane = lax.broadcasted_iota(jnp.int32, (1, LANES), 1)
    keys = [doubled(piece[:, :LANES], lane, head) for piece in pieces]
    values = [doubled(piece[:, LANES:], lane, head) for piece in pieces]
    query = query_ref[...]
    parts = []
    for side in range(2):
        chosen = (lane < HD) if side == 0 else (lane >= HD)
        scores = masked_scores(order, keys, jnp.where(chosen, query, jnp.zeros_like(query)))
        top = functools.reduce(jnp.maximum, [jnp.max(s, axis=0, keepdims=True) for s in scores])
        powers = [jnp.exp(s - top) for s in scores]
        total = sum(jnp.sum(p, axis=0, keepdims=True) for p in powers)
        low = jnp.concatenate([p.astype(BF16) for p in powers], axis=0)
        whole = jnp.concatenate(values, axis=0)
        mixed = lax.dot_general(whole, low, (((0,), (0,)), ((), ())), preferred_element_type=F32)
        parts.append(mixed / total)
        logs[side : side + 1, :] = top + jnp.log(total)
    row = lax.broadcasted_iota(jnp.int32, (LANES, 1), 0)
    mixture[...] = jnp.where(row < HD, parts[0], parts[1]).T.astype(BF16)


def attend_specs(order, queries, pieces, group_pairs):
    seqs = order.shape[0]
    rows = queries.shape[0] // seqs
    tiles = rows // BLK
    grid = (seqs, 2, group_pairs, tiles)
    q_spec = pl.BlockSpec((BLK, LANES), lambda s, h, g, t: (s * tiles + t, h * group_pairs + g))
    kv_spec = pl.BlockSpec((rows, 2 * LANES), lambda s, h, g, t: (s, 0))
    kv_ins = [pl.BlockSpec((None, rows, 2 * LANES), lambda s, h, g, t, r=r: (r, s, 0)) for r in range(pieces.shape[0])]
    log_spec = pl.BlockSpec((None, 2, BLK), lambda s, h, g, t: (h * group_pairs + g, 0, s * tiles + t))
    return grid, q_spec, kv_spec, kv_ins, log_spec


def attend(order, queries, pieces):
    rows, q_width = queries.shape
    pairs = q_width // LANES
    grid, q_spec, _, kv_ins, log_spec = attend_specs(order, queries, pieces, pairs // 2)
    keys = rows * pieces.shape[0] // order.shape[0]
    return pl.pallas_call(
        functools.partial(attend_body, pieces.shape[0]),
        grid=grid,
        in_specs=[pl.BlockSpec(memory_space=pltpu.SMEM), q_spec] + kv_ins,
        out_specs=[q_spec, log_spec],
        out_shape=[jax.ShapeDtypeStruct((rows, q_width), BF16), jax.ShapeDtypeStruct((pairs, 2, rows), F32)],
        compiler_params=params(4),
        cost_estimate=pl.CostEstimate(
            flops=8 * rows * keys * q_width * 2, bytes_accessed=8 * rows * q_width, transcendentals=rows * keys * q_width // HD
        ),
        name="attend",
    )(order, queries, *[pieces] * pieces.shape[0])


def attend_back_body(count, order, query_ref, grad_ref, logs, *rest):
    pieces, rest = rest[:count], rest[count:]
    d_query, outs, (d_key_sum, d_value_sum) = rest[0], rest[1 : 1 + count], rest[1 + count :]
    head, pair, tile = pl.program_id(1), pl.program_id(2), pl.program_id(3)
    lane = lax.broadcasted_iota(jnp.int32, (1, LANES), 1)
    keys = [doubled(piece[:, :LANES], lane, head) for piece in pieces]
    values = jnp.concatenate([doubled(piece[:, LANES:], lane, head) for piece in pieces], axis=0)
    whole_keys = jnp.concatenate(keys, axis=0)
    parts, d_keys, d_values = [], 0.0, 0.0
    for side in range(2):
        chosen = (lane < HD) if side == 0 else (lane >= HD)
        query = jnp.where(chosen, query_ref[...], jnp.zeros_like(query_ref[...]))
        grad = jnp.where(chosen, grad_ref[...], jnp.zeros_like(grad_ref[...]))
        scores = jnp.concatenate(masked_scores(order, keys, query), axis=0)
        soft = jnp.exp(scores - logs[side : side + 1, :])
        d_soft = lax.dot_general(values, grad, (((1,), (1,)), ((), ())), preferred_element_type=F32)
        inner = jnp.sum(soft * d_soft, axis=0, keepdims=True)
        d_scores = (soft * (d_soft - inner)).astype(BF16)
        d_values += jnp.dot(soft.astype(BF16), grad, preferred_element_type=F32)
        d_keys += jnp.dot(d_scores, query, preferred_element_type=F32)
        parts.append(lax.dot_general(whole_keys, d_scores, (((0,), (0,)), ((), ())), preferred_element_type=F32))
    row = lax.broadcasted_iota(jnp.int32, (LANES, 1), 0)
    d_query[...] = jnp.where(row < HD, parts[0], parts[1]).T * SCORE_SCALE

    first = (pair == 0) & (tile == 0)
    last = (pair == pl.num_programs(2) - 1) & (tile == pl.num_programs(3) - 1)

    @pl.when(first)
    def _():
        d_key_sum[...] = d_keys
        d_value_sum[...] = d_values

    @pl.when(jnp.logical_not(first))
    def _():
        d_key_sum[...] += d_keys
        d_value_sum[...] += d_values

    @pl.when(last)
    def _():
        wanted = (lane < HD) == (head == 0)
        rows = outs[0].shape[0]
        for r, out in enumerate(outs):
            for base, total in ((0, d_key_sum), (LANES, d_value_sum)):
                part = total[r * rows : (r + 1) * rows, :]
                both = (part + pltpu.roll(part, HD, 1)).astype(out.dtype)
                spot = pl.ds(base, LANES)

                @pl.when(head == 0)
                def _():
                    out[:, spot] = both

                @pl.when(head == 1)
                def _():
                    out[:, spot] = jnp.where(wanted, both.astype(F32), out[:, spot].astype(F32)).astype(out.dtype)


def attend_back(order, queries, grads, logs, pieces):
    rows, q_width = queries.shape
    pairs = q_width // LANES
    grid, q_spec, kv_spec, kv_ins, log_spec = attend_specs(order, queries, pieces, pairs // 2)
    keys = rows * pieces.shape[0] // order.shape[0]
    return pl.pallas_call(
        functools.partial(attend_back_body, pieces.shape[0]),
        grid=grid,
        in_specs=[pl.BlockSpec(memory_space=pltpu.SMEM), q_spec, q_spec, log_spec] + kv_ins,
        out_specs=[q_spec] + [kv_spec] * pieces.shape[0],
        out_shape=[jax.ShapeDtypeStruct((rows, q_width), F32)]
        + [jax.ShapeDtypeStruct((rows, 2 * LANES), F32 if r % 2 == 0 else BF16) for r in range(pieces.shape[0])],
        scratch_shapes=[pltpu.VMEM((keys, LANES), F32), pltpu.VMEM((keys, LANES), F32)],
        compiler_params=params(4),
        cost_estimate=pl.CostEstimate(
            flops=20 * rows * keys * q_width * 2, bytes_accessed=12 * rows * q_width, transcendentals=rows * keys * q_width // HD
        ),
        name="attend_back",
    )(order, queries, grads, logs, *[pieces] * pieces.shape[0])


def line_steps(rows):
    half = rows // 2
    sub = 16
    return half, sub, half // sub


def plane_peer(r):
    return {"shard": lax.axis_index("shard") ^ (r // 4), "context": lax.axis_index("context") ^ (r % 4)}


def gains_parts(own_gain, other_gain, out, refs, inner, to_outer, to_peer):
    held, total, landed, z_send, z_recv, send, recv = refs
    me = plane_index()
    extent = out.shape[1]
    mesh_ids = pl.DeviceIdType.MESH

    def along(source, target, where):
        return pltpu.make_async_remote_copy(
            src_ref=held.at[source],
            dst_ref=held.at[target],
            send_sem=z_send.at[source + target - 1],
            recv_sem=z_recv.at[target],
            device_id={"tensor": where},
            device_id_type=mesh_ids,
        )

    def columns(r):
        return pl.ds(pl.multiple_of((me ^ r) * extent, extent), extent)

    def share(r):
        return pltpu.make_async_remote_copy(
            src_ref=total.at[:, columns(r)],
            dst_ref=landed.at[r],
            send_sem=send.at[r],
            recv_sem=recv.at[r],
            device_id=plane_peer(r),
            device_id_type=mesh_ids,
        )

    @pl.when(inner)
    def _():
        held[0, 0:8, :] = own_gain[...]
        held[0, 8:16, :] = other_gain[...]
        to_mate = along(0, 1, to_peer)
        to_mate.start()
        to_mate.wait()
        held[2] = held[0] + held[1]
        down = along(2, 1, to_outer)
        down.start()
        total[...] = held[2]
        down.wait_send()

    @pl.when(jnp.logical_not(inner))
    def _():
        along(2, 1, to_outer).wait_recv()
        total[...] = held[1]

    for r in range(1, 8):
        share(r).start()
    value = total[:, columns(0)]
    for r in range(1, 8):
        share(r).wait_recv()
        value = value + landed[r]
    out[...] = value
    for r in range(1, 8):
        share(r).wait_send()


def line_body(finish, keep_state, gain_sum, n_in, extra, *refs):
    partial, ins, rest = refs[0], refs[1 : 1 + n_in], refs[1 + n_in :]
    if extra:
        world, n_grad, plan, whole_plane = extra
        ffn_out, rest = rest[0], rest[1:]
        grad_ins, rest = rest[:n_grad], rest[n_grad:]
    result, rest = rest[0], rest[1:]
    state_out, rest = (rest[0], rest[1:]) if keep_state else (None, rest)
    gain_out, rest = (rest[0], rest[1:]) if gain_sum else (None, rest)
    if extra:
        spread = len(plan) if whole_plane else world // 2 * len(plan)
        n_parts = 1 if whole_plane else 4
        out_parts, grad_outs, rest = rest[:n_parts], rest[n_parts : n_parts + spread], rest[n_parts + spread :]
    from_outer, from_peer, staged, send, recv = rest[:5]
    half, sub, count = line_steps(partial.shape[0])
    me = lax.axis_index("tensor")
    side = me // 2
    inner = lax.rem(me, 3) != 0
    to_outer, to_inner, to_peer = side * 3, 1 + side, 3 - me
    near, far = side * half, (1 - side) * half

    def rows(base, k):
        return pl.ds(pl.multiple_of(base + k * sub, sub), sub)

    def remote(source, target, s, r, k, where):
        return pltpu.make_async_remote_copy(
            src_ref=source,
            dst_ref=target,
            send_sem=send.at[s, k],
            recv_sem=recv.at[r, k],
            device_id={"tensor": where},
            device_id_type=pl.DeviceIdType.MESH,
        )

    def up_far(k):
        return remote(partial.at[rows(far, k)], from_outer.at[0, rows(0, k)], 0, 0, k, to_inner)

    def up_near(k):
        return remote(partial.at[rows(near, k)], from_outer.at[1, rows(0, k)], 1, 1, k, to_inner)

    def across(k):
        return remote(staged.at[rows(0, k)], from_peer.at[rows(0, k)], 0, 2, k, to_peer)

    def over(k, base):
        return remote(result.at[rows(base, k)], result.at[rows(base, k)], 2, 4, k, to_peer)

    def down_near(k):
        return remote(result.at[rows(near, k)], result.at[rows(near, k)], 1, 3, k, to_outer)

    def down_far(k):
        return remote(result.at[rows(far, k)], result.at[rows(far, k)], 3, 4, k, to_outer)

    barrier = pltpu.get_barrier_semaphore()

    def greet(where):
        pl.semaphore_signal(barrier, inc=1, device_id={"tensor": where}, device_id_type=pl.DeviceIdType.MESH)

    if extra:
        mate = {"context": lax.axis_index("context") ^ 1}
        pl.semaphore_signal(barrier, inc=1, device_id=mate, device_id_type=pl.DeviceIdType.MESH)
        known = (2, 3, 4, 5, 6, 7) if whole_plane else (2, 4)
        for r in known:
            pl.semaphore_signal(barrier, inc=1, device_id=plane_peer(r), device_id_type=pl.DeviceIdType.MESH)
        if whole_plane:
            gain_refs, rest = rest[-7:], rest[:-7]
            grad_work, grad_rest, grad_finish = plane_parts(world, plan, grad_ins, grad_outs, rest[5:])
        else:
            jobs = len(plan)
            crossed, grad_outs = grad_outs[-jobs:], grad_outs[:-jobs]
            grad_work, grad_finish = grads_parts(
                world, plan, grad_ins, grad_outs, rest[5:-2], crossed, rest[-2:]
            )
            grad_rest = lambda: None
    block = partial.shape[0] // world if extra else 0
    more_greetings = (7 if whole_plane else 3) if extra else 0
    last_work = world + 1 if extra and whole_plane else world if extra else 0

    def work(q):
        grad_work(q)
        if not whole_plane:
            out_work(q)

    def out_work(q):
        rows_q = pl.ds(pl.multiple_of(q * block, block), block)
        value = RESIDUAL_SCALE * ffn_out[rows_q, :].astype(F32)
        quarter = 2 * block * world // 8
        chunk = lax.rem(q * 4 // world - me + 4, 4)
        place = pl.ds(pl.multiple_of(lax.rem(q * block, quarter), block), block)
        owned = inner & (q * 2 // world == side)

        for part in range(4):

            @pl.when(owned & (chunk == part))
            def _():
                mine = pl.ds(pl.multiple_of(lax.rem(q * block, half), block), block)
                out_parts[part][place, :] = (value + ins[0][mine, :]).astype(BF16)

            @pl.when(jnp.logical_not(owned) & (chunk == part))
            def _():
                out_parts[part][place, :] = value.astype(BF16)

    if gain_sum:
        gain_out[...] = jnp.zeros_like(gain_out)

    @pl.when(inner)
    def _():
        greet(to_outer)
        greet(to_peer)
        pl.semaphore_wait(barrier, 2 + more_greetings)

        def step(k, carry):
            @pl.when(k < count)
            def _():
                up_far(k).wait_recv()
                total = partial[rows(far, k), :].astype(F32) + from_outer[0, rows(0, k), :].astype(F32)
                staged[rows(0, k), :] = total.astype(BF16)
                across(k).start()

            @pl.when((k >= 1) & (k <= count))
            def _():
                j = k - 1
                up_near(j).wait_recv()
                across(j).wait_recv()
                total = partial[rows(near, j), :].astype(F32) + from_outer[1, rows(0, j), :].astype(F32)
                total = total + from_peer[rows(0, j), :].astype(F32)
                low, state, gains = finish(total, rows(near, j), rows(0, j), ins)
                result[rows(near, j), :] = low
                if keep_state:
                    state_out[rows(0, j), :] = state
                if gain_sum:
                    gain_out[...] += jnp.sum(gains.reshape(sub // 8, 8, gains.shape[1]), axis=0)
                down_near(j).start()
                over(j, near).start()

            @pl.when(k >= 3)
            def _():
                over(k - 3, far).wait_recv()
                down_far(k - 3).start()

            if extra:

                @pl.when((lax.rem(k, count // world) == 0) & (k < last_work * (count // world)))
                def _():
                    work(k // (count // world))

            return carry

        lax.fori_loop(0, count + 3, step, 0)

        def drain(k, carry):
            across(k).wait_send()
            down_near(k).wait_send()
            over(k, near).wait_send()
            down_far(k).wait_send()
            return carry

        lax.fori_loop(0, count, drain, 0)

    @pl.when(jnp.logical_not(inner))
    def _():
        greet(to_inner)
        pl.semaphore_wait(barrier, 1 + more_greetings)

        def step(k, carry):
            up_far(k).start()
            up_near(k).start()
            return carry

        lax.fori_loop(0, count, step, 0)
        if extra:

            def busy(q, carry):
                work(q)
                return carry

            lax.fori_loop(0, last_work, busy, 0)

        def drain(k, carry):
            down_near(k).wait_recv()
            down_far(k).wait_recv()
            up_far(k).wait_send()
            up_near(k).wait_send()
            return carry

        lax.fori_loop(0, count, drain, 0)

    if extra:
        if whole_plane:
            gains_parts(gain_out, ffn_out, out_parts[0], gain_refs, inner, to_outer, to_peer)
        grad_rest()
        grad_finish()


def line_sum(partial, ins, finish, keep_state, gain_sum, identity, ffn_out=None, pairs=(), ffn_gain=None):
    rows, width = partial.shape
    half, _, count = line_steps(rows)
    vmem = pl.BlockSpec(memory_space=pltpu.VMEM)
    shapes = [jax.ShapeDtypeStruct((rows, width), BF16)]
    if keep_state:
        shapes.append(jax.ShapeDtypeStruct((half, width), F32))
    if gain_sum:
        shapes.append(jax.ShapeDtypeStruct((8, width), F32))
    specs, more, scratch, extra = [vmem] * len(shapes), [], [], None
    if pairs:
        arrays, plan = unique_arrays(pairs)
        whole_plane = ffn_gain is not None
        extra = (plane_size(), len(arrays), plan, whole_plane)
        outs, scratch = grads_shapes(pairs)
        if whole_plane:
            more = [ffn_gain] + arrays
            pieces = [(left.shape[1] // plane_size(), high - low) for left, right, low, high in pairs]
            slots = (16, width // plane_size())
            shapes += [jax.ShapeDtypeStruct(slots, F32)] + [jax.ShapeDtypeStruct(shape, F32) for shape in pieces]
            specs += [vmem] * (1 + len(pieces))
            scratch = scratch[:-1] + [pltpu.VMEM((3,) + shape, BF16) for shape in pieces]
            scratch += [pltpu.SemaphoreType.DMA((3, len(pairs)))] * 2
            scratch += [pltpu.VMEM((3, 16, width), F32), pltpu.VMEM((16, width), F32), pltpu.VMEM((8,) + slots, F32)]
            scratch += [pltpu.SemaphoreType.DMA((3,))] * 2 + [pltpu.SemaphoreType.DMA((8,))] * 2
        else:
            more = [ffn_out] + arrays
            shapes += [jax.ShapeDtypeStruct((rows // 4, width), BF16)] * 4 + outs
            specs += [vmem] * 4 + [ANYWHERE] * len(outs)
            scratch = scratch + [pltpu.SemaphoreType.DMA((len(pairs),))] * 2
    return pl.pallas_call(
        functools.partial(line_body, finish, keep_state, gain_sum, len(ins), extra),
        in_specs=[vmem] * (1 + len(ins) + len(more)),
        out_specs=specs,
        out_shape=shapes,
        scratch_shapes=[
            pltpu.VMEM((2, half, width), BF16),
            pltpu.VMEM((half, width), BF16),
            pltpu.VMEM((half, width), BF16),
            pltpu.SemaphoreType.DMA((4, count)),
            pltpu.SemaphoreType.DMA((5, count)),
        ]
        + scratch,
        compiler_params=pltpu.CompilerParams(
            collective_id=identity, has_side_effects=True, vmem_limit_bytes=VMEM_BYTES
        ),
        cost_estimate=pl.CostEstimate(flops=0, bytes_accessed=100 * rows * width, transcendentals=0),
    )(partial, *ins, *more)


def mean_square(values):
    return lax.rsqrt(jnp.mean(values * values, axis=1, keepdims=True) + EPSILON)


def finish_attention(total, whole, own, ins):
    tokens, gain = ins
    hidden = tokens[whole, :].astype(F32) + RESIDUAL_SCALE * total
    return (hidden * mean_square(hidden) * gain[...]).astype(BF16), hidden, None


def norm_pull(d_normed, values, gain):
    inverse = mean_square(values)
    scaled = gain * d_normed
    inner = jnp.mean(scaled * values, axis=1, keepdims=True)
    return inverse * scaled - values * inverse * inverse * inverse * inner, d_normed * values * inverse


def finish_ffn_back(total, whole, own, ins):
    hidden, grads, gain = ins
    pulled, gains = norm_pull(total, hidden[own, :], gain[...])
    d_hidden = grads[whole, :].astype(F32) + pulled
    return (RESIDUAL_SCALE * d_hidden).astype(BF16), d_hidden, gains


def finish_attention_back(total, whole, own, ins):
    tokens, d_hidden, gain = ins
    pulled, gains = norm_pull(total, tokens[whole, :].astype(F32), gain[...])
    return (d_hidden[own, :] + pulled).astype(BF16), None, gains


def front_fits():
    return lax.axis_size("shard") == 2 and lax.axis_size("context") == 4


def front_body(*refs):
    tokens, gain_piece, cosine, sine, w_query, w_key, w_value, w_output = refs[:8]
    normed, queries, kv, weight, output, gains = refs[8:14]
    local_sem, send, recv = refs[14:]
    me = plane_index()
    extent = weight.shape[0] // 8
    q_width = queries.shape[1]
    k_width = kv.shape[2] // 2
    context, shard = lax.axis_index("context"), lax.axis_index("shard")
    peers = {1: {"context": context ^ 1}, 2: {"context": context ^ 2}, 4: {"shard": shard ^ 1}}
    mesh_ids = pl.DeviceIdType.MESH
    barrier = pltpu.get_barrier_semaphore()
    for bit in (1, 2, 4):
        pl.semaphore_signal(barrier, inc=1, device_id=peers[bit], device_id_type=mesh_ids)

    def start(r):
        return pl.multiple_of((me ^ r) * extent, extent)

    def qkv_at(r, part=None):
        size = extent if part is None else extent // 2
        base = start(r) + (part or 0) * size
        return weight.at[pl.ds(pl.multiple_of(base, size), size)]

    def output_at(r, part=None):
        columns = pl.ds(start(r), extent)
        if part is None:
            return output.at[:, columns]
        size = output.shape[0] // 2
        return output.at[pl.ds(part * size, size), columns]

    def gains_at(r):
        return gains.at[:, pl.ds(start(r), extent)]

    spots = {}

    def remote(name, ref, bit, target=None):
        index = spots.setdefault(name, len(spots))
        return pltpu.make_async_remote_copy(
            src_ref=ref,
            dst_ref=ref if target is None else target,
            send_sem=send.at[index],
            recv_sem=recv.at[index],
            device_id=peers[bit],
            device_id_type=mesh_ids,
        )

    locals_ = [
        pltpu.make_async_copy(gain_piece, gains_at(0), local_sem.at[0]),
        pltpu.make_async_copy(w_query, weight.at[pl.ds(start(0), extent), pl.ds(0, q_width)], local_sem.at[1]),
        pltpu.make_async_copy(w_key, weight.at[pl.ds(start(0), extent), pl.ds(q_width, k_width)], local_sem.at[2]),
        pltpu.make_async_copy(
            w_value, weight.at[pl.ds(start(0), extent), pl.ds(q_width + k_width, k_width)], local_sem.at[3]
        ),
        pltpu.make_async_copy(w_output, output_at(0), local_sem.at[4]),
    ]
    for copy in locals_:
        copy.start()

    begun = []

    def begin(copy):
        copy.start()
        begun.append(copy)
        return copy

    pl.semaphore_wait(barrier, 3)
    locals_[0].wait()
    gain_in = [begin(remote("g2", gains_at(0), 2)), begin(remote("g4", gains_at(0), 4))]
    gain_core = [begin(remote("gc0", gains_at(0), 1))]
    for copy in locals_[1:4]:
        copy.wait()
    near, far = begin(remote("q2", qkv_at(0), 2)), begin(remote("q4", qkv_at(0), 4))
    core = [begin(remote("qc0", qkv_at(0), 1))]
    locals_[4].wait()
    out_near, out_far = begin(remote("o2", output_at(0), 2)), begin(remote("o4", output_at(0), 4))
    out_core = [begin(remote("oc0", output_at(0), 1))]

    gain_in[0].wait_recv()
    gain_in[1].wait_recv()
    diagonal = begin(remote("g6", gains_at(4), 2))
    gain_core += [begin(remote("gc2", gains_at(2), 1)), begin(remote("gc4", gains_at(4), 1))]
    diagonal.wait_recv()
    gain_core.append(begin(remote("gc6", gains_at(6), 1)))
    for copy in gain_core:
        copy.wait_recv()

    rows = tokens.shape[0]
    tile = 128

    def norm(i, carry):
        spot = pl.ds(pl.multiple_of(i * tile, tile), tile)
        values = tokens[spot, :].astype(F32)
        normed[spot, :] = (values * mean_square(values) * gains[0:1, :]).astype(BF16)
        return carry

    lax.fori_loop(0, rows // tile, norm, 0)

    far.wait_recv()
    cross = [begin(remote("q6a", qkv_at(4, 0), 2))]
    core.append(begin(remote("qc4", qkv_at(4), 1)))
    near.wait_recv()
    cross.append(begin(remote("q6b", qkv_at(2, 1), 4)))
    core.append(begin(remote("qc2", qkv_at(2), 1)))
    cross[0].wait_recv()
    cross[1].wait_recv()
    core.append(begin(remote("qc6", qkv_at(6), 1)))
    out_far.wait_recv()
    out_cross = [begin(remote("o6a", output_at(4, 0), 2))]
    out_core.append(begin(remote("oc4", output_at(4), 1)))
    out_near.wait_recv()
    out_cross.append(begin(remote("o6b", output_at(2, 1), 4)))
    out_core.append(begin(remote("oc2", output_at(2), 1)))
    for copy in core:
        copy.wait_recv()

    lane = lax.broadcasted_iota(jnp.int32, (1, LANES), 1)

    def rotated(part, spot):
        return part * cosine[spot, :] + turned(part, lane, 1.0) * sine[spot, :]

    def keys(i, carry):
        spot = pl.ds(pl.multiple_of(i * 256, 256), 256)
        part = jnp.dot(normed[spot, :], weight[:, q_width:], preferred_element_type=F32)
        kv[0, spot, :k_width] = rotated(part[:, :k_width], spot).astype(BF16)
        kv[0, spot, k_width:] = part[:, k_width:].astype(BF16)
        return carry

    lax.fori_loop(0, rows // 256, keys, 0)
    kv_near = begin(remote("k2", kv.at[0], 2, kv.at[2]))
    kv_core = begin(remote("k1", kv.at[0], 1, kv.at[1]))

    def query(i, carry):
        spot = pl.ds(pl.multiple_of(i * 256, 256), 256)
        part = jnp.dot(normed[spot, :], weight[:, :q_width], preferred_element_type=F32)
        for base in range(0, q_width, LANES):
            turned_part = rotated(part[:, base : base + LANES], spot).astype(BF16)
            queries[spot, base : base + LANES] = (turned_part * SCORE_SCALE).astype(BF16)
        return carry

    lax.fori_loop(0, rows // 256, query, 0)
    kv_near.wait_recv()
    kv_last = begin(remote("k3", kv.at[2], 1, kv.at[3]))
    out_cross[0].wait_recv()
    out_cross[1].wait_recv()
    out_core.append(begin(remote("oc6", output_at(6), 1)))
    for copy in out_core:
        copy.wait_recv()
    kv_core.wait_recv()
    kv_last.wait_recv()
    for copy in begun:
        copy.wait_send()


def front(tokens, gains, cosine, sine, w_query, w_key, w_value, w_output):
    rows, width = tokens.shape
    q_width, k_width = w_query.shape[1], w_key.shape[1]
    total = q_width + 2 * k_width
    vmem = pl.BlockSpec(memory_space=pltpu.VMEM)
    return pl.pallas_call(
        front_body,
        in_specs=[vmem] * 4 + [ANYWHERE] * 4,
        out_specs=[vmem] * 6,
        out_shape=[
            jax.ShapeDtypeStruct((rows, width), BF16),
            jax.ShapeDtypeStruct((rows, q_width), BF16),
            jax.ShapeDtypeStruct((4, rows, 2 * k_width), BF16),
            jax.ShapeDtypeStruct((width, total), BF16),
            jax.ShapeDtypeStruct((w_output.shape[0], width), BF16),
            jax.ShapeDtypeStruct((8, width), F32),
        ],
        scratch_shapes=[
            pltpu.SemaphoreType.DMA((5,)),
            pltpu.SemaphoreType.DMA((27,)),
            pltpu.SemaphoreType.DMA((27,)),
        ],
        compiler_params=pltpu.CompilerParams(collective_id=6, has_side_effects=True, vmem_limit_bytes=VMEM_BYTES),
        cost_estimate=pl.CostEstimate(
            flops=2 * rows * width * total, bytes_accessed=10 * rows * width, transcendentals=0
        ),
        name="front",
    )(tokens, gains, cosine, sine, w_query, w_key, w_value, w_output)


def unique_arrays(pairs):
    arrays, plan = [], []
    for left, right, low, high in pairs:
        spots = []
        for value in (left, right):
            known = [i for i, array in enumerate(arrays) if array is value]
            if not known:
                arrays.append(value)
            spots.append(known[0] if known else len(arrays) - 1)
        plan.append((spots[0], spots[1], low, high))
    return arrays, tuple(plan)


def grads_parts(count, plan, ins, outs, scratch, crossed=(), cross_sems=()):
    halves, jobs = count // 2, len(plan)
    sent, got, own = scratch[:jobs], scratch[jobs : 2 * jobs], scratch[2 * jobs : 3 * jobs]
    send, recv, done = scratch[3 * jobs : 3 * jobs + 3]
    kept = halves - 1 if crossed else halves
    cross = []
    for j, landed in enumerate(crossed):
        ways = ({"shard": lax.axis_index("shard") ^ 1}, {"context": lax.axis_index("context") ^ 2})
        cross.append(
            pltpu.make_async_remote_copy(
                src_ref=got[j].at[halves - 1],
                dst_ref=landed,
                send_sem=cross_sems[0].at[j],
                recv_sem=cross_sems[1].at[j],
                device_id=ways[j % 2],
                device_id_type=pl.DeviceIdType.MESH,
            )
        )
    me = plane_index()
    mate = {"context": lax.axis_index("context") ^ 1}

    def piece(j, r):
        left, right, low, high = plan[j]
        extent = ins[left].shape[1] // count
        columns = pl.ds(pl.multiple_of((me ^ r) * extent, extent), extent)
        return lax.dot_general(
            ins[left][:, columns], ins[right][:, low:high], (((0,), (0,)), ((), ())), preferred_element_type=F32
        )

    def across(j, i):
        return pltpu.make_async_remote_copy(
            src_ref=sent[j].at[i],
            dst_ref=got[j].at[i],
            send_sem=send.at[j, i],
            recv_sem=recv.at[j, i],
            device_id=mate,
            device_id_type=pl.DeviceIdType.MESH,
        )

    def odd(i):
        for j in range(jobs):
            sent[j][i] = piece(j, 2 * i + 1).astype(BF16)
            across(j, i).start()

    def even(i):
        for j in range(jobs):
            value = piece(j, 2 * i)
            across(j, i).wait_recv()
            value = value + got[j][i].astype(F32)

            @pl.when(i > 0)
            def _():
                got[j][i] = value.astype(BF16)

            @pl.when(i == 0)
            def _():
                own[j][...] = value

        for known in range(kept):

            @pl.when(i == known)
            def _():
                for j in range(jobs):
                    source = got[j].at[known] if known else own[j]
                    pltpu.make_async_copy(source, outs[known * jobs + j], done.at[known, j]).start()

        if crossed:

            @pl.when(i == halves - 1)
            def _():
                for copy in cross:
                    copy.start()

    def work(q):
        @pl.when(q < halves)
        def _():
            odd(halves - 1 - q)

        @pl.when(q >= halves)
        def _():
            even(count - 1 - q)

    def finish():
        for known in range(halves):
            for j in range(jobs):
                source = got[j].at[known] if known else own[j]
                if known < kept:
                    pltpu.make_async_copy(source, outs[known * jobs + j], done.at[known, j]).wait()
                across(j, known).wait_send()
        for copy in cross:
            copy.wait()

    return work, finish


def plane_parts(count, plan, ins, outs, scratch):
    jobs = len(plan)
    sent, got, own = scratch[:jobs], scratch[jobs : 2 * jobs], scratch[2 * jobs : 3 * jobs]
    send, recv = scratch[3 * jobs : 3 * jobs + 2]
    landed = scratch[3 * jobs + 2 : 4 * jobs + 2]
    plane_send, plane_recv = scratch[4 * jobs + 2 :]
    me = plane_index()
    core = {"context": lax.axis_index("context") ^ 1}
    peers = ({"context": lax.axis_index("context") ^ 2}, {"shard": lax.axis_index("shard") ^ 1})

    def piece(j, r):
        left, right, low, high = plan[j]
        extent = ins[left].shape[1] // count
        columns = pl.ds(pl.multiple_of((me ^ r) * extent, extent), extent)
        return lax.dot_general(
            ins[left][:, columns], ins[right][:, low:high], (((0,), (0,)), ((), ())), preferred_element_type=F32
        )

    def across(j, i):
        return pltpu.make_async_remote_copy(
            src_ref=sent[j].at[i],
            dst_ref=got[j].at[i],
            send_sem=send.at[j, i],
            recv_sem=recv.at[j, i],
            device_id=core,
            device_id_type=pl.DeviceIdType.MESH,
        )

    def move(j, i, slot, way):
        return pltpu.make_async_remote_copy(
            src_ref=got[j].at[i],
            dst_ref=landed[j].at[slot],
            send_sem=plane_send.at[slot, j],
            recv_sem=plane_recv.at[slot, j],
            device_id=peers[way],
            device_id_type=pl.DeviceIdType.MESH,
        )

    first = [(j + 1) % 2 for j in range(jobs)]
    cross = [move(j, 3, 2, first[j]) for j in range(jobs)]
    early = [move(j, 2 if first[j] else 1, 1 if first[j] else 0, first[j]) for j in range(jobs)]
    late = [move(j, 1 if first[j] else 2, 0 if first[j] else 1, 1 - first[j]) for j in range(jobs)]

    def work(q):
        @pl.when(q < 4)
        def _():
            i = 3 - q
            for j in range(jobs):
                sent[j][i] = piece(j, 2 * i + 1).astype(BF16)
                across(j, i).start()

        @pl.when(q == 8)
        def _():
            for j in range(jobs):
                kept = 1 if first[j] else 2
                cross[j].wait_recv()
                got[j][kept] = (got[j][kept].astype(F32) + landed[j][2].astype(F32)).astype(BF16)
                late[j].start()

        @pl.when((q >= 4) & (q < 8))
        def _():
            i = 7 - q
            for j in range(jobs):
                value = piece(j, 2 * i)
                across(j, i).wait_recv()
                value = value + got[j][i].astype(F32)

                @pl.when(i > 0)
                def _():
                    got[j][i] = value.astype(BF16)

                @pl.when(i == 0)
                def _():
                    own[j][...] = value

        @pl.when(q == 4)
        def _():
            for j in range(jobs):
                cross[j].start()

        @pl.when(q == 7)
        def _():
            for j in range(jobs):
                early[j].start()

    def rest():
        for j in range(jobs):
            early[j].wait_recv()
            late[j].wait_recv()
            outs[j][...] = own[j][...] + landed[j][0].astype(F32) + landed[j][1].astype(F32)

    def finish():
        for j in range(jobs):
            for copy in (cross[j], early[j], late[j]):
                copy.wait_send()
            for i in range(4):
                across(j, i).wait_send()

    return work, rest, finish


def grads_body(count, n_in, plan, *refs):
    ins, rest = refs[:n_in], refs[n_in:]
    spread = count // 2 * len(plan)
    outs, scratch = rest[:spread], rest[spread:]
    work, finish = grads_parts(count, plan, ins, outs, scratch)
    barrier = pltpu.get_barrier_semaphore()
    mate = {"context": lax.axis_index("context") ^ 1}
    pl.semaphore_signal(barrier, inc=1, device_id=mate, device_id_type=pl.DeviceIdType.MESH)
    pl.semaphore_wait(barrier, 1)

    def step(q, carry):
        work(q)
        return carry

    lax.fori_loop(0, count, step, 0)
    finish()


def grads_shapes(pairs):
    count = plane_size()
    halves = count // 2
    shapes = [(left.shape[1] // count, high - low) for left, right, low, high in pairs]
    outs = [jax.ShapeDtypeStruct(shape, BF16 if i else F32) for i in range(halves) for shape in shapes]
    scratch = [pltpu.VMEM((halves,) + shape, BF16) for shape in shapes] * 2
    scratch += [pltpu.VMEM(shape, F32) for shape in shapes]
    sems = [(len(pairs), halves), (len(pairs), halves), (halves, len(pairs))]
    return outs, scratch + [pltpu.SemaphoreType.DMA(shape) for shape in sems]


def grads_named(flat, jobs):
    return [{2 * i: flat[i * jobs + j] for i in range(len(flat) // jobs)} for j in range(jobs)]


def grads_fit(pairs):
    return all((pair[0].shape[1] // plane_size()) % LANES == 0 for pair in pairs)


def plane_grads(pairs, identity):
    count = plane_size()
    jobs = len(pairs)
    extents = [pair[0].shape[1] // count for pair in pairs]
    arrays, plan = unique_arrays(pairs)
    if not grads_fit(pairs):
        me = plane_index()
        sides = []
        for (left, right, low, high), e in zip(pairs, extents):
            columns = lambda r: lax.dynamic_slice_in_dim(left, (me ^ r) * e, e, 1)
            whole = {r: weight_grad(columns(r), right[:, low:high]).astype(BF16) for r in range(count)}
            sides.append({r: take_sum(whole, 1, r) for r in range(0, count, 2)})
        return sides
    outs, scratch = grads_shapes(pairs)
    flat = pl.pallas_call(
        functools.partial(grads_body, count, len(arrays), plan),
        in_specs=[pl.BlockSpec(memory_space=pltpu.VMEM)] * len(arrays),
        out_specs=[ANYWHERE] * len(outs),
        out_shape=outs,
        scratch_shapes=scratch,
        compiler_params=pltpu.CompilerParams(
            collective_id=identity, has_side_effects=True, vmem_limit_bytes=VMEM_BYTES
        ),
        cost_estimate=pl.CostEstimate(
            flops=sum(2 * left.shape[0] * left.shape[1] * (high - low) for left, _, low, high in pairs),
            bytes_accessed=sum(2 * left.shape[1] * (high - low) for left, _, low, high in pairs),
            transcendentals=0,
        ),
    )(*arrays)
    return grads_named(flat, jobs)


def after(value, *others):
    return lax.optimization_barrier((value,) + others)[0] if others else value


def gather_context(piece):
    size = lax.axis_size("context")
    held = {0: piece}
    bit = size // 2
    while bit:
        for r in list(held):
            held[r | bit] = swap(held[r], "context", size, bit)
        bit //= 2
    return [held[r] for r in range(size)]


def reduce_context(pieces, *waits):
    size = len(pieces)
    held = dict(enumerate(pieces))
    bit = 1
    while bit < size:
        final = 2 * bit == size
        held = {
            r: after(held[r], *(waits if final else ())).astype(F32)
            + swap(held[r | bit].astype(BF16), "context", size, bit).astype(F32)
            for r in held
            if not r & bit
        }
        bit *= 2
    return held[0]


def stored_places(order_row, first, count):
    stored = first + jnp.arange(count, dtype=jnp.int32)
    picks = (stored // BLK)[:, None] == jnp.arange(order_row.shape[0], dtype=jnp.int32)[None, :]
    return jnp.sum(jnp.where(picks, order_row[None, :], 0), axis=1) * BLK + stored % BLK


def rope_tables(order, local_len):
    first = lax.axis_index("context") * local_len
    places = jnp.concatenate([stored_places(order[s], first, local_len) for s in range(order.shape[0])])
    half = HD // 2
    inverse = jnp.exp(jnp.arange(half, dtype=F32) * (-2.0 * math.log(ROPE_BASE) / HD))
    angles = places.astype(F32)[:, None] * jnp.tile(inverse, LANES // half)[None, :]
    return jnp.cos(angles), jnp.sin(angles)


def weight_grad(left, right):
    return lax.dot_general(left, right, (((0,), (0,)), ((), ())), preferred_element_type=F32)


def local(
    tokens, block_order, w_query, w_key, w_value, w_output, w_gate, w_up, w_down, norm_attn, norm_ffn, grad_out
):
    seqs, local_len, width = tokens.shape
    rows = seqs * local_len
    size = plane_size()
    z = lax.axis_index("tensor")
    token_rows = tokens.reshape(rows, width)
    grad_rows = grad_out.reshape(rows, width)
    q_width, kv_width = w_query.shape[1], w_key.shape[1]
    units = w_down.shape[0]
    half = units // 2

    cosine, sine = rope_tables(block_order, local_len)
    if front_fits():
        gain_piece = jnp.pad(jnp.stack([norm_attn, norm_ffn]).astype(F32), ((0, 6), (0, 0)))
        normed, queries, kv_pieces, w_qkv, w_out, gains = front(
            token_rows, gain_piece, cosine, sine, w_query, w_key, w_value, w_output
        )
        qkv_pieces, output_pieces = [w_qkv], [w_out]
        early, late = [queries], [queries]
        gain_attn, gain_ffn = gains[0:1], gains[1:2]
    else:
        gains = gather_small(jnp.stack([norm_attn, norm_ffn])).reshape(2, width)
        gain_attn, gain_ffn = gains[0:1], gains[1:2]
        w_qkv = jnp.concatenate([w_query, w_key, w_value], axis=1)
        qkv_pieces, output_pieces = gather_pair(w_qkv, w_output)
        normed, queries, keys_values = project_qkv(token_rows, gain_attn, cosine, sine, qkv_pieces, q_width)
        kv_pieces = jnp.stack(gather_context(keys_values))
        early, late = [qkv_pieces[-2]], [kv_pieces]
        output_pieces = widened(output_pieces)
    mixture, logs = attend(block_order, queries, kv_pieces)
    branch = gathered_matmul(mixture, output_pieces, 1, False)
    normed_ffn, hidden = line_sum(branch, [token_rows, gain_ffn], finish_attention, True, False, 0)
    extent = width // size
    pushed = extent % (2 * LANES) == 0
    order = (early, late, [mixture], [normed_ffn], not pushed)
    gate_pieces, up_pieces = gather_pair(w_gate, w_up, *order)
    order = (early, late, [normed_ffn], [normed_ffn], not pushed)
    if pushed:
        low_pieces, high_pieces = gather_pair(w_down[:, : extent // 2], w_down[:, extent // 2 :], *order)
    else:
        low_pieces, high_pieces = gather_pair(w_down[:half], w_down[half:], *order)
        low_pieces, high_pieces = widened(low_pieces), widened(high_pieces)
    d_ffn = (RESIDUAL_SCALE * grad_rows.astype(F32)).astype(BF16)
    active, d_gate, d_up, ffn_out, d_normed_ffn = ffn(
        normed_ffn, d_ffn, gate_pieces, up_pieces, low_pieces, high_pieces, pushed
    )
    pairs = [
        (normed_ffn, d_gate, 0, units),
        (normed_ffn, d_up, 0, units),
        (d_ffn, active, 0, half),
        (d_ffn, active, half, units),
    ]
    sum_ins = [hidden, grad_rows, gain_ffn]
    fused = grads_fit(pairs) and front_fits()
    if fused:
        d_branch, d_hidden, ffn_gain, *flat = line_sum(
            d_normed_ffn, sum_ins, finish_ffn_back, True, True, 1, ffn_out, pairs
        )
        out_chunks, jobs = flat[:4], len(pairs)
        grad_gate, grad_up, grad_low, grad_high = grads_named(flat[4:], jobs)
    else:
        grad_gate, grad_up, grad_low, grad_high = plane_grads(pairs, 3)
        d_branch, d_hidden, ffn_gain = line_sum(
            after(d_normed_ffn, grad_gate[0]), sum_ins, finish_ffn_back, True, True, 1
        )
        padded = lax.dynamic_update_slice_in_dim(jnp.zeros((rows, width), F32), hidden, (z // 2) * (rows // 2), 0)
        out_part = RESIDUAL_SCALE * ffn_out.astype(F32) + jnp.where(lax.rem(z, 3) != 0, padded, 0.0)
        out_chunks = [chunk_of(out_part.astype(BF16), lax.rem(z + shift, 4), rows // 4) for shift in range(4)]
    layer_out = rows_gather(rows_sum(out_chunks).astype(BF16))

    d_mixture = gathered_matmul(d_branch, output_pieces, 1, True)
    d_queries, *d_pieces = attend_back(block_order, queries, d_mixture, logs, kv_pieces)
    if fused:
        grad_gate = crossed_sum(grad_gate, 2, d_mixture, ())
        grad_low = crossed_sum(grad_low, 2, d_mixture, ())
        d_keys_values = reduce_context(d_pieces, grad_gate)
        grad_up = crossed_sum(grad_up, 4, d_mixture, [d_keys_values])
        grad_high = crossed_sum(grad_high, 4, d_mixture, [d_keys_values])
    else:
        d_keys_values = reduce_context(d_pieces)
        grad_gate, grad_up = reduce_pair(grad_gate, grad_up, [d_keys_values])
        grad_low, grad_high = reduce_pair(grad_low, grad_high, [d_keys_values])
    d_qkv, d_normed = project_qkv_back(d_queries, d_keys_values, cosine, sine, qkv_pieces)
    pairs = [(normed, d_qkv, 0, d_qkv.shape[1]), (d_branch, mixture, 0, q_width)]
    sum_ins = [token_rows, d_hidden, gain_attn]
    if grads_fit(pairs) and front_fits():
        grad_tokens, attn_gain, gain_rows, grad_qkv, grad_output = line_sum(
            d_normed, sum_ins, finish_attention_back, False, True, 2, None, pairs, ffn_gain
        )
        gain_grads = jnp.sum(gain_rows.reshape(2, 8, width // size), axis=1)
    else:
        grad_qkv, grad_output = plane_grads(pairs, 4)
        grad_tokens, attn_gain = line_sum(after(d_normed, grad_qkv[0]), sum_ins, finish_attention_back, False, True, 2)
        grad_qkv, grad_output = reduce_pair(grad_qkv, grad_output)
        gain_grads = gains_sum(jnp.stack([jnp.sum(attn_gain, axis=0), jnp.sum(ffn_gain, axis=0)]))
    grad_tokens = grad_tokens.astype(F32)
    return (
        layer_out.reshape(seqs, local_len, width),
        grad_tokens.reshape(seqs, local_len, width),
        grad_qkv[:, :q_width],
        grad_qkv[:, q_width : q_width + kv_width],
        grad_qkv[:, q_width + kv_width :],
        grad_output.T,
        grad_gate,
        grad_up,
        jnp.concatenate([grad_low.T, grad_high.T], axis=0),
        gain_grads[0],
        gain_grads[1],
    )


def solution(mesh):
    split = P("shard", "context", None)
    inward, outward = P(PLANE, "tensor"), P("tensor", PLANE)
    gain = P(PLANE)
    return jax.shard_map(
        local,
        mesh=mesh,
        in_specs=(split, P("shard", None), inward, inward, inward, outward, inward, inward, outward, gain, gain, split),
        out_specs=(split, split, inward, inward, inward, outward, inward, inward, outward, gain, gain),
        check_vma=False,
    )
```
